32 devices in a mesh: dp: 8 (over y, x, core), tensor: 4 (over z).
Axes of the slice: x: 2, y: 2, z: 4, core: 2. Of those that a mesh axis runs over, the one named last changes fastest.
Arguments:
- tokens_in: bfloat16 [16384, 1024], P(('dp', 'tensor'))
- out_grad: bfloat16 [16384, 1024], P(('dp', 'tensor')), may hold values from -6 to 6
- lengths: int32 [8, 4], P('dp'), may hold values from 1 to 1024, 2048 in all within a row
- owners: int32 [12], replicated, may hold values from 0 to 7, as said below
- matrix_master: float32 [4, 16, 256, 1024], P('tensor', 'dp')
- matrix_m1: float32 [4, 16, 256, 1024], P('tensor', 'dp')
- matrix_m2: float32 [4, 16, 256, 1024], P('tensor', 'dp'), as said below
- shared_params: float32 [3, 6, 1024], replicated, as said below
- bias_params: float32 [3, 4, 1792], P(None, 'tensor'), as said below
Outputs:
- layer_out: float32 [16384, 1024], P(('dp', 'tensor'))
- input_grad: float32 [16384, 1024], P(('dp', 'tensor'))
- head_max: float32 [16], P('tensor')
- matrix_grad: float32 [4, 16, 256, 1024], P('tensor', 'dp')
- matrix_moment1: float32 [4, 16, 256, 1024], P('tensor', 'dp')
- matrix_moment2: float32 [4, 16, 256, 1024], P('tensor', 'dp')
- matrix_new: float32 [4, 16, 256, 1024], P('tensor', 'dp')
- shared_out: float32 [2, 6, 1024], replicated
- shared_second: float32 [6, 1024], replicated
- shared_new: float32 [6, 1024], replicated
- bias_out: float32 [2, 4, 1792], P(None, 'tensor')
- bias_second: float32 [4, 1792], P('tensor')
- bias_new: float32 [4, 1792], P('tensor')
The draws below stay inside these ranges and needn't reach their ends.
Inputs may be any that keep to these rules, and one draw needn't show every extreme that they name: `owners`: each index of dp owns at most 2 units, and some index owns exactly 2. `matrix_m2`: entries are positive. `shared_params`: second moments (first index 2) are positive. `bias_params`: second moments (first index 2) are positive.
All inputs are finite; a program needn't handle non-finite values.
Results may differ from the reference program's by a relative error of at most 0.017.
Values may be sent and summed in bfloat16 or wider, within the bound.
A program may use at most 192 MiB of HBM per device.

```python
import math
import jax
import jax.numpy as jnp
import numpy as np
from jax import lax

D = 1024
H = 16
HD = 64
FF = 4096
SEQ = 2048
BLK = 512
CAP = 2
STEP = 10
DOCS = 4
DOC_MOST = 1024
TOKENS = 16384
NU = 12
U = 256
BW = 1792
N_DP = 8
N_TENSOR = 4


def owner_table(key):
    shuffled = jax.random.permutation(jax.random.fold_in(key, 11), N_DP * CAP)
    return (shuffled[:NU] // CAP).astype(jnp.int32)


def slot_units(key):
    owner_list = owner_table(key)
    unit_order = jnp.arange(NU, dtype=jnp.int32)
    same_owner = owner_list[:, None] == owner_list[None, :]
    earlier = unit_order[None, :] < unit_order[:, None]
    rank_counts = jnp.sum((same_owner & earlier).astype(jnp.int32), axis=1)
    slot_of_unit = owner_list * CAP + rank_counts
    matches = jnp.arange(N_DP * CAP, dtype=jnp.int32)[:, None] == slot_of_unit[None, :]
    return jnp.sum(matches.astype(jnp.int32) * unit_order[None, :], axis=1)


def row_scales(key):
    unit_of_slot = slot_units(key)
    head_rows = D // N_TENSOR
    ff_rows = FF // N_TENSOR
    heads_here = H // N_TENSOR
    row_index = (unit_of_slot[:, None] * U + jnp.arange(U, dtype=jnp.int32)[None, :])[None]
    head_factors = jnp.exp(jax.random.uniform(jax.random.fold_in(key, 23), (2, H), minval=0.0, maxval=math.log(1.7)))
    local_head = jnp.minimum(jnp.where(row_index < head_rows, row_index // HD, (row_index - head_rows) // HD), heads_here - 1)
    head_index = jnp.arange(N_TENSOR, dtype=jnp.int32)[:, None, None] * heads_here + local_head
    drawn_std = 1.0 / math.sqrt(D)
    weight_std = jnp.where(row_index < head_rows, head_factors[0][head_index] * drawn_std, jnp.where(row_index < 2 * head_rows, head_factors[1][head_index] * drawn_std, jnp.where(row_index < 3 * head_rows, drawn_std, jnp.where(row_index < 4 * head_rows, 1.0 / math.sqrt(D // 8), jnp.where(row_index < 4 * head_rows + ff_rows, drawn_std, 1.0 / math.sqrt(FF))))))
    grad_size = jnp.where(row_index < 3 * head_rows, 1.5, jnp.where(row_index < 4 * head_rows, 0.5, jnp.where(row_index < 4 * head_rows + ff_rows, 0.3, 0.65))) * math.sqrt(TOKENS)
    return (weight_std.astype(jnp.float32), grad_size.astype(jnp.float32))


def signed_noise(key, shape):
    return jax.random.normal(key, shape)


def positive_factor(key, shape):
    return jnp.exp(jax.random.uniform(key, shape, minval=0.0, maxval=math.log(4.0)))


def draw_owners(key, part):
    return owner_table(key)


def draw_matrix_master(key, part):
    weight_std, grad_size = row_scales(key)
    noise_draw = signed_noise(jax.random.fold_in(key, 31), (N_TENSOR, N_DP * CAP, U, D))
    return (noise_draw * weight_std[..., None]).astype(jnp.float32)


def draw_matrix_m1(key, part):
    weight_std, grad_size = row_scales(key)
    noise_draw = signed_noise(jax.random.fold_in(key, 37), (N_TENSOR, N_DP * CAP, U, D))
    return (noise_draw * grad_size[..., None] / 9.0).astype(jnp.float32)


def draw_matrix_m2(key, part):
    weight_std, grad_size = row_scales(key)
    factor_draw = positive_factor(jax.random.fold_in(key, 41), (N_TENSOR, N_DP * CAP, U, D))
    return (factor_draw * (grad_size * grad_size)[..., None] * (0.05 / 0.95)).astype(jnp.float32)


def draw_shared_params(key, part):
    gain_rows = jnp.array([1.0, 0.0, 0.0, 1.0, 0.0, 0.0], jnp.float32)[:, None]
    gains_draw = jnp.exp(jax.random.uniform(jax.random.fold_in(key, 51), (6, D), minval=math.log(0.5), maxval=math.log(2.0)))
    shifts_draw = 0.3 * signed_noise(jax.random.fold_in(key, 52), (6, D))
    values_now = gain_rows * gains_draw + (1.0 - gain_rows) * shifts_draw
    grad_size = jnp.array([2.5, 2.5, 1.1, 0.6, 0.6, 1.0], jnp.float32)[:, None] * math.sqrt(TOKENS)
    first_draw = signed_noise(jax.random.fold_in(key, 53), (6, D)) * grad_size / 9.0
    second_draw = positive_factor(jax.random.fold_in(key, 54), (6, D)) * grad_size * grad_size * (0.05 / 0.95)
    return jnp.stack([values_now, first_draw, second_draw]).astype(jnp.float32)


def draw_bias_params(key, part):
    columns = jnp.arange(BW, dtype=jnp.int32)[None, :]
    values_now = 0.2 * signed_noise(jax.random.fold_in(key, 61), (N_TENSOR, BW))
    grad_size = jnp.where(columns < 3 * (D // N_TENSOR), 1.5, 0.3) * math.sqrt(TOKENS)
    first_draw = signed_noise(jax.random.fold_in(key, 62), (N_TENSOR, BW)) * grad_size / 9.0
    second_draw = positive_factor(jax.random.fold_in(key, 63), (N_TENSOR, BW)) * grad_size * grad_size * (0.05 / 0.95)
    return jnp.stack([values_now, first_draw, second_draw]).astype(jnp.float32)


def draw_tokens_in(key, part):
    row_scale = jnp.exp(jax.random.uniform(jax.random.fold_in(key, 71), (TOKENS, 1), minval=math.log(0.4), maxval=math.log(4.0)))
    column_scale = jnp.exp(jax.random.uniform(jax.random.fold_in(key, 72), (1, D), minval=math.log(0.6), maxval=math.log(1.7)))
    offsets = jax.random.uniform(jax.random.fold_in(key, 73), (TOKENS, 1), minval=-0.5, maxval=0.5)
    noise_draw = signed_noise(jax.random.fold_in(key, 74), (TOKENS, D))
    return (row_scale * (noise_draw * column_scale + offsets)).astype(jnp.bfloat16)


def block_levels(rng, dims, shards, low, top_value):
    def one(position, blocks):
        heights = jax.random.uniform(jax.random.fold_in(jax.random.fold_in(rng, 6), position), (blocks,), jnp.float32, low / len(shards), top_value / len(shards))
        return jnp.repeat(jnp.exp(heights), dims[position] // blocks).reshape((-1,) + (1,) * (len(dims) - position - 1))

    loudness = one(*shards[0])
    for cut in shards[1:]:
        loudness = loudness * one(*cut)
    return loudness


def length_profile(count, total, limit, skew):
    loads = [(1 << 20) // math.isqrt(standing ** skew) + 1 for standing in range(2, count + 1)]
    rest, given = total - limit - (count - 1), [1] * (count - 1)
    while rest > 0:
        candidates = [i for i in range(count - 1) if given[i] < limit]
        mass, budget = sum([loads[i] for i in candidates]), rest
        for i in candidates:
            addition = min(limit - given[i], max(1, budget * loads[i] // mass), rest)
            given[i] = given[i] + addition
            rest = rest - addition
    return np.array([limit] + given)


def uneven(key, count, total, limit, lean):
    if count == 2:
        one = jax.random.randint(key, (), max(1, total - limit), min(limit, total - 1) + 1)
        return jnp.stack([one, total - one])
    sizes = jnp.asarray(length_profile(count, total, limit, lean), jnp.int32)
    couples = (count - 1) // 2
    donor, sink = sizes[1:1 + 2 * couples:2], sizes[2:2 + 2 * couples:2]
    room = jnp.minimum(donor - 1, limit - sink)
    moved = jax.random.randint(jax.random.fold_in(key, 1), (couples,), 0, 1 << 20) % (room + 1)
    sizes = sizes.at[1:1 + 2 * couples:2].set(donor - moved).at[2:2 + 2 * couples:2].set(sink + moved)
    return sizes[jax.random.permutation(jax.random.fold_in(key, 2), count)]


def bell_draw(rng, dims, scale, bound, shards=(), kind=jnp.bfloat16):
    level = block_levels(rng, dims, shards, -0.22, 0.18) if shards else 1.0
    entries = jax.random.normal(rng, dims, jnp.float32) * scale * level
    return jnp.minimum(jnp.maximum(entries, -bound), bound).astype(kind)


def setup_inputs(seed: int = 0) -> dict:
    arg_keys = jax.random.split(jax.random.key(seed), 10)
    return {
        "tokens_in": draw_tokens_in(jax.random.fold_in(arg_keys[9], 71), 0),
        "out_grad": bell_draw(arg_keys[1], (TOKENS, D), 1.0, 6.0, ((0, 32),)),
        "lengths": jax.vmap(lambda own: uneven(own, DOCS, SEQ, DOC_MOST, 2))(jax.random.split(arg_keys[2], N_DP)).reshape((N_DP, DOCS)).astype(jnp.int32),
        "owners": draw_owners(jax.random.fold_in(arg_keys[9], 71), 0),
        "matrix_master": draw_matrix_master(jax.random.fold_in(arg_keys[9], 71), 0),
        "matrix_m1": draw_matrix_m1(jax.random.fold_in(arg_keys[9], 71), 0),
        "matrix_m2": draw_matrix_m2(jax.random.fold_in(arg_keys[9], 71), 0),
        "shared_params": draw_shared_params(jax.random.fold_in(arg_keys[9], 71), 0),
        "bias_params": draw_bias_params(jax.random.fold_in(arg_keys[9], 71), 0),
    }


@jax.custom_vjp
def low(v):
    return lax.optimization_barrier(v.astype(jnp.bfloat16)).astype(jnp.float32)

@jax.custom_vjp
def low_back(v):
    return v

def low_keep(v):
    return (low(v), None)

def low_pass(kept, grad):
    return (grad,)

def back_keep(v):
    return (v, None)

def back_low(kept, grad):
    return (low(grad),)
low.defvjp(low_keep, low_pass)
low_back.defvjp(back_keep, back_low)
EPS_NORM = 1e-05
BETA_ONE = 0.9
BETA_TWO = 0.95
LEARN_RATE = 0.08
WEIGHT_DECAY = 0.1
EPS_ADAM = 1e-08
CLIP_TAU = 10.0
MASKED = -1e+30

def matmul(left, right):
    return jnp.dot(left, right, precision=lax.Precision.HIGHEST)

def norm_rows(values_in, gain, shift):
    centre = lax.optimization_barrier(jnp.mean(values_in, axis=-1, keepdims=True))
    shifted = values_in - centre
    spread = lax.optimization_barrier(jnp.mean(shifted * shifted, axis=-1, keepdims=True))
    return shifted * lax.rsqrt(spread + EPS_NORM) * gain + shift

def segment_ids(lengths, seq_len):
    bounds = jnp.cumsum(lengths, axis=-1)
    places = jnp.arange(seq_len, dtype=jnp.int32)
    return lax.optimization_barrier(jnp.sum((places[None, :, None] >= bounds[:, None, :]).astype(jnp.int32), axis=-1))

def slot_tables(owners, n_slots, slot_cap):
    n_units = owners.shape[0]
    unit_order = jnp.arange(n_units, dtype=jnp.int32)
    same_owner = owners[:, None] == owners[None, :]
    earlier = unit_order[None, :] < unit_order[:, None]
    rank_counts = lax.optimization_barrier(jnp.sum((same_owner & earlier).astype(jnp.int32), axis=1))
    slot_of_unit = (owners * slot_cap + rank_counts).astype(jnp.int32)
    matches = jnp.arange(n_slots, dtype=jnp.int32)[:, None] == slot_of_unit[None, :]
    occupied = jnp.any(matches, axis=1)
    unit_of_slot = lax.optimization_barrier(jnp.sum(matches.astype(jnp.int32) * unit_order[None, :], axis=1)).astype(jnp.int32)
    return (slot_of_unit, unit_of_slot, occupied)

def attend(queries, keys_in, values_in, segments):
    seq_len = queries.shape[0]
    n_blocks = seq_len // BLK
    score_scale = 1.0 / math.sqrt(HD)
    places = jnp.arange(seq_len, dtype=jnp.int32)

    def one_block(block_index):
        q_blk = lax.dynamic_slice_in_dim(queries, block_index * BLK, BLK, 0)
        q_places = lax.dynamic_slice_in_dim(places, block_index * BLK, BLK, 0)
        q_segments = lax.dynamic_slice_in_dim(segments, block_index * BLK, BLK, 0)
        raw_scores = jnp.einsum('qhd,khd->hqk', q_blk, keys_in, precision=lax.Precision.HIGHEST)
        scores = low_back(raw_scores * score_scale)
        allowed = (q_places[:, None] >= places[None, :]) & (q_segments[:, None] == segments[None, :])
        masked = jnp.where(allowed[None], scores, MASKED)
        log_norm = jax.nn.logsumexp(masked, axis=-1, keepdims=True)
        weights = low(jnp.exp(masked - log_norm))
        block_out = jnp.einsum('hqk,khd->qhd', weights, values_in, precision=lax.Precision.HIGHEST)
        return (block_out, lax.optimization_barrier(jnp.max(masked, axis=(1, 2))))
    block_outs, peaks = lax.map(jax.checkpoint(one_block), jnp.arange(n_blocks, dtype=jnp.int32))
    return (block_outs.reshape(seq_len, H * HD), lax.optimization_barrier(jnp.max(peaks, axis=0)))

def adam_step(param, grad, first, second, steps_done, decay):
    first_new = BETA_ONE * first + (1.0 - BETA_ONE) * grad
    second_new = BETA_TWO * second + (1.0 - BETA_TWO) * grad * grad
    fix_one = 1.0 - BETA_ONE ** steps_done
    fix_two = 1.0 - BETA_TWO ** steps_done
    direction = first_new / fix_one / (jnp.sqrt(second_new / fix_two) + EPS_ADAM)
    return (first_new, second_new, param - LEARN_RATE * (direction + decay * param))

def reference(tokens_in, out_grad, lengths, owners, matrix_master, matrix_m1, matrix_m2, shared_params, bias_params):
    head_rows = D // N_TENSOR
    ff_rows = FF // N_TENSOR
    heads_here = H // N_TENSOR
    n_units = owners.shape[0]
    stack_rows = n_units * U
    slot_of_unit, unit_of_slot, occupied = slot_tables(owners, N_DP * CAP, CAP)
    segments = segment_ids(lengths, SEQ)
    inputs_all = tokens_in.astype(jnp.float32).reshape(N_DP, SEQ, D)
    cotangent = out_grad.astype(jnp.float32).reshape(N_DP, SEQ, D)

    def whole_layer(inputs_in, master, shared, biases):
        weights = low(master)
        stacked = jnp.take(weights, slot_of_unit, axis=1).reshape(N_TENSOR, stack_rows, D)

        def matrix_part(first_row, row_count, total_rows):
            return stacked[:, first_row:first_row + row_count].reshape(total_rows, D)
        w_query = matrix_part(0, head_rows, D)
        w_key = matrix_part(head_rows, head_rows, D)
        w_value = matrix_part(2 * head_rows, head_rows, D)
        w_out = matrix_part(3 * head_rows, head_rows, D)
        w_fc = matrix_part(4 * head_rows, ff_rows, FF)
        w_proj = matrix_part(4 * head_rows + ff_rows, ff_rows, FF)
        b_query = biases[:, :head_rows].reshape(D)
        b_key = biases[:, head_rows:2 * head_rows].reshape(D)
        b_value = biases[:, 2 * head_rows:3 * head_rows].reshape(D)
        b_fc = biases[:, 3 * head_rows:].reshape(FF)

        def one_sequence(pair):
            seq_in, seq_segments = pair
            normed = low(norm_rows(seq_in, shared[0], shared[1]))
            queries = low(low_back(matmul(normed, w_query.T) + b_query)).reshape(SEQ, H, HD)
            keys_in = low(low_back(matmul(normed, w_key.T) + b_key)).reshape(SEQ, H, HD)
            values_in = low(low_back(matmul(normed, w_value.T) + b_value)).reshape(SEQ, H, HD)
            attended, peak_max = attend(queries, keys_in, values_in, seq_segments)
            attended = low(low_back(attended))
            hidden = seq_in + low_back(matmul(attended, w_out) + shared[2])
            normed_two = low(norm_rows(hidden, shared[3], shared[4]))
            pre_act = low_back(matmul(normed_two, w_fc.T) + b_fc)
            activ = low(jax.nn.gelu(pre_act, approximate=True))
            result = hidden + low_back(matmul(activ, w_proj) + shared[5])
            return (result, peak_max)
        return lax.map(jax.checkpoint(one_sequence), (inputs_in, segments))
    layer_out, vjp_fn, peaks = jax.vjp(whole_layer, inputs_all, matrix_master, shared_params[0], bias_params[0], has_aux=True)
    grad_inputs, grad_master, grad_shared, grad_bias = vjp_fn(cotangent)
    head_max = lax.optimization_barrier(jnp.max(peaks, axis=0))
    steps_done = float(STEP)
    keep = occupied[None, :, None, None]
    grad_master = jnp.where(keep, grad_master, 0.0)
    first_new, second_new, master_new = adam_step(matrix_master, grad_master, matrix_m1, matrix_m2, steps_done, WEIGHT_DECAY)
    root_gamma = jnp.sqrt(CLIP_TAU / jnp.maximum(head_max, CLIP_TAU))
    row_index = unit_of_slot[:, None] * U + jnp.arange(U, dtype=jnp.int32)[None, :]
    local_head = jnp.where(row_index < head_rows, row_index // HD, (row_index - head_rows) // HD)
    local_head = jnp.minimum(local_head, heads_here - 1)
    head_index = jnp.arange(N_TENSOR, dtype=jnp.int32)[:, None, None] * heads_here + local_head[None]
    factor = jnp.where((row_index < 2 * head_rows)[None], root_gamma[head_index], 1.0)
    master_new = jnp.where(keep, master_new * factor[..., None], 0.0)
    first_new = jnp.where(keep, first_new, 0.0)
    second_new = jnp.where(keep, second_new, 0.0)
    shared_first, shared_second, shared_new = adam_step(shared_params[0], grad_shared, shared_params[1], shared_params[2], steps_done, 0.0)
    bias_first, bias_second, bias_new = adam_step(bias_params[0], grad_bias, bias_params[1], bias_params[2], steps_done, 0.0)
    shared_out = jnp.stack([grad_shared, shared_first])
    bias_out = jnp.stack([grad_bias, bias_first])
    return (layer_out.reshape(TOKENS, D), grad_inputs.reshape(TOKENS, D), head_max, grad_master, first_new, second_new, master_new, shared_out, shared_second, shared_new, bias_out, bias_second, bias_new)
```

```python
import functools
import math

import jax
import jax.numpy as jnp
from jax import lax
from jax.experimental import pallas as pl
from jax.experimental.pallas import tpu as pltpu
from jax.sharding import PartitionSpec as P

HD = 64
DOC_MOST = 1024
STEP = 10
PAIR = 2 * HD

EPS_NORM = 1e-05
BETA_ONE = 0.9
BETA_TWO = 0.95
LEARN_RATE = 0.08
WEIGHT_DECAY = 0.1
EPS_ADAM = 1e-08
CLIP_TAU = 10.0
MASKED = -1e30
BF = jnp.bfloat16
F32 = jnp.float32


def plain_dot(left, right):
    return jnp.dot(left, right, preferred_element_type=F32)


def rows_by_rows(left, right):
    return lax.dot_general(left, right, (((1,), (1,)), ((), ())), preferred_element_type=F32)


def cols_by_cols(left, right):
    return lax.dot_general(left, right, (((0,), (0,)), ((), ())), preferred_element_type=F32)


def gelu_tanh(values_in):
    return jax.nn.gelu(values_in, approximate=True)


def norm_rows(values_in, gain, shift):
    centre = jnp.mean(values_in, axis=-1, keepdims=True)
    shifted = values_in - centre
    inverse = lax.rsqrt(jnp.mean(shifted * shifted, axis=-1, keepdims=True) + EPS_NORM)
    normed = shifted * inverse
    return (normed * gain + shift, normed, inverse)


def norm_back(grad_in, normed, inverse, gain):
    scaled = grad_in * gain
    return inverse * (
        scaled
        - jnp.mean(scaled, axis=-1, keepdims=True)
        - normed * jnp.mean(scaled * normed, axis=-1, keepdims=True)
    )


def slot_tables(owners, n_slots, slot_cap):
    n_units = owners.shape[0]
    unit_order = jnp.arange(n_units, dtype=jnp.int32)
    same_owner = owners[:, None] == owners[None, :]
    earlier = unit_order[None, :] < unit_order[:, None]
    rank_counts = jnp.sum((same_owner & earlier).astype(jnp.int32), axis=1)
    slot_of_unit = owners * slot_cap + rank_counts
    matches = jnp.arange(n_slots, dtype=jnp.int32)[:, None] == slot_of_unit[None, :]
    occupied = jnp.any(matches, axis=1)
    unit_of_slot = jnp.sum(matches.astype(jnp.int32) * unit_order[None, :], axis=1)
    return (slot_of_unit, unit_of_slot, occupied)


def head_lanes(head):
    lane = lax.broadcasted_iota(jnp.int32, (1, PAIR), 1)
    return (lane < HD) if head == 0 else (lane >= HD)


def q_tiles(n_query, n_keys):
    size = min(256, n_query)
    reach = n_keys - n_query
    return size, reach + size


def fill_bias(bias_ref, first_ref):
    n_keys, n_query = bias_ref.shape
    reach = n_keys - n_query
    key = lax.broadcasted_iota(jnp.int32, (n_keys, n_query), 0)
    query = lax.broadcasted_iota(jnp.int32, (n_keys, n_query), 1) + reach
    seen = (key <= query) & (key >= first_ref[...])
    bias_ref[...] = jnp.where(seen, 0.0, MASKED)


def attend_kernel(first_ref, q_ref, k_ref, v_ref, o_ref, lse_ref, peak_ref, bias_ref):
    @pl.when(pl.program_id(0) == 0)
    def _():
        fill_bias(bias_ref, first_ref)

    n_keys, n_query = bias_ref.shape
    size, span = q_tiles(n_query, n_keys)
    for j in range(n_query // size):
        rows, keys = pl.ds(j * size, size), pl.ds(j * size, span)
        v_t = v_ref[keys, :].T
        outs = []
        for h in range(2):
            k_h = jnp.where(head_lanes(h), k_ref[keys, :], 0)
            s = rows_by_rows(k_h, q_ref[rows, :]) + bias_ref[keys, rows]
            top = jnp.max(s, axis=0, keepdims=True)
            p = jnp.exp(s - top)
            total = jnp.sum(p, axis=0, keepdims=True)
            o_t = plain_dot(v_t[h * HD : (h + 1) * HD], p.astype(BF))
            outs.append(o_t / total)
            lse_ref[0, h : h + 1, rows] = top + jnp.log(total)
            peak_ref[0, h : h + 1, rows] = top
        o_ref[rows, :] = jnp.concatenate(outs, axis=0).T.astype(BF)


def attend_forward(q_scaled, keys_in, values_in, first_seen):
    n_query, width = q_scaled.shape
    n_keys = keys_in.shape[0]
    pairs = width // PAIR
    column = lambda i: (0, i)
    stats = jax.ShapeDtypeStruct((pairs, 2, n_query), F32)
    stat_spec = pl.BlockSpec((1, 2, n_query), lambda i: (i, 0, 0))
    return pl.pallas_call(
        attend_kernel,
        grid=(pairs,),
        in_specs=[
            pl.BlockSpec((1, n_query), lambda i: (0, 0)),
            pl.BlockSpec((n_query, PAIR), column),
            pl.BlockSpec((n_keys, PAIR), column),
            pl.BlockSpec((n_keys, PAIR), column),
        ],
        out_specs=[pl.BlockSpec((n_query, PAIR), column), stat_spec, stat_spec],
        out_shape=[jax.ShapeDtypeStruct((n_query, width), BF), stats, stats],
        scratch_shapes=[pltpu.VMEM((n_keys, n_query), F32)],
        compiler_params=pltpu.CompilerParams(vmem_limit_bytes=48 << 20),
        name="attend_forward",
    )(first_seen, q_scaled, keys_in, values_in)


def attend_back_kernel(
    first_ref, q_ref, k_ref, v_ref, o_ref, do_ref, lse_ref, dq_ref, dk_ref, dv_ref,
    bias_ref, dk_acc, dv_acc, *, scale
):
    @pl.when(pl.program_id(0) == 0)
    def _():
        fill_bias(bias_ref, first_ref)

    n_keys, n_query = bias_ref.shape
    size, span = q_tiles(n_query, n_keys)
    dk_acc[...] = jnp.zeros_like(dk_acc)
    dv_acc[...] = jnp.zeros_like(dv_acc)
    for j in range(n_query // size):
        rows, keys = pl.ds(j * size, size), pl.ds(j * size, span)
        q_here, do_here = q_ref[rows, :], do_ref[rows, :]
        k_here, v_here = k_ref[keys, :], v_ref[keys, :]
        k_t = k_here.T
        meet = (do_here.astype(F32) * o_ref[rows, :].astype(F32)).T
        outs = []
        for h in range(2):
            lanes = head_lanes(h)
            delta = jnp.sum(meet[h * HD : (h + 1) * HD], axis=0, keepdims=True)
            s = rows_by_rows(jnp.where(lanes, k_here, 0), q_here) + bias_ref[keys, rows]
            p = jnp.exp(s - lse_ref[0, h : h + 1, rows])
            dp = rows_by_rows(jnp.where(lanes, v_here, 0), do_here)
            ds = (p * (dp - delta)).astype(BF)
            dv_acc[keys, :] += plain_dot(p.astype(BF), jnp.where(lanes, do_here, 0))
            dk_acc[keys, :] += plain_dot(ds, jnp.where(lanes, q_here, 0))
            outs.append(plain_dot(k_t[h * HD : (h + 1) * HD], ds))
        dq_ref[rows, :] = (jnp.concatenate(outs, axis=0).T * scale).astype(BF)
    dk_ref[...] = dk_acc[...].astype(BF)
    dv_ref[...] = dv_acc[...].astype(BF)


def attend_backward(q_scaled, keys_in, values_in, attended, grads_out, log_norms, first_seen):
    n_query, width = q_scaled.shape
    n_keys = keys_in.shape[0]
    pairs = width // PAIR
    column = lambda i: (0, i)
    q_spec = pl.BlockSpec((n_query, PAIR), column)
    k_spec = pl.BlockSpec((n_keys, PAIR), column)
    q_out = jax.ShapeDtypeStruct((n_query, width), BF)
    k_out = jax.ShapeDtypeStruct((n_keys, width), BF)
    return pl.pallas_call(
        functools.partial(attend_back_kernel, scale=1.0 / math.sqrt(HD)),
        grid=(pairs,),
        in_specs=[
            pl.BlockSpec((1, n_query), lambda i: (0, 0)),
            q_spec, k_spec, k_spec, q_spec, q_spec,
            pl.BlockSpec((1, 2, n_query), lambda i: (i, 0, 0)),
        ],
        out_specs=[q_spec, k_spec, k_spec],
        out_shape=[q_out, k_out, k_out],
        scratch_shapes=[
            pltpu.VMEM((n_keys, n_query), F32),
            pltpu.VMEM((n_keys, PAIR), F32),
            pltpu.VMEM((n_keys, PAIR), F32),
        ],
        compiler_params=pltpu.CompilerParams(vmem_limit_bytes=48 << 20),
        name="attend_backward",
    )(first_seen, q_scaled, keys_in, values_in, attended, grads_out, log_norms)


def adam_step(param, grad, first, second, steps_done, decay):
    first_new = BETA_ONE * first + (1.0 - BETA_ONE) * grad
    second_new = BETA_TWO * second + (1.0 - BETA_TWO) * grad * grad
    fix_one = 1.0 - BETA_ONE**steps_done
    fix_two = 1.0 - BETA_TWO**steps_done
    direction = first_new / fix_one / (jnp.sqrt(second_new / fix_two) + EPS_ADAM)
    return (first_new, second_new, param - LEARN_RATE * (direction + decay * param))


def take_kernel(picks_ref, from_ref, to_ref):
    to_ref[...] = from_ref[...]


def take_blocks(blocks, picks):
    shape = (blocks.shape[0], 1, *blocks.shape[2:])
    return pl.pallas_call(
        take_kernel,
        grid_spec=pltpu.PrefetchScalarGridSpec(
            num_scalar_prefetch=1,
            grid=picks.shape,
            in_specs=[pl.BlockSpec(shape, lambda i, p: (0, p[i], 0, 0))],
            out_specs=pl.BlockSpec(shape, lambda i, p: (0, i, 0, 0)),
        ),
        out_shape=jax.ShapeDtypeStruct((shape[0], picks.shape[0], *shape[2:]), blocks.dtype),
        compiler_params=pltpu.CompilerParams(vmem_limit_bytes=32 << 20),
        name="take_blocks",
    )(picks, blocks)


def gather_units(master, slot_of_unit):
    slots = lax.all_gather(master.astype(BF), ("tensor", "dp"), axis=0, tiled=True)
    n_tensor = lax.axis_size("tensor")
    slots = slots.reshape(n_tensor, -1, *master.shape[1:])
    return take_blocks(slots, slot_of_unit)


def scatter_units(units, unit_of_slot):
    slots = take_blocks(units, unit_of_slot)
    slots = slots.reshape(-1, *units.shape[2:])
    return lax.psum_scatter(slots, ("tensor", "dp"), scatter_dimension=0, tiled=True)


def per_device(
    tokens_in,
    out_grad,
    lengths,
    owners,
    matrix_master,
    matrix_m1,
    matrix_m2,
    shared_params,
    bias_params,
):
    n_tensor = lax.axis_size("tensor")
    n_data = lax.axis_size("dp")
    tensor_index = lax.axis_index("tensor")
    data_index = lax.axis_index("dp")
    rows_here, width = tokens_in.shape
    slot_cap = matrix_master.shape[1]
    unit_rows = matrix_master.shape[2]
    n_units = owners.shape[0]
    n_slots = n_data * slot_cap
    head_rows = width // n_tensor
    heads_here = head_rows // HD
    ff_rows = (n_units * unit_rows - 4 * head_rows) // 2
    slot_of_unit, unit_of_slot, occupied = slot_tables(owners, n_slots, slot_cap)

    units = gather_units(matrix_master[0], slot_of_unit)
    stacks = units.reshape(n_tensor, n_units * unit_rows, width)
    part = lambda first, count: stacks[:, first : first + count].reshape(-1, width)
    w_q, w_k, w_v, w_out = (part(i * head_rows, head_rows) for i in range(4))
    w_fc = part(4 * head_rows, ff_rows)
    w_proj = part(4 * head_rows + ff_rows, ff_rows)
    all_bias = lax.all_gather(bias_params[0], "tensor", axis=0, tiled=True)
    bias = lambda first, count: all_bias[:, first : first + count].reshape(-1)
    b_q, b_k, b_v = (bias(i * head_rows, head_rows) for i in range(3))
    b_fc = bias(3 * head_rows, ff_rows)

    back = -(-(DOC_MOST - 1) // rows_here)
    reach = back * rows_here
    sizes = lengths[0]
    upto = jnp.arange(sizes.shape[0])[:, None] >= jnp.arange(sizes.shape[0])[None, :]
    bounds = jnp.sum(jnp.where(upto, sizes[None, :], 0), axis=1)
    places = tensor_index * rows_here + jnp.arange(rows_here, dtype=jnp.int32)
    starts = jnp.max(jnp.where(places[:, None] >= bounds[None, :], bounds[None, :], 0), axis=1)
    first_seen = (starts - tensor_index * rows_here + reach)[None, :]

    shared = shared_params[0]
    inputs_f32 = tokens_in.astype(F32)
    normed_one, hat_one, inverse_one = norm_rows(inputs_f32, shared[0], shared[1])
    normed_low = normed_one.astype(BF)
    before = [
        lax.ppermute(normed_low, "tensor", [(i, i + r) for i in range(n_tensor - r)])
        for r in range(min(back, n_tensor - 1), 0, -1)
    ]
    blank = [jnp.zeros_like(normed_low)] * (back - len(before))
    normed_all = jnp.concatenate([*blank, *before, normed_low], axis=0)
    scale = 1.0 / math.sqrt(HD)
    q_scaled = (rows_by_rows(normed_low, w_q) + b_q).astype(BF) * jnp.asarray(scale, BF)
    keys_in = (rows_by_rows(normed_all, w_k) + b_k).astype(BF)
    values_in = (rows_by_rows(normed_all, w_v) + b_v).astype(BF)
    attended, log_norms, peaks = attend_forward(q_scaled, keys_in, values_in, first_seen)
    hidden = inputs_f32 + (plain_dot(attended, w_out) + shared[2])
    normed_two, hat_two, inverse_two = norm_rows(hidden, shared[3], shared[4])
    second_low = normed_two.astype(BF)
    pre_act = rows_by_rows(second_low, w_fc) + b_fc
    activ, gelu_back = jax.vjp(gelu_tanh, pre_act)
    activ_low = activ.astype(BF)
    layer_out = hidden + (plain_dot(activ_low, w_proj) + shared[5])

    grad_y = out_grad.astype(F32)
    grad_proj_w = cols_by_cols(activ_low, out_grad)
    grad_activ = rows_by_rows(out_grad, w_proj)
    grad_pre_low = gelu_back(grad_activ)[0].astype(BF)
    grad_fc_b = jnp.sum(grad_pre_low, axis=0, dtype=F32)
    grad_fc_w = cols_by_cols(grad_pre_low, second_low)
    grad_second = plain_dot(grad_pre_low, w_fc)
    grad_hidden = grad_y + norm_back(grad_second, hat_two, inverse_two, shared[3])
    grad_hidden_low = grad_hidden.astype(BF)
    grad_out_w = cols_by_cols(attended, grad_hidden_low)
    grad_attended = rows_by_rows(grad_hidden_low, w_out).astype(BF)
    grad_q, grad_k, grad_v = attend_backward(
        q_scaled, keys_in, values_in, attended, grad_attended, log_norms, first_seen
    )
    grad_q_w = cols_by_cols(grad_q, normed_low)
    grad_k_w = cols_by_cols(grad_k, normed_all)
    grad_v_w = cols_by_cols(grad_v, normed_all)
    grad_wide = plain_dot(grad_k, w_k) + plain_dot(grad_v, w_v)
    grad_first = grad_wide[reach:] + plain_dot(grad_q, w_q)
    for r in range(1, min(back, n_tensor - 1) + 1):
        away = grad_wide[reach - r * rows_here : reach - (r - 1) * rows_here].astype(BF)
        grad_first += lax.ppermute(away, "tensor", [(i, i - r) for i in range(r, n_tensor)]).astype(F32)
    input_grad = grad_hidden + norm_back(grad_first, hat_one, inverse_one, shared[0])

    head_all = lax.pmax(jnp.max(peaks, axis=2).reshape(-1), ("dp", "tensor"))
    head_peak = lax.dynamic_slice_in_dim(head_all, tensor_index * heads_here, heads_here)
    grad_qkv_b = [jnp.sum(g, axis=0, dtype=F32) for g in (grad_q, grad_k, grad_v)]
    shared_part = jnp.stack(
        [
            jnp.sum(grad_first * hat_one, axis=0),
            jnp.sum(grad_first, axis=0),
            jnp.sum(grad_hidden_low, axis=0, dtype=F32),
            jnp.sum(grad_second * hat_two, axis=0),
            jnp.sum(grad_second, axis=0),
            jnp.sum(grad_y, axis=0),
        ]
    )
    by_tensor = lambda v: v.reshape(n_tensor, -1)
    bias_part = jnp.concatenate([by_tensor(v) for v in (*grad_qkv_b, grad_fc_b)], axis=1)
    shared_grad, bias_total = lax.psum((shared_part, bias_part), ("dp", "tensor"))
    bias_grad = lax.dynamic_index_in_dim(bias_total, tensor_index, 0, keepdims=False)

    by_stack = lambda g: g.astype(BF).reshape(n_tensor, -1, width)
    grad_units = jnp.concatenate(
        [by_stack(g) for g in (grad_q_w, grad_k_w, grad_v_w, grad_out_w, grad_fc_w, grad_proj_w)], axis=1
    ).reshape(units.shape)
    my_grads = scatter_units(grad_units, unit_of_slot).astype(F32)

    my_units = lax.dynamic_slice_in_dim(unit_of_slot, data_index * slot_cap, slot_cap, 0)
    my_occupied = lax.dynamic_slice_in_dim(occupied, data_index * slot_cap, slot_cap, 0)[:, None, None]
    steps_done = float(STEP)
    first_new, second_new, master_new = adam_step(
        matrix_master[0], my_grads, matrix_m1[0], matrix_m2[0], steps_done, WEIGHT_DECAY
    )
    root_gamma = jnp.sqrt(CLIP_TAU / jnp.maximum(head_peak, CLIP_TAU))
    row_index = my_units[:, None] * unit_rows + jnp.arange(unit_rows, dtype=jnp.int32)[None, :]
    local_head = jnp.where(row_index < head_rows, row_index // HD, (row_index - head_rows) // HD)
    head_match = local_head[..., None] == jnp.arange(heads_here, dtype=jnp.int32)[None, None, :]
    picked_root = jnp.sum(jnp.where(head_match, root_gamma, 0.0), axis=-1)
    factor = jnp.where(row_index < 2 * head_rows, picked_root, 1.0)
    my_grads = jnp.where(my_occupied, my_grads, 0.0)
    master_new = jnp.where(my_occupied, master_new * factor[..., None], 0.0)
    first_new = jnp.where(my_occupied, first_new, 0.0)
    second_new = jnp.where(my_occupied, second_new, 0.0)
    shared_first, shared_second, shared_new = adam_step(
        shared, shared_grad, shared_params[1], shared_params[2], steps_done, 0.0
    )
    bias_first, bias_second, bias_new = adam_step(
        bias_params[0, 0], bias_grad, bias_params[1, 0], bias_params[2, 0], steps_done, 0.0
    )
    shared_out = jnp.stack([shared_grad, shared_first])
    bias_out = jnp.stack([bias_grad, bias_first])[:, None, :]
    return (
        layer_out,
        input_grad,
        head_peak,
        my_grads[None],
        first_new[None],
        second_new[None],
        master_new[None],
        shared_out,
        shared_second,
        shared_new,
        bias_out,
        bias_second[None],
        bias_new[None],
    )


def solution(mesh):
    in_specs = (
        P(("dp", "tensor"), None),
        P(("dp", "tensor"), None),
        P("dp", None),
        P(),
        P("tensor", "dp", None, None),
        P("tensor", "dp", None, None),
        P("tensor", "dp", None, None),
        P(),
        P(None, "tensor", None),
    )
    out_specs = (
        P(("dp", "tensor"), None),
        P(("dp", "tensor"), None),
        P("tensor"),
        P("tensor", "dp", None, None),
        P("tensor", "dp", None, None),
        P("tensor", "dp", None, None),
        P("tensor", "dp", None, None),
        P(),
        P(),
        P(),
        P(None, "tensor", None),
        P("tensor", None),
        P("tensor", None),
    )
    return jax.shard_map(
        per_device, mesh=mesh, in_specs=in_specs, out_specs=out_specs, check_vma=False
    )
```

```python
import functools
import math

import jax
import jax.numpy as jnp
from jax import lax
from jax.experimental import pallas as pl
from jax.experimental.pallas import tpu as pltpu
from jax.sharding import PartitionSpec as P

HD = 64
DOC_MOST = 1024
STEP = 10
PAIR = 2 * HD

EPS_NORM = 1e-05
BETA_ONE = 0.9
BETA_TWO = 0.95
LEARN_RATE = 0.08
WEIGHT_DECAY = 0.1
EPS_ADAM = 1e-08
CLIP_TAU = 10.0
MASKED = -1e30
BF = jnp.bfloat16
F32 = jnp.float32
MESH = pl.DeviceIdType.MESH
MAX_ROW = 13


def plain_dot(left, right):
    return jnp.dot(left, right, preferred_element_type=F32)


def rows_by_rows(left, right):
    return lax.dot_general(left, right, (((1,), (1,)), ((), ())), preferred_element_type=F32)


def cols_by_cols(left, right):
    return lax.dot_general(left, right, (((0,), (0,)), ((), ())), preferred_element_type=F32)


def gelu_tanh(values_in):
    return jax.nn.gelu(values_in, approximate=True)


def norm_rows(values_in, gain, shift):
    centre = jnp.mean(values_in, axis=-1, keepdims=True)
    shifted = values_in - centre
    inverse = lax.rsqrt(jnp.mean(shifted * shifted, axis=-1, keepdims=True) + EPS_NORM)
    normed = shifted * inverse
    return (normed * gain + shift, normed, inverse)


def norm_back(grad_in, normed, inverse, gain):
    scaled = grad_in * gain
    return inverse * (
        scaled
        - jnp.mean(scaled, axis=-1, keepdims=True)
        - normed * jnp.mean(scaled * normed, axis=-1, keepdims=True)
    )


def slot_tables(owners, n_slots, slot_cap):
    n_units = owners.shape[0]
    unit_order = jnp.arange(n_units, dtype=jnp.int32)
    same_owner = owners[:, None] == owners[None, :]
    earlier = unit_order[None, :] < unit_order[:, None]
    rank_counts = jnp.sum((same_owner & earlier).astype(jnp.int32), axis=1)
    slot_of_unit = owners * slot_cap + rank_counts
    matches = jnp.arange(n_slots, dtype=jnp.int32)[:, None] == slot_of_unit[None, :]
    occupied = jnp.any(matches, axis=1)
    unit_of_slot = jnp.sum(matches.astype(jnp.int32) * unit_order[None, :], axis=1)
    return (slot_of_unit, unit_of_slot, occupied)


def head_lanes(head):
    lane = lax.broadcasted_iota(jnp.int32, (1, PAIR), 1)
    return (lane < HD) if head == 0 else (lane >= HD)


def q_tiles(n_query, n_keys):
    size = min(256, n_query)
    reach = n_keys - n_query
    return size, reach + size


def fill_bias(bias_ref, first_ref):
    n_keys, n_query = bias_ref.shape
    reach = n_keys - n_query
    key = lax.broadcasted_iota(jnp.int32, (n_keys, n_query), 0)
    query = lax.broadcasted_iota(jnp.int32, (n_keys, n_query), 1) + reach
    seen = (key <= query) & (key >= first_ref[...])
    bias_ref[...] = jnp.where(seen, 0.0, MASKED)


def attend_kernel(first_ref, q_ref, k_ref, v_ref, o_ref, lse_ref, peak_ref, bias_ref):
    @pl.when(pl.program_id(0) == 0)
    def _():
        fill_bias(bias_ref, first_ref)

    n_keys, n_query = bias_ref.shape
    size, span = q_tiles(n_query, n_keys)
    for j in range(n_query // size):
        rows, keys = pl.ds(j * size, size), pl.ds(j * size, span)
        v_t = v_ref[keys, :].T
        outs = []
        for h in range(2):
            k_h = jnp.where(head_lanes(h), k_ref[keys, :], 0)
            s = rows_by_rows(k_h, q_ref[rows, :]) + bias_ref[keys, rows]
            top = jnp.max(s, axis=0, keepdims=True)
            p = jnp.exp(s - top)
            total = jnp.sum(p, axis=0, keepdims=True)
            o_t = plain_dot(v_t[h * HD : (h + 1) * HD], p.astype(BF))
            outs.append(o_t / total)
            lse_ref[0, h : h + 1, rows] = top + jnp.log(total)
            peak_ref[0, h : h + 1, rows] = top
        o_ref[rows, :] = jnp.concatenate(outs, axis=0).T.astype(BF)


def attend_forward(q_scaled, keys_in, values_in, first_seen):
    n_query, width = q_scaled.shape
    n_keys = keys_in.shape[0]
    pairs = width // PAIR
    column = lambda i: (0, i)
    stats = jax.ShapeDtypeStruct((pairs, 2, n_query), F32)
    stat_spec = pl.BlockSpec((1, 2, n_query), lambda i: (i, 0, 0))
    return pl.pallas_call(
        attend_kernel,
        grid=(pairs,),
        in_specs=[
            pl.BlockSpec((1, n_query), lambda i: (0, 0)),
            pl.BlockSpec((n_query, PAIR), column),
            pl.BlockSpec((n_keys, PAIR), column),
            pl.BlockSpec((n_keys, PAIR), column),
        ],
        out_specs=[pl.BlockSpec((n_query, PAIR), column), stat_spec, stat_spec],
        out_shape=[jax.ShapeDtypeStruct((n_query, width), BF), stats, stats],
        scratch_shapes=[pltpu.VMEM((n_keys, n_query), F32)],
        compiler_params=pltpu.CompilerParams(vmem_limit_bytes=48 << 20),
        name="attend_forward",
    )(first_seen, q_scaled, keys_in, values_in)


def attend_back_kernel(
    first_ref, q_ref, k_ref, v_ref, o_ref, do_ref, lse_ref, dq_ref, dk_ref, dv_ref,
    bias_ref, dk_acc, dv_acc, *, scale
):
    @pl.when(pl.program_id(0) == 0)
    def _():
        fill_bias(bias_ref, first_ref)

    n_keys, n_query = bias_ref.shape
    size, span = q_tiles(n_query, n_keys)
    dk_acc[...] = jnp.zeros_like(dk_acc)
    dv_acc[...] = jnp.zeros_like(dv_acc)
    for j in range(n_query // size):
        rows, keys = pl.ds(j * size, size), pl.ds(j * size, span)
        q_here, do_here = q_ref[rows, :], do_ref[rows, :]
        k_here, v_here = k_ref[keys, :], v_ref[keys, :]
        k_t = k_here.T
        meet = (do_here.astype(F32) * o_ref[rows, :].astype(F32)).T
        outs = []
        for h in range(2):
            lanes = head_lanes(h)
            delta = jnp.sum(meet[h * HD : (h + 1) * HD], axis=0, keepdims=True)
            s = rows_by_rows(jnp.where(lanes, k_here, 0), q_here) + bias_ref[keys, rows]
            p = jnp.exp(s - lse_ref[0, h : h + 1, rows])
            dp = rows_by_rows(jnp.where(lanes, v_here, 0), do_here)
            ds = (p * (dp - delta)).astype(BF)
            dv_acc[keys, :] += plain_dot(p.astype(BF), jnp.where(lanes, do_here, 0))
            dk_acc[keys, :] += plain_dot(ds, jnp.where(lanes, q_here, 0))
            outs.append(plain_dot(k_t[h * HD : (h + 1) * HD], ds))
        dq_ref[rows, :] = (jnp.concatenate(outs, axis=0).T * scale).astype(BF)
    dk_ref[...] = dk_acc[...].astype(BF)
    dv_ref[...] = dv_acc[...].astype(BF)


def attend_backward(q_scaled, keys_in, values_in, attended, grads_out, log_norms, first_seen):
    n_query, width = q_scaled.shape
    n_keys = keys_in.shape[0]
    pairs = width // PAIR
    column = lambda i: (0, i)
    q_spec = pl.BlockSpec((n_query, PAIR), column)
    k_spec = pl.BlockSpec((n_keys, PAIR), column)
    q_out = jax.ShapeDtypeStruct((n_query, width), BF)
    k_out = jax.ShapeDtypeStruct((n_keys, width), BF)
    return pl.pallas_call(
        functools.partial(attend_back_kernel, scale=1.0 / math.sqrt(HD)),
        grid=(pairs,),
        in_specs=[
            pl.BlockSpec((1, n_query), lambda i: (0, 0)),
            q_spec, k_spec, k_spec, q_spec, q_spec,
            pl.BlockSpec((1, 2, n_query), lambda i: (i, 0, 0)),
        ],
        out_specs=[q_spec, k_spec, k_spec],
        out_shape=[q_out, k_out, k_out],
        scratch_shapes=[
            pltpu.VMEM((n_keys, n_query), F32),
            pltpu.VMEM((n_keys, PAIR), F32),
            pltpu.VMEM((n_keys, PAIR), F32),
        ],
        compiler_params=pltpu.CompilerParams(vmem_limit_bytes=48 << 20),
        name="attend_backward",
    )(first_seen, q_scaled, keys_in, values_in, attended, grads_out, log_norms)


def adam_step(param, grad, first, second, steps_done, decay):
    first_new = BETA_ONE * first + (1.0 - BETA_ONE) * grad
    second_new = BETA_TWO * second + (1.0 - BETA_TWO) * grad * grad
    fix_one = 1.0 - BETA_ONE**steps_done
    fix_two = 1.0 - BETA_TWO**steps_done
    direction = first_new / fix_one / (jnp.sqrt(second_new / fix_two) + EPS_ADAM)
    return (first_new, second_new, param - LEARN_RATE * (direction + decay * param))


def take_kernel(picks_ref, from_ref, to_ref):
    to_ref[...] = from_ref[...]


def take_blocks(blocks, picks):
    shape = (blocks.shape[0], 1, *blocks.shape[2:])
    return pl.pallas_call(
        take_kernel,
        grid_spec=pltpu.PrefetchScalarGridSpec(
            num_scalar_prefetch=1,
            grid=picks.shape,
            in_specs=[pl.BlockSpec(shape, lambda i, p: (0, p[i], 0, 0))],
            out_specs=pl.BlockSpec(shape, lambda i, p: (0, i, 0, 0)),
        ),
        out_shape=jax.ShapeDtypeStruct((shape[0], picks.shape[0], *shape[2:]), blocks.dtype),
        compiler_params=pltpu.CompilerParams(vmem_limit_bytes=32 << 20),
        name="take_blocks",
    )(picks, blocks)


def gather_units(master, slot_of_unit):
    slots = lax.all_gather(master.astype(BF), ("tensor", "dp"), axis=0, tiled=True)
    n_tensor = lax.axis_size("tensor")
    slots = slots.reshape(n_tensor, -1, *master.shape[1:])
    return take_blocks(slots, slot_of_unit)


def scatter_units(units, unit_of_slot):
    slots = take_blocks(units, unit_of_slot)
    slots = slots.reshape(-1, *units.shape[2:])
    return lax.psum_scatter(slots, ("tensor", "dp"), scatter_dimension=0, tiled=True)


def send(src, dst, send_sem, recv_sem, to):
    copy = pltpu.make_async_remote_copy(
        src_ref=src, dst_ref=dst, send_sem=send_sem, recv_sem=recv_sem,
        device_id=to, device_id_type=MESH,
    )
    copy.start()
    return copy


def arrived(ref, sem):
    pltpu.make_async_copy(ref, ref, sem).wait()


def place():
    d, t = lax.axis_index("dp"), lax.axis_index("tensor")
    core, x, y = d % 2, (d // 2) % 2, d // 4
    return d, t, core, x, y


def greet(d, t, n_tensor):
    barrier = pltpu.get_barrier_semaphore()
    for k in range(1, 8):
        pl.semaphore_signal(barrier, inc=1, device_id=((d + k) % 8, t), device_id_type=MESH)
    for k in range(1, n_tensor):
        pl.semaphore_signal(barrier, inc=1, device_id=(d, (t + k) % n_tensor), device_id_type=MESH)
    pl.semaphore_wait(barrier, 6 + n_tensor)


def spread_kernel(
    groups, n_tensor, back,
    slot_ref, master_ref, a_ref, bias_ref, w_ref, wide_ref, biases_ref,
    pieces, own, blank, swap_send, swap_recv, local_sem, a_send, a_recv, bias_send, bias_recv,
    z_send, z_recv, xy_send, xy_recv, core_send, core_recv,
):
    d, t, core, x, y = place()
    column = y * 2 + x
    by_x, by_y = d + 2 - 4 * x, d + 4 - 8 * y
    sibling = d + 1 - 2 * core
    greet(d, t, n_tensor)
    first, last = t > 0, t < n_tensor - 1
    for k in range(1, n_tensor):
        send(bias_ref, biases_ref.at[t], bias_send.at[k - 1], bias_recv.at[k - 1], (d, (t + k) % n_tensor))
    biases_ref[t] = bias_ref[...]

    @pl.when(last)
    def _():
        send(a_ref, wide_ref.at[back - 1], a_send.at[0], a_recv.at[0], (d, t + 1))

    cap = master_ref.shape[0]
    for k in range(1, 8):
        to = (d + k) % 8
        send(master_ref.at[:, to], pieces.at[d], swap_send.at[k - 1], swap_recv.at[k - 1], (to, t))
    mine = pltpu.make_async_copy(master_ref.at[:, d], pieces.at[d], local_sem.at[0])
    mine.start()
    keep = pltpu.make_async_copy(a_ref, wide_ref.at[back], local_sem.at[1])
    keep.start()
    blank[...] = jnp.zeros_like(blank)
    for r in range(back):
        @pl.when(t < back - r)
        def _(r=r):
            fill = pltpu.make_async_copy(blank, wide_ref.at[r], local_sem.at[2])
            fill.start()
            fill.wait()
    mine.wait()
    for k in range(1, 8):
        arrived(pieces.at[(d + 8 - k) % 8], swap_recv.at[k - 1])
    for u in range(own.shape[0]):
        slot = slot_ref[u]
        own[u] = pieces[slot // cap, slot % cap]

    def block(g, at, col, c):
        u0, u1 = groups[g]
        return w_ref.at[u0:u1, at, col, c]

    def onward(g, k, at, source):
        side = at * 2 // n_tensor
        one, two = by_x + (by_y - by_x) * side, by_y + (by_x - by_y) * side
        here = block(g, at, column, core)
        send(source, here, xy_send.at[g, k, 0], xy_recv.at[g, k, 0], (one, t))
        send(source, here, xy_send.at[g, k, 1], xy_recv.at[g, k, 1], (two, t))
        send(source, here, core_send.at[g, k, 0], core_recv.at[g, k, 0], (sibling, t))

    def columns(at):
        side = at * 2 // n_tensor
        col_x, col_y, col_xy = y * 2 + 1 - x, (1 - y) * 2 + x, (1 - y) * 2 + 1 - x
        return col_x + (col_y - col_x) * side, col_y + (col_x - col_y) * side, col_xy, by_y + (by_x - by_y) * side

    def forward(g, k, at):
        one, two, both, to = columns(at)
        got = block(g, at, one, core)
        arrived(got, xy_recv.at[g, k, 0])
        send(got, got, xy_send.at[g, k, 2], xy_recv.at[g, k, 2], (to, t))
        send(got, got, core_send.at[g, k, 1], core_recv.at[g, k, 1], (sibling, t))

    def finish(g, k, at):
        one, two, both, to = columns(at)
        for i, col in ((1, two), (2, both)):
            got = block(g, at, col, core)
            arrived(got, xy_recv.at[g, k, i])
            send(got, got, core_send.at[g, k, i + 1], core_recv.at[g, k, i + 1], (sibling, t))

    def done(g, k, at):
        one, two, both, to = columns(at)
        cols = (column, one, two, both)
        for i, col in enumerate(cols):
            arrived(block(g, at, col, 1 - core), core_recv.at[g, k, i])
        for i in range(3):
            arrived(block(g, at, cols[min(i, 1)], core), xy_send.at[g, k, i])
        for i, col in enumerate(cols):
            arrived(block(g, at, col, core), core_send.at[g, k, i])

    def z_step(g, s, up):
        k = 1 + 2 * s + (0 if up else 1)
        at = t - 1 - s if up else t + 1 + s
        return k, at, (at >= 0) if up else (at < n_tensor)

    def z_go(g, s, up, at, source):
        i = 0 if up else 1

        @pl.when(last if up else first)
        def _():
            send(source, block(g, at, column, core), z_send.at[g, i, s], z_recv.at[g, i, s], (d, t + 1 if up else t - 1))

    def z_sent(g, s, up, at, have):
        i = 0 if up else 1

        @pl.when(have & (last if up else first))
        def _():
            arrived(block(g, at, column, core), z_send.at[g, i, s])

    n_groups = len(groups)
    local = []
    for g, (u0, u1) in enumerate(groups):
        source = own.at[u0:u1]
        for up in (True, False):
            z_go(g, 0, up, t, source)
        onward(g, 0, t, source)
        copy = pltpu.make_async_copy(source, block(g, t, column, core), local_sem.at[3 + g])
        copy.start()
        local.append(copy)

    @pl.when(first)
    def _():
        arrived(wide_ref.at[back - 1], a_recv.at[0])
    for r in range(1, back):
        @pl.when(last & (t >= r))
        def _(r=r):
            send(wide_ref.at[back - r], wide_ref.at[back - r - 1], a_send.at[r], a_recv.at[r], (d, t + 1))

        if r + 1 <= back:
            @pl.when(t > r)
            def _(r=r):
                arrived(wide_ref.at[back - r - 1], a_recv.at[r])

    for g in range(n_groups):
        queue = [(0, t, None)]
        for s in range(n_tensor - 1):
            for up in (True, False):
                k, at, have = z_step(g, s, up)

                @pl.when(have)
                def _(k=k, at=at, s=s, up=up):
                    got = block(g, at, column, core)
                    arrived(got, z_recv.at[g, 0 if up else 1, s])
                    if s + 1 < n_tensor - 1:
                        z_go(g, s + 1, up, at, got)
                    onward(g, k, at, got)
                queue.append((k, at, have))
            while queue:
                k, at, have = queue.pop(0)
                guard = pl.when(have) if have is not None else (lambda f: f())
                guard(functools.partial(forward, g, k, at))
                guard(functools.partial(finish, g, k, at))

    for g in range(n_groups):
        local[g].wait()
        for k, at, have in [(0, t, None)] + [z_step(g, s, up) for s in range(n_tensor - 1) for up in (True, False)]:
            guard = pl.when(have) if have is not None else (lambda f: f())
            guard(functools.partial(done, g, k, at))
        for up in (True, False):
            z_sent(g, 0, up, t, t >= 0)
            for s in range(n_tensor - 2):
                k, at, have = z_step(g, s, up)
                z_sent(g, s + 1, up, at, have)
    keep.wait()
    for k in range(1, n_tensor):
        arrived(biases_ref.at[(t + n_tensor - k) % n_tensor], bias_recv.at[k - 1])
        arrived(bias_ref, bias_send.at[k - 1])
    for k in range(1, 8):
        arrived(pieces.at[0], swap_send.at[k - 1])
    for r in range(back):
        @pl.when(last & (t >= r))
        def _(r=r):
            arrived(a_ref, a_send.at[r])


def unit_groups(n_units):
    half = (n_units - 4) // 2
    return ((0, 4), (4, 4 + half), (4 + half, n_units))


def spread(master_low, normed_low, bias_row, slot_of_unit, n_tensor, back, groups):
    cap, unit_rows, width = master_low.shape
    n_units = slot_of_unit.shape[0]
    piece = unit_rows // 8
    n_groups, slots = len(groups), 2 * n_tensor - 1
    rows = normed_low.shape[0]
    bias_row = bias_row.reshape(-1, 128)
    any_spec = pl.BlockSpec(memory_space=pl.ANY)
    vmem = pl.BlockSpec(memory_space=pltpu.VMEM)
    dma = pltpu.SemaphoreType.DMA
    w, wide, biases = pl.pallas_call(
        functools.partial(spread_kernel, groups, n_tensor, back),
        out_shape=[
            jax.ShapeDtypeStruct((n_units, n_tensor, 4, 2, piece, width), BF),
            jax.ShapeDtypeStruct((back + 1, rows, width), BF),
            jax.ShapeDtypeStruct((n_tensor, *bias_row.shape), F32),
        ],
        in_specs=[pl.BlockSpec(memory_space=pltpu.SMEM), any_spec, any_spec, vmem],
        out_specs=[any_spec, any_spec, vmem],
        scratch_shapes=[
            pltpu.VMEM((8, cap, piece, width), BF),
            pltpu.VMEM((n_units, piece, width), BF),
            pltpu.VMEM((rows, width), BF),
            dma((7,)), dma((7,)), dma((3 + n_groups,)), dma((back,)), dma((back,)),
            dma((n_tensor - 1,)), dma((n_tensor - 1,)),
            dma((n_groups, 2, n_tensor - 1)), dma((n_groups, 2, n_tensor - 1)),
            dma((n_groups, slots, 3)), dma((n_groups, slots, 3)),
            dma((n_groups, slots, 4)), dma((n_groups, slots, 4)),
        ],
        compiler_params=pltpu.CompilerParams(collective_id=0, has_side_effects=True, vmem_limit_bytes=24 << 20),
        name="spread",
    )(slot_of_unit, master_low.reshape(cap, 8, piece, width), normed_low, bias_row)
    return w.reshape(n_units, -1, width), wide.reshape(-1, width), biases.reshape(n_tensor, -1)


def add_block(into, part, count):
    def body(i, _):
        a, b = into(i), part(i)
        a[...] = a[...] + b[...]
        return 0
    lax.fori_loop(0, count, body, 0)


def join(row, a, b):
    return jnp.where(row == MAX_ROW, jnp.maximum(a, b), a + b)


def reduce_kernel(
    groups, n_tensor,
    unit_ref, g_ref, v_ref, out_ref, vsum_ref,
    half, other, plane_one, plane_two, up_in, down_in, final, outgo, v_in, v_z,
    load_sem, core_send, core_recv, one_send, one_recv, two_send, two_recv, z_send, z_recv,
    swap_send, swap_recv, v_send, v_recv, local_sem,
):
    d, t, core, x, y = place()
    by_x, by_y = d + 2 - 4 * x, d + 4 - 8 * y
    sibling = d + 1 - 2 * core
    greet(d, t, n_tensor)
    n_groups = len(groups)
    ends = lambda g: (groups[g][0], groups[g][1] - groups[g][0])
    order = sorted(range(n_tensor), key=lambda a: -abs(2 * a - n_tensor + 1))

    loads = {}
    for g in range(n_groups):
        u0, n = ends(g)
        us = pl.ds(u0, n)
        send(g_ref.at[us, :, :, :, 1 - core], other.at[us], core_send.at[g], core_recv.at[g], (sibling, t))
        loads[g] = pltpu.make_async_copy(g_ref.at[us, :, :, :, core], half.at[us], load_sem.at[g])
        loads[g].start()

    row = lax.broadcasted_iota(jnp.int32, v_ref.shape, 0)
    vsum_ref[...] = v_ref[...]
    for i, to in enumerate((sibling, by_x, by_y)):
        send(vsum_ref, v_in.at[i], v_send.at[i], v_recv.at[i], (to, t))
        arrived(v_in.at[i], v_recv.at[i])
        arrived(v_in.at[i], v_send.at[i])
        vsum_ref[...] = join(row, vsum_ref[...], v_in[i])
    for k in range(1, n_tensor):
        to = (t + k) % n_tensor
        send(vsum_ref, v_z.at[k - 1], v_send.at[2 + k], v_recv.at[2 + k], (d, to))

    def merge(g, at):
        u0, n = ends(g)
        lead = half.shape[2] * half.shape[3]
        def pick(ref):
            return lambda i: ref.at[u0 + i // lead, at, (i % lead) // 2, i % 2]
        add_block(pick(half), pick(other), n * lead)

    def first_hop(g, at):
        u0, n = ends(g)
        us = pl.ds(u0, n)
        by_rows = at * 2 < n_tensor
        source = half.at[us, at, 1 - y] if by_rows else half.at[us, at, :, 1 - x]
        send(source, plane_one.at[us, at], one_send.at[g, at], one_recv.at[g, at], (by_y if by_rows else by_x, t))

    def second_hop(g, at):
        u0, n = ends(g)
        us = pl.ds(u0, n)
        by_rows = at * 2 < n_tensor
        arrived(plane_one.at[us, at], one_recv.at[g, at])
        if by_rows:
            into = lambda i: half.at[u0 + i // 2, at, y, i % 2]
        else:
            into = lambda i: half.at[u0 + i // 2, at, i % 2, x]
        add_block(into, lambda i: plane_one.at[u0 + i // 2, at, i % 2], 2 * n)
        source = half.at[us, at, y, 1 - x] if by_rows else half.at[us, at, 1 - y, x]
        send(source, plane_two.at[us, at], two_send.at[g, at], two_recv.at[g, at], (by_x if by_rows else by_y, t))

    def line(g, at):
        u0, n = ends(g)
        us = pl.ds(u0, n)
        arrived(plane_two.at[us, at], two_recv.at[g, at])
        mine = lambda i: half.at[u0 + i, at, y, x]
        add_block(mine, lambda i: plane_two.at[u0 + i, at], n)

        def take(buffer, way):
            arrived(buffer.at[us, at], z_recv.at[g, at, way])
            add_block(mine, lambda i: buffer.at[u0 + i, at], n)

        @pl.when((t <= at) & (t > 0))
        def _():
            take(up_in, 0)

        @pl.when((t >= at) & (t < n_tensor - 1))
        def _():
            take(down_in, 1)

        source = half.at[us, at, y, x]

        @pl.when(t < at)
        def _():
            send(source, up_in.at[us, at], z_send.at[g, at], z_recv.at[g, at, 0], (d, t + 1))

        @pl.when(t > at)
        def _():
            send(source, down_in.at[us, at], z_send.at[g, at], z_recv.at[g, at, 1], (d, t - 1))

        @pl.when(t == at)
        def _():
            add_block(lambda i: final.at[u0 + i], lambda i: half.at[u0 + i, at, y, x], n)

    final[...] = jnp.zeros_like(final)
    for g in range(n_groups):
        u0, n = ends(g)
        loads[g].wait()
        arrived(other.at[pl.ds(u0, n)], core_recv.at[g])
        for at in order:
            merge(g, at)
            first_hop(g, at)
        if g == 0:
            for k in range(1, n_tensor):
                arrived(v_z.at[k - 1], v_recv.at[2 + k])
                arrived(v_z.at[k - 1], v_send.at[2 + k])
            for k in range(1, n_tensor):
                vsum_ref[...] = join(row, vsum_ref[...], v_z[k - 1])
        if g > 0:
            for at in order:
                line(g - 1, at)
        for at in order:
            second_hop(g, at)
    for at in order:
        line(n_groups - 1, at)

    cap = out_ref.shape[0]
    for k in range(1, 9):
        to = (d + k) % 8
        for j in range(cap):
            outgo[to, j] = final[unit_ref[to * cap + j]]
        if k < 8:
            send(outgo.at[to], out_ref.at[:, d], swap_send.at[k - 1], swap_recv.at[k - 1], (to, t))
    keep = pltpu.make_async_copy(outgo.at[d], out_ref.at[:, d], local_sem.at[0])
    keep.start()
    for k in range(1, 8):
        arrived(out_ref.at[:, (d + 8 - k) % 8], swap_recv.at[k - 1])
    for g in range(n_groups):
        us = pl.ds(*ends(g))
        arrived(other.at[us], core_send.at[g])
        for at in range(n_tensor):
            arrived(plane_one.at[us, at], one_send.at[g, at])
            arrived(plane_two.at[us, at], two_send.at[g, at])

            @pl.when(t != at)
            def _():
                arrived(up_in.at[us, at], z_send.at[g, at])
    for k in range(1, 8):
        arrived(outgo.at[0], swap_send.at[k - 1])
    keep.wait()


def reduce_units(grads, vectors, unit_of_slot, n_tensor, cap, groups):
    n_units, _, width = grads.shape
    piece = grads.shape[1] // (8 * n_tensor)
    grads = grads.reshape(n_units, n_tensor, 2, 2, 2, piece, width)
    n_groups = len(groups)
    any_spec = pl.BlockSpec(memory_space=pl.ANY)
    vmem = pl.BlockSpec(memory_space=pltpu.VMEM)
    dma = pltpu.SemaphoreType.DMA
    block = (piece, width)
    out, vsum = pl.pallas_call(
        functools.partial(reduce_kernel, groups, n_tensor),
        out_shape=[
            jax.ShapeDtypeStruct((cap, 8, *block), BF),
            jax.ShapeDtypeStruct(vectors.shape, F32),
        ],
        in_specs=[pl.BlockSpec(memory_space=pltpu.SMEM), any_spec, vmem],
        out_specs=[vmem, vmem],
        scratch_shapes=[
            pltpu.VMEM((n_units, n_tensor, 2, 2, *block), BF),
            pltpu.VMEM((n_units, n_tensor, 2, 2, *block), BF),
            pltpu.VMEM((n_units, n_tensor, 2, *block), BF),
            pltpu.VMEM((n_units, n_tensor, *block), BF),
            pltpu.VMEM((n_units, n_tensor, *block), BF),
            pltpu.VMEM((n_units, n_tensor, *block), BF),
            pltpu.VMEM((n_units, *block), BF),
            pltpu.VMEM((8, cap, *block), BF),
            pltpu.VMEM((3, *vectors.shape), F32),
            pltpu.VMEM((n_tensor - 1, *vectors.shape), F32),
            dma((n_groups,)), dma((n_groups,)), dma((n_groups,)),
            dma((n_groups, n_tensor)), dma((n_groups, n_tensor)),
            dma((n_groups, n_tensor)), dma((n_groups, n_tensor)),
            dma((n_groups, n_tensor)), dma((n_groups, n_tensor, 2)),
            dma((7,)), dma((7,)), dma((2 + n_tensor,)), dma((2 + n_tensor,)), dma((1,)),
        ],
        compiler_params=pltpu.CompilerParams(collective_id=1, has_side_effects=True, vmem_limit_bytes=56 << 20),
        name="reduce_units",
    )(unit_of_slot, grads, vectors)
    return out.reshape(cap, -1, width), vsum


def per_device(
    tokens_in,
    out_grad,
    lengths,
    owners,
    matrix_master,
    matrix_m1,
    matrix_m2,
    shared_params,
    bias_params,
):
    n_tensor = lax.axis_size("tensor")
    n_data = lax.axis_size("dp")
    tensor_index = lax.axis_index("tensor")
    data_index = lax.axis_index("dp")
    rows_here, width = tokens_in.shape
    slot_cap = matrix_master.shape[1]
    unit_rows = matrix_master.shape[2]
    n_units = owners.shape[0]
    n_slots = n_data * slot_cap
    head_rows = width // n_tensor
    heads_here = head_rows // HD
    ff_rows = (n_units * unit_rows - 4 * head_rows) // 2
    slot_of_unit, unit_of_slot, occupied = slot_tables(owners, n_slots, slot_cap)

    own_kernels = n_data == 8 and head_rows == unit_rows and unit_rows % 128 == 0 and n_tensor > 1

    back = -(-(DOC_MOST - 1) // rows_here)
    reach = back * rows_here
    sizes = lengths[0]
    upto = jnp.arange(sizes.shape[0])[:, None] >= jnp.arange(sizes.shape[0])[None, :]
    bounds = jnp.sum(jnp.where(upto, sizes[None, :], 0), axis=1)
    places = tensor_index * rows_here + jnp.arange(rows_here, dtype=jnp.int32)
    starts = jnp.max(jnp.where(places[:, None] >= bounds[None, :], bounds[None, :], 0), axis=1)
    first_seen = (starts - tensor_index * rows_here + reach)[None, :]

    shared = shared_params[0]
    inputs_f32 = tokens_in.astype(F32)
    normed_one, hat_one, inverse_one = norm_rows(inputs_f32, shared[0], shared[1])
    normed_low = normed_one.astype(BF)
    if own_kernels:
        units, normed_all, all_bias = spread(
            matrix_master[0].astype(BF), normed_low, bias_params[0, 0], slot_of_unit, n_tensor, back, unit_groups(n_units)
        )
        w_q, w_k, w_v, w_out = (units[i] for i in range(4))
        w_fc, w_proj = (units[4 + i * (n_units - 4) // 2 :][: (n_units - 4) // 2].reshape(-1, width) for i in range(2))
    else:
        units = gather_units(matrix_master[0], slot_of_unit)
        stacks = units.reshape(n_tensor, n_units * unit_rows, width)
        part = lambda first, count: stacks[:, first : first + count].reshape(-1, width)
        w_q, w_k, w_v, w_out = (part(i * head_rows, head_rows) for i in range(4))
        w_fc = part(4 * head_rows, ff_rows)
        w_proj = part(4 * head_rows + ff_rows, ff_rows)
        all_bias = lax.all_gather(bias_params[0], "tensor", axis=0, tiled=True).reshape(n_tensor, -1)
        before = [
            lax.ppermute(normed_low, "tensor", [(i, i + r) for i in range(n_tensor - r)])
            for r in range(min(back, n_tensor - 1), 0, -1)
        ]
        blank = [jnp.zeros_like(normed_low)] * (back - len(before))
        normed_all = jnp.concatenate([*blank, *before, normed_low], axis=0)
    bias = lambda first, count: all_bias[:, first : first + count].reshape(-1)
    b_q, b_k, b_v = (bias(i * head_rows, head_rows) for i in range(3))
    swap = (lambda v: v.swapaxes(0, 1)) if own_kernels else (lambda v: v)
    b_fc = swap(all_bias[:, 3 * head_rows :].reshape(n_tensor, -1, unit_rows)).reshape(-1)
    scale = 1.0 / math.sqrt(HD)
    q_scaled = (rows_by_rows(normed_low, w_q) + b_q).astype(BF) * jnp.asarray(scale, BF)
    keys_in = (rows_by_rows(normed_all, w_k) + b_k).astype(BF)
    values_in = (rows_by_rows(normed_all, w_v) + b_v).astype(BF)
    attended, log_norms, peaks = attend_forward(q_scaled, keys_in, values_in, first_seen)
    hidden = inputs_f32 + (plain_dot(attended, w_out) + shared[2])
    normed_two, hat_two, inverse_two = norm_rows(hidden, shared[3], shared[4])
    second_low = normed_two.astype(BF)
    pre_act = rows_by_rows(second_low, w_fc) + b_fc
    activ, gelu_back = jax.vjp(gelu_tanh, pre_act)
    activ_low = activ.astype(BF)
    layer_out = hidden + (plain_dot(activ_low, w_proj) + shared[5])

    grad_y = out_grad.astype(F32)
    grad_proj_w = cols_by_cols(activ_low, out_grad)
    grad_activ = rows_by_rows(out_grad, w_proj)
    grad_pre_low = gelu_back(grad_activ)[0].astype(BF)
    grad_fc_b = jnp.sum(grad_pre_low, axis=0, dtype=F32)
    grad_fc_w = cols_by_cols(grad_pre_low, second_low)
    grad_second = plain_dot(grad_pre_low, w_fc)
    grad_hidden = grad_y + norm_back(grad_second, hat_two, inverse_two, shared[3])
    grad_hidden_low = grad_hidden.astype(BF)
    grad_out_w = cols_by_cols(attended, grad_hidden_low)
    grad_attended = rows_by_rows(grad_hidden_low, w_out).astype(BF)
    grad_q, grad_k, grad_v = attend_backward(
        q_scaled, keys_in, values_in, attended, grad_attended, log_norms, first_seen
    )
    grad_q_w = cols_by_cols(grad_q, normed_low)
    grad_k_w = cols_by_cols(grad_k, normed_all)
    grad_v_w = cols_by_cols(grad_v, normed_all)
    grad_wide = plain_dot(grad_k, w_k) + plain_dot(grad_v, w_v)
    grad_first = grad_wide[reach:] + plain_dot(grad_q, w_q)
    for r in range(1, min(back, n_tensor - 1) + 1):
        away = grad_wide[reach - r * rows_here : reach - (r - 1) * rows_here].astype(BF)
        grad_first += lax.ppermute(away, "tensor", [(i, i - r) for i in range(r, n_tensor)]).astype(F32)
    input_grad = grad_hidden + norm_back(grad_first, hat_one, inverse_one, shared[0])

    head_here = jnp.max(peaks, axis=2).reshape(-1)
    grad_qkv_b = [jnp.sum(g, axis=0, dtype=F32) for g in (grad_q, grad_k, grad_v)]
    shared_part = jnp.stack(
        [
            jnp.sum(grad_first * hat_one, axis=0),
            jnp.sum(grad_first, axis=0),
            jnp.sum(grad_hidden_low, axis=0, dtype=F32),
            jnp.sum(grad_second * hat_two, axis=0),
            jnp.sum(grad_second, axis=0),
            jnp.sum(grad_y, axis=0),
        ]
    )
    by_tensor = lambda v: v.reshape(n_tensor, -1)
    fc_shape = (-1, n_tensor, unit_rows) if own_kernels else (n_tensor, -1, unit_rows)
    grad_fc_b = swap(grad_fc_b.reshape(fc_shape))
    bias_part = jnp.concatenate([by_tensor(v) for v in (*grad_qkv_b, grad_fc_b)], axis=1)
    if own_kernels:
        head_row = jnp.pad(head_here, (0, width - head_here.shape[0]))[None]
        vectors = jnp.concatenate([shared_part, bias_part.reshape(-1, width), head_row], axis=0)
        vectors = jnp.pad(vectors, ((0, 16 - vectors.shape[0]), (0, 0)))
        grad_units = jnp.concatenate(
            [g.astype(BF) for g in (grad_q_w, grad_k_w, grad_v_w, grad_out_w, grad_fc_w, grad_proj_w)], axis=0
        ).reshape(units.shape)
        my_grads, totals = reduce_units(
            grad_units, vectors, unit_of_slot, n_tensor, slot_cap, unit_groups(n_units)[::-1]
        )
        my_grads = my_grads.astype(F32)
        shared_grad, bias_total = totals[:6], totals[6:MAX_ROW].reshape(n_tensor, -1)
        head_all = totals[MAX_ROW, : head_here.shape[0]]
    else:
        head_all = lax.pmax(head_here, ("dp", "tensor"))
        shared_grad, bias_total = lax.psum((shared_part, bias_part), ("dp", "tensor"))
        by_stack = lambda g: g.astype(BF).reshape(n_tensor, -1, width)
        grad_units = jnp.concatenate(
            [by_stack(g) for g in (grad_q_w, grad_k_w, grad_v_w, grad_out_w, grad_fc_w, grad_proj_w)], axis=1
        ).reshape(units.shape)
        my_grads = scatter_units(grad_units, unit_of_slot).astype(F32)
    head_peak = lax.dynamic_slice_in_dim(head_all, tensor_index * heads_here, heads_here)
    bias_grad = lax.dynamic_index_in_dim(bias_total, tensor_index, 0, keepdims=False)

    my_units = lax.dynamic_slice_in_dim(unit_of_slot, data_index * slot_cap, slot_cap, 0)
    my_occupied = lax.dynamic_slice_in_dim(occupied, data_index * slot_cap, slot_cap, 0)[:, None, None]
    steps_done = float(STEP)
    first_new, second_new, master_new = adam_step(
        matrix_master[0], my_grads, matrix_m1[0], matrix_m2[0], steps_done, WEIGHT_DECAY
    )
    root_gamma = jnp.sqrt(CLIP_TAU / jnp.maximum(head_peak, CLIP_TAU))
    row_index = my_units[:, None] * unit_rows + jnp.arange(unit_rows, dtype=jnp.int32)[None, :]
    local_head = jnp.where(row_index < head_rows, row_index // HD, (row_index - head_rows) // HD)
    head_match = local_head[..., None] == jnp.arange(heads_here, dtype=jnp.int32)[None, None, :]
    picked_root = jnp.sum(jnp.where(head_match, root_gamma, 0.0), axis=-1)
    factor = jnp.where(row_index < 2 * head_rows, picked_root, 1.0)
    my_grads = jnp.where(my_occupied, my_grads, 0.0)
    master_new = jnp.where(my_occupied, master_new * factor[..., None], 0.0)
    first_new = jnp.where(my_occupied, first_new, 0.0)
    second_new = jnp.where(my_occupied, second_new, 0.0)
    shared_first, shared_second, shared_new = adam_step(
        shared, shared_grad, shared_params[1], shared_params[2], steps_done, 0.0
    )
    bias_first, bias_second, bias_new = adam_step(
        bias_params[0, 0], bias_grad, bias_params[1, 0], bias_params[2, 0], steps_done, 0.0
    )
    shared_out = jnp.stack([shared_grad, shared_first])
    bias_out = jnp.stack([bias_grad, bias_first])[:, None, :]
    return (
        layer_out,
        input_grad,
        head_peak,
        my_grads[None],
        first_new[None],
        second_new[None],
        master_new[None],
        shared_out,
        shared_second,
        shared_new,
        bias_out,
        bias_second[None],
        bias_new[None],
    )


def solution(mesh):
    in_specs = (
        P(("dp", "tensor"), None),
        P(("dp", "tensor"), None),
        P("dp", None),
        P(),
        P("tensor", "dp", None, None),
        P("tensor", "dp", None, None),
        P("tensor", "dp", None, None),
        P(),
        P(None, "tensor", None),
    )
    out_specs = (
        P(("dp", "tensor"), None),
        P(("dp", "tensor"), None),
        P("tensor"),
        P("tensor", "dp", None, None),
        P("tensor", "dp", None, None),
        P("tensor", "dp", None, None),
        P("tensor", "dp", None, None),
        P(),
        P(),
        P(),
        P(None, "tensor", None),
        P("tensor", None),
        P("tensor", None),
    )
    return jax.shard_map(
        per_device, mesh=mesh, in_specs=in_specs, out_specs=out_specs, check_vma=False
    )
```

```python
import functools
import math

import jax
import jax.numpy as jnp
from jax import lax
from jax.experimental import pallas as pl
from jax.experimental.pallas import tpu as pltpu
from jax.sharding import PartitionSpec as P

HD = 64
DOC_MOST = 1024
STEP = 10
PAIR = 2 * HD

EPS_NORM = 1e-05
BETA_ONE = 0.9
BETA_TWO = 0.95
LEARN_RATE = 0.08
WEIGHT_DECAY = 0.1
EPS_ADAM = 1e-08
CLIP_TAU = 10.0
MASKED = -1e30
BF = jnp.bfloat16
F32 = jnp.float32
MESH = pl.DeviceIdType.MESH
MAX_ROW = 13


def plain_dot(left, right):
    return jnp.dot(left, right, preferred_element_type=F32)


def rows_by_rows(left, right):
    return lax.dot_general(left, right, (((1,), (1,)), ((), ())), preferred_element_type=F32)


def cols_by_cols(left, right):
    return lax.dot_general(left, right, (((0,), (0,)), ((), ())), preferred_element_type=F32)


def gelu_tanh(values_in):
    return jax.nn.gelu(values_in, approximate=True)


def norm_rows(values_in, gain, shift):
    centre = jnp.mean(values_in, axis=-1, keepdims=True)
    shifted = values_in - centre
    inverse = lax.rsqrt(jnp.mean(shifted * shifted, axis=-1, keepdims=True) + EPS_NORM)
    normed = shifted * inverse
    return (normed * gain + shift, normed, inverse)


def norm_back(grad_in, normed, inverse, gain):
    scaled = grad_in * gain
    return inverse * (
        scaled
        - jnp.mean(scaled, axis=-1, keepdims=True)
        - normed * jnp.mean(scaled * normed, axis=-1, keepdims=True)
    )


def slot_tables(owners, n_slots, slot_cap):
    n_units = owners.shape[0]
    unit_order = jnp.arange(n_units, dtype=jnp.int32)
    same_owner = owners[:, None] == owners[None, :]
    earlier = unit_order[None, :] < unit_order[:, None]
    rank_counts = jnp.sum((same_owner & earlier).astype(jnp.int32), axis=1)
    slot_of_unit = owners * slot_cap + rank_counts
    matches = jnp.arange(n_slots, dtype=jnp.int32)[:, None] == slot_of_unit[None, :]
    occupied = jnp.any(matches, axis=1)
    unit_of_slot = jnp.sum(matches.astype(jnp.int32) * unit_order[None, :], axis=1)
    return (slot_of_unit, unit_of_slot, occupied)


def head_lanes(head):
    lane = lax.broadcasted_iota(jnp.int32, (1, PAIR), 1)
    return (lane < HD) if head == 0 else (lane >= HD)


def q_tiles(n_query, n_keys):
    size = min(256, n_query)
    reach = n_keys - n_query
    return size, reach + size


def fill_bias(bias_ref, first_ref):
    n_keys, n_query = bias_ref.shape
    reach = n_keys - n_query
    key = lax.broadcasted_iota(jnp.int32, (n_keys, n_query), 0)
    query = lax.broadcasted_iota(jnp.int32, (n_keys, n_query), 1) + reach
    seen = (key <= query) & (key >= first_ref[...])
    bias_ref[...] = jnp.where(seen, 0.0, MASKED)


def attend_kernel(first_ref, q_ref, k_ref, v_ref, o_ref, lse_ref, peak_ref, bias_ref):
    @pl.when(pl.program_id(0) == 0)
    def _():
        fill_bias(bias_ref, first_ref)

    n_keys, n_query = bias_ref.shape
    size, span = q_tiles(n_query, n_keys)
    for j in range(n_query // size):
        rows, keys = pl.ds(j * size, size), pl.ds(j * size, span)
        v_t = v_ref[keys, :].T
        outs = []
        for h in range(2):
            k_h = jnp.where(head_lanes(h), k_ref[keys, :], 0)
            s = rows_by_rows(k_h, q_ref[rows, :]) + bias_ref[keys, rows]
            top = jnp.max(s, axis=0, keepdims=True)
            p = jnp.exp(s - top)
            total = jnp.sum(p, axis=0, keepdims=True)
            o_t = plain_dot(v_t[h * HD : (h + 1) * HD], p.astype(BF))
            outs.append(o_t / total)
            lse_ref[0, h : h + 1, rows] = top + jnp.log(total)
            peak_ref[0, h : h + 1, rows] = top
        o_ref[rows, :] = jnp.concatenate(outs, axis=0).T.astype(BF)


def attend_forward(q_scaled, keys_in, values_in, first_seen):
    n_query, width = q_scaled.shape
    n_keys = keys_in.shape[0]
    pairs = width // PAIR
    column = lambda i: (0, i)
    stats = jax.ShapeDtypeStruct((pairs, 2, n_query), F32)
    stat_spec = pl.BlockSpec((1, 2, n_query), lambda i: (i, 0, 0))
    return pl.pallas_call(
        attend_kernel,
        grid=(pairs,),
        in_specs=[
            pl.BlockSpec((1, n_query), lambda i: (0, 0)),
            pl.BlockSpec((n_query, PAIR), column),
            pl.BlockSpec((n_keys, PAIR), column),
            pl.BlockSpec((n_keys, PAIR), column),
        ],
        out_specs=[pl.BlockSpec((n_query, PAIR), column), stat_spec, stat_spec],
        out_shape=[jax.ShapeDtypeStruct((n_query, width), BF), stats, stats],
        scratch_shapes=[pltpu.VMEM((n_keys, n_query), F32)],
        compiler_params=pltpu.CompilerParams(vmem_limit_bytes=48 << 20),
        name="attend_forward",
    )(first_seen, q_scaled, keys_in, values_in)


def attend_back_kernel(
    first_ref, q_ref, k_ref, v_ref, o_ref, do_ref, lse_ref, dq_ref, dk_ref, dv_ref,
    bias_ref, dk_acc, dv_acc, *, scale
):
    @pl.when(pl.program_id(0) == 0)
    def _():
        fill_bias(bias_ref, first_ref)

    n_keys, n_query = bias_ref.shape
    size, span = q_tiles(n_query, n_keys)
    dk_acc[...] = jnp.zeros_like(dk_acc)
    dv_acc[...] = jnp.zeros_like(dv_acc)
    for j in range(n_query // size):
        rows, keys = pl.ds(j * size, size), pl.ds(j * size, span)
        q_here, do_here = q_ref[rows, :], do_ref[rows, :]
        k_here, v_here = k_ref[keys, :], v_ref[keys, :]
        k_t = k_here.T
        meet = (do_here.astype(F32) * o_ref[rows, :].astype(F32)).T
        outs = []
        for h in range(2):
            lanes = head_lanes(h)
            delta = jnp.sum(meet[h * HD : (h + 1) * HD], axis=0, keepdims=True)
            s = rows_by_rows(jnp.where(lanes, k_here, 0), q_here) + bias_ref[keys, rows]
            p = jnp.exp(s - lse_ref[0, h : h + 1, rows])
            dp = rows_by_rows(jnp.where(lanes, v_here, 0), do_here)
            ds = (p * (dp - delta)).astype(BF)
            dv_acc[keys, :] += plain_dot(p.astype(BF), jnp.where(lanes, do_here, 0))
            dk_acc[keys, :] += plain_dot(ds, jnp.where(lanes, q_here, 0))
            outs.append(plain_dot(k_t[h * HD : (h + 1) * HD], ds))
        dq_ref[rows, :] = (jnp.concatenate(outs, axis=0).T * scale).astype(BF)
    dk_ref[...] = dk_acc[...].astype(BF)
    dv_ref[...] = dv_acc[...].astype(BF)


def attend_backward(q_scaled, keys_in, values_in, attended, grads_out, log_norms, first_seen):
    n_query, width = q_scaled.shape
    n_keys = keys_in.shape[0]
    pairs = width // PAIR
    column = lambda i: (0, i)
    q_spec = pl.BlockSpec((n_query, PAIR), column)
    k_spec = pl.BlockSpec((n_keys, PAIR), column)
    q_out = jax.ShapeDtypeStruct((n_query, width), BF)
    k_out = jax.ShapeDtypeStruct((n_keys, width), BF)
    return pl.pallas_call(
        functools.partial(attend_back_kernel, scale=1.0 / math.sqrt(HD)),
        grid=(pairs,),
        in_specs=[
            pl.BlockSpec((1, n_query), lambda i: (0, 0)),
            q_spec, k_spec, k_spec, q_spec, q_spec,
            pl.BlockSpec((1, 2, n_query), lambda i: (i, 0, 0)),
        ],
        out_specs=[q_spec, k_spec, k_spec],
        out_shape=[q_out, k_out, k_out],
        scratch_shapes=[
            pltpu.VMEM((n_keys, n_query), F32),
            pltpu.VMEM((n_keys, PAIR), F32),
            pltpu.VMEM((n_keys, PAIR), F32),
        ],
        compiler_params=pltpu.CompilerParams(vmem_limit_bytes=48 << 20),
        name="attend_backward",
    )(first_seen, q_scaled, keys_in, values_in, attended, grads_out, log_norms)


def adam_step(param, grad, first, second, steps_done, decay):
    first_new = BETA_ONE * first + (1.0 - BETA_ONE) * grad
    second_new = BETA_TWO * second + (1.0 - BETA_TWO) * grad * grad
    fix_one = 1.0 - BETA_ONE**steps_done
    fix_two = 1.0 - BETA_TWO**steps_done
    direction = first_new / fix_one / (jnp.sqrt(second_new / fix_two) + EPS_ADAM)
    return (first_new, second_new, param - LEARN_RATE * (direction + decay * param))


def take_kernel(picks_ref, from_ref, to_ref):
    to_ref[...] = from_ref[...]


def take_blocks(blocks, picks):
    shape = (blocks.shape[0], 1, *blocks.shape[2:])
    return pl.pallas_call(
        take_kernel,
        grid_spec=pltpu.PrefetchScalarGridSpec(
            num_scalar_prefetch=1,
            grid=picks.shape,
            in_specs=[pl.BlockSpec(shape, lambda i, p: (0, p[i], 0, 0))],
            out_specs=pl.BlockSpec(shape, lambda i, p: (0, i, 0, 0)),
        ),
        out_shape=jax.ShapeDtypeStruct((shape[0], picks.shape[0], *shape[2:]), blocks.dtype),
        compiler_params=pltpu.CompilerParams(vmem_limit_bytes=32 << 20),
        name="take_blocks",
    )(picks, blocks)


def gather_units(master, slot_of_unit):
    slots = lax.all_gather(master.astype(BF), ("tensor", "dp"), axis=0, tiled=True)
    n_tensor = lax.axis_size("tensor")
    slots = slots.reshape(n_tensor, -1, *master.shape[1:])
    return take_blocks(slots, slot_of_unit)


def scatter_units(units, unit_of_slot):
    slots = take_blocks(units, unit_of_slot)
    slots = slots.reshape(-1, *units.shape[2:])
    return lax.psum_scatter(slots, ("tensor", "dp"), scatter_dimension=0, tiled=True)


def send(src, dst, send_sem, recv_sem, to):
    copy = pltpu.make_async_remote_copy(
        src_ref=src, dst_ref=dst, send_sem=send_sem, recv_sem=recv_sem,
        device_id=to, device_id_type=MESH,
    )
    copy.start()


def arrived(ref, sem):
    pltpu.make_async_copy(ref, ref, sem).wait()


def place():
    d, t = lax.axis_index("dp"), lax.axis_index("tensor")
    return d, t, d % 2, (d // 2) % 2, d // 4


def greet(d, t, n_tensor):
    barrier = pltpu.get_barrier_semaphore()
    for k in range(1, 8):
        pl.semaphore_signal(barrier, inc=1, device_id=((d + k) % 8, t), device_id_type=MESH)
    for k in range(1, n_tensor):
        pl.semaphore_signal(barrier, inc=1, device_id=(d, (t + k) % n_tensor), device_id_type=MESH)
    pl.semaphore_wait(barrier, 6 + n_tensor)


def loop_with(count, body, events):
    per = -(-len(events) // count)

    def step(i, carry):
        body(i)
        for n in range(count):
            mine = events[n * per : (n + 1) * per]
            if mine:
                @pl.when(i == n)
                def _(mine=mine):
                    for event in mine:
                        event()
        return carry

    lax.fori_loop(0, count, step, 0)


def attend_pair(i, q_ref, k_ref, v_ref, o_ref, lse_ref, peak_ref, bias_ref):
    n_keys, n_query = bias_ref.shape
    size, span = q_tiles(n_query, n_keys)
    lanes = pl.ds(pl.multiple_of(i * PAIR, PAIR), PAIR)
    for j in range(n_query // size):
        rows, keys = pl.ds(j * size, size), pl.ds(j * size, span)
        v_t = v_ref[keys, lanes].T
        outs = []
        for h in range(2):
            k_h = jnp.where(head_lanes(h), k_ref[keys, lanes], 0)
            s = rows_by_rows(k_h, q_ref[rows, lanes]) + bias_ref[keys, rows]
            top = jnp.max(s, axis=0, keepdims=True)
            p = jnp.exp(s - top)
            total = jnp.sum(p, axis=0, keepdims=True)
            o_t = plain_dot(v_t[h * HD : (h + 1) * HD], p.astype(BF))
            outs.append(o_t / total)
            lse_ref[i, h : h + 1, rows] = top + jnp.log(total)
            peak_ref[i, h : h + 1, rows] = top
        o_ref[rows, lanes] = jnp.concatenate(outs, axis=0).T.astype(BF)


def forward_kernel(
    n_tensor, back, scale,
    slot_ref, master_ref, a_ref, x_ref, bias_in_ref, first_ref, shared_ref,
    att_ref, fc_ref, proj_ref, wide_ref, biases_ref, q_ref, k_ref, v_ref, o_ref, lse_ref, peak_ref, hidden_ref,
    pieces, own, seen_ref, bias_rows, swap_send, swap_recv, local_sem, a_send, a_recv, bias_send, bias_recv,
    z_send, z_recv, xy_send, xy_recv, core_send, core_recv,
):
    d, t, core, x, y = place()
    column = y * 2 + x
    by_x, by_y = d + 2 - 4 * x, d + 4 - 8 * y
    sibling = d + 1 - 2 * core
    first, last = t > 0, t < n_tensor - 1
    rows_here, width = a_ref.shape
    weights = (att_ref, fc_ref, proj_ref)
    starts = [0]
    for w in weights:
        starts.append(starts[-1] + w.shape[0])
    greet(d, t, n_tensor)

    def tokens_up(r):
        @pl.when(last & (t >= r))
        def _():
            source = a_ref if r == 0 else wide_ref.at[back - r]
            send(source, wide_ref.at[back - r - 1], a_send.at[r], a_recv.at[r], (d, t + 1))

    def tokens_in(r):
        @pl.when(t > r)
        def _():
            arrived(wide_ref.at[back - r - 1], a_recv.at[r])
        if r + 1 < back:
            tokens_up(r + 1)

    tokens_up(0)
    for k in range(1, 8):
        to = (d + k) % 8
        send(master_ref.at[:, to], pieces.at[d], swap_send.at[k - 1], swap_recv.at[k - 1], (to, t))
    mine = pltpu.make_async_copy(master_ref.at[:, d], pieces.at[d], local_sem.at[0])
    mine.start()
    for k in range(1, n_tensor):
        send(bias_in_ref, biases_ref.at[t], bias_send.at[k - 1], bias_recv.at[k - 1], (d, (t + k) % n_tensor))
    biases_ref[t] = bias_in_ref[...]
    wide_ref[back] = a_ref[...]
    for r in range(back):
        @pl.when(t < back - r)
        def _(r=r):
            wide_ref[r] = jnp.zeros((rows_here, width), BF)
    fill_bias(seen_ref, first_ref)
    mine.wait()
    for k in range(1, 8):
        arrived(pieces.at[(d + 8 - k) % 8], swap_recv.at[k - 1])
    cap = master_ref.shape[0]
    for u in range(own.shape[0]):
        slot = slot_ref[u]
        own[u] = pieces[slot // cap, slot % cap]

    def block(g, at, col, c):
        return weights[g].at[:, at, col, c]

    def route(at):
        side = at * 2 // n_tensor
        one, two = by_x + (by_y - by_x) * side, by_y + (by_x - by_y) * side
        col_x, col_y, col_xy = y * 2 + 1 - x, (1 - y) * 2 + x, (1 - y) * 2 + 1 - x
        return one, two, col_x + (col_y - col_x) * side, col_y + (col_x - col_y) * side, col_xy

    def onward(g, k, at, source):
        one, two, _, _, _ = route(at)
        here = block(g, at, column, core)
        send(source, here, xy_send.at[g], xy_recv.at[g, k, 0], (one, t))
        send(source, here, xy_send.at[g], xy_recv.at[g, k, 1], (two, t))

    def forward(g, k, at):
        one, two, from_one, _, _ = route(at)
        got = block(g, at, from_one, core)
        arrived(got, xy_recv.at[g, k, 0])
        send(got, got, xy_send.at[g], xy_recv.at[g, k, 2], (two, t))

    def settle(g, k, at):
        _, _, _, from_two, beyond = route(at)
        arrived(block(g, at, from_two, core), xy_recv.at[g, k, 1])
        arrived(block(g, at, beyond, core), xy_recv.at[g, k, 2])
        got = weights[g].at[:, at, :, core]
        send(got, got, core_send.at[g, k], core_recv.at[g, k], (sibling, t))

    def done(g, k, at):
        arrived(weights[g].at[:, at, :, 1 - core], core_recv.at[g, k])
        arrived(weights[g].at[:, at, :, core], core_send.at[g, k])

    def z_go(g, s, up, source, at):
        i = 0 if up else 1

        @pl.when(last if up else first)
        def _():
            send(source, block(g, at, column, core), z_send.at[g, i, s], z_recv.at[g, i, s], (d, t + 1 if up else t - 1))

    def z_step(s, up):
        at = t - 1 - s if up else t + 1 + s
        return 1 + 2 * s + (0 if up else 1), at, (at >= 0) if up else (at < n_tensor)

    def z_event(g, s):
        for up in (True, False):
            k, at, have = z_step(s, up)

            @pl.when(have)
            def _(k=k, at=at, up=up):
                got = block(g, at, column, core)
                arrived(got, z_recv.at[g, 0 if up else 1, s])
                if s + 1 < n_tensor - 1:
                    z_go(g, s + 1, up, got, at)
                onward(g, k, at, got)

    def each(fn, g, s):
        if s < 0:
            fn(g, 0, t)
        else:
            for up in (True, False):
                k, at, have = z_step(s, up)
                pl.when(have)(functools.partial(fn, g, k, at))

    n_groups, steps = len(weights), n_tensor - 1
    local = []
    for g in range(n_groups):
        source = own.at[starts[g] : starts[g + 1]]
        for up in (True, False):
            z_go(g, 0, up, source, t)
        copy = pltpu.make_async_copy(source, block(g, t, column, core), local_sem.at[1 + g])
        copy.start()
        local.append(copy)
        onward(g, 0, t, source)

    def chain(g):
        events = []
        for s in range(steps + 2):
            if s < steps:
                events.append(functools.partial(z_event, g, s))
            if s <= steps:
                events.append(functools.partial(each, forward, g, s - 1))
            if s >= 1:
                if s == 1:
                    events.append(local[g].wait)
                events.append(functools.partial(each, settle, g, s - 2))
        return events

    events = chain(0)
    for r in range(back):
        events.insert(1 + 4 * r, functools.partial(tokens_in, r))
    early = [functools.partial(z_event, g, 0) for g in range(1, n_groups)]
    events[3:3] = early
    for event in events:
        event()
    late = []
    for g in range(1, n_groups):
        late += chain(g)[1:]
    for k in range(1, n_tensor):
        arrived(biases_ref.at[(t + n_tensor - k) % n_tensor], bias_recv.at[k - 1])
        arrived(bias_in_ref, bias_send.at[k - 1])
    per = width // n_tensor // 128
    for n in range(3):
        for at in range(n_tensor):
            for i in range(per):
                lanes = pl.ds((at * per + i) * 128, 128)
                bias_rows[n : n + 1, lanes] = biases_ref[at, n * per + i : n * per + i + 1]
    for s in range(-1, steps):
        each(done, 0, s)

    tile = 256

    def project(n, source_ref, into_ref, factor):
        def body(i):
            cols = pl.ds(pl.multiple_of(i * tile, tile), tile)
            w = att_ref[n, pl.ds(i * tile // (width // n_tensor), 1)].reshape(tile, width)
            for r in range(into_ref.shape[0] // rows_here):
                a = wide_ref[r] if source_ref is None else source_ref[...]
                full = rows_by_rows(a, w) + bias_rows[n : n + 1, cols]
                into_ref[r * rows_here : (r + 1) * rows_here, cols] = (full.astype(BF) * jnp.asarray(factor, BF)) if factor else full.astype(BF)
        return body

    tiles = width // tile
    n_late = len(late)
    cut = n_late // 5
    loop_with(tiles, project(0, a_ref, q_ref, scale), late[:0])
    loop_with(tiles, project(1, None, k_ref, None), late[:cut])
    loop_with(tiles, project(2, None, v_ref, None), late[cut : 2 * cut])
    loop_with(
        width // PAIR,
        lambda i: attend_pair(i, q_ref, k_ref, v_ref, o_ref, lse_ref, peak_ref, seen_ref),
        late[2 * cut :],
    )
    w_out = att_ref[3].reshape(width, width)
    half = rows_here // 2
    for r in range(2):
        rows = pl.ds(r * half, half)
        hidden_ref[rows, :] = x_ref[rows, :].astype(F32) + (plain_dot(o_ref[rows, :], w_out) + shared_ref[2:3, :])

    for g in range(n_groups):
        if g > 0:
            for s in range(-1, steps):
                each(done, g, s)
        arrived(weights[g].at[:, :, pl.ds(0, 3), 0], xy_send.at[g])
        for up in (True, False):
            for s in range(steps):
                have = last if up else first
                if s > 0:
                    have = have & z_step(s - 1, up)[2]

                @pl.when(have)
                def _(g=g, s=s, up=up):
                    arrived(block(g, t, column, core), z_send.at[g, 0 if up else 1, s])
    for r in range(back):
        @pl.when(last & (t >= r))
        def _(r=r):
            arrived(a_ref, a_send.at[r])
    for k in range(1, 8):
        arrived(pieces.at[0], swap_send.at[k - 1])


def forward_spread(master_low, normed_low, tokens, bias_row, first_seen, shared, slot_of_unit, n_tensor, back):
    cap, unit_rows, width = master_low.shape
    n_units = slot_of_unit.shape[0]
    n_ff = (n_units - 4) // 2
    piece = unit_rows // 8
    rows = normed_low.shape[0]
    n_keys = (back + 1) * rows
    bias_row = bias_row.reshape(-1, 128)
    any_spec = pl.BlockSpec(memory_space=pl.ANY)
    vmem = pl.BlockSpec(memory_space=pltpu.VMEM)
    dma = pltpu.SemaphoreType.DMA
    shape = jax.ShapeDtypeStruct
    units = lambda n: shape((n, n_tensor, 4, 2, piece, width), BF)
    stats = shape((width // PAIR, 2, rows), F32)
    outs = pl.pallas_call(
        functools.partial(forward_kernel, n_tensor, back, 1.0 / math.sqrt(HD)),
        out_shape=[
            units(4), units(n_ff), units(n_ff),
            shape((back + 1, rows, width), BF), shape((n_tensor, *bias_row.shape), F32),
            shape((rows, width), BF), shape((n_keys, width), BF), shape((n_keys, width), BF), shape((rows, width), BF),
            stats, stats, shape((rows, width), F32),
        ],
        in_specs=[pl.BlockSpec(memory_space=pltpu.SMEM), any_spec, vmem, vmem, vmem, vmem, vmem],
        out_specs=[vmem, any_spec, any_spec, vmem, vmem, vmem, vmem, vmem, vmem, vmem, vmem, vmem],
        scratch_shapes=[
            pltpu.VMEM((8, cap, piece, width), BF),
            pltpu.VMEM((n_units, piece, width), BF),
            pltpu.VMEM((n_keys, rows), F32),
            pltpu.VMEM((3, width), F32),
            dma((7,)), dma((7,)), dma((4,)), dma((back,)), dma((back,)),
            dma((n_tensor - 1,)), dma((n_tensor - 1,)),
            dma((3, 2, n_tensor - 1)), dma((3, 2, n_tensor - 1)),
            dma((3,)), dma((3, 2 * n_tensor - 1, 3)),
            dma((3, 2 * n_tensor - 1)), dma((3, 2 * n_tensor - 1)),
        ],
        compiler_params=pltpu.CompilerParams(collective_id=0, has_side_effects=True, vmem_limit_bytes=56 << 20),
        name="forward_spread",
    )(slot_of_unit, master_low.reshape(cap, 8, piece, width), normed_low, tokens, bias_row, first_seen, shared)
    att, fc, proj, wide, biases, q, k, v, o, lse, peaks, hidden = outs
    return (
        att.reshape(4, -1, width), fc.reshape(-1, width), proj.reshape(-1, width), wide.reshape(-1, width),
        biases.reshape(n_tensor, -1), q, k, v, o, lse, peaks, hidden,
    )


def unit_groups(n_units):
    half = (n_units - 4) // 2
    return ((0, 4), (4, 4 + half), (4 + half, n_units))


def add_block(into, part, count):
    def body(i, _):
        a, b = into(i), part(i)
        a[...] = a[...] + b[...]
        return 0
    lax.fori_loop(0, count, body, 0)


def join(row, a, b):
    return jnp.where(row == MAX_ROW, jnp.maximum(a, b), a + b)


def reduce_kernel(
    groups, n_tensor,
    unit_ref, g_ref, v_ref, out_ref, vsum_ref,
    half, other, plane_one, plane_two, up_in, down_in, final, outgo, v_in, v_z,
    load_sem, core_send, core_recv, one_send, one_recv, two_send, two_recv, z_send, z_recv,
    swap_send, swap_recv, v_send, v_recv, local_sem,
):
    d, t, core, x, y = place()
    by_x, by_y = d + 2 - 4 * x, d + 4 - 8 * y
    sibling = d + 1 - 2 * core
    greet(d, t, n_tensor)
    n_groups = len(groups)
    ends = lambda g: (groups[g][0], groups[g][1] - groups[g][0])
    order = sorted(range(n_tensor), key=lambda a: -abs(2 * a - n_tensor + 1))

    loads = {}
    for g in range(n_groups):
        u0, n = ends(g)
        us = pl.ds(u0, n)
        send(g_ref.at[us, :, :, :, 1 - core], other.at[us], core_send.at[g], core_recv.at[g], (sibling, t))
        loads[g] = pltpu.make_async_copy(g_ref.at[us, :, :, :, core], half.at[us], load_sem.at[g])
        loads[g].start()

    row = lax.broadcasted_iota(jnp.int32, v_ref.shape, 0)
    vsum_ref[...] = v_ref[...]
    for i, to in enumerate((sibling, by_x, by_y)):
        send(vsum_ref, v_in.at[i], v_send.at[i], v_recv.at[i], (to, t))
        arrived(v_in.at[i], v_recv.at[i])
        arrived(v_in.at[i], v_send.at[i])
        vsum_ref[...] = join(row, vsum_ref[...], v_in[i])
    for k in range(1, n_tensor):
        to = (t + k) % n_tensor
        send(vsum_ref, v_z.at[k - 1], v_send.at[2 + k], v_recv.at[2 + k], (d, to))

    def merge(g, at):
        u0, n = ends(g)
        lead = half.shape[2] * half.shape[3]
        def pick(ref):
            return lambda i: ref.at[u0 + i // lead, at, (i % lead) // 2, i % 2]
        add_block(pick(half), pick(other), n * lead)

    def first_hop(g, at):
        u0, n = ends(g)
        us = pl.ds(u0, n)
        by_rows = at * 2 < n_tensor
        source = half.at[us, at, 1 - y] if by_rows else half.at[us, at, :, 1 - x]
        send(source, plane_one.at[us, at], one_send.at[g, at], one_recv.at[g, at], (by_y if by_rows else by_x, t))

    def second_hop(g, at):
        u0, n = ends(g)
        us = pl.ds(u0, n)
        by_rows = at * 2 < n_tensor
        arrived(plane_one.at[us, at], one_recv.at[g, at])
        if by_rows:
            into = lambda i: half.at[u0 + i // 2, at, y, i % 2]
        else:
            into = lambda i: half.at[u0 + i // 2, at, i % 2, x]
        add_block(into, lambda i: plane_one.at[u0 + i // 2, at, i % 2], 2 * n)
        source = half.at[us, at, y, 1 - x] if by_rows else half.at[us, at, 1 - y, x]
        send(source, plane_two.at[us, at], two_send.at[g, at], two_recv.at[g, at], (by_x if by_rows else by_y, t))

    def line(g, at):
        u0, n = ends(g)
        us = pl.ds(u0, n)
        arrived(plane_two.at[us, at], two_recv.at[g, at])
        mine = lambda i: half.at[u0 + i, at, y, x]
        add_block(mine, lambda i: plane_two.at[u0 + i, at], n)

        def take(buffer, way):
            arrived(buffer.at[us, at], z_recv.at[g, at, way])
            add_block(mine, lambda i: buffer.at[u0 + i, at], n)

        @pl.when((t <= at) & (t > 0))
        def _():
            take(up_in, 0)

        @pl.when((t >= at) & (t < n_tensor - 1))
        def _():
            take(down_in, 1)

        source = half.at[us, at, y, x]

        @pl.when(t < at)
        def _():
            send(source, up_in.at[us, at], z_send.at[g, at], z_recv.at[g, at, 0], (d, t + 1))

        @pl.when(t > at)
        def _():
            send(source, down_in.at[us, at], z_send.at[g, at], z_recv.at[g, at, 1], (d, t - 1))

        @pl.when(t == at)
        def _():
            add_block(lambda i: final.at[u0 + i], lambda i: half.at[u0 + i, at, y, x], n)

    final[...] = jnp.zeros_like(final)
    for g in range(n_groups):
        u0, n = ends(g)
        loads[g].wait()
        arrived(other.at[pl.ds(u0, n)], core_recv.at[g])
        for at in order:
            merge(g, at)
            first_hop(g, at)
        if g == 0:
            for k in range(1, n_tensor):
                arrived(v_z.at[k - 1], v_recv.at[2 + k])
                arrived(v_z.at[k - 1], v_send.at[2 + k])
            for k in range(1, n_tensor):
                vsum_ref[...] = join(row, vsum_ref[...], v_z[k - 1])
        if g > 0:
            for at in order:
                line(g - 1, at)
        for at in order:
            second_hop(g, at)
    for at in order:
        line(n_groups - 1, at)

    cap = out_ref.shape[0]
    for k in range(1, 9):
        to = (d + k) % 8
        for j in range(cap):
            outgo[to, j] = final[unit_ref[to * cap + j]]
        if k < 8:
            send(outgo.at[to], out_ref.at[:, d], swap_send.at[k - 1], swap_recv.at[k - 1], (to, t))
    keep = pltpu.make_async_copy(outgo.at[d], out_ref.at[:, d], local_sem.at[0])
    keep.start()
    for k in range(1, 8):
        arrived(out_ref.at[:, (d + 8 - k) % 8], swap_recv.at[k - 1])
    for g in range(n_groups):
        us = pl.ds(*ends(g))
        arrived(other.at[us], core_send.at[g])
        for at in range(n_tensor):
            arrived(plane_one.at[us, at], one_send.at[g, at])
            arrived(plane_two.at[us, at], two_send.at[g, at])

            @pl.when(t != at)
            def _():
                arrived(up_in.at[us, at], z_send.at[g, at])
    for k in range(1, 8):
        arrived(outgo.at[0], swap_send.at[k - 1])
    keep.wait()


def reduce_units(grads, vectors, unit_of_slot, n_tensor, cap, groups):
    n_units, _, width = grads.shape
    piece = grads.shape[1] // (8 * n_tensor)
    grads = grads.reshape(n_units, n_tensor, 2, 2, 2, piece, width)
    n_groups = len(groups)
    any_spec = pl.BlockSpec(memory_space=pl.ANY)
    vmem = pl.BlockSpec(memory_space=pltpu.VMEM)
    dma = pltpu.SemaphoreType.DMA
    block = (piece, width)
    out, vsum = pl.pallas_call(
        functools.partial(reduce_kernel, groups, n_tensor),
        out_shape=[
            jax.ShapeDtypeStruct((cap, 8, *block), BF),
            jax.ShapeDtypeStruct(vectors.shape, F32),
        ],
        in_specs=[pl.BlockSpec(memory_space=pltpu.SMEM), any_spec, vmem],
        out_specs=[vmem, vmem],
        scratch_shapes=[
            pltpu.VMEM((n_units, n_tensor, 2, 2, *block), BF),
            pltpu.VMEM((n_units, n_tensor, 2, 2, *block), BF),
            pltpu.VMEM((n_units, n_tensor, 2, *block), BF),
            pltpu.VMEM((n_units, n_tensor, *block), BF),
            pltpu.VMEM((n_units, n_tensor, *block), BF),
            pltpu.VMEM((n_units, n_tensor, *block), BF),
            pltpu.VMEM((n_units, *block), BF),
            pltpu.VMEM((8, cap, *block), BF),
            pltpu.VMEM((3, *vectors.shape), F32),
            pltpu.VMEM((n_tensor - 1, *vectors.shape), F32),
            dma((n_groups,)), dma((n_groups,)), dma((n_groups,)),
            dma((n_groups, n_tensor)), dma((n_groups, n_tensor)),
            dma((n_groups, n_tensor)), dma((n_groups, n_tensor)),
            dma((n_groups, n_tensor)), dma((n_groups, n_tensor, 2)),
            dma((7,)), dma((7,)), dma((2 + n_tensor,)), dma((2 + n_tensor,)), dma((1,)),
        ],
        compiler_params=pltpu.CompilerParams(collective_id=1, has_side_effects=True, vmem_limit_bytes=56 << 20),
        name="reduce_units",
    )(unit_of_slot, grads, vectors)
    return out.reshape(cap, -1, width), vsum


def per_device(
    tokens_in,
    out_grad,
    lengths,
    owners,
    matrix_master,
    matrix_m1,
    matrix_m2,
    shared_params,
    bias_params,
):
    n_tensor = lax.axis_size("tensor")
    n_data = lax.axis_size("dp")
    tensor_index = lax.axis_index("tensor")
    data_index = lax.axis_index("dp")
    rows_here, width = tokens_in.shape
    slot_cap = matrix_master.shape[1]
    unit_rows = matrix_master.shape[2]
    n_units = owners.shape[0]
    n_slots = n_data * slot_cap
    head_rows = width // n_tensor
    heads_here = head_rows // HD
    ff_rows = (n_units * unit_rows - 4 * head_rows) // 2
    slot_of_unit, unit_of_slot, occupied = slot_tables(owners, n_slots, slot_cap)

    own_kernels = n_data == 8 and head_rows == unit_rows and unit_rows % 128 == 0 and n_tensor > 1

    back = -(-(DOC_MOST - 1) // rows_here)
    reach = back * rows_here
    sizes = lengths[0]
    upto = jnp.arange(sizes.shape[0])[:, None] >= jnp.arange(sizes.shape[0])[None, :]
    bounds = jnp.sum(jnp.where(upto, sizes[None, :], 0), axis=1)
    places = tensor_index * rows_here + jnp.arange(rows_here, dtype=jnp.int32)
    starts = jnp.max(jnp.where(places[:, None] >= bounds[None, :], bounds[None, :], 0), axis=1)
    first_seen = (starts - tensor_index * rows_here + reach)[None, :]

    shared = shared_params[0]
    inputs_f32 = tokens_in.astype(F32)
    normed_one, hat_one, inverse_one = norm_rows(inputs_f32, shared[0], shared[1])
    normed_low = normed_one.astype(BF)
    if own_kernels:
        (
            w_att, w_fc, w_proj, normed_all, all_bias,
            q_scaled, keys_in, values_in, attended, log_norms, peaks, hidden,
        ) = forward_spread(
            matrix_master[0].astype(BF), normed_low, tokens_in, bias_params[0, 0], first_seen, shared,
            slot_of_unit, n_tensor, back,
        )
        w_q, w_k, w_v, w_out = (w_att[i] for i in range(4))
    else:
        units = gather_units(matrix_master[0], slot_of_unit)
        stacks = units.reshape(n_tensor, n_units * unit_rows, width)
        part = lambda first, count: stacks[:, first : first + count].reshape(-1, width)
        w_q, w_k, w_v, w_out = (part(i * head_rows, head_rows) for i in range(4))
        w_fc = part(4 * head_rows, ff_rows)
        w_proj = part(4 * head_rows + ff_rows, ff_rows)
        all_bias = lax.all_gather(bias_params[0], "tensor", axis=0, tiled=True).reshape(n_tensor, -1)
        before = [
            lax.ppermute(normed_low, "tensor", [(i, i + r) for i in range(n_tensor - r)])
            for r in range(min(back, n_tensor - 1), 0, -1)
        ]
        blank = [jnp.zeros_like(normed_low)] * (back - len(before))
        normed_all = jnp.concatenate([*blank, *before, normed_low], axis=0)
    if not own_kernels:
        bias = lambda first, count: all_bias[:, first : first + count].reshape(-1)
        b_q, b_k, b_v = (bias(i * head_rows, head_rows) for i in range(3))
        q_scaled = (rows_by_rows(normed_low, w_q) + b_q).astype(BF) * jnp.asarray(1.0 / math.sqrt(HD), BF)
        keys_in = (rows_by_rows(normed_all, w_k) + b_k).astype(BF)
        values_in = (rows_by_rows(normed_all, w_v) + b_v).astype(BF)
        attended, log_norms, peaks = attend_forward(q_scaled, keys_in, values_in, first_seen)
        hidden = inputs_f32 + (plain_dot(attended, w_out) + shared[2])
    swap = (lambda v: v.swapaxes(0, 1)) if own_kernels else (lambda v: v)
    b_fc = swap(all_bias[:, 3 * head_rows :].reshape(n_tensor, -1, unit_rows)).reshape(-1)
    normed_two, hat_two, inverse_two = norm_rows(hidden, shared[3], shared[4])
    second_low = normed_two.astype(BF)
    pre_act = rows_by_rows(second_low, w_fc) + b_fc
    activ, gelu_back = jax.vjp(gelu_tanh, pre_act)
    activ_low = activ.astype(BF)
    layer_out = hidden + (plain_dot(activ_low, w_proj) + shared[5])

    grad_y = out_grad.astype(F32)
    grad_proj_w = cols_by_cols(activ_low, out_grad)
    grad_activ = rows_by_rows(out_grad, w_proj)
    grad_pre_low = gelu_back(grad_activ)[0].astype(BF)
    grad_fc_b = jnp.sum(grad_pre_low, axis=0, dtype=F32)
    grad_fc_w = cols_by_cols(grad_pre_low, second_low)
    grad_second = plain_dot(grad_pre_low, w_fc)
    grad_hidden = grad_y + norm_back(grad_second, hat_two, inverse_two, shared[3])
    grad_hidden_low = grad_hidden.astype(BF)
    grad_out_w = cols_by_cols(attended, grad_hidden_low)
    grad_attended = rows_by_rows(grad_hidden_low, w_out).astype(BF)
    grad_q, grad_k, grad_v = attend_backward(
        q_scaled, keys_in, values_in, attended, grad_attended, log_norms, first_seen
    )
    grad_q_w = cols_by_cols(grad_q, normed_low)
    grad_k_w = cols_by_cols(grad_k, normed_all)
    grad_v_w = cols_by_cols(grad_v, normed_all)
    grad_wide = plain_dot(grad_k, w_k) + plain_dot(grad_v, w_v)
    grad_first = grad_wide[reach:] + plain_dot(grad_q, w_q)
    for r in range(1, min(back, n_tensor - 1) + 1):
        away = grad_wide[reach - r * rows_here : reach - (r - 1) * rows_here].astype(BF)
        grad_first += lax.ppermute(away, "tensor", [(i, i - r) for i in range(r, n_tensor)]).astype(F32)
    input_grad = grad_hidden + norm_back(grad_first, hat_one, inverse_one, shared[0])

    head_here = jnp.max(peaks, axis=2).reshape(-1)
    grad_qkv_b = [jnp.sum(g, axis=0, dtype=F32) for g in (grad_q, grad_k, grad_v)]
    shared_part = jnp.stack(
        [
            jnp.sum(grad_first * hat_one, axis=0),
            jnp.sum(grad_first, axis=0),
            jnp.sum(grad_hidden_low, axis=0, dtype=F32),
            jnp.sum(grad_second * hat_two, axis=0),
            jnp.sum(grad_second, axis=0),
            jnp.sum(grad_y, axis=0),
        ]
    )
    by_tensor = lambda v: v.reshape(n_tensor, -1)
    fc_shape = (-1, n_tensor, unit_rows) if own_kernels else (n_tensor, -1, unit_rows)
    grad_fc_b = swap(grad_fc_b.reshape(fc_shape))
    bias_part = jnp.concatenate([by_tensor(v) for v in (*grad_qkv_b, grad_fc_b)], axis=1)
    if own_kernels:
        head_row = jnp.pad(head_here, (0, width - head_here.shape[0]))[None]
        vectors = jnp.concatenate([shared_part, bias_part.reshape(-1, width), head_row], axis=0)
        vectors = jnp.pad(vectors, ((0, 16 - vectors.shape[0]), (0, 0)))
        grad_units = jnp.concatenate(
            [g.astype(BF) for g in (grad_q_w, grad_k_w, grad_v_w, grad_out_w, grad_fc_w, grad_proj_w)], axis=0
        ).reshape(n_units, -1, width)
        my_grads, totals = reduce_units(
            grad_units, vectors, unit_of_slot, n_tensor, slot_cap, unit_groups(n_units)[::-1]
        )
        my_grads = my_grads.astype(F32)
        shared_grad, bias_total = totals[:6], totals[6:MAX_ROW].reshape(n_tensor, -1)
        head_all = totals[MAX_ROW, : head_here.shape[0]]
    else:
        head_all = lax.pmax(head_here, ("dp", "tensor"))
        shared_grad, bias_total = lax.psum((shared_part, bias_part), ("dp", "tensor"))
        by_stack = lambda g: g.astype(BF).reshape(n_tensor, -1, width)
        grad_units = jnp.concatenate(
            [by_stack(g) for g in (grad_q_w, grad_k_w, grad_v_w, grad_out_w, grad_fc_w, grad_proj_w)], axis=1
        ).reshape(units.shape)
        my_grads = scatter_units(grad_units, unit_of_slot).astype(F32)
    head_peak = lax.dynamic_slice_in_dim(head_all, tensor_index * heads_here, heads_here)
    bias_grad = lax.dynamic_index_in_dim(bias_total, tensor_index, 0, keepdims=False)

    my_units = lax.dynamic_slice_in_dim(unit_of_slot, data_index * slot_cap, slot_cap, 0)
    my_occupied = lax.dynamic_slice_in_dim(occupied, data_index * slot_cap, slot_cap, 0)[:, None, None]
    steps_done = float(STEP)
    first_new, second_new, master_new = adam_step(
        matrix_master[0], my_grads, matrix_m1[0], matrix_m2[0], steps_done, WEIGHT_DECAY
    )
    root_gamma = jnp.sqrt(CLIP_TAU / jnp.maximum(head_peak, CLIP_TAU))
    row_index = my_units[:, None] * unit_rows + jnp.arange(unit_rows, dtype=jnp.int32)[None, :]
    local_head = jnp.where(row_index < head_rows, row_index // HD, (row_index - head_rows) // HD)
    head_match = local_head[..., None] == jnp.arange(heads_here, dtype=jnp.int32)[None, None, :]
    picked_root = jnp.sum(jnp.where(head_match, root_gamma, 0.0), axis=-1)
    factor = jnp.where(row_index < 2 * head_rows, picked_root, 1.0)
    my_grads = jnp.where(my_occupied, my_grads, 0.0)
    master_new = jnp.where(my_occupied, master_new * factor[..., None], 0.0)
    first_new = jnp.where(my_occupied, first_new, 0.0)
    second_new = jnp.where(my_occupied, second_new, 0.0)
    shared_first, shared_second, shared_new = adam_step(
        shared, shared_grad, shared_params[1], shared_params[2], steps_done, 0.0
    )
    bias_first, bias_second, bias_new = adam_step(
        bias_params[0, 0], bias_grad, bias_params[1, 0], bias_params[2, 0], steps_done, 0.0
    )
    shared_out = jnp.stack([shared_grad, shared_first])
    bias_out = jnp.stack([bias_grad, bias_first])[:, None, :]
    return (
        layer_out,
        input_grad,
        head_peak,
        my_grads[None],
        first_new[None],
        second_new[None],
        master_new[None],
        shared_out,
        shared_second,
        shared_new,
        bias_out,
        bias_second[None],
        bias_new[None],
    )


def solution(mesh):
    in_specs = (
        P(("dp", "tensor"), None),
        P(("dp", "tensor"), None),
        P("dp", None),
        P(),
        P("tensor", "dp", None, None),
        P("tensor", "dp", None, None),
        P("tensor", "dp", None, None),
        P(),
        P(None, "tensor", None),
    )
    out_specs = (
        P(("dp", "tensor"), None),
        P(("dp", "tensor"), None),
        P("tensor"),
        P("tensor", "dp", None, None),
        P("tensor", "dp", None, None),
        P("tensor", "dp", None, None),
        P("tensor", "dp", None, None),
        P(),
        P(),
        P(),
        P(None, "tensor", None),
        P("tensor", None),
        P("tensor", None),
    )
    return jax.shard_map(
        per_device, mesh=mesh, in_specs=in_specs, out_specs=out_specs, check_vma=False
    )
```

```python
import functools
import math

import jax
import jax.numpy as jnp
from jax import lax
from jax.experimental import pallas as pl
from jax.experimental.pallas import tpu as pltpu
from jax.sharding import PartitionSpec as P

HD = 64
DOC_MOST = 1024
STEP = 10
PAIR = 2 * HD

EPS_NORM = 1e-05
BETA_ONE = 0.9
BETA_TWO = 0.95
LEARN_RATE = 0.08
WEIGHT_DECAY = 0.1
EPS_ADAM = 1e-08
CLIP_TAU = 10.0
MASKED = -1e30
GELU_A = 0.7978845608
GELU_B = 0.044715
BF = jnp.bfloat16
F32 = jnp.float32
MESH = pl.DeviceIdType.MESH
MAX_ROW = 13


def plain_dot(left, right):
    return jnp.dot(left, right, preferred_element_type=F32)


def rows_by_rows(left, right):
    return lax.dot_general(left, right, (((1,), (1,)), ((), ())), preferred_element_type=F32)


def cols_by_cols(left, right):
    return lax.dot_general(left, right, (((0,), (0,)), ((), ())), preferred_element_type=F32)


def gelu_tanh(values_in):
    return jax.nn.gelu(values_in, approximate=True)


def norm_rows(values_in, gain, shift):
    centre = jnp.mean(values_in, axis=-1, keepdims=True)
    shifted = values_in - centre
    inverse = lax.rsqrt(jnp.mean(shifted * shifted, axis=-1, keepdims=True) + EPS_NORM)
    normed = shifted * inverse
    return (normed * gain + shift, normed, inverse)


def norm_back(grad_in, normed, inverse, gain):
    scaled = grad_in * gain
    return inverse * (
        scaled
        - jnp.mean(scaled, axis=-1, keepdims=True)
        - normed * jnp.mean(scaled * normed, axis=-1, keepdims=True)
    )


def slot_tables(owners, n_slots, slot_cap):
    n_units = owners.shape[0]
    unit_order = jnp.arange(n_units, dtype=jnp.int32)
    same_owner = owners[:, None] == owners[None, :]
    earlier = unit_order[None, :] < unit_order[:, None]
    rank_counts = jnp.sum((same_owner & earlier).astype(jnp.int32), axis=1)
    slot_of_unit = owners * slot_cap + rank_counts
    matches = jnp.arange(n_slots, dtype=jnp.int32)[:, None] == slot_of_unit[None, :]
    occupied = jnp.any(matches, axis=1)
    unit_of_slot = jnp.sum(matches.astype(jnp.int32) * unit_order[None, :], axis=1)
    return (slot_of_unit, unit_of_slot, occupied)


def head_lanes(head):
    lane = lax.broadcasted_iota(jnp.int32, (1, PAIR), 1)
    return (lane < HD) if head == 0 else (lane >= HD)


def q_tiles(n_query, n_keys):
    size = min(256, n_query)
    reach = n_keys - n_query
    return size, reach + size


def fill_bias(bias_ref, first_ref):
    n_keys, n_query = bias_ref.shape
    reach = n_keys - n_query
    key = lax.broadcasted_iota(jnp.int32, (n_keys, n_query), 0)
    query = lax.broadcasted_iota(jnp.int32, (n_keys, n_query), 1) + reach
    seen = (key <= query) & (key >= first_ref[...])
    bias_ref[...] = jnp.where(seen, 0.0, MASKED)


def attend_kernel(first_ref, q_ref, k_ref, v_ref, o_ref, lse_ref, peak_ref, bias_ref):
    @pl.when(pl.program_id(0) == 0)
    def _():
        fill_bias(bias_ref, first_ref)

    n_keys, n_query = bias_ref.shape
    size, span = q_tiles(n_query, n_keys)
    for j in range(n_query // size):
        rows, keys = pl.ds(j * size, size), pl.ds(j * size, span)
        v_t = v_ref[keys, :].T
        outs = []
        for h in range(2):
            k_h = jnp.where(head_lanes(h), k_ref[keys, :], 0)
            s = rows_by_rows(k_h, q_ref[rows, :]) + bias_ref[keys, rows]
            top = jnp.max(s, axis=0, keepdims=True)
            p = jnp.exp(s - top)
            total = jnp.sum(p, axis=0, keepdims=True)
            o_t = plain_dot(v_t[h * HD : (h + 1) * HD], p.astype(BF))
            outs.append(o_t / total)
            lse_ref[0, h : h + 1, rows] = top + jnp.log(total)
            peak_ref[0, h : h + 1, rows] = top
        o_ref[rows, :] = jnp.concatenate(outs, axis=0).T.astype(BF)


def attend_forward(q_scaled, keys_in, values_in, first_seen):
    n_query, width = q_scaled.shape
    n_keys = keys_in.shape[0]
    pairs = width // PAIR
    column = lambda i: (0, i)
    stats = jax.ShapeDtypeStruct((pairs, 2, n_query), F32)
    stat_spec = pl.BlockSpec((1, 2, n_query), lambda i: (i, 0, 0))
    return pl.pallas_call(
        attend_kernel,
        grid=(pairs,),
        in_specs=[
            pl.BlockSpec((1, n_query), lambda i: (0, 0)),
            pl.BlockSpec((n_query, PAIR), column),
            pl.BlockSpec((n_keys, PAIR), column),
            pl.BlockSpec((n_keys, PAIR), column),
        ],
        out_specs=[pl.BlockSpec((n_query, PAIR), column), stat_spec, stat_spec],
        out_shape=[jax.ShapeDtypeStruct((n_query, width), BF), stats, stats],
        scratch_shapes=[pltpu.VMEM((n_keys, n_query), F32)],
        compiler_params=pltpu.CompilerParams(vmem_limit_bytes=48 << 20),
        name="attend_forward",
    )(first_seen, q_scaled, keys_in, values_in)


def attend_back_kernel(
    first_ref, q_ref, k_ref, v_ref, o_ref, do_ref, lse_ref, dq_ref, dk_ref, dv_ref,
    bias_ref, dk_acc, dv_acc, *, scale
):
    @pl.when(pl.program_id(0) == 0)
    def _():
        fill_bias(bias_ref, first_ref)

    n_keys, n_query = bias_ref.shape
    size, span = q_tiles(n_query, n_keys)
    dk_acc[...] = jnp.zeros_like(dk_acc)
    dv_acc[...] = jnp.zeros_like(dv_acc)
    for j in range(n_query // size):
        rows, keys = pl.ds(j * size, size), pl.ds(j * size, span)
        q_here, do_here = q_ref[rows, :], do_ref[rows, :]
        k_here, v_here = k_ref[keys, :], v_ref[keys, :]
        k_t = k_here.T
        meet = (do_here.astype(F32) * o_ref[rows, :].astype(F32)).T
        outs = []
        for h in range(2):
            lanes = head_lanes(h)
            delta = jnp.sum(meet[h * HD : (h + 1) * HD], axis=0, keepdims=True)
            s = rows_by_rows(jnp.where(lanes, k_here, 0), q_here) + bias_ref[keys, rows]
            p = jnp.exp(s - lse_ref[0, h : h + 1, rows])
            dp = rows_by_rows(jnp.where(lanes, v_here, 0), do_here)
            ds = (p * (dp - delta)).astype(BF)
            dv_acc[keys, :] += plain_dot(p.astype(BF), jnp.where(lanes, do_here, 0))
            dk_acc[keys, :] += plain_dot(ds, jnp.where(lanes, q_here, 0))
            outs.append(plain_dot(k_t[h * HD : (h + 1) * HD], ds))
        dq_ref[rows, :] = (jnp.concatenate(outs, axis=0).T * scale).astype(BF)
    dk_ref[...] = dk_acc[...].astype(BF)
    dv_ref[...] = dv_acc[...].astype(BF)


def attend_backward(q_scaled, keys_in, values_in, attended, grads_out, log_norms, first_seen):
    n_query, width = q_scaled.shape
    n_keys = keys_in.shape[0]
    pairs = width // PAIR
    column = lambda i: (0, i)
    q_spec = pl.BlockSpec((n_query, PAIR), column)
    k_spec = pl.BlockSpec((n_keys, PAIR), column)
    q_out = jax.ShapeDtypeStruct((n_query, width), BF)
    k_out = jax.ShapeDtypeStruct((n_keys, width), BF)
    return pl.pallas_call(
        functools.partial(attend_back_kernel, scale=1.0 / math.sqrt(HD)),
        grid=(pairs,),
        in_specs=[
            pl.BlockSpec((1, n_query), lambda i: (0, 0)),
            q_spec, k_spec, k_spec, q_spec, q_spec,
            pl.BlockSpec((1, 2, n_query), lambda i: (i, 0, 0)),
        ],
        out_specs=[q_spec, k_spec, k_spec],
        out_shape=[q_out, k_out, k_out],
        scratch_shapes=[
            pltpu.VMEM((n_keys, n_query), F32),
            pltpu.VMEM((n_keys, PAIR), F32),
            pltpu.VMEM((n_keys, PAIR), F32),
        ],
        compiler_params=pltpu.CompilerParams(vmem_limit_bytes=48 << 20),
        name="attend_backward",
    )(first_seen, q_scaled, keys_in, values_in, attended, grads_out, log_norms)


def adam_step(param, grad, first, second, steps_done, decay):
    first_new = BETA_ONE * first + (1.0 - BETA_ONE) * grad
    second_new = BETA_TWO * second + (1.0 - BETA_TWO) * grad * grad
    fix_one = 1.0 - BETA_ONE**steps_done
    fix_two = 1.0 - BETA_TWO**steps_done
    direction = first_new / fix_one / (jnp.sqrt(second_new / fix_two) + EPS_ADAM)
    return (first_new, second_new, param - LEARN_RATE * (direction + decay * param))


def take_kernel(picks_ref, from_ref, to_ref):
    to_ref[...] = from_ref[...]


def take_blocks(blocks, picks):
    shape = (blocks.shape[0], 1, *blocks.shape[2:])
    return pl.pallas_call(
        take_kernel,
        grid_spec=pltpu.PrefetchScalarGridSpec(
            num_scalar_prefetch=1,
            grid=picks.shape,
            in_specs=[pl.BlockSpec(shape, lambda i, p: (0, p[i], 0, 0))],
            out_specs=pl.BlockSpec(shape, lambda i, p: (0, i, 0, 0)),
        ),
        out_shape=jax.ShapeDtypeStruct((shape[0], picks.shape[0], *shape[2:]), blocks.dtype),
        compiler_params=pltpu.CompilerParams(vmem_limit_bytes=32 << 20),
        name="take_blocks",
    )(picks, blocks)


def gather_units(master, slot_of_unit):
    slots = lax.all_gather(master.astype(BF), ("tensor", "dp"), axis=0, tiled=True)
    n_tensor = lax.axis_size("tensor")
    slots = slots.reshape(n_tensor, -1, *master.shape[1:])
    return take_blocks(slots, slot_of_unit)


def scatter_units(units, unit_of_slot):
    slots = take_blocks(units, unit_of_slot)
    slots = slots.reshape(-1, *units.shape[2:])
    return lax.psum_scatter(slots, ("tensor", "dp"), scatter_dimension=0, tiled=True)


def send(src, dst, send_sem, recv_sem, to):
    copy = pltpu.make_async_remote_copy(
        src_ref=src, dst_ref=dst, send_sem=send_sem, recv_sem=recv_sem,
        device_id=to, device_id_type=MESH,
    )
    copy.start()


def arrived(ref, sem):
    pltpu.make_async_copy(ref, ref, sem).wait()


def place():
    d, t = lax.axis_index("dp"), lax.axis_index("tensor")
    return d, t, d % 2, (d // 2) % 2, d // 4


def greet(d, t, n_tensor):
    barrier = pltpu.get_barrier_semaphore()
    for k in range(1, 8):
        pl.semaphore_signal(barrier, inc=1, device_id=((d + k) % 8, t), device_id_type=MESH)
    for k in range(1, n_tensor):
        pl.semaphore_signal(barrier, inc=1, device_id=(d, (t + k) % n_tensor), device_id_type=MESH)
    pl.semaphore_wait(barrier, 6 + n_tensor)


def loop_with(count, body, events):
    def step(i, carry):
        body(i)
        for n, mine in events.items():
            @pl.when(i == n)
            def _(mine=mine):
                for event in mine:
                    event()
        return carry

    lax.fori_loop(0, count, step, 0)


def spaced(count, events):
    per = -(-len(events) // count)
    return {n: events[n * per : (n + 1) * per] for n in range(count) if events[n * per : (n + 1) * per]}


def attend_pair(i, q_ref, k_ref, v_ref, o_ref, lse_ref, peak_ref, bias_ref):
    n_keys, n_query = bias_ref.shape
    size, span = q_tiles(n_query, n_keys)
    lanes = pl.ds(pl.multiple_of(i * PAIR, PAIR), PAIR)
    for j in range(n_query // size):
        rows, keys = pl.ds(j * size, size), pl.ds(j * size, span)
        v_t = v_ref[keys, lanes].T
        outs = []
        for h in range(2):
            k_h = jnp.where(head_lanes(h), k_ref[keys, lanes], 0)
            s = rows_by_rows(k_h, q_ref[rows, lanes]) + bias_ref[keys, rows]
            top = jnp.max(s, axis=0, keepdims=True)
            p = jnp.exp(s - top)
            total = jnp.sum(p, axis=0, keepdims=True)
            o_t = plain_dot(v_t[h * HD : (h + 1) * HD], p.astype(BF))
            outs.append(o_t / total)
            lse_ref[i, h : h + 1, rows] = top + jnp.log(total)
            peak_ref[i, h : h + 1, rows] = top
        o_ref[rows, lanes] = jnp.concatenate(outs, axis=0).T.astype(BF)


def forward_kernel(
    n_tensor, back, scale,
    slot_ref, master_ref, a_ref, x_ref, bias_in_ref, first_ref, shared_ref,
    att_ref, fc_ref, proj_ref, wide_ref, biases_ref, q_ref, k_ref, v_ref, o_ref, lse_ref, peak_ref, hidden_ref,
    pieces, own, seen_ref, bias_rows, swap_send, swap_recv, local_sem, a_send, a_recv, bias_send, bias_recv,
    z_send, z_recv, xy_send, xy_recv, core_send, core_recv,
):
    d, t, core, x, y = place()
    column = y * 2 + x
    by_x, by_y = d + 2 - 4 * x, d + 4 - 8 * y
    sibling = d + 1 - 2 * core
    first, last = t > 0, t < n_tensor - 1
    rows_here, width = a_ref.shape
    weights = (att_ref, fc_ref, proj_ref)
    starts = [0]
    for w in weights:
        starts.append(starts[-1] + w.shape[0])
    greet(d, t, n_tensor)

    def tokens_up(r):
        @pl.when(last & (t >= r))
        def _():
            source = a_ref if r == 0 else wide_ref.at[back - r]
            send(source, wide_ref.at[back - r - 1], a_send.at[r], a_recv.at[r], (d, t + 1))

    def tokens_in(r):
        @pl.when(t > r)
        def _():
            arrived(wide_ref.at[back - r - 1], a_recv.at[r])
        if r + 1 < back:
            tokens_up(r + 1)

    tokens_up(0)
    for k in range(1, 8):
        to = (d + k) % 8
        send(master_ref.at[:, to], pieces.at[d], swap_send.at[k - 1], swap_recv.at[k - 1], (to, t))
    mine = pltpu.make_async_copy(master_ref.at[:, d], pieces.at[d], local_sem.at[0])
    mine.start()
    for k in range(1, n_tensor):
        send(bias_in_ref, biases_ref.at[t], bias_send.at[k - 1], bias_recv.at[k - 1], (d, (t + k) % n_tensor))
    biases_ref[t] = bias_in_ref[...]
    wide_ref[back] = a_ref[...]
    for r in range(back):
        @pl.when(t < back - r)
        def _(r=r):
            wide_ref[r] = jnp.zeros((rows_here, width), BF)
    fill_bias(seen_ref, first_ref)
    mine.wait()
    for k in range(1, 8):
        arrived(pieces.at[(d + 8 - k) % 8], swap_recv.at[k - 1])
    cap = master_ref.shape[0]
    for u in range(own.shape[0]):
        slot = slot_ref[u]
        own[u] = pieces[slot // cap, slot % cap]

    def block(g, at, col, c):
        return weights[g].at[:, at, col, c]

    def route(at):
        side = at * 2 // n_tensor
        one, two = by_x + (by_y - by_x) * side, by_y + (by_x - by_y) * side
        col_x, col_y, col_xy = y * 2 + 1 - x, (1 - y) * 2 + x, (1 - y) * 2 + 1 - x
        return one, two, col_x + (col_y - col_x) * side, col_y + (col_x - col_y) * side, col_xy

    def onward(g, k, at, source):
        one, two, _, _, _ = route(at)
        here = block(g, at, column, core)
        send(source, here, xy_send.at[g], xy_recv.at[g, k, 0], (one, t))
        send(source, here, xy_send.at[g], xy_recv.at[g, k, 1], (two, t))

    def forward(g, k, at):
        one, two, from_one, _, _ = route(at)
        got = block(g, at, from_one, core)
        arrived(got, xy_recv.at[g, k, 0])
        send(got, got, xy_send.at[g], xy_recv.at[g, k, 2], (two, t))

    def settle(g, k, at):
        _, _, _, from_two, beyond = route(at)
        arrived(block(g, at, from_two, core), xy_recv.at[g, k, 1])
        arrived(block(g, at, beyond, core), xy_recv.at[g, k, 2])
        got = weights[g].at[:, at, :, core]
        send(got, got, core_send.at[g, k], core_recv.at[g, k], (sibling, t))

    def done(g, k, at):
        arrived(weights[g].at[:, at, :, 1 - core], core_recv.at[g, k])
        arrived(weights[g].at[:, at, :, core], core_send.at[g, k])

    def z_go(g, s, up, source, at):
        i = 0 if up else 1

        @pl.when(last if up else first)
        def _():
            send(source, block(g, at, column, core), z_send.at[g, i, s], z_recv.at[g, i, s], (d, t + 1 if up else t - 1))

    def z_step(s, up):
        at = t - 1 - s if up else t + 1 + s
        return 1 + 2 * s + (0 if up else 1), at, (at >= 0) if up else (at < n_tensor)

    def z_event(g, s):
        for up in (True, False):
            k, at, have = z_step(s, up)

            @pl.when(have)
            def _(k=k, at=at, up=up):
                got = block(g, at, column, core)
                arrived(got, z_recv.at[g, 0 if up else 1, s])
                if s + 1 < n_tensor - 1:
                    z_go(g, s + 1, up, got, at)
                onward(g, k, at, got)

    def each(fn, g, s):
        if s < 0:
            fn(g, 0, t)
        else:
            for up in (True, False):
                k, at, have = z_step(s, up)
                pl.when(have)(functools.partial(fn, g, k, at))

    n_groups, steps = len(weights), n_tensor - 1
    local = []
    for g in range(n_groups):
        source = own.at[starts[g] : starts[g + 1]]
        for up in (True, False):
            z_go(g, 0, up, source, t)
        copy = pltpu.make_async_copy(source, block(g, t, column, core), local_sem.at[1 + g])
        copy.start()
        local.append(copy)
        onward(g, 0, t, source)

    def chain(g):
        events = []
        for s in range(steps + 2):
            if s < steps:
                events.append(functools.partial(z_event, g, s))
            if s <= steps:
                events.append(functools.partial(each, forward, g, s - 1))
            if s >= 1:
                if s == 1:
                    events.append(local[g].wait)
                events.append(functools.partial(each, settle, g, s - 2))
        return events

    events = chain(0)
    for r in range(back):
        events.insert(1 + 4 * r, functools.partial(tokens_in, r))
    early = [functools.partial(z_event, g, 0) for g in range(1, n_groups)]
    events[3:3] = early
    for event in events:
        event()
    late = []
    for g in range(1, n_groups):
        late += chain(g)[1:]
    for k in range(1, n_tensor):
        arrived(biases_ref.at[(t + n_tensor - k) % n_tensor], bias_recv.at[k - 1])
        arrived(bias_in_ref, bias_send.at[k - 1])
    per = width // n_tensor // 128
    for n in range(3):
        for at in range(n_tensor):
            for i in range(per):
                lanes = pl.ds((at * per + i) * 128, 128)
                bias_rows[n : n + 1, lanes] = biases_ref[at, n * per + i : n * per + i + 1]
    for s in range(-1, steps):
        each(done, 0, s)

    tile = 256

    def project(n, source_ref, into_ref, factor):
        def body(i):
            cols = pl.ds(pl.multiple_of(i * tile, tile), tile)
            w = att_ref[n, pl.ds(i * tile // (width // n_tensor), 1)].reshape(tile, width)
            for r in range(into_ref.shape[0] // rows_here):
                a = wide_ref[r] if source_ref is None else source_ref[...]
                full = rows_by_rows(a, w) + bias_rows[n : n + 1, cols]
                into_ref[r * rows_here : (r + 1) * rows_here, cols] = (full.astype(BF) * jnp.asarray(factor, BF)) if factor else full.astype(BF)
        return body

    tiles = width // tile
    n_late = len(late)
    cut = n_late // 5
    loop_with(tiles, project(0, a_ref, q_ref, scale), {})
    loop_with(tiles, project(1, None, k_ref, None), spaced(tiles, late[:cut]))
    loop_with(tiles, project(2, None, v_ref, None), spaced(tiles, late[cut : 2 * cut]))
    loop_with(
        width // PAIR,
        lambda i: attend_pair(i, q_ref, k_ref, v_ref, o_ref, lse_ref, peak_ref, seen_ref),
        spaced(width // PAIR, late[2 * cut :]),
    )
    w_out = att_ref[3].reshape(width, width)
    half = rows_here // 2
    for r in range(2):
        rows = pl.ds(r * half, half)
        hidden_ref[rows, :] = x_ref[rows, :].astype(F32) + (plain_dot(o_ref[rows, :], w_out) + shared_ref[2:3, :])

    for g in range(n_groups):
        if g > 0:
            for s in range(-1, steps):
                each(done, g, s)
        arrived(weights[g].at[:, :, pl.ds(0, 3), 0], xy_send.at[g])
        for up in (True, False):
            for s in range(steps):
                have = last if up else first
                if s > 0:
                    have = have & z_step(s - 1, up)[2]

                @pl.when(have)
                def _(g=g, s=s, up=up):
                    arrived(block(g, t, column, core), z_send.at[g, 0 if up else 1, s])
    for r in range(back):
        @pl.when(last & (t >= r))
        def _(r=r):
            arrived(a_ref, a_send.at[r])
    for k in range(1, 8):
        arrived(pieces.at[0], swap_send.at[k - 1])


def forward_spread(master_low, normed_low, tokens, bias_row, first_seen, shared, slot_of_unit, n_tensor, back):
    cap, unit_rows, width = master_low.shape
    n_units = slot_of_unit.shape[0]
    n_ff = (n_units - 4) // 2
    piece = unit_rows // 8
    rows = normed_low.shape[0]
    n_keys = (back + 1) * rows
    bias_row = bias_row.reshape(-1, 128)
    any_spec = pl.BlockSpec(memory_space=pl.ANY)
    vmem = pl.BlockSpec(memory_space=pltpu.VMEM)
    dma = pltpu.SemaphoreType.DMA
    shape = jax.ShapeDtypeStruct
    units = lambda n: shape((n, n_tensor, 4, 2, piece, width), BF)
    stats = shape((width // PAIR, 2, rows), F32)
    outs = pl.pallas_call(
        functools.partial(forward_kernel, n_tensor, back, 1.0 / math.sqrt(HD)),
        out_shape=[
            units(4), units(n_ff), units(n_ff),
            shape((back + 1, rows, width), BF), shape((n_tensor, *bias_row.shape), F32),
            shape((rows, width), BF), shape((n_keys, width), BF), shape((n_keys, width), BF), shape((rows, width), BF),
            stats, stats, shape((rows, width), F32),
        ],
        in_specs=[pl.BlockSpec(memory_space=pltpu.SMEM), any_spec, vmem, vmem, vmem, vmem, vmem],
        out_specs=[vmem, any_spec, any_spec, vmem, vmem, vmem, vmem, vmem, vmem, vmem, vmem, vmem],
        scratch_shapes=[
            pltpu.VMEM((8, cap, piece, width), BF),
            pltpu.VMEM((n_units, piece, width), BF),
            pltpu.VMEM((n_keys, rows), F32),
            pltpu.VMEM((3, width), F32),
            dma((7,)), dma((7,)), dma((4,)), dma((back,)), dma((back,)),
            dma((n_tensor - 1,)), dma((n_tensor - 1,)),
            dma((3, 2, n_tensor - 1)), dma((3, 2, n_tensor - 1)),
            dma((3,)), dma((3, 2 * n_tensor - 1, 3)),
            dma((3, 2 * n_tensor - 1)), dma((3, 2 * n_tensor - 1)),
        ],
        compiler_params=pltpu.CompilerParams(collective_id=0, has_side_effects=True, vmem_limit_bytes=56 << 20),
        name="forward_spread",
    )(slot_of_unit, master_low.reshape(cap, 8, piece, width), normed_low, tokens, bias_row, first_seen, shared)
    att, fc, proj, wide, biases, q, k, v, o, lse, peaks, hidden = outs
    return (
        att.reshape(4, -1, width), fc.reshape(-1, width), proj.reshape(-1, width), wide.reshape(-1, width),
        biases.reshape(n_tensor, -1), q, k, v, o, lse, peaks, hidden,
    )


def add_blocks(into, part, count):
    def body(i, carry):
        a = into(i)
        a[...] = a[...] + part(i)[...]
        return carry

    lax.fori_loop(0, count, body, 0)


class Reducer:
    def __init__(self, groups, n_tensor, other, near, one, two, up_in, down_in, final, sems):
        self.groups, self.n_tensor = groups, n_tensor
        self.other, self.near, self.one, self.two = other, near, one, two
        self.up_in, self.down_in, self.final = up_in, down_in, final
        (
            self.near_sem, self.core_send, self.core_recv, self.one_send, self.one_recv,
            self.two_send, self.two_recv, self.z_send, self.z_recv,
        ) = sems
        self.d, self.t, self.core, self.x, self.y = place()
        self.by_x, self.by_y = self.d + 2 - 4 * self.x, self.d + 4 - 8 * self.y
        self.sibling = self.d + 1 - 2 * self.core
        self.order = sorted(range(n_tensor), key=lambda a: -abs(2 * a - n_tensor + 1))
        self.merges = [(g, at) for g in range(len(groups)) for at in self.order]
        self.starts, total = [], 0
        for refs in groups:
            self.starts.append(total)
            total += sum(r.shape[0] for r in refs)
        self.ends = [*self.starts[1:], total]

    @staticmethod
    def scratch(n_units, n_group, n_groups, n_refs, n_tensor, block):
        dma = pltpu.SemaphoreType.DMA
        return [
            pltpu.VMEM((n_units, n_tensor, 2, 2, *block), BF),
            pltpu.VMEM((2, n_group, 2, 2, *block), BF),
            pltpu.VMEM((n_units, n_tensor, 2, *block), BF),
            pltpu.VMEM((n_units, n_tensor, *block), BF),
            pltpu.VMEM((n_units, n_tensor, *block), BF),
            pltpu.VMEM((n_units, n_tensor, *block), BF),
            dma((2, n_refs)), dma((n_groups, n_refs)), dma((n_groups, n_refs)),
            dma((n_groups, n_tensor)), dma((n_groups, n_tensor)),
            dma((n_groups, n_tensor)), dma((n_groups, n_tensor)),
            dma((n_groups, n_tensor)), dma((n_groups, n_tensor, 2)),
        ]

    def parts(self, g):
        u = self.starts[g]
        for n, ref in enumerate(self.groups[g]):
            yield n, ref, u, ref.shape[0]
            u += ref.shape[0]

    def units(self, g):
        return pl.ds(self.starts[g], self.ends[g] - self.starts[g])

    def count(self, g):
        return self.ends[g] - self.starts[g]

    def near_copies(self, m):
        g, at = self.merges[m]
        for n, ref, u, many in self.parts(g):
            yield pltpu.make_async_copy(
                ref.at[:, at, :, :, self.core],
                self.near.at[m % 2, pl.ds(u - self.starts[g], many)],
                self.near_sem.at[m % 2, n],
            )

    def start(self):
        for g in range(len(self.groups)):
            for n, ref, u, many in self.parts(g):
                send(
                    ref.at[:, :, :, :, 1 - self.core], self.other.at[pl.ds(u, many)],
                    self.core_send.at[g, n], self.core_recv.at[g, n], (self.sibling, self.t),
                )
        for m in range(2):
            for copy in self.near_copies(m):
                copy.start()

    def by_rows(self, at):
        return at * 2 < self.n_tensor

    def first_hop(self, m):
        g, at = self.merges[m]
        if m % self.n_tensor == 0:
            for n, ref, u, many in self.parts(g):
                arrived(self.other.at[pl.ds(u, many)], self.core_recv.at[g, n])
        for copy in self.near_copies(m):
            copy.wait()
        u0 = self.starts[g]
        add_blocks(
            lambda i: self.other.at[u0 + i // 4, at, (i // 2) % 2, i % 2],
            lambda i: self.near.at[m % 2, i // 4, (i // 2) % 2, i % 2],
            4 * self.count(g),
        )
        if m + 2 < len(self.merges):
            for copy in self.near_copies(m + 2):
                copy.start()
        us = self.units(g)
        rows = self.by_rows(at)
        source = self.other.at[us, at, 1 - self.y] if rows else self.other.at[us, at, :, 1 - self.x]
        to = self.by_y if rows else self.by_x
        send(source, self.one.at[us, at], self.one_send.at[g, at], self.one_recv.at[g, at], (to, self.t))

    def second_hop(self, m):
        g, at = self.merges[m]
        us, u0 = self.units(g), self.starts[g]
        arrived(self.one.at[us, at], self.one_recv.at[g, at])
        if self.by_rows(at):
            into = lambda i: self.other.at[u0 + i // 2, at, self.y, i % 2]
            source, to = self.other.at[us, at, self.y, 1 - self.x], self.by_x
        else:
            into = lambda i: self.other.at[u0 + i // 2, at, i % 2, self.x]
            source, to = self.other.at[us, at, 1 - self.y, self.x], self.by_y
        add_blocks(into, lambda i: self.one.at[u0 + i // 2, at, i % 2], 2 * self.count(g))
        send(source, self.two.at[us, at], self.two_send.at[g, at], self.two_recv.at[g, at], (to, self.t))

    def plane_sum(self, m):
        g, at = self.merges[m]
        us, u0, n = self.units(g), self.starts[g], self.count(g)
        arrived(self.two.at[us, at], self.two_recv.at[g, at])
        add_blocks(lambda i: self.other.at[u0 + i, at, self.y, self.x], lambda i: self.two.at[u0 + i, at], n)
        if at > 0:
            pl.when(self.t == 0)(functools.partial(self.line_go, g, at, True))
        if at < self.n_tensor - 1:
            pl.when(self.t == self.n_tensor - 1)(functools.partial(self.line_go, g, at, False))

    def line_go(self, g, at, up):
        us = self.units(g)
        into, way, to = (self.up_in, 0, self.t + 1) if up else (self.down_in, 1, self.t - 1)
        send(self.other.at[us, at, self.y, self.x], into.at[us, at], self.z_send.at[g, at], self.z_recv.at[g, at, way], (self.d, to))

    def line_in(self, g, at, up):
        us, u0, n, t = self.units(g), self.starts[g], self.count(g), self.t
        buffer, way = (self.up_in, 0) if up else (self.down_in, 1)
        arrived(buffer.at[us, at], self.z_recv.at[g, at, way])
        add_blocks(lambda i: self.other.at[u0 + i, at, self.y, self.x], lambda i: buffer.at[u0 + i, at], n)
        pl.when(t < at if up else t > at)(functools.partial(self.line_go, g, at, up))

    def line(self, g, k):
        n, t = self.n_tensor, self.t
        high, low = n - 1 - k, k
        near_top = t * 2 >= n
        came_down = (t >= low) & (t < n - 1)
        pl.when(came_down & near_top)(functools.partial(self.line_in, g, low, False))
        pl.when((t <= high) & (t > 0))(functools.partial(self.line_in, g, high, True))
        pl.when(came_down & (t * 2 < n))(functools.partial(self.line_in, g, low, False))

    def keep(self, g):
        us = self.units(g)
        self.final[us] = self.other[us, self.t, self.y, self.x]

    def events(self):
        n, count = self.n_tensor, len(self.groups)
        first, second, third = (
            [[functools.partial(f, g * n + i) for i in range(n)] for g in range(count)]
            for f in (self.first_hop, self.second_hop, self.plane_sum)
        )
        lines = [[functools.partial(self.line, g, k) for k in range(n - 1)] + [functools.partial(self.keep, g)] for g in range(count)]
        return first, second, third, lines

    def finish(self):
        for g in range(len(self.groups)):
            us = self.units(g)
            for n, ref, u, many in self.parts(g):
                arrived(self.other.at[pl.ds(u, many)], self.core_send.at[g, n])
            for at in range(self.n_tensor):
                arrived(self.one.at[us, at], self.one_send.at[g, at])
                arrived(self.two.at[us, at], self.two_send.at[g, at])

                @pl.when(self.t != at)
                def _(us=us, g=g, at=at):
                    arrived(self.up_in.at[us, at], self.z_send.at[g, at])


REDUCER = 15


def backward_kernel(
    n_tensor, back, scale,
    proj_ref, fc_ref, q_ref, k_ref, v_ref, o_ref, do_ref, lse_ref, first_ref, wide_ref, att_ref,
    shard_ref, grad_ref, gq_ref, gk_ref, gv_ref, sums_ref, *scratch,
):
    reducer_scratch, (
        seen_ref, q_in, k_in, v_in, o_in, do_in, dq_ref, dk_ref, dv_ref, big, away, away_in, stage, dk_acc, dv_acc,
        pair_sem, load_sem, stage_sem, away_send, away_recv,
    ) = scratch[:REDUCER], scratch[REDUCER:]
    d, t, core, x, y = place()
    greet(d, t, n_tensor)
    n_fc = fc_ref.shape[0]
    other, near, one, two, up_in, down_in, *sems = reducer_scratch
    reducer = Reducer([[fc_ref], [proj_ref]], n_tensor, other, near, one, two, up_in, down_in, shard_ref, sems)
    reducer.start()
    rows_here, width = do_ref.shape
    n_keys = k_ref.shape[0]
    size, span = q_tiles(rows_here, n_keys)
    sources = ((q_ref, q_in), (k_ref, k_in), (v_ref, v_in), (o_ref, o_in), (do_ref, do_in))

    def pair_copies(i):
        lanes = pl.ds(pl.multiple_of(i * PAIR, PAIR), PAIR)
        return [
            pltpu.make_async_copy(ref.at[:, lanes], buffer.at[i % 2], pair_sem.at[i % 2, n])
            for n, (ref, buffer) in enumerate(sources)
        ]

    for copy in pair_copies(0):
        copy.start()
    weights = pltpu.make_async_copy(att_ref.at[pl.ds(0, 3 * width)], big, load_sem.at[0])
    weights.start()
    fill_bias(seen_ref, first_ref)
    pairs = width // PAIR

    def attend_back(i):
        for copy in pair_copies(i):
            copy.wait()

        @pl.when(i + 1 < pairs)
        def _():
            for copy in pair_copies(i + 1):
                copy.start()

        slot = i % 2
        lanes_here = pl.ds(pl.multiple_of(i * PAIR, PAIR), PAIR)
        dk_acc[...] = jnp.zeros_like(dk_acc)
        dv_acc[...] = jnp.zeros_like(dv_acc)
        dq_sum = jnp.zeros((1, PAIR), F32)
        for j in range(rows_here // size):
            rows, keys = pl.ds(j * size, size), pl.ds(j * size, span)
            q_here, do_here = q_in[slot, rows, :], do_in[slot, rows, :]
            k_here, v_here = k_in[slot, keys, :], v_in[slot, keys, :]
            k_t = k_here.T
            meet = (do_here.astype(F32) * o_in[slot, rows, :].astype(F32)).T
            outs = []
            for h in range(2):
                lanes = head_lanes(h)
                delta = jnp.sum(meet[h * HD : (h + 1) * HD], axis=0, keepdims=True)
                s = rows_by_rows(jnp.where(lanes, k_here, 0), q_here) + seen_ref[keys, rows]
                p = jnp.exp(s - lse_ref[i, h : h + 1, rows])
                dp = rows_by_rows(jnp.where(lanes, v_here, 0), do_here)
                ds = (p * (dp - delta)).astype(BF)
                dv_acc[keys, :] += plain_dot(p.astype(BF), jnp.where(lanes, do_here, 0))
                dk_acc[keys, :] += plain_dot(ds, jnp.where(lanes, q_here, 0))
                outs.append(plain_dot(k_t[h * HD : (h + 1) * HD], ds))
            dq = (jnp.concatenate(outs, axis=0).T * scale).astype(BF)
            dq_ref[rows, lanes_here] = dq
            dq_sum += jnp.sum(dq.astype(F32), axis=0, keepdims=True)
        dk, dv = dk_acc[...].astype(BF), dv_acc[...].astype(BF)
        dk_ref[:, lanes_here] = dk
        dv_ref[:, lanes_here] = dv
        sums_ref[0:1, lanes_here] = dq_sum
        sums_ref[1:2, lanes_here] = jnp.sum(dk.astype(F32), axis=0, keepdims=True)
        sums_ref[2:3, lanes_here] = jnp.sum(dv.astype(F32), axis=0, keepdims=True)

    tile = 256
    tiles = width // tile

    def input_grad(r):
        rows = pl.ds((back - r) * rows_here, rows_here)

        def body(i):
            cols = pl.ds(pl.multiple_of(i * tile, tile), tile)
            total = plain_dot(dk_ref[rows, :], big[width : 2 * width, cols]) + plain_dot(dv_ref[rows, :], big[2 * width :, cols])
            if r == 0:
                grad_ref[:, cols] = total + plain_dot(dq_ref[...], big[:width, cols])
            else:
                away[r - 1, :, cols] = total.astype(BF)

        return body

    def have_down(r):
        return (t + 1 >= r) & (t + 1 < n_tensor)

    def give(r):
        if r < back:
            @pl.when(have_down(r + 1) & (t >= r))
            def _():
                arrived(away_in.at[r], away_recv.at[r])
                away[r - 1] = (away[r - 1].astype(F32) + away_in[r].astype(F32)).astype(BF)

        @pl.when(t >= r)
        def _():
            send(away.at[r - 1], away_in.at[r - 1], away_send.at[r - 1], away_recv.at[r - 1], (d, t - 1))

    def weight_grad(n, from_ref, into_ref, first_row, many):
        def body(i):
            cols = pl.ds(pl.multiple_of(i * tile, tile), tile)
            slot = i % 2
            out = pltpu.make_async_copy(stage.at[slot], into_ref.at[pl.ds(i * tile, tile)], stage_sem.at[slot])

            @pl.when((i >= 2) | (n > 0))
            def _():
                out.wait()

            total = lax.dot_general(
                from_ref[:, cols], tokens_of(first_row, many), (((0,), (0,)), ((), ())), preferred_element_type=F32
            )
            stage[slot] = total.astype(BF)
            out.start()

        return body

    def tokens_of(first_row, many):
        return big[pl.ds(first_row, many), :]

    first, second, third, lines = reducer.events()
    loop_with(pairs, attend_back, {1: first[0], 3: first[1]})
    weights.wait()
    for r in range(back, -1, -1):
        loop_with(tiles, input_grad(r), {})
        if r == back:
            give(r)
    load = pltpu.make_async_copy(wide_ref, big.at[pl.ds(0, n_keys)], load_sem.at[1])
    load.start()
    for event in second[0]:
        event()
    load.wait()
    own = n_keys - rows_here
    loop_with(tiles, weight_grad(0, dq_ref, gq_ref, own, rows_here), {})
    loop_with(tiles, weight_grad(1, dk_ref, gk_ref, 0, n_keys), {1: third[0]})
    loop_with(tiles, weight_grad(2, dv_ref, gv_ref, 0, n_keys), {1: lines[0][:1]})
    for r in range(back - 1, 0, -1):
        give(r)
    for event in lines[0][1:] + second[1] + third[1] + lines[1]:
        event()
    for slot in range(2):
        arrived(stage.at[slot], stage_sem.at[slot])

    @pl.when(have_down(1))
    def _():
        arrived(away_in.at[0], away_recv.at[0])
        grad_ref[...] = grad_ref[...] + away_in[0].astype(F32)
    for r in range(1, back + 1):
        @pl.when(t >= r)
        def _(r=r):
            arrived(away.at[r - 1], away_send.at[r - 1])
    reducer.finish()


def backward_reduce(grad_proj, grad_fc, q, k, v, o, do, lse, first_seen, wide, w_att, n_tensor, back):
    rows, width = q.shape
    n_keys = k.shape[0]
    n_ff = grad_fc.shape[0]
    block = grad_fc.shape[-2:]
    any_spec = pl.BlockSpec(memory_space=pl.ANY)
    vmem = pl.BlockSpec(memory_space=pltpu.VMEM)
    dma = pltpu.SemaphoreType.DMA
    shape = jax.ShapeDtypeStruct
    square = shape((width, width), BF)
    pair = lambda n: pltpu.VMEM((2, n, PAIR), BF)
    return pl.pallas_call(
        functools.partial(backward_kernel, n_tensor, back, 1.0 / math.sqrt(HD)),
        out_shape=[shape((2 * n_ff, *block), BF), shape((rows, width), F32), square, square, square, shape((3, width), F32)],
        in_specs=[any_spec] * 7 + [vmem, vmem] + [any_spec] * 2,
        out_specs=[vmem, vmem, any_spec, any_spec, any_spec, vmem],
        scratch_shapes=[
            *Reducer.scratch(2 * n_ff, n_ff, 2, 1, n_tensor, block),
            pltpu.VMEM((n_keys, rows), F32),
            pair(rows), pair(n_keys), pair(n_keys), pair(rows), pair(rows),
            pltpu.VMEM((rows, width), BF), pltpu.VMEM((n_keys, width), BF), pltpu.VMEM((n_keys, width), BF),
            pltpu.VMEM((3 * width, width), BF),
            pltpu.VMEM((back, rows, width), BF), pltpu.VMEM((back, rows, width), BF),
            pltpu.VMEM((2, 256, width), BF),
            pltpu.VMEM((n_keys, PAIR), F32), pltpu.VMEM((n_keys, PAIR), F32),
            dma((2, 5)), dma((2,)), dma((2,)), dma((back,)), dma((back,)),
        ],
        compiler_params=pltpu.CompilerParams(collective_id=1, has_side_effects=True, vmem_limit_bytes=60 << 20),
        name="backward_reduce",
    )(grad_proj, grad_fc, q, k, v, o, do, lse, first_seen, wide, w_att)


def join(row, a, b):
    return jnp.where(row == MAX_ROW, jnp.maximum(a, b), a + b)


def finish_kernel(
    n_tensor,
    unit_ref, gq_ref, gk_ref, gv_ref, go_ref, shard_ref, grad_ref, hidden_ref, x_ref, shared_ref, v_ref,
    out_ref, vsum_ref, input_ref, *scratch,
):
    reducer_scratch, (final, outgo, v_in, v_z, swap_send, swap_recv, v_send, v_recv, local_sem) = (
        scratch[:REDUCER], scratch[REDUCER:]
    )
    d, t, core, x, y = place()
    greet(d, t, n_tensor)
    other, near, one, two, up_in, down_in, *sems = reducer_scratch
    reducer = Reducer([[gq_ref, gk_ref], [gv_ref, go_ref]], n_tensor, other, near, one, two, up_in, down_in, final, sems)
    reducer.start()
    rows_here = x_ref.shape[0]
    n_att = other.shape[0]
    final[n_att:] = shard_ref[...]

    vsum_ref[...] = v_ref[...]
    part = 128
    gain = shared_ref[0:1, :]

    def norm_back_rows(i, carry):
        rows = pl.ds(pl.multiple_of(i * part, part), part)
        _, hat, inverse = norm_rows(x_ref[rows, :].astype(F32), 1.0, 0.0)
        grad = grad_ref[rows, :]
        input_ref[rows, :] = hidden_ref[rows, :] + norm_back(grad, hat, inverse, gain)
        vsum_ref[0:1, :] += jnp.sum(grad * hat, axis=0, keepdims=True)
        vsum_ref[1:2, :] += jnp.sum(grad, axis=0, keepdims=True)
        return carry

    lax.fori_loop(0, rows_here // part, norm_back_rows, 0)
    row = lax.broadcasted_iota(jnp.int32, vsum_ref.shape, 0)
    hops = (reducer.sibling, reducer.by_x, reducer.by_y)

    def vector_go(i):
        send(vsum_ref, v_in.at[i], v_send.at[i], v_recv.at[i], (hops[i], t))

    def vector_in(i):
        arrived(v_in.at[i], v_recv.at[i])
        arrived(v_in.at[i], v_send.at[i])
        vsum_ref[...] = join(row, vsum_ref[...], v_in[i])
        if i + 1 < len(hops):
            vector_go(i + 1)
        else:
            for k in range(1, n_tensor):
                send(vsum_ref, v_z.at[k - 1], v_send.at[2 + k], v_recv.at[2 + k], (d, (t + k) % n_tensor))

    def vector_end():
        for k in range(1, n_tensor):
            arrived(v_z.at[k - 1], v_recv.at[2 + k])
            arrived(v_z.at[k - 1], v_send.at[2 + k])
        for k in range(1, n_tensor):
            vsum_ref[...] = join(row, vsum_ref[...], v_z[k - 1])

    vector_go(0)
    first, second, third, lines = reducer.events()
    events = first[0] + first[1] + second[0] + third[0] + second[1] + lines[0] + third[1] + lines[1]
    for n, event in enumerate((functools.partial(vector_in, 0), functools.partial(vector_in, 1), functools.partial(vector_in, 2), vector_end)):
        events.insert(4 + 5 * n, event)
    for event in events:
        event()

    cap = out_ref.shape[0]
    for k in range(1, 9):
        to = (d + k) % 8
        for j in range(cap):
            outgo[to, j] = final[unit_ref[to * cap + j]]
        if k < 8:
            send(outgo.at[to], out_ref.at[:, d], swap_send.at[k - 1], swap_recv.at[k - 1], (to, t))
    keep = pltpu.make_async_copy(outgo.at[d], out_ref.at[:, d], local_sem.at[0])
    keep.start()
    for k in range(1, 8):
        arrived(out_ref.at[:, (d + 8 - k) % 8], swap_recv.at[k - 1])
    reducer.finish()
    for k in range(1, 8):
        arrived(outgo.at[0], swap_send.at[k - 1])
    keep.wait()


def finish_reduce(grads, shard, grad_first, grad_hidden, tokens, shared, vectors, unit_of_slot, n_tensor, cap):
    block = shard.shape[1:]
    n_units = len(grads) + shard.shape[0]
    rows, width = tokens.shape
    any_spec = pl.BlockSpec(memory_space=pl.ANY)
    vmem = pl.BlockSpec(memory_space=pltpu.VMEM)
    dma = pltpu.SemaphoreType.DMA
    shape = jax.ShapeDtypeStruct
    out, vsum, input_grad = pl.pallas_call(
        functools.partial(finish_kernel, n_tensor),
        out_shape=[shape((cap, 8, *block), BF), shape(vectors.shape, F32), shape((rows, width), F32)],
        in_specs=[pl.BlockSpec(memory_space=pltpu.SMEM)] + [any_spec] * 4 + [vmem] * 6,
        out_specs=[vmem, vmem, vmem],
        scratch_shapes=[
            *Reducer.scratch(len(grads), 2, 2, 2, n_tensor, block),
            pltpu.VMEM((n_units, *block), BF),
            pltpu.VMEM((8, cap, *block), BF),
            pltpu.VMEM((3, *vectors.shape), F32),
            pltpu.VMEM((n_tensor - 1, *vectors.shape), F32),
            dma((7,)), dma((7,)), dma((2 + n_tensor,)), dma((2 + n_tensor,)), dma((1,)),
        ],
        compiler_params=pltpu.CompilerParams(collective_id=2, has_side_effects=True, vmem_limit_bytes=48 << 20),
        name="finish_reduce",
    )(unit_of_slot, *grads, shard, grad_first, grad_hidden, tokens, shared, vectors)
    return out.reshape(cap, -1, width), vsum, input_grad


def feed_forward_kernel(
    hidden_ref, dy_ref, shared_ref, bias_ref, fc_ref, proj_ref,
    out_ref, grad_ref, low_ref, fc_grad_ref, proj_grad_ref, fc_bias_ref, sums_ref,
    second_ref, acc_ref,
):
    step = pl.program_id(0)

    @pl.when(step == 0)
    def _():
        normed, _, _ = norm_rows(hidden_ref[...], shared_ref[3:4, :], shared_ref[4:5, :])
        second_ref[...] = normed.astype(BF)
        out_ref[...] = hidden_ref[...] + shared_ref[5:6, :]
        acc_ref[...] = jnp.zeros_like(acc_ref)

    dy, second = dy_ref[...], second_ref[...]
    pre = rows_by_rows(second, fc_ref[...]) + bias_ref[0]
    cube = pre * pre
    inner = jnp.tanh(GELU_A * (pre + GELU_B * (cube * pre)))
    half = 0.5 * pre
    activ = (half + half * inner).astype(BF)
    slope = 0.5 + 0.5 * inner + half * (1.0 - inner * inner) * (GELU_A + (3.0 * GELU_A * GELU_B) * cube)
    out_ref[...] += plain_dot(activ, proj_ref[...])
    proj_grad_ref[...] = cols_by_cols(activ, dy).astype(BF)
    grad_pre = (rows_by_rows(dy, proj_ref[...]) * slope).astype(BF)
    fc_bias_ref[0] = jnp.sum(grad_pre.astype(F32), axis=0, keepdims=True)
    fc_grad_ref[...] = cols_by_cols(grad_pre, second).astype(BF)
    acc_ref[...] += plain_dot(grad_pre, fc_ref[...])

    @pl.when(step == pl.num_programs(0) - 1)
    def _():
        _, hat, inverse = norm_rows(hidden_ref[...], 1.0, 0.0)
        grad_second, grad_y = acc_ref[...], dy.astype(F32)
        grad = grad_y + norm_back(grad_second, hat, inverse, shared_ref[3:4, :])
        low = grad.astype(BF)
        grad_ref[...] = grad
        low_ref[...] = low
        for n, rows in enumerate((low.astype(F32), grad_second * hat, grad_second, grad_y)):
            sums_ref[n : n + 1, :] = jnp.sum(rows, axis=0, keepdims=True)


def feed_forward(hidden, out_grad, shared, b_fc, w_fc, w_proj):
    rows, width = hidden.shape
    tile = 256
    steps = w_fc.shape[0] // tile
    whole = lambda *dims: pl.BlockSpec(dims, lambda i: (0,) * len(dims))
    strip = pl.BlockSpec((tile, width), lambda i: (i, 0))
    bias = pl.BlockSpec((1, 1, tile), lambda i: (i, 0, 0))
    shape = jax.ShapeDtypeStruct
    out = pl.pallas_call(
        feed_forward_kernel,
        grid=(steps,),
        in_specs=[whole(rows, width), whole(rows, width), whole(*shared.shape), bias, strip, strip],
        out_specs=[whole(rows, width)] * 3 + [strip, strip, bias, whole(4, width)],
        out_shape=[
            shape((rows, width), F32), shape((rows, width), F32), shape((rows, width), BF),
            shape(w_fc.shape, BF), shape(w_proj.shape, BF), shape((steps, 1, tile), F32), shape((4, width), F32),
        ],
        scratch_shapes=[pltpu.VMEM((rows, width), BF), pltpu.VMEM((rows, width), F32)],
        compiler_params=pltpu.CompilerParams(vmem_limit_bytes=48 << 20),
        name="feed_forward",
    )(hidden, out_grad, shared, b_fc.reshape(steps, 1, tile), w_fc, w_proj)
    return (*out[:5], out[5].reshape(-1), out[6])


def per_device(
    tokens_in,
    out_grad,
    lengths,
    owners,
    matrix_master,
    matrix_m1,
    matrix_m2,
    shared_params,
    bias_params,
):
    n_tensor = lax.axis_size("tensor")
    n_data = lax.axis_size("dp")
    tensor_index = lax.axis_index("tensor")
    data_index = lax.axis_index("dp")
    rows_here, width = tokens_in.shape
    slot_cap = matrix_master.shape[1]
    unit_rows = matrix_master.shape[2]
    n_units = owners.shape[0]
    n_slots = n_data * slot_cap
    head_rows = width // n_tensor
    heads_here = head_rows // HD
    ff_rows = (n_units * unit_rows - 4 * head_rows) // 2
    slot_of_unit, unit_of_slot, occupied = slot_tables(owners, n_slots, slot_cap)

    own_kernels = n_data == 8 and head_rows == unit_rows and unit_rows % 128 == 0 and n_tensor > 1

    back = -(-(DOC_MOST - 1) // rows_here)
    reach = back * rows_here
    sizes = lengths[0]
    upto = jnp.arange(sizes.shape[0])[:, None] >= jnp.arange(sizes.shape[0])[None, :]
    bounds = jnp.sum(jnp.where(upto, sizes[None, :], 0), axis=1)
    places = tensor_index * rows_here + jnp.arange(rows_here, dtype=jnp.int32)
    starts = jnp.max(jnp.where(places[:, None] >= bounds[None, :], bounds[None, :], 0), axis=1)
    first_seen = (starts - tensor_index * rows_here + reach)[None, :]

    shared = shared_params[0]
    inputs_f32 = tokens_in.astype(F32)
    normed_one, hat_one, inverse_one = norm_rows(inputs_f32, shared[0], shared[1])
    normed_low = normed_one.astype(BF)
    if own_kernels:
        (
            w_att, w_fc, w_proj, normed_all, all_bias,
            q_scaled, keys_in, values_in, attended, log_norms, peaks, hidden,
        ) = forward_spread(
            matrix_master[0].astype(BF), normed_low, tokens_in, bias_params[0, 0], first_seen, shared,
            slot_of_unit, n_tensor, back,
        )
        w_q, w_k, w_v, w_out = (w_att[i] for i in range(4))
    else:
        units = gather_units(matrix_master[0], slot_of_unit)
        stacks = units.reshape(n_tensor, n_units * unit_rows, width)
        part = lambda first, count: stacks[:, first : first + count].reshape(-1, width)
        w_q, w_k, w_v, w_out = (part(i * head_rows, head_rows) for i in range(4))
        w_fc = part(4 * head_rows, ff_rows)
        w_proj = part(4 * head_rows + ff_rows, ff_rows)
        all_bias = lax.all_gather(bias_params[0], "tensor", axis=0, tiled=True).reshape(n_tensor, -1)
        before = [
            lax.ppermute(normed_low, "tensor", [(i, i + r) for i in range(n_tensor - r)])
            for r in range(min(back, n_tensor - 1), 0, -1)
        ]
        blank = [jnp.zeros_like(normed_low)] * (back - len(before))
        normed_all = jnp.concatenate([*blank, *before, normed_low], axis=0)
    if not own_kernels:
        bias = lambda first, count: all_bias[:, first : first + count].reshape(-1)
        b_q, b_k, b_v = (bias(i * head_rows, head_rows) for i in range(3))
        q_scaled = (rows_by_rows(normed_low, w_q) + b_q).astype(BF) * jnp.asarray(1.0 / math.sqrt(HD), BF)
        keys_in = (rows_by_rows(normed_all, w_k) + b_k).astype(BF)
        values_in = (rows_by_rows(normed_all, w_v) + b_v).astype(BF)
        attended, log_norms, peaks = attend_forward(q_scaled, keys_in, values_in, first_seen)
        hidden = inputs_f32 + (plain_dot(attended, w_out) + shared[2])
    swap = (lambda v: v.swapaxes(0, 1)) if own_kernels else (lambda v: v)
    b_fc = swap(all_bias[:, 3 * head_rows :].reshape(n_tensor, -1, unit_rows)).reshape(-1)
    layer_out, grad_hidden, grad_hidden_low, grad_fc_w, grad_proj_w, grad_fc_b, shared_rows = feed_forward(
        hidden, out_grad, shared, b_fc, w_fc, w_proj
    )
    grad_out_w = cols_by_cols(attended, grad_hidden_low).astype(BF)
    grad_attended = rows_by_rows(grad_hidden_low, w_out).astype(BF)
    head_here = jnp.max(peaks, axis=2).reshape(-1)
    if own_kernels:
        in_blocks = lambda g: g.reshape(-1, n_tensor, 2, 2, 2, unit_rows // 8, width)
        shard, grad_first, grad_q_w, grad_k_w, grad_v_w, sums = backward_reduce(
            in_blocks(grad_proj_w), in_blocks(grad_fc_w), q_scaled, keys_in, values_in, attended, grad_attended,
            log_norms, first_seen, normed_all, w_att.reshape(-1, width), n_tensor, back,
        )
        vectors = jnp.concatenate(
            [
                jnp.zeros((2, width), F32), shared_rows, sums, grad_fc_b.reshape(-1, width),
                jnp.pad(head_here, (0, width - head_here.shape[0]))[None], jnp.zeros((2, width), F32),
            ],
            axis=0,
        )
        grads = [in_blocks(g) for g in (grad_q_w, grad_k_w, grad_v_w, grad_out_w)]
        my_grads, totals, input_grad = finish_reduce(
            grads, shard, grad_first, grad_hidden, tokens_in, shared, vectors, unit_of_slot, n_tensor, slot_cap
        )
        my_grads = my_grads.astype(F32)
        shared_grad = totals[:6]
        head_all = totals[MAX_ROW, : head_here.shape[0]]
        bias_total = totals[6:MAX_ROW].reshape(-1, n_tensor, unit_rows)
        bias_grad = lax.dynamic_index_in_dim(bias_total, tensor_index, 1, keepdims=False).reshape(-1)
    else:
        grad_q, grad_k, grad_v = attend_backward(
            q_scaled, keys_in, values_in, attended, grad_attended, log_norms, first_seen
        )
        grad_q_w = cols_by_cols(grad_q, normed_low)
        grad_k_w = cols_by_cols(grad_k, normed_all)
        grad_v_w = cols_by_cols(grad_v, normed_all)
        grad_wide = plain_dot(grad_k, w_k) + plain_dot(grad_v, w_v)
        grad_first = grad_wide[reach:] + plain_dot(grad_q, w_q)
        for r in range(1, min(back, n_tensor - 1) + 1):
            away = grad_wide[reach - r * rows_here : reach - (r - 1) * rows_here].astype(BF)
            grad_first += lax.ppermute(away, "tensor", [(i, i - r) for i in range(r, n_tensor)]).astype(F32)
        input_grad = grad_hidden + norm_back(grad_first, hat_one, inverse_one, shared[0])
        grad_qkv_b = [jnp.sum(g, axis=0, dtype=F32) for g in (grad_q, grad_k, grad_v)]
        first_rows = jnp.stack([jnp.sum(grad_first * hat_one, axis=0), jnp.sum(grad_first, axis=0)])
        shared_part = jnp.concatenate([first_rows, shared_rows], axis=0)
        by_tensor = lambda v: v.reshape(n_tensor, -1)
        bias_part = jnp.concatenate([by_tensor(v) for v in (*grad_qkv_b, grad_fc_b)], axis=1)
        head_all = lax.pmax(head_here, ("dp", "tensor"))
        shared_grad, bias_total = lax.psum((shared_part, bias_part), ("dp", "tensor"))
        bias_grad = lax.dynamic_index_in_dim(bias_total, tensor_index, 0, keepdims=False)
        by_stack = lambda g: g.astype(BF).reshape(n_tensor, -1, width)
        grad_units = jnp.concatenate(
            [by_stack(g) for g in (grad_q_w, grad_k_w, grad_v_w, grad_out_w, grad_fc_w, grad_proj_w)], axis=1
        ).reshape(units.shape)
        my_grads = scatter_units(grad_units, unit_of_slot).astype(F32)
    head_peak = lax.dynamic_slice_in_dim(head_all, tensor_index * heads_here, heads_here)

    my_units = lax.dynamic_slice_in_dim(unit_of_slot, data_index * slot_cap, slot_cap, 0)
    my_occupied = lax.dynamic_slice_in_dim(occupied, data_index * slot_cap, slot_cap, 0)[:, None, None]
    steps_done = float(STEP)
    first_new, second_new, master_new = adam_step(
        matrix_master[0], my_grads, matrix_m1[0], matrix_m2[0], steps_done, WEIGHT_DECAY
    )
    root_gamma = jnp.sqrt(CLIP_TAU / jnp.maximum(head_peak, CLIP_TAU))
    row_index = my_units[:, None] * unit_rows + jnp.arange(unit_rows, dtype=jnp.int32)[None, :]
    local_head = jnp.where(row_index < head_rows, row_index // HD, (row_index - head_rows) // HD)
    head_match = local_head[..., None] == jnp.arange(heads_here, dtype=jnp.int32)[None, None, :]
    picked_root = jnp.sum(jnp.where(head_match, root_gamma, 0.0), axis=-1)
    factor = jnp.where(row_index < 2 * head_rows, picked_root, 1.0)
    my_grads = jnp.where(my_occupied, my_grads, 0.0)
    master_new = jnp.where(my_occupied, master_new * factor[..., None], 0.0)
    first_new = jnp.where(my_occupied, first_new, 0.0)
    second_new = jnp.where(my_occupied, second_new, 0.0)
    shared_first, shared_second, shared_new = adam_step(
        shared, shared_grad, shared_params[1], shared_params[2], steps_done, 0.0
    )
    bias_first, bias_second, bias_new = adam_step(
        bias_params[0, 0], bias_grad, bias_params[1, 0], bias_params[2, 0], steps_done, 0.0
    )
    shared_out = jnp.stack([shared_grad, shared_first])
    bias_out = jnp.stack([bias_grad, bias_first])[:, None, :]
    return (
        layer_out,
        input_grad,
        head_peak,
        my_grads[None],
        first_new[None],
        second_new[None],
        master_new[None],
        shared_out,
        shared_second,
        shared_new,
        bias_out,
        bias_second[None],
        bias_new[None],
    )


def solution(mesh):
    in_specs = (
        P(("dp", "tensor"), None),
        P(("dp", "tensor"), None),
        P("dp", None),
        P(),
        P("tensor", "dp", None, None),
        P("tensor", "dp", None, None),
        P("tensor", "dp", None, None),
        P(),
        P(None, "tensor", None),
    )
    out_specs = (
        P(("dp", "tensor"), None),
        P(("dp", "tensor"), None),
        P("tensor"),
        P("tensor", "dp", None, None),
        P("tensor", "dp", None, None),
        P("tensor", "dp", None, None),
        P("tensor", "dp", None, None),
        P(),
        P(),
        P(),
        P(None, "tensor", None),
        P("tensor", None),
        P("tensor", None),
    )
    return jax.shard_map(
        per_device, mesh=mesh, in_specs=in_specs, out_specs=out_specs, check_vma=False
    )
```

```python
import functools
import math

import jax
import jax.numpy as jnp
from jax import lax
from jax.experimental import pallas as pl
from jax.experimental.pallas import tpu as pltpu
from jax.sharding import PartitionSpec as P

HD = 64
DOC_MOST = 1024
STEP = 10
PAIR = 2 * HD

EPS_NORM = 1e-05
BETA_ONE = 0.9
BETA_TWO = 0.95
LEARN_RATE = 0.08
WEIGHT_DECAY = 0.1
EPS_ADAM = 1e-08
CLIP_TAU = 10.0
MASKED = -1e30
GELU_A = 0.7978845608
GELU_B = 0.044715
BF = jnp.bfloat16
F32 = jnp.float32
MESH = pl.DeviceIdType.MESH
MAX_ROW = 13


def plain_dot(left, right):
    return jnp.dot(left, right, preferred_element_type=F32)


def rows_by_rows(left, right):
    return lax.dot_general(left, right, (((1,), (1,)), ((), ())), preferred_element_type=F32)


def cols_by_cols(left, right):
    return lax.dot_general(left, right, (((0,), (0,)), ((), ())), preferred_element_type=F32)


def gelu_tanh(values_in):
    return jax.nn.gelu(values_in, approximate=True)


def norm_rows(values_in, gain, shift):
    centre = jnp.mean(values_in, axis=-1, keepdims=True)
    shifted = values_in - centre
    inverse = lax.rsqrt(jnp.mean(shifted * shifted, axis=-1, keepdims=True) + EPS_NORM)
    normed = shifted * inverse
    return (normed * gain + shift, normed, inverse)


def norm_back(grad_in, normed, inverse, gain):
    scaled = grad_in * gain
    return inverse * (
        scaled
        - jnp.mean(scaled, axis=-1, keepdims=True)
        - normed * jnp.mean(scaled * normed, axis=-1, keepdims=True)
    )


def slot_tables(owners, n_slots, slot_cap):
    n_units = owners.shape[0]
    unit_order = jnp.arange(n_units, dtype=jnp.int32)
    same_owner = owners[:, None] == owners[None, :]
    earlier = unit_order[None, :] < unit_order[:, None]
    rank_counts = jnp.sum((same_owner & earlier).astype(jnp.int32), axis=1)
    slot_of_unit = owners * slot_cap + rank_counts
    matches = jnp.arange(n_slots, dtype=jnp.int32)[:, None] == slot_of_unit[None, :]
    occupied = jnp.any(matches, axis=1)
    unit_of_slot = jnp.sum(matches.astype(jnp.int32) * unit_order[None, :], axis=1)
    return (slot_of_unit, unit_of_slot, occupied)


def head_lanes(head):
    lane = lax.broadcasted_iota(jnp.int32, (1, PAIR), 1)
    return (lane < HD) if head == 0 else (lane >= HD)


def q_tiles(n_query, n_keys):
    size = min(256, n_query)
    reach = n_keys - n_query
    return size, reach + size


def fill_bias(bias_ref, first_ref):
    n_keys, n_query = bias_ref.shape
    reach = n_keys - n_query
    key = lax.broadcasted_iota(jnp.int32, (n_keys, n_query), 0)
    query = lax.broadcasted_iota(jnp.int32, (n_keys, n_query), 1) + reach
    seen = (key <= query) & (key >= first_ref[...])
    bias_ref[...] = jnp.where(seen, 0.0, MASKED)


def attend_kernel(first_ref, q_ref, k_ref, v_ref, o_ref, lse_ref, peak_ref, bias_ref):
    @pl.when(pl.program_id(0) == 0)
    def _():
        fill_bias(bias_ref, first_ref)

    n_keys, n_query = bias_ref.shape
    size, span = q_tiles(n_query, n_keys)
    for j in range(n_query // size):
        rows, keys = pl.ds(j * size, size), pl.ds(j * size, span)
        v_t = v_ref[keys, :].T
        outs = []
        for h in range(2):
            k_h = jnp.where(head_lanes(h), k_ref[keys, :], 0)
            s = rows_by_rows(k_h, q_ref[rows, :]) + bias_ref[keys, rows]
            top = jnp.max(s, axis=0, keepdims=True)
            p = jnp.exp(s - top)
            total = jnp.sum(p, axis=0, keepdims=True)
            o_t = plain_dot(v_t[h * HD : (h + 1) * HD], p.astype(BF))
            outs.append(o_t / total)
            lse_ref[0, h : h + 1, rows] = top + jnp.log(total)
            peak_ref[0, h : h + 1, rows] = top
        o_ref[rows, :] = jnp.concatenate(outs, axis=0).T.astype(BF)


def attend_forward(q_scaled, keys_in, values_in, first_seen):
    n_query, width = q_scaled.shape
    n_keys = keys_in.shape[0]
    pairs = width // PAIR
    column = lambda i: (0, i)
    stats = jax.ShapeDtypeStruct((pairs, 2, n_query), F32)
    stat_spec = pl.BlockSpec((1, 2, n_query), lambda i: (i, 0, 0))
    return pl.pallas_call(
        attend_kernel,
        grid=(pairs,),
        in_specs=[
            pl.BlockSpec((1, n_query), lambda i: (0, 0)),
            pl.BlockSpec((n_query, PAIR), column),
            pl.BlockSpec((n_keys, PAIR), column),
            pl.BlockSpec((n_keys, PAIR), column),
        ],
        out_specs=[pl.BlockSpec((n_query, PAIR), column), stat_spec, stat_spec],
        out_shape=[jax.ShapeDtypeStruct((n_query, width), BF), stats, stats],
        scratch_shapes=[pltpu.VMEM((n_keys, n_query), F32)],
        compiler_params=pltpu.CompilerParams(vmem_limit_bytes=48 << 20),
        name="attend_forward",
    )(first_seen, q_scaled, keys_in, values_in)


def attend_back_kernel(
    first_ref, q_ref, k_ref, v_ref, o_ref, do_ref, lse_ref, dq_ref, dk_ref, dv_ref,
    bias_ref, dk_acc, dv_acc, *, scale
):
    @pl.when(pl.program_id(0) == 0)
    def _():
        fill_bias(bias_ref, first_ref)

    n_keys, n_query = bias_ref.shape
    size, span = q_tiles(n_query, n_keys)
    dk_acc[...] = jnp.zeros_like(dk_acc)
    dv_acc[...] = jnp.zeros_like(dv_acc)
    for j in range(n_query // size):
        rows, keys = pl.ds(j * size, size), pl.ds(j * size, span)
        q_here, do_here = q_ref[rows, :], do_ref[rows, :]
        k_here, v_here = k_ref[keys, :], v_ref[keys, :]
        k_t = k_here.T
        meet = (do_here.astype(F32) * o_ref[rows, :].astype(F32)).T
        outs = []
        for h in range(2):
            lanes = head_lanes(h)
            delta = jnp.sum(meet[h * HD : (h + 1) * HD], axis=0, keepdims=True)
            s = rows_by_rows(jnp.where(lanes, k_here, 0), q_here) + bias_ref[keys, rows]
            p = jnp.exp(s - lse_ref[0, h : h + 1, rows])
            dp = rows_by_rows(jnp.where(lanes, v_here, 0), do_here)
            ds = (p * (dp - delta)).astype(BF)
            dv_acc[keys, :] += plain_dot(p.astype(BF), jnp.where(lanes, do_here, 0))
            dk_acc[keys, :] += plain_dot(ds, jnp.where(lanes, q_here, 0))
            outs.append(plain_dot(k_t[h * HD : (h + 1) * HD], ds))
        dq_ref[rows, :] = (jnp.concatenate(outs, axis=0).T * scale).astype(BF)
    dk_ref[...] = dk_acc[...].astype(BF)
    dv_ref[...] = dv_acc[...].astype(BF)


def attend_backward(q_scaled, keys_in, values_in, attended, grads_out, log_norms, first_seen):
    n_query, width = q_scaled.shape
    n_keys = keys_in.shape[0]
    pairs = width // PAIR
    column = lambda i: (0, i)
    q_spec = pl.BlockSpec((n_query, PAIR), column)
    k_spec = pl.BlockSpec((n_keys, PAIR), column)
    q_out = jax.ShapeDtypeStruct((n_query, width), BF)
    k_out = jax.ShapeDtypeStruct((n_keys, width), BF)
    return pl.pallas_call(
        functools.partial(attend_back_kernel, scale=1.0 / math.sqrt(HD)),
        grid=(pairs,),
        in_specs=[
            pl.BlockSpec((1, n_query), lambda i: (0, 0)),
            q_spec, k_spec, k_spec, q_spec, q_spec,
            pl.BlockSpec((1, 2, n_query), lambda i: (i, 0, 0)),
        ],
        out_specs=[q_spec, k_spec, k_spec],
        out_shape=[q_out, k_out, k_out],
        scratch_shapes=[
            pltpu.VMEM((n_keys, n_query), F32),
            pltpu.VMEM((n_keys, PAIR), F32),
            pltpu.VMEM((n_keys, PAIR), F32),
        ],
        compiler_params=pltpu.CompilerParams(vmem_limit_bytes=48 << 20),
        name="attend_backward",
    )(first_seen, q_scaled, keys_in, values_in, attended, grads_out, log_norms)


def adam_step(param, grad, first, second, steps_done, decay):
    first_new = BETA_ONE * first + (1.0 - BETA_ONE) * grad
    second_new = BETA_TWO * second + (1.0 - BETA_TWO) * grad * grad
    fix_one = 1.0 - BETA_ONE**steps_done
    fix_two = 1.0 - BETA_TWO**steps_done
    direction = first_new / fix_one / (jnp.sqrt(second_new / fix_two) + EPS_ADAM)
    return (first_new, second_new, param - LEARN_RATE * (direction + decay * param))


def take_kernel(picks_ref, from_ref, to_ref):
    to_ref[...] = from_ref[...]


def take_blocks(blocks, picks):
    shape = (blocks.shape[0], 1, *blocks.shape[2:])
    return pl.pallas_call(
        take_kernel,
        grid_spec=pltpu.PrefetchScalarGridSpec(
            num_scalar_prefetch=1,
            grid=picks.shape,
            in_specs=[pl.BlockSpec(shape, lambda i, p: (0, p[i], 0, 0))],
            out_specs=pl.BlockSpec(shape, lambda i, p: (0, i, 0, 0)),
        ),
        out_shape=jax.ShapeDtypeStruct((shape[0], picks.shape[0], *shape[2:]), blocks.dtype),
        compiler_params=pltpu.CompilerParams(vmem_limit_bytes=32 << 20),
        name="take_blocks",
    )(picks, blocks)


def gather_units(master, slot_of_unit):
    slots = lax.all_gather(master.astype(BF), ("tensor", "dp"), axis=0, tiled=True)
    n_tensor = lax.axis_size("tensor")
    slots = slots.reshape(n_tensor, -1, *master.shape[1:])
    return take_blocks(slots, slot_of_unit)


def scatter_units(units, unit_of_slot):
    slots = take_blocks(units, unit_of_slot)
    slots = slots.reshape(-1, *units.shape[2:])
    return lax.psum_scatter(slots, ("tensor", "dp"), scatter_dimension=0, tiled=True)


def send(src, dst, send_sem, recv_sem, to):
    copy = pltpu.make_async_remote_copy(
        src_ref=src, dst_ref=dst, send_sem=send_sem, recv_sem=recv_sem,
        device_id=to, device_id_type=MESH,
    )
    copy.start()


def arrived(ref, sem):
    pltpu.make_async_copy(ref, ref, sem).wait()


def place():
    d, t = lax.axis_index("dp"), lax.axis_index("tensor")
    return d, t, d % 2, (d // 2) % 2, d // 4


def greet(d, t, n_tensor):
    barrier = pltpu.get_barrier_semaphore()
    for k in range(1, 8):
        pl.semaphore_signal(barrier, inc=1, device_id=((d + k) % 8, t), device_id_type=MESH)
    for k in range(1, n_tensor):
        pl.semaphore_signal(barrier, inc=1, device_id=(d, (t + k) % n_tensor), device_id_type=MESH)
    pl.semaphore_wait(barrier, 6 + n_tensor)


def loop_with(count, body, events):
    def step(i, carry):
        body(i)
        for n, mine in events.items():
            @pl.when(i == n)
            def _(mine=mine):
                for event in mine:
                    event()
        return carry

    lax.fori_loop(0, count, step, 0)


def spaced(count, events):
    per = -(-len(events) // count)
    return {n: events[n * per : (n + 1) * per] for n in range(count) if events[n * per : (n + 1) * per]}


def attend_pair(i, q_ref, k_ref, v_ref, o_ref, lse_ref, peak_ref, bias_ref):
    n_keys, n_query = bias_ref.shape
    size, span = q_tiles(n_query, n_keys)
    lanes = pl.ds(pl.multiple_of(i * PAIR, PAIR), PAIR)
    for j in range(n_query // size):
        rows, keys = pl.ds(j * size, size), pl.ds(j * size, span)
        v_t = v_ref[keys, lanes].T
        outs = []
        for h in range(2):
            k_h = jnp.where(head_lanes(h), k_ref[keys, lanes], 0)
            s = rows_by_rows(k_h, q_ref[rows, lanes]) + bias_ref[keys, rows]
            top = jnp.max(s, axis=0, keepdims=True)
            p = jnp.exp(s - top)
            total = jnp.sum(p, axis=0, keepdims=True)
            o_t = plain_dot(v_t[h * HD : (h + 1) * HD], p.astype(BF))
            outs.append(o_t / total)
            lse_ref[i, h : h + 1, rows] = top + jnp.log(total)
            peak_ref[i, h : h + 1, rows] = top
        o_ref[rows, lanes] = jnp.concatenate(outs, axis=0).T.astype(BF)


def paired(n_units):
    half = (n_units - 4) // 2
    return [0, 1, 2, 3] + [4 + i + half * b for i in range(half) for b in range(2)]


def gelu_parts(pre):
    square = pre * pre
    inner = jnp.tanh(GELU_A * (pre + GELU_B * (square * pre)))
    half = 0.5 * pre
    slope = 0.5 + 0.5 * inner + half * (1.0 - inner * inner) * (GELU_A + (3.0 * GELU_A * GELU_B) * square)
    return half + half * inner, slope


ORDER = (
    "o2", "g0d", "o0", "z00d", "g0u", "z01d", "z02d", "z00u", "z01u", "f01d", "g2d", "z02u", "f01u", "t0", "g1d",
    "f0o", "f02d", "f02u", "f00d", "f00u", "e01u", "e01d", "z10d", "e00d", "e0o", "e02u", "o1", "d2", "e02d",
    "e00u", "g1u", "d0", "f1o", "d1", "d3", "Q", "Q", "Q", "g2u", "t1", "z20d", "Q", "z11d", "K", "K", "K", "K",
    "z10u", "V", "V", "V", "z20u", "V", "A", "z11u", "z21d", "A", "A", "z21u", "z22d", "A", "f11d", "z12u",
    "f10u", "A", "z12d", "f11u", "f10d", "A", "e1o", "A", "z22u", "A", "f20d", "f12u", "f20u", "e10u", "e11u",
    "e11d", "f12d", "f2o", "O", "e10d", "F", "e12u", "f21u", "f22d", "F", "e12d", "e20d", "F", "f21d", "e2o",
    "e22d", "e20u", "F", "f22u", "F", "F", "F", "F", "e21u", "e21d", "F", "e22u", "F", "F", "F", "F", "F",
)


def forward_kernel(
    n_tensor, back, scale,
    slot_ref, master_ref, a_ref, x_ref, dy_ref, bias_in_ref, first_ref, shared_ref,
    att_ref, ff_ref, wide_ref, q_ref, k_ref, v_ref, o_ref, lse_ref, peak_ref,
    out_ref, grad_ref, do_ref, ff_grad_ref, go_ref, fc_bias_ref, sums_ref,
    pieces, own, seen_ref, bias_rows, biases_ref, fc_rows, hidden_ref, second_ref, acc_ref, tiles_in, stage,
    swap_send, swap_recv, local_sem, a_send, a_recv, bias_send, bias_recv,
    z_send, z_recv, xy_send, xy_recv, core_send, core_recv, tile_sem, stage_sem,
):
    d, t, core, x, y = place()
    column = y * 2 + x
    by_x, by_y = d + 2 - 4 * x, d + 4 - 8 * y
    sibling = d + 1 - 2 * core
    first, last = t > 0, t < n_tensor - 1
    rows_here, width = a_ref.shape
    n_half = ff_ref.shape[0] // 2
    weights = (att_ref, ff_ref.at[pl.ds(0, n_half)], ff_ref.at[pl.ds(n_half, n_half)])
    starts = (0, 4, 4 + n_half, 4 + 2 * n_half)
    n_groups, steps = len(weights), n_tensor - 1
    slots = 2 * n_tensor - 1
    greet(d, t, n_tensor)

    def tokens_up(r):
        @pl.when(last & (t >= r))
        def _():
            source = a_ref if r == 0 else wide_ref.at[back - r]
            send(source, wide_ref.at[back - r - 1], a_send.at[r], a_recv.at[r], (d, t + 1))

    def tokens_in(r):
        @pl.when(t > r)
        def _():
            arrived(wide_ref.at[back - r - 1], a_recv.at[r])
        if r + 1 < back:
            tokens_up(r + 1)

    for k in range(1, 8):
        to = (d + k) % 8
        send(master_ref.at[:, to], pieces.at[d], swap_send.at[k - 1], swap_recv.at[k - 1], (to, t))
    tokens_up(0)
    mine = pltpu.make_async_copy(master_ref.at[:, d], pieces.at[d], local_sem.at[0])
    mine.start()
    for k in range(1, n_tensor):
        send(bias_in_ref, biases_ref.at[t], bias_send.at[k - 1], bias_recv.at[k - 1], (d, (t + k) % n_tensor))
    biases_ref[t] = bias_in_ref[...]
    wide_ref[back] = a_ref[...]
    for r in range(back):
        @pl.when(t < back - r)
        def _(r=r):
            wide_ref[r] = jnp.zeros((rows_here, width), BF)
    fill_bias(seen_ref, first_ref)
    mine.wait()
    for k in range(1, 8):
        arrived(pieces.at[(d + 8 - k) % 8], swap_recv.at[k - 1])
    cap = master_ref.shape[0]
    for n, u in enumerate(paired(own.shape[0])):
        slot = slot_ref[u]
        own[n] = pieces[slot // cap, slot % cap]

    def block(g, at, col, c):
        return weights[g].at[:, at, col, c]

    def route(at):
        side = at * 2 // n_tensor
        one, two = by_x + (by_y - by_x) * side, by_y + (by_x - by_y) * side
        col_x, col_y, col_xy = y * 2 + 1 - x, (1 - y) * 2 + x, (1 - y) * 2 + 1 - x
        return one, two, col_x + (col_y - col_x) * side, col_y + (col_x - col_y) * side, col_xy

    def onward(g, k, at, source):
        one, two, _, _, _ = route(at)
        here = block(g, at, column, core)
        send(source, here, xy_send.at[g], xy_recv.at[g, k, 0], (one, t))
        send(source, here, xy_send.at[g], xy_recv.at[g, k, 1], (two, t))

    def forward(g, k, at):
        one, two, from_one, _, _ = route(at)
        got = block(g, at, from_one, core)
        arrived(got, xy_recv.at[g, k, 0])
        send(got, got, xy_send.at[g], xy_recv.at[g, k, 2], (two, t))

    def settle(g, k, at):
        _, _, _, from_two, beyond = route(at)
        arrived(block(g, at, from_two, core), xy_recv.at[g, k, 1])
        arrived(block(g, at, beyond, core), xy_recv.at[g, k, 2])
        got = weights[g].at[:, at, :, core]
        send(got, got, core_send.at[g, k], core_recv.at[g, k], (sibling, t))

    def done(g, k, at):
        arrived(weights[g].at[:, at, :, 1 - core], core_recv.at[g, k])

    def given(g, k, at):
        arrived(weights[g].at[:, at, :, core], core_send.at[g, k])

    def z_go(g, s, up, source):
        i = 0 if up else 1

        @pl.when(last if up else first)
        def _():
            here = block(g, t if s == 0 else (t - s if up else t + s), column, core)
            send(source, here, z_send.at[g, i, s], z_recv.at[g, i, s], (d, t + 1 if up else t - 1))

    def z_step(s, up):
        at = t - 1 - s if up else t + 1 + s
        return 1 + 2 * s + (0 if up else 1), at, (at >= 0) if up else (at < n_tensor)

    def z_event(g, s, up):
        k, at, have = z_step(s, up)

        @pl.when(have)
        def _():
            got = block(g, at, column, core)
            arrived(got, z_recv.at[g, 0 if up else 1, s])
            if s + 1 < steps:
                z_go(g, s + 1, up, got)
            onward(g, k, at, got)

    def step(fn, g, s, up):
        k, at, have = z_step(s, up)
        pl.when(have)(functools.partial(fn, g, k, at))

    def each(fn, g, s):
        if s < 0:
            fn(g, 0, t)
        else:
            for up in (True, False):
                step(fn, g, s, up)

    local = []
    mine_of = [own.at[starts[g] : starts[g + 1]] for g in range(n_groups)]
    for g in range(n_groups):
        copy = pltpu.make_async_copy(mine_of[g], block(g, t, column, core), local_sem.at[1 + g])
        copy.start()
        local.append(copy)

    def own_settled(g):
        local[g].wait()
        settle(g, 0, t)

    by_code = {f"t{r}": functools.partial(tokens_in, r) for r in range(back)}
    by_code |= {f"d{s + 1}": functools.partial(each, done, 0, s) for s in range(-1, steps)}
    for g in range(n_groups):
        by_code[f"o{g}"] = functools.partial(onward, g, 0, t, mine_of[g])
        by_code[f"f{g}o"] = functools.partial(forward, g, 0, t)
        by_code[f"e{g}o"] = functools.partial(own_settled, g)
        for way, up in (("u", True), ("d", False)):
            by_code[f"g{g}{way}"] = functools.partial(z_go, g, 0, up, mine_of[g])
            for s in range(steps):
                by_code[f"z{g}{s}{way}"] = functools.partial(z_event, g, s, up)
                by_code[f"f{g}{s}{way}"] = functools.partial(step, forward, g, s, up)
                by_code[f"e{g}{s}{way}"] = functools.partial(step, settle, g, s, up)
    tile = 256
    tiles = width // tile
    early, during = [], {}
    counts = {"Q": tiles, "K": tiles, "V": tiles, "A": width // PAIR, "O": 1, "F": 2 * slots}
    now, seen = None, 0
    for code in ORDER:
        if code in counts:
            now, seen = code, 0 if code != now else seen + 1
            during.setdefault(code, {})
        elif now is None:
            early.append(by_code[code])
        else:
            during[now].setdefault(seen, []).append(by_code[code])
    for event in early:
        event()
    for k in range(1, n_tensor):
        arrived(biases_ref.at[(t + n_tensor - k) % n_tensor], bias_recv.at[k - 1])
        arrived(bias_in_ref, bias_send.at[k - 1])
    per = width // n_tensor // 128
    for n in range(3):
        for at in range(n_tensor):
            for i in range(per):
                lanes = pl.ds((at * per + i) * 128, 128)
                bias_rows[n : n + 1, lanes] = biases_ref[at, n * per + i : n * per + i + 1]
    strip = fc_rows.shape[-1]
    for h in range(2):
        for at in range(n_tensor):
            for i in range(strip // 128):
                row = 3 * per + h * (strip // 128) + i
                fc_rows[h, at, 0:1, i * 128 : (i + 1) * 128] = biases_ref[at, row : row + 1]

    def project(n, own_only, into_ref, factor):
        def body(i):
            cols = pl.ds(pl.multiple_of(i * tile, tile), tile)
            w = att_ref[n, pl.ds(i * tile // (width // n_tensor), 1)].reshape(tile, width)
            for r in range(into_ref.shape[0] // rows_here):
                a = a_ref[...] if own_only else wide_ref[r]
                full = (rows_by_rows(a, w) + bias_rows[n : n + 1, cols]).astype(BF)
                into_ref[r * rows_here : (r + 1) * rows_here, cols] = full * jnp.asarray(factor, BF) if factor else full
        return body

    loop_with(tiles, project(0, True, q_ref, scale), during["Q"])
    loop_with(tiles, project(1, False, k_ref, None), during["K"])
    loop_with(tiles, project(2, False, v_ref, None), during["V"])
    loop_with(
        width // PAIR,
        lambda i: attend_pair(i, q_ref, k_ref, v_ref, o_ref, lse_ref, peak_ref, seen_ref),
        during["A"],
    )
    w_out = att_ref[3].reshape(width, width)
    half = rows_here // 2
    for r in range(2):
        rows = pl.ds(r * half, half)
        hidden = x_ref[rows, :].astype(F32) + (plain_dot(o_ref[rows, :], w_out) + shared_ref[2:3, :])
        hidden_ref[rows, :] = hidden
        normed, _, _ = norm_rows(hidden, shared_ref[3:4, :], shared_ref[4:5, :])
        second_ref[rows, :] = normed.astype(BF)
        out_ref[rows, :] = hidden + shared_ref[5:6, :]
    acc_ref[...] = jnp.zeros_like(acc_ref)

    def tile_copies(h, at, b):
        for i in range(n_half // 2):
            yield pltpu.make_async_copy(
                ff_ref.at[h * n_half + 2 * i + b, at], tiles_in.at[b, i], tile_sem.at[b, i]
            )

    def grad_copies(h, at):
        for b in range(2):
            for i in range(n_half // 2):
                part = stage.at[b, i]
                yield pltpu.make_async_copy(part, ff_grad_ref.at[h * n_half + 2 * i + b, at], stage_sem.at[b, i])

    def feed(n):
        h, k = n // slots, n % slots
        at = t + (k + 1) // 2 * (1 - 2 * (k % 2))

        @pl.when((at >= 0) & (at < n_tensor))
        def _():
            arrived(ff_ref.at[pl.ds(h * n_half, n_half), at, :, 1 - core], core_recv.at[1 + h, k])
            for b in range(2):
                for copy in tile_copies(h, at, b):
                    copy.start()
            for copy in tile_copies(h, at, 0):
                copy.wait()
            w_fc = tiles_in[0].reshape(strip, width)
            second, dy = second_ref[...], dy_ref[...]
            activ, slope = gelu_parts(rows_by_rows(second, w_fc) + fc_rows[h, at])
            activ = activ.astype(BF)
            for copy in tile_copies(h, at, 1):
                copy.wait()
            w_proj = tiles_in[1].reshape(strip, width)
            grad_pre = (rows_by_rows(dy, w_proj) * slope).astype(BF)
            out_ref[...] += plain_dot(activ, w_proj)
            acc_ref[...] += plain_dot(grad_pre, w_fc)
            fc_bias_ref[h, at] = jnp.sum(grad_pre.astype(F32), axis=0, keepdims=True)

            @pl.when(n > 0)
            def _():
                for copy in grad_copies(h, at):
                    copy.wait()

            stage[0] = cols_by_cols(grad_pre, second).astype(BF).reshape(stage.shape[1:])
            stage[1] = cols_by_cols(activ, dy).astype(BF).reshape(stage.shape[1:])
            for copy in grad_copies(h, at):
                copy.start()

    for event in during["O"].get(0, []):
        event()
    loop_with(2 * slots, feed, during["F"])
    for copy in grad_copies(0, 0):
        copy.wait()

    part = min(128, rows_here)
    sums_ref[...] = jnp.zeros_like(sums_ref)

    def norm_back_rows(i, carry):
        rows = pl.ds(pl.multiple_of(i * part, part), part)
        _, hat, inverse = norm_rows(hidden_ref[rows, :], 1.0, 0.0)
        grad_second, grad_y = acc_ref[rows, :], dy_ref[rows, :].astype(F32)
        grad = grad_y + norm_back(grad_second, hat, inverse, shared_ref[3:4, :])
        low = grad.astype(BF)
        grad_ref[rows, :] = grad
        second_ref[rows, :] = low
        for n, term in enumerate((low.astype(F32), grad_second * hat, grad_second, grad_y)):
            sums_ref[n : n + 1, :] += jnp.sum(term, axis=0, keepdims=True)
        return carry

    lax.fori_loop(0, rows_here // part, norm_back_rows, 0)

    def out_back(i):
        cols = pl.ds(pl.multiple_of(i * tile, tile), tile)
        w = att_ref[3, pl.ds(i * tile // (width // n_tensor), 1)].reshape(tile, width)
        do_ref[:, cols] = rows_by_rows(second_ref[...], w).astype(BF)
        go_ref[pl.ds(pl.multiple_of(i * tile, tile), tile), :] = cols_by_cols(o_ref[:, cols], second_ref[...]).astype(BF)

    loop_with(tiles, out_back, {})

    for g in range(n_groups):
        for s in range(-1, steps):
            each(given, g, s)
        arrived(weights[g].at[:, :, pl.ds(0, 3), 0], xy_send.at[g])
        for up in (True, False):
            for s in range(steps):
                have = last if up else first
                if s > 0:
                    have = have & z_step(s - 1, up)[2]

                @pl.when(have)
                def _(g=g, s=s, up=up):
                    arrived(block(g, t, column, core), z_send.at[g, 0 if up else 1, s])
    for r in range(back):
        @pl.when(last & (t >= r))
        def _(r=r):
            arrived(a_ref, a_send.at[r])
    for k in range(1, 8):
        arrived(pieces.at[0], swap_send.at[k - 1])


def forward_spread(master_low, normed_low, tokens, out_grad, bias_row, first_seen, shared, slot_of_unit, n_tensor, back):
    cap, unit_rows, width = master_low.shape
    n_units = slot_of_unit.shape[0]
    n_ff = n_units - 4
    piece = unit_rows // 8
    rows = normed_low.shape[0]
    n_keys = (back + 1) * rows
    strip = n_ff // 4 * unit_rows
    bias_row = bias_row.reshape(-1, 128)
    any_spec = pl.BlockSpec(memory_space=pl.ANY)
    vmem = pl.BlockSpec(memory_space=pltpu.VMEM)
    dma = pltpu.SemaphoreType.DMA
    shape = jax.ShapeDtypeStruct
    units = lambda n: shape((n, n_tensor, 4, 2, piece, width), BF)
    stats = shape((width // PAIR, 2, rows), F32)
    low, high = shape((rows, width), BF), shape((rows, width), F32)
    keys = shape((n_keys, width), BF)
    outs = pl.pallas_call(
        functools.partial(forward_kernel, n_tensor, back, 1.0 / math.sqrt(HD)),
        out_shape=[
            units(4), units(n_ff), shape((back + 1, rows, width), BF), low, keys, keys, low, stats, stats,
            high, high, low, shape((n_ff, n_tensor, 4, 2, piece, width), BF), shape((width, width), BF),
            shape((2, n_tensor, 1, strip), F32), shape((4, width), F32),
        ],
        in_specs=[pl.BlockSpec(memory_space=pltpu.SMEM), any_spec] + [vmem] * 6,
        out_specs=[vmem, any_spec] + [vmem] * 10 + [any_spec] + [vmem] * 3,
        scratch_shapes=[
            pltpu.VMEM((8, cap, piece, width), BF),
            pltpu.VMEM((n_units, piece, width), BF),
            pltpu.VMEM((n_keys, rows), F32),
            pltpu.VMEM((3, width), F32),
            pltpu.VMEM((n_tensor, *bias_row.shape), F32),
            pltpu.VMEM((2, n_tensor, 1, strip), F32),
            pltpu.VMEM((rows, width), F32),
            pltpu.VMEM((rows, width), BF),
            pltpu.VMEM((rows, width), F32),
            pltpu.VMEM((2, n_ff // 4, 4, 2, piece, width), BF),
            pltpu.VMEM((2, n_ff // 4, 4, 2, piece, width), BF),
            dma((7,)), dma((7,)), dma((4,)), dma((back,)), dma((back,)),
            dma((n_tensor - 1,)), dma((n_tensor - 1,)),
            dma((3, 2, n_tensor - 1)), dma((3, 2, n_tensor - 1)),
            dma((3,)), dma((3, 2 * n_tensor - 1, 3)),
            dma((3, 2 * n_tensor - 1)), dma((3, 2 * n_tensor - 1)),
            dma((2, n_ff // 4)), dma((2, n_ff // 4)),
        ],
        compiler_params=pltpu.CompilerParams(collective_id=0, has_side_effects=True, vmem_limit_bytes=60 << 20),
        name="forward_spread",
    )(
        slot_of_unit, master_low.reshape(cap, 8, piece, width), normed_low, tokens, out_grad, bias_row, first_seen, shared
    )
    att, _, wide, *rest = outs
    return att.reshape(-1, width), wide.reshape(-1, width), *rest


def add_blocks(into, part, count):
    def body(i, carry):
        a = into(i)
        a[...] = a[...] + part(i)[...]
        return carry

    lax.fori_loop(0, count, body, 0)


class Reducer:
    def __init__(self, groups, n_tensor, other, near, one, two, up_in, down_in, final, sems):
        self.groups, self.n_tensor = groups, n_tensor
        self.other, self.near, self.one, self.two = other, near, one, two
        self.up_in, self.down_in, self.final = up_in, down_in, final
        (
            self.near_sem, self.core_send, self.core_recv, self.one_send, self.one_recv,
            self.two_send, self.two_recv, self.z_send, self.z_recv,
        ) = sems
        self.d, self.t, self.core, self.x, self.y = place()
        self.by_x, self.by_y = self.d + 2 - 4 * self.x, self.d + 4 - 8 * self.y
        self.sibling = self.d + 1 - 2 * self.core
        self.order = sorted(range(n_tensor), key=lambda a: -abs(2 * a - n_tensor + 1))
        self.merges = [(g, at) for g in range(len(groups)) for at in self.order]
        self.starts, total = [], 0
        for refs in groups:
            self.starts.append(total)
            total += sum(r.shape[0] for r in refs)
        self.ends = [*self.starts[1:], total]

    @staticmethod
    def scratch(n_units, n_group, n_groups, n_refs, n_tensor, block):
        dma = pltpu.SemaphoreType.DMA
        return [
            pltpu.VMEM((n_units, n_tensor, 2, 2, *block), BF),
            pltpu.VMEM((2, n_group, 2, 2, *block), BF),
            pltpu.VMEM((n_units, n_tensor, 2, *block), BF),
            pltpu.VMEM((n_units, n_tensor, *block), BF),
            pltpu.VMEM((n_units, n_tensor, *block), BF),
            pltpu.VMEM((n_units, n_tensor, *block), BF),
            dma((2, n_refs)), dma((n_groups, n_refs)), dma((n_groups, n_refs)),
            dma((n_groups, n_tensor)), dma((n_groups, n_tensor)),
            dma((n_groups, n_tensor)), dma((n_groups, n_tensor)),
            dma((n_groups, n_tensor)), dma((n_groups, n_tensor, 2)),
        ]

    def parts(self, g):
        u = self.starts[g]
        for n, ref in enumerate(self.groups[g]):
            yield n, ref, u, ref.shape[0]
            u += ref.shape[0]

    def units(self, g):
        return pl.ds(self.starts[g], self.ends[g] - self.starts[g])

    def count(self, g):
        return self.ends[g] - self.starts[g]

    def near_copies(self, m):
        g, at = self.merges[m]
        for n, ref, u, many in self.parts(g):
            yield pltpu.make_async_copy(
                ref.at[:, at, :, :, self.core],
                self.near.at[m % 2, pl.ds(u - self.starts[g], many)],
                self.near_sem.at[m % 2, n],
            )

    def start(self):
        for g in range(len(self.groups)):
            for n, ref, u, many in self.parts(g):
                send(
                    ref.at[:, :, :, :, 1 - self.core], self.other.at[pl.ds(u, many)],
                    self.core_send.at[g, n], self.core_recv.at[g, n], (self.sibling, self.t),
                )
        for m in range(2):
            for copy in self.near_copies(m):
                copy.start()

    def by_rows(self, at):
        return at * 2 < self.n_tensor

    def first_hop(self, m):
        g, at = self.merges[m]
        if m % self.n_tensor == 0:
            for n, ref, u, many in self.parts(g):
                arrived(self.other.at[pl.ds(u, many)], self.core_recv.at[g, n])
        for copy in self.near_copies(m):
            copy.wait()
        u0 = self.starts[g]
        add_blocks(
            lambda i: self.other.at[u0 + i // 4, at, (i // 2) % 2, i % 2],
            lambda i: self.near.at[m % 2, i // 4, (i // 2) % 2, i % 2],
            4 * self.count(g),
        )
        if m + 2 < len(self.merges):
            for copy in self.near_copies(m + 2):
                copy.start()
        us = self.units(g)
        rows = self.by_rows(at)
        source = self.other.at[us, at, 1 - self.y] if rows else self.other.at[us, at, :, 1 - self.x]
        to = self.by_y if rows else self.by_x
        send(source, self.one.at[us, at], self.one_send.at[g, at], self.one_recv.at[g, at], (to, self.t))

    def second_hop(self, m):
        g, at = self.merges[m]
        us, u0 = self.units(g), self.starts[g]
        arrived(self.one.at[us, at], self.one_recv.at[g, at])
        if self.by_rows(at):
            into = lambda i: self.other.at[u0 + i // 2, at, self.y, i % 2]
            source, to = self.other.at[us, at, self.y, 1 - self.x], self.by_x
        else:
            into = lambda i: self.other.at[u0 + i // 2, at, i % 2, self.x]
            source, to = self.other.at[us, at, 1 - self.y, self.x], self.by_y
        add_blocks(into, lambda i: self.one.at[u0 + i // 2, at, i % 2], 2 * self.count(g))
        send(source, self.two.at[us, at], self.two_send.at[g, at], self.two_recv.at[g, at], (to, self.t))

    def plane_sum(self, m):
        g, at = self.merges[m]
        us, u0, n = self.units(g), self.starts[g], self.count(g)
        arrived(self.two.at[us, at], self.two_recv.at[g, at])
        add_blocks(lambda i: self.other.at[u0 + i, at, self.y, self.x], lambda i: self.two.at[u0 + i, at], n)
        if at > 0:
            pl.when(self.t == 0)(functools.partial(self.line_go, g, at, True))
        if at < self.n_tensor - 1:
            pl.when(self.t == self.n_tensor - 1)(functools.partial(self.line_go, g, at, False))

    def line_go(self, g, at, up):
        us = self.units(g)
        into, way, to = (self.up_in, 0, self.t + 1) if up else (self.down_in, 1, self.t - 1)
        send(self.other.at[us, at, self.y, self.x], into.at[us, at], self.z_send.at[g, at], self.z_recv.at[g, at, way], (self.d, to))

    def line_in(self, g, at, up):
        us, u0, n, t = self.units(g), self.starts[g], self.count(g), self.t
        buffer, way = (self.up_in, 0) if up else (self.down_in, 1)
        arrived(buffer.at[us, at], self.z_recv.at[g, at, way])
        add_blocks(lambda i: self.other.at[u0 + i, at, self.y, self.x], lambda i: buffer.at[u0 + i, at], n)
        pl.when(t < at if up else t > at)(functools.partial(self.line_go, g, at, up))

    def line(self, g, k):
        n, t = self.n_tensor, self.t
        high, low = n - 1 - k, k
        near_top = t * 2 >= n
        came_down = (t >= low) & (t < n - 1)
        pl.when(came_down & near_top)(functools.partial(self.line_in, g, low, False))
        pl.when((t <= high) & (t > 0))(functools.partial(self.line_in, g, high, True))
        pl.when(came_down & (t * 2 < n))(functools.partial(self.line_in, g, low, False))

    def keep(self, g):
        us = self.units(g)
        self.final[us] = self.other[us, self.t, self.y, self.x]

    def events(self):
        n, count = self.n_tensor, len(self.groups)
        first, second, third = (
            [[functools.partial(f, g * n + i) for i in range(n)] for g in range(count)]
            for f in (self.first_hop, self.second_hop, self.plane_sum)
        )
        lines = [[functools.partial(self.line, g, k) for k in range(n - 1)] + [functools.partial(self.keep, g)] for g in range(count)]
        return first, second, third, lines

    def finish(self):
        for g in range(len(self.groups)):
            us = self.units(g)
            for n, ref, u, many in self.parts(g):
                arrived(self.other.at[pl.ds(u, many)], self.core_send.at[g, n])
            for at in range(self.n_tensor):
                arrived(self.one.at[us, at], self.one_send.at[g, at])
                arrived(self.two.at[us, at], self.two_send.at[g, at])

                @pl.when(self.t != at)
                def _(us=us, g=g, at=at):
                    arrived(self.up_in.at[us, at], self.z_send.at[g, at])


REDUCER = 15


def backward_kernel(
    n_tensor, back, scale,
    ff_grad_ref, q_ref, k_ref, v_ref, o_ref, do_ref, lse_ref, first_ref, wide_ref, att_ref,
    shard_ref, grad_ref, gq_ref, gk_ref, gv_ref, sums_ref, *scratch,
):
    reducer_scratch, (
        seen_ref, q_in, k_in, v_in, o_in, do_in, dq_ref, dk_ref, dv_ref, big, away, away_in, stage, dk_acc, dv_acc,
        pair_sem, load_sem, stage_sem, away_send, away_recv,
    ) = scratch[:REDUCER], scratch[REDUCER:]
    d, t, core, x, y = place()
    greet(d, t, n_tensor)
    other, near, one, two, up_in, down_in, *sems = reducer_scratch
    half = ff_grad_ref.shape[0] // 2
    groups = [[ff_grad_ref.at[pl.ds(0, half)]], [ff_grad_ref.at[pl.ds(half, half)]]]
    reducer = Reducer(groups, n_tensor, other, near, one, two, up_in, down_in, shard_ref, sems)
    reducer.start()
    rows_here, width = do_ref.shape
    n_keys = k_ref.shape[0]
    size, span = q_tiles(rows_here, n_keys)
    sources = ((q_ref, q_in), (k_ref, k_in), (v_ref, v_in), (o_ref, o_in), (do_ref, do_in))

    def pair_copies(i):
        lanes = pl.ds(pl.multiple_of(i * PAIR, PAIR), PAIR)
        return [
            pltpu.make_async_copy(ref.at[:, lanes], buffer.at[i % 2], pair_sem.at[i % 2, n])
            for n, (ref, buffer) in enumerate(sources)
        ]

    for copy in pair_copies(0):
        copy.start()
    weights = pltpu.make_async_copy(att_ref.at[pl.ds(0, 3 * width)], big, load_sem.at[0])
    weights.start()
    fill_bias(seen_ref, first_ref)
    pairs = width // PAIR

    def attend_back(i):
        for copy in pair_copies(i):
            copy.wait()

        @pl.when(i + 1 < pairs)
        def _():
            for copy in pair_copies(i + 1):
                copy.start()

        slot = i % 2
        lanes_here = pl.ds(pl.multiple_of(i * PAIR, PAIR), PAIR)
        dk_acc[...] = jnp.zeros_like(dk_acc)
        dv_acc[...] = jnp.zeros_like(dv_acc)
        dq_sum = jnp.zeros((1, PAIR), F32)
        for j in range(rows_here // size):
            rows, keys = pl.ds(j * size, size), pl.ds(j * size, span)
            q_here, do_here = q_in[slot, rows, :], do_in[slot, rows, :]
            k_here, v_here = k_in[slot, keys, :], v_in[slot, keys, :]
            k_t = k_here.T
            meet = (do_here.astype(F32) * o_in[slot, rows, :].astype(F32)).T
            outs = []
            for h in range(2):
                lanes = head_lanes(h)
                delta = jnp.sum(meet[h * HD : (h + 1) * HD], axis=0, keepdims=True)
                s = rows_by_rows(jnp.where(lanes, k_here, 0), q_here) + seen_ref[keys, rows]
                p = jnp.exp(s - lse_ref[i, h : h + 1, rows])
                dp = rows_by_rows(jnp.where(lanes, v_here, 0), do_here)
                ds = (p * (dp - delta)).astype(BF)
                dv_acc[keys, :] += plain_dot(p.astype(BF), jnp.where(lanes, do_here, 0))
                dk_acc[keys, :] += plain_dot(ds, jnp.where(lanes, q_here, 0))
                outs.append(plain_dot(k_t[h * HD : (h + 1) * HD], ds))
            dq = (jnp.concatenate(outs, axis=0).T * scale).astype(BF)
            dq_ref[rows, lanes_here] = dq
            dq_sum += jnp.sum(dq.astype(F32), axis=0, keepdims=True)
        dk, dv = dk_acc[...].astype(BF), dv_acc[...].astype(BF)
        dk_ref[:, lanes_here] = dk
        dv_ref[:, lanes_here] = dv
        sums_ref[0:1, lanes_here] = dq_sum
        sums_ref[1:2, lanes_here] = jnp.sum(dk.astype(F32), axis=0, keepdims=True)
        sums_ref[2:3, lanes_here] = jnp.sum(dv.astype(F32), axis=0, keepdims=True)

    tile = 256
    tiles = width // tile

    def input_grad(r):
        rows = pl.ds((back - r) * rows_here, rows_here)

        def body(i):
            cols = pl.ds(pl.multiple_of(i * tile, tile), tile)
            total = plain_dot(dk_ref[rows, :], big[width : 2 * width, cols]) + plain_dot(dv_ref[rows, :], big[2 * width :, cols])
            if r == 0:
                grad_ref[:, cols] = total + plain_dot(dq_ref[...], big[:width, cols])
            else:
                away[r - 1, :, cols] = total.astype(BF)

        return body

    def have_down(r):
        return (t + 1 >= r) & (t + 1 < n_tensor)

    def give(r):
        if r < back:
            @pl.when(have_down(r + 1) & (t >= r))
            def _():
                arrived(away_in.at[r], away_recv.at[r])
                away[r - 1] = (away[r - 1].astype(F32) + away_in[r].astype(F32)).astype(BF)

        @pl.when(t >= r)
        def _():
            send(away.at[r - 1], away_in.at[r - 1], away_send.at[r - 1], away_recv.at[r - 1], (d, t - 1))

    def weight_grad(n, from_ref, into_ref, first_row, many):
        def body(i):
            cols = pl.ds(pl.multiple_of(i * tile, tile), tile)
            slot = i % 2
            out = pltpu.make_async_copy(stage.at[slot], into_ref.at[pl.ds(i * tile, tile)], stage_sem.at[slot])

            @pl.when((i >= 2) | (n > 0))
            def _():
                out.wait()

            total = lax.dot_general(
                from_ref[:, cols], tokens_of(first_row, many), (((0,), (0,)), ((), ())), preferred_element_type=F32
            )
            stage[slot] = total.astype(BF)
            out.start()

        return body

    def tokens_of(first_row, many):
        return big[pl.ds(first_row, many), :]

    first, second, third, lines = reducer.events()
    loop_with(pairs, attend_back, {1: first[0], 3: first[1]})
    weights.wait()
    for r in range(back, -1, -1):
        loop_with(tiles, input_grad(r), {})
        if r == back:
            give(r)
    load = pltpu.make_async_copy(wide_ref, big.at[pl.ds(0, n_keys)], load_sem.at[1])
    load.start()
    for event in second[0]:
        event()
    load.wait()
    own = n_keys - rows_here
    loop_with(tiles, weight_grad(0, dq_ref, gq_ref, own, rows_here), {})
    loop_with(tiles, weight_grad(1, dk_ref, gk_ref, 0, n_keys), {1: third[0]})
    loop_with(tiles, weight_grad(2, dv_ref, gv_ref, 0, n_keys), {1: lines[0][:1]})
    for r in range(back - 1, 0, -1):
        give(r)
    for event in lines[0][1:] + second[1] + third[1] + lines[1]:
        event()
    for slot in range(2):
        arrived(stage.at[slot], stage_sem.at[slot])

    @pl.when(have_down(1))
    def _():
        arrived(away_in.at[0], away_recv.at[0])
        grad_ref[...] = grad_ref[...] + away_in[0].astype(F32)
    for r in range(1, back + 1):
        @pl.when(t >= r)
        def _(r=r):
            arrived(away.at[r - 1], away_send.at[r - 1])
    reducer.finish()


def backward_reduce(grad_ff, q, k, v, o, do, lse, first_seen, wide, w_att, n_tensor, back):
    rows, width = q.shape
    n_keys = k.shape[0]
    n_ff = grad_ff.shape[0]
    block = grad_ff.shape[-2:]
    any_spec = pl.BlockSpec(memory_space=pl.ANY)
    vmem = pl.BlockSpec(memory_space=pltpu.VMEM)
    dma = pltpu.SemaphoreType.DMA
    shape = jax.ShapeDtypeStruct
    square = shape((width, width), BF)
    pair = lambda n: pltpu.VMEM((2, n, PAIR), BF)
    return pl.pallas_call(
        functools.partial(backward_kernel, n_tensor, back, 1.0 / math.sqrt(HD)),
        out_shape=[shape((n_ff, *block), BF), shape((rows, width), F32), square, square, square, shape((3, width), F32)],
        in_specs=[any_spec] * 6 + [vmem, vmem] + [any_spec] * 2,
        out_specs=[vmem, vmem, any_spec, any_spec, any_spec, vmem],
        scratch_shapes=[
            *Reducer.scratch(n_ff, n_ff // 2, 2, 1, n_tensor, block),
            pltpu.VMEM((n_keys, rows), F32),
            pair(rows), pair(n_keys), pair(n_keys), pair(rows), pair(rows),
            pltpu.VMEM((rows, width), BF), pltpu.VMEM((n_keys, width), BF), pltpu.VMEM((n_keys, width), BF),
            pltpu.VMEM((3 * width, width), BF),
            pltpu.VMEM((back, rows, width), BF), pltpu.VMEM((back, rows, width), BF),
            pltpu.VMEM((2, 256, width), BF),
            pltpu.VMEM((n_keys, PAIR), F32), pltpu.VMEM((n_keys, PAIR), F32),
            dma((2, 5)), dma((2,)), dma((2,)), dma((back,)), dma((back,)),
        ],
        compiler_params=pltpu.CompilerParams(collective_id=1, has_side_effects=True, vmem_limit_bytes=60 << 20),
        name="backward_reduce",
    )(grad_ff, q, k, v, o, do, lse, first_seen, wide, w_att)


def join(row, a, b):
    return jnp.where(row == MAX_ROW, jnp.maximum(a, b), a + b)


def finish_kernel(
    n_tensor,
    unit_ref, gq_ref, gk_ref, gv_ref, go_ref, shard_ref, grad_ref, hidden_ref, x_ref, shared_ref, v_ref,
    out_ref, vsum_ref, input_ref, *scratch,
):
    reducer_scratch, (final, outgo, v_in, v_z, swap_send, swap_recv, v_send, v_recv, local_sem) = (
        scratch[:REDUCER], scratch[REDUCER:]
    )
    d, t, core, x, y = place()
    greet(d, t, n_tensor)
    other, near, one, two, up_in, down_in, *sems = reducer_scratch
    reducer = Reducer([[gq_ref, gk_ref], [gv_ref, go_ref]], n_tensor, other, near, one, two, up_in, down_in, final, sems)
    reducer.start()
    rows_here = x_ref.shape[0]
    n_att = other.shape[0]
    final[n_att:] = shard_ref[...]

    vsum_ref[...] = v_ref[...]
    part = 128
    gain = shared_ref[0:1, :]

    def norm_back_rows(i, carry):
        rows = pl.ds(pl.multiple_of(i * part, part), part)
        _, hat, inverse = norm_rows(x_ref[rows, :].astype(F32), 1.0, 0.0)
        grad = grad_ref[rows, :]
        input_ref[rows, :] = hidden_ref[rows, :] + norm_back(grad, hat, inverse, gain)
        vsum_ref[0:1, :] += jnp.sum(grad * hat, axis=0, keepdims=True)
        vsum_ref[1:2, :] += jnp.sum(grad, axis=0, keepdims=True)
        return carry

    lax.fori_loop(0, rows_here // part, norm_back_rows, 0)
    row = lax.broadcasted_iota(jnp.int32, vsum_ref.shape, 0)
    hops = (reducer.sibling, reducer.by_x, reducer.by_y)

    def vector_go(i):
        send(vsum_ref, v_in.at[i], v_send.at[i], v_recv.at[i], (hops[i], t))

    def vector_in(i):
        arrived(v_in.at[i], v_recv.at[i])
        arrived(v_in.at[i], v_send.at[i])
        vsum_ref[...] = join(row, vsum_ref[...], v_in[i])
        if i + 1 < len(hops):
            vector_go(i + 1)
        else:
            for k in range(1, n_tensor):
                send(vsum_ref, v_z.at[k - 1], v_send.at[2 + k], v_recv.at[2 + k], (d, (t + k) % n_tensor))

    def vector_end():
        for k in range(1, n_tensor):
            arrived(v_z.at[k - 1], v_recv.at[2 + k])
            arrived(v_z.at[k - 1], v_send.at[2 + k])
        for k in range(1, n_tensor):
            vsum_ref[...] = join(row, vsum_ref[...], v_z[k - 1])

    vector_go(0)
    first, second, third, lines = reducer.events()
    events = first[0] + first[1] + second[0] + third[0] + second[1] + lines[0] + third[1] + lines[1]
    for n, event in enumerate((functools.partial(vector_in, 0), functools.partial(vector_in, 1), functools.partial(vector_in, 2), vector_end)):
        events.insert(4 + 5 * n, event)
    for event in events:
        event()

    cap = out_ref.shape[0]
    for k in range(1, 9):
        to = (d + k) % 8
        for j in range(cap):
            outgo[to, j] = final[unit_ref[to * cap + j]]
        if k < 8:
            send(outgo.at[to], out_ref.at[:, d], swap_send.at[k - 1], swap_recv.at[k - 1], (to, t))
    keep = pltpu.make_async_copy(outgo.at[d], out_ref.at[:, d], local_sem.at[0])
    keep.start()
    for k in range(1, 8):
        arrived(out_ref.at[:, (d + 8 - k) % 8], swap_recv.at[k - 1])
    reducer.finish()
    for k in range(1, 8):
        arrived(outgo.at[0], swap_send.at[k - 1])
    keep.wait()


def finish_reduce(grads, shard, grad_first, grad_hidden, tokens, shared, vectors, unit_of_slot, n_tensor, cap):
    block = shard.shape[1:]
    n_units = len(grads) + shard.shape[0]
    rows, width = tokens.shape
    any_spec = pl.BlockSpec(memory_space=pl.ANY)
    vmem = pl.BlockSpec(memory_space=pltpu.VMEM)
    dma = pltpu.SemaphoreType.DMA
    shape = jax.ShapeDtypeStruct
    out, vsum, input_grad = pl.pallas_call(
        functools.partial(finish_kernel, n_tensor),
        out_shape=[shape((cap, 8, *block), BF), shape(vectors.shape, F32), shape((rows, width), F32)],
        in_specs=[pl.BlockSpec(memory_space=pltpu.SMEM)] + [any_spec] * 4 + [vmem] * 6,
        out_specs=[vmem, vmem, vmem],
        scratch_shapes=[
            *Reducer.scratch(len(grads), 2, 2, 2, n_tensor, block),
            pltpu.VMEM((n_units, *block), BF),
            pltpu.VMEM((8, cap, *block), BF),
            pltpu.VMEM((3, *vectors.shape), F32),
            pltpu.VMEM((n_tensor - 1, *vectors.shape), F32),
            dma((7,)), dma((7,)), dma((2 + n_tensor,)), dma((2 + n_tensor,)), dma((1,)),
        ],
        compiler_params=pltpu.CompilerParams(collective_id=2, has_side_effects=True, vmem_limit_bytes=48 << 20),
        name="finish_reduce",
    )(unit_of_slot, *grads, shard, grad_first, grad_hidden, tokens, shared, vectors)
    return out.reshape(cap, -1, width), vsum, input_grad


def feed_forward_kernel(
    hidden_ref, dy_ref, shared_ref, bias_ref, fc_ref, proj_ref,
    out_ref, grad_ref, low_ref, fc_grad_ref, proj_grad_ref, fc_bias_ref, sums_ref,
    second_ref, acc_ref,
):
    step = pl.program_id(0)

    @pl.when(step == 0)
    def _():
        normed, _, _ = norm_rows(hidden_ref[...], shared_ref[3:4, :], shared_ref[4:5, :])
        second_ref[...] = normed.astype(BF)
        out_ref[...] = hidden_ref[...] + shared_ref[5:6, :]
        acc_ref[...] = jnp.zeros_like(acc_ref)

    dy, second = dy_ref[...], second_ref[...]
    pre = rows_by_rows(second, fc_ref[...]) + bias_ref[0]
    cube = pre * pre
    inner = jnp.tanh(GELU_A * (pre + GELU_B * (cube * pre)))
    half = 0.5 * pre
    activ = (half + half * inner).astype(BF)
    slope = 0.5 + 0.5 * inner + half * (1.0 - inner * inner) * (GELU_A + (3.0 * GELU_A * GELU_B) * cube)
    out_ref[...] += plain_dot(activ, proj_ref[...])
    proj_grad_ref[...] = cols_by_cols(activ, dy).astype(BF)
    grad_pre = (rows_by_rows(dy, proj_ref[...]) * slope).astype(BF)
    fc_bias_ref[0] = jnp.sum(grad_pre.astype(F32), axis=0, keepdims=True)
    fc_grad_ref[...] = cols_by_cols(grad_pre, second).astype(BF)
    acc_ref[...] += plain_dot(grad_pre, fc_ref[...])

    @pl.when(step == pl.num_programs(0) - 1)
    def _():
        _, hat, inverse = norm_rows(hidden_ref[...], 1.0, 0.0)
        grad_second, grad_y = acc_ref[...], dy.astype(F32)
        grad = grad_y + norm_back(grad_second, hat, inverse, shared_ref[3:4, :])
        low = grad.astype(BF)
        grad_ref[...] = grad
        low_ref[...] = low
        for n, rows in enumerate((low.astype(F32), grad_second * hat, grad_second, grad_y)):
            sums_ref[n : n + 1, :] = jnp.sum(rows, axis=0, keepdims=True)


def feed_forward(hidden, out_grad, shared, b_fc, w_fc, w_proj):
    rows, width = hidden.shape
    tile = 512
    steps = w_fc.shape[0] // tile
    whole = lambda *dims: pl.BlockSpec(dims, lambda i: (0,) * len(dims))
    strip = pl.BlockSpec((tile, width), lambda i: (i, 0))
    bias = pl.BlockSpec((1, 1, tile), lambda i: (i, 0, 0))
    shape = jax.ShapeDtypeStruct
    out = pl.pallas_call(
        feed_forward_kernel,
        grid=(steps,),
        in_specs=[whole(rows, width), whole(rows, width), whole(*shared.shape), bias, strip, strip],
        out_specs=[whole(rows, width)] * 3 + [strip, strip, bias, whole(4, width)],
        out_shape=[
            shape((rows, width), F32), shape((rows, width), F32), shape((rows, width), BF),
            shape(w_fc.shape, BF), shape(w_proj.shape, BF), shape((steps, 1, tile), F32), shape((4, width), F32),
        ],
        scratch_shapes=[pltpu.VMEM((rows, width), BF), pltpu.VMEM((rows, width), F32)],
        compiler_params=pltpu.CompilerParams(vmem_limit_bytes=48 << 20),
        name="feed_forward",
    )(hidden, out_grad, shared, b_fc.reshape(steps, 1, tile), w_fc, w_proj)
    return (*out[:5], out[5].reshape(-1), out[6])


def per_device(
    tokens_in,
    out_grad,
    lengths,
    owners,
    matrix_master,
    matrix_m1,
    matrix_m2,
    shared_params,
    bias_params,
):
    n_tensor = lax.axis_size("tensor")
    n_data = lax.axis_size("dp")
    tensor_index = lax.axis_index("tensor")
    data_index = lax.axis_index("dp")
    rows_here, width = tokens_in.shape
    slot_cap = matrix_master.shape[1]
    unit_rows = matrix_master.shape[2]
    n_units = owners.shape[0]
    n_slots = n_data * slot_cap
    head_rows = width // n_tensor
    heads_here = head_rows // HD
    ff_rows = (n_units * unit_rows - 4 * head_rows) // 2
    slot_of_unit, unit_of_slot, occupied = slot_tables(owners, n_slots, slot_cap)


    back = -(-(DOC_MOST - 1) // rows_here)
    reach = back * rows_here
    own_kernels = n_data == 8 and n_tensor == 4 and back == 2 and head_rows == unit_rows and unit_rows % 128 == 0
    sizes = lengths[0]
    upto = jnp.arange(sizes.shape[0])[:, None] >= jnp.arange(sizes.shape[0])[None, :]
    bounds = jnp.sum(jnp.where(upto, sizes[None, :], 0), axis=1)
    places = tensor_index * rows_here + jnp.arange(rows_here, dtype=jnp.int32)
    starts = jnp.max(jnp.where(places[:, None] >= bounds[None, :], bounds[None, :], 0), axis=1)
    first_seen = (starts - tensor_index * rows_here + reach)[None, :]

    shared = shared_params[0]
    inputs_f32 = tokens_in.astype(F32)
    normed_one, hat_one, inverse_one = norm_rows(inputs_f32, shared[0], shared[1])
    normed_low = normed_one.astype(BF)
    if own_kernels:
        (
            w_att, normed_all, q_scaled, keys_in, values_in, attended, log_norms, peaks,
            layer_out, grad_hidden, grad_attended, grad_ff_w, grad_out_w, grad_fc_b, shared_rows,
        ) = forward_spread(
            matrix_master[0].astype(BF), normed_low, tokens_in, out_grad, bias_params[0, 0], first_seen, shared,
            slot_of_unit, n_tensor, back,
        )
    else:
        units = gather_units(matrix_master[0], slot_of_unit)
        stacks = units.reshape(n_tensor, n_units * unit_rows, width)
        part = lambda first, count: stacks[:, first : first + count].reshape(-1, width)
        w_q, w_k, w_v, w_out = (part(i * head_rows, head_rows) for i in range(4))
        w_fc = part(4 * head_rows, ff_rows)
        w_proj = part(4 * head_rows + ff_rows, ff_rows)
        all_bias = lax.all_gather(bias_params[0], "tensor", axis=0, tiled=True).reshape(n_tensor, -1)
        before = [
            lax.ppermute(normed_low, "tensor", [(i, i + r) for i in range(n_tensor - r)])
            for r in range(min(back, n_tensor - 1), 0, -1)
        ]
        blank = [jnp.zeros_like(normed_low)] * (back - len(before))
        normed_all = jnp.concatenate([*blank, *before, normed_low], axis=0)
        bias = lambda first, count: all_bias[:, first : first + count].reshape(-1)
        b_q, b_k, b_v = (bias(i * head_rows, head_rows) for i in range(3))
        b_fc = bias(3 * head_rows, ff_rows)
        q_scaled = (rows_by_rows(normed_low, w_q) + b_q).astype(BF) * jnp.asarray(1.0 / math.sqrt(HD), BF)
        keys_in = (rows_by_rows(normed_all, w_k) + b_k).astype(BF)
        values_in = (rows_by_rows(normed_all, w_v) + b_v).astype(BF)
        attended, log_norms, peaks = attend_forward(q_scaled, keys_in, values_in, first_seen)
        hidden = inputs_f32 + (plain_dot(attended, w_out) + shared[2])
        layer_out, grad_hidden, grad_hidden_low, grad_fc_w, grad_proj_w, grad_fc_b, shared_rows = feed_forward(
            hidden, out_grad, shared, b_fc, w_fc, w_proj
        )
        grad_out_w = cols_by_cols(attended, grad_hidden_low).astype(BF)
        grad_attended = rows_by_rows(grad_hidden_low, w_out).astype(BF)
    head_here = jnp.max(peaks, axis=2).reshape(-1)
    if own_kernels:
        in_blocks = lambda g: g.reshape(-1, n_tensor, 2, 2, 2, unit_rows // 8, width)
        shard, grad_first, grad_q_w, grad_k_w, grad_v_w, sums = backward_reduce(
            in_blocks(grad_ff_w), q_scaled, keys_in, values_in, attended, grad_attended,
            log_norms, first_seen, normed_all, w_att, n_tensor, back,
        )
        grad_fc_b = grad_fc_b.reshape(2, n_tensor, -1, unit_rows).swapaxes(1, 2)
        vectors = jnp.concatenate(
            [
                jnp.zeros((2, width), F32), shared_rows, sums, grad_fc_b.reshape(-1, width),
                jnp.pad(head_here, (0, width - head_here.shape[0]))[None], jnp.zeros((2, width), F32),
            ],
            axis=0,
        )
        grads = [in_blocks(g) for g in (grad_q_w, grad_k_w, grad_v_w, grad_out_w)]
        half = (n_units - 4) // 2
        later = unit_of_slot - 4
        spot_of_slot = jnp.where(later < 0, unit_of_slot, 4 + jnp.where(later < half, 2 * later, 2 * (later - half) + 1))
        my_grads, totals, input_grad = finish_reduce(
            grads, shard, grad_first, grad_hidden, tokens_in, shared, vectors, spot_of_slot, n_tensor, slot_cap
        )
        my_grads = my_grads.astype(F32)
        shared_grad = totals[:6]
        head_all = totals[MAX_ROW, : head_here.shape[0]]
        bias_total = totals[6:MAX_ROW].reshape(-1, n_tensor, unit_rows)
        bias_grad = lax.dynamic_index_in_dim(bias_total, tensor_index, 1, keepdims=False).reshape(-1)
    else:
        grad_q, grad_k, grad_v = attend_backward(
            q_scaled, keys_in, values_in, attended, grad_attended, log_norms, first_seen
        )
        grad_q_w = cols_by_cols(grad_q, normed_low)
        grad_k_w = cols_by_cols(grad_k, normed_all)
        grad_v_w = cols_by_cols(grad_v, normed_all)
        grad_wide = plain_dot(grad_k, w_k) + plain_dot(grad_v, w_v)
        grad_first = grad_wide[reach:] + plain_dot(grad_q, w_q)
        for r in range(1, min(back, n_tensor - 1) + 1):
            away = grad_wide[reach - r * rows_here : reach - (r - 1) * rows_here].astype(BF)
            grad_first += lax.ppermute(away, "tensor", [(i, i - r) for i in range(r, n_tensor)]).astype(F32)
        input_grad = grad_hidden + norm_back(grad_first, hat_one, inverse_one, shared[0])
        grad_qkv_b = [jnp.sum(g, axis=0, dtype=F32) for g in (grad_q, grad_k, grad_v)]
        first_rows = jnp.stack([jnp.sum(grad_first * hat_one, axis=0), jnp.sum(grad_first, axis=0)])
        shared_part = jnp.concatenate([first_rows, shared_rows], axis=0)
        by_tensor = lambda v: v.reshape(n_tensor, -1)
        bias_part = jnp.concatenate([by_tensor(v) for v in (*grad_qkv_b, grad_fc_b)], axis=1)
        head_all = lax.pmax(head_here, ("dp", "tensor"))
        shared_grad, bias_total = lax.psum((shared_part, bias_part), ("dp", "tensor"))
        bias_grad = lax.dynamic_index_in_dim(bias_total, tensor_index, 0, keepdims=False)
        by_stack = lambda g: g.astype(BF).reshape(n_tensor, -1, width)
        grad_units = jnp.concatenate(
            [by_stack(g) for g in (grad_q_w, grad_k_w, grad_v_w, grad_out_w, grad_fc_w, grad_proj_w)], axis=1
        ).reshape(units.shape)
        my_grads = scatter_units(grad_units, unit_of_slot).astype(F32)
    head_peak = lax.dynamic_slice_in_dim(head_all, tensor_index * heads_here, heads_here)

    my_units = lax.dynamic_slice_in_dim(unit_of_slot, data_index * slot_cap, slot_cap, 0)
    my_occupied = lax.dynamic_slice_in_dim(occupied, data_index * slot_cap, slot_cap, 0)[:, None, None]
    steps_done = float(STEP)
    first_new, second_new, master_new = adam_step(
        matrix_master[0], my_grads, matrix_m1[0], matrix_m2[0], steps_done, WEIGHT_DECAY
    )
    root_gamma = jnp.sqrt(CLIP_TAU / jnp.maximum(head_peak, CLIP_TAU))
    row_index = my_units[:, None] * unit_rows + jnp.arange(unit_rows, dtype=jnp.int32)[None, :]
    local_head = jnp.where(row_index < head_rows, row_index // HD, (row_index - head_rows) // HD)
    head_match = local_head[..., None] == jnp.arange(heads_here, dtype=jnp.int32)[None, None, :]
    picked_root = jnp.sum(jnp.where(head_match, root_gamma, 0.0), axis=-1)
    factor = jnp.where(row_index < 2 * head_rows, picked_root, 1.0)
    my_grads = jnp.where(my_occupied, my_grads, 0.0)
    master_new = jnp.where(my_occupied, master_new * factor[..., None], 0.0)
    first_new = jnp.where(my_occupied, first_new, 0.0)
    second_new = jnp.where(my_occupied, second_new, 0.0)
    shared_first, shared_second, shared_new = adam_step(
        shared, shared_grad, shared_params[1], shared_params[2], steps_done, 0.0
    )
    bias_first, bias_second, bias_new = adam_step(
        bias_params[0, 0], bias_grad, bias_params[1, 0], bias_params[2, 0], steps_done, 0.0
    )
    shared_out = jnp.stack([shared_grad, shared_first])
    bias_out = jnp.stack([bias_grad, bias_first])[:, None, :]
    return (
        layer_out,
        input_grad,
        head_peak,
        my_grads[None],
        first_new[None],
        second_new[None],
        master_new[None],
        shared_out,
        shared_second,
        shared_new,
        bias_out,
        bias_second[None],
        bias_new[None],
    )


def solution(mesh):
    in_specs = (
        P(("dp", "tensor"), None),
        P(("dp", "tensor"), None),
        P("dp", None),
        P(),
        P("tensor", "dp", None, None),
        P("tensor", "dp", None, None),
        P("tensor", "dp", None, None),
        P(),
        P(None, "tensor", None),
    )
    out_specs = (
        P(("dp", "tensor"), None),
        P(("dp", "tensor"), None),
        P("tensor"),
        P("tensor", "dp", None, None),
        P("tensor", "dp", None, None),
        P("tensor", "dp", None, None),
        P("tensor", "dp", None, None),
        P(),
        P(),
        P(),
        P(None, "tensor", None),
        P("tensor", None),
        P("tensor", None),
    )
    return jax.shard_map(
        per_device, mesh=mesh, in_specs=in_specs, out_specs=out_specs, check_vma=False
    )
```

```python
import functools
import math

import jax
import jax.numpy as jnp
from jax import lax
from jax.experimental import pallas as pl
from jax.experimental.pallas import tpu as pltpu
from jax.sharding import PartitionSpec as P

HD = 64
DOC_MOST = 1024
STEP = 10
PAIR = 2 * HD

EPS_NORM = 1e-05
BETA_ONE = 0.9
BETA_TWO = 0.95
LEARN_RATE = 0.08
WEIGHT_DECAY = 0.1
EPS_ADAM = 1e-08
CLIP_TAU = 10.0
MASKED = -1e30
GELU_A = 0.7978845608
GELU_B = 0.044715
BF = jnp.bfloat16
F32 = jnp.float32
MESH = pl.DeviceIdType.MESH
MAX_ROW = 13
BACK_GROUPS = 4
LAST_GROUPS = 2


def plain_dot(left, right):
    return jnp.dot(left, right, preferred_element_type=F32)


def rows_by_rows(left, right):
    return lax.dot_general(left, right, (((1,), (1,)), ((), ())), preferred_element_type=F32)


def cols_by_cols(left, right):
    return lax.dot_general(left, right, (((0,), (0,)), ((), ())), preferred_element_type=F32)


def gelu_tanh(values_in):
    return jax.nn.gelu(values_in, approximate=True)


def norm_rows(values_in, gain, shift):
    centre = jnp.mean(values_in, axis=-1, keepdims=True)
    shifted = values_in - centre
    inverse = lax.rsqrt(jnp.mean(shifted * shifted, axis=-1, keepdims=True) + EPS_NORM)
    normed = shifted * inverse
    return (normed * gain + shift, normed, inverse)


def norm_back(grad_in, normed, inverse, gain):
    scaled = grad_in * gain
    return inverse * (
        scaled
        - jnp.mean(scaled, axis=-1, keepdims=True)
        - normed * jnp.mean(scaled * normed, axis=-1, keepdims=True)
    )


def slot_tables(owners, n_slots, slot_cap):
    n_units = owners.shape[0]
    unit_order = jnp.arange(n_units, dtype=jnp.int32)
    same_owner = owners[:, None] == owners[None, :]
    earlier = unit_order[None, :] < unit_order[:, None]
    rank_counts = jnp.sum((same_owner & earlier).astype(jnp.int32), axis=1)
    slot_of_unit = owners * slot_cap + rank_counts
    matches = jnp.arange(n_slots, dtype=jnp.int32)[:, None] == slot_of_unit[None, :]
    occupied = jnp.any(matches, axis=1)
    unit_of_slot = jnp.sum(matches.astype(jnp.int32) * unit_order[None, :], axis=1)
    return (slot_of_unit, unit_of_slot, occupied)


def head_lanes(head):
    lane = lax.broadcasted_iota(jnp.int32, (1, PAIR), 1)
    return (lane < HD) if head == 0 else (lane >= HD)


def q_tiles(n_query, n_keys):
    size = min(256, n_query)
    reach = n_keys - n_query
    return size, reach + size


def fill_bias(bias_ref, first_ref):
    n_keys, n_query = bias_ref.shape
    reach = n_keys - n_query
    key = lax.broadcasted_iota(jnp.int32, (n_keys, n_query), 0)
    query = lax.broadcasted_iota(jnp.int32, (n_keys, n_query), 1) + reach
    seen = (key <= query) & (key >= first_ref[...])
    bias_ref[...] = jnp.where(seen, 0.0, MASKED)


def attend_kernel(first_ref, q_ref, k_ref, v_ref, o_ref, lse_ref, peak_ref, bias_ref):
    @pl.when(pl.program_id(0) == 0)
    def _():
        fill_bias(bias_ref, first_ref)

    n_keys, n_query = bias_ref.shape
    size, span = q_tiles(n_query, n_keys)
    for j in range(n_query // size):
        rows, keys = pl.ds(j * size, size), pl.ds(j * size, span)
        v_t = v_ref[keys, :].T
        outs = []
        for h in range(2):
            k_h = jnp.where(head_lanes(h), k_ref[keys, :], 0)
            s = rows_by_rows(k_h, q_ref[rows, :]) + bias_ref[keys, rows]
            top = jnp.max(s, axis=0, keepdims=True)
            p = jnp.exp(s - top)
            total = jnp.sum(p, axis=0, keepdims=True)
            o_t = plain_dot(v_t[h * HD : (h + 1) * HD], p.astype(BF))
            outs.append(o_t / total)
            lse_ref[0, h : h + 1, rows] = top + jnp.log(total)
            peak_ref[0, h : h + 1, rows] = top
        o_ref[rows, :] = jnp.concatenate(outs, axis=0).T.astype(BF)


def attend_forward(q_scaled, keys_in, values_in, first_seen):
    n_query, width = q_scaled.shape
    n_keys = keys_in.shape[0]
    pairs = width // PAIR
    column = lambda i: (0, i)
    stats = jax.ShapeDtypeStruct((pairs, 2, n_query), F32)
    stat_spec = pl.BlockSpec((1, 2, n_query), lambda i: (i, 0, 0))
    return pl.pallas_call(
        attend_kernel,
        grid=(pairs,),
        in_specs=[
            pl.BlockSpec((1, n_query), lambda i: (0, 0)),
            pl.BlockSpec((n_query, PAIR), column),
            pl.BlockSpec((n_keys, PAIR), column),
            pl.BlockSpec((n_keys, PAIR), column),
        ],
        out_specs=[pl.BlockSpec((n_query, PAIR), column), stat_spec, stat_spec],
        out_shape=[jax.ShapeDtypeStruct((n_query, width), BF), stats, stats],
        scratch_shapes=[pltpu.VMEM((n_keys, n_query), F32)],
        compiler_params=pltpu.CompilerParams(vmem_limit_bytes=48 << 20),
        name="attend_forward",
    )(first_seen, q_scaled, keys_in, values_in)


def attend_back_kernel(
    first_ref, q_ref, k_ref, v_ref, o_ref, do_ref, lse_ref, dq_ref, dk_ref, dv_ref,
    bias_ref, dk_acc, dv_acc, *, scale
):
    @pl.when(pl.program_id(0) == 0)
    def _():
        fill_bias(bias_ref, first_ref)

    n_keys, n_query = bias_ref.shape
    size, span = q_tiles(n_query, n_keys)
    dk_acc[...] = jnp.zeros_like(dk_acc)
    dv_acc[...] = jnp.zeros_like(dv_acc)
    for j in range(n_query // size):
        rows, keys = pl.ds(j * size, size), pl.ds(j * size, span)
        q_here, do_here = q_ref[rows, :], do_ref[rows, :]
        k_here, v_here = k_ref[keys, :], v_ref[keys, :]
        k_t = k_here.T
        meet = (do_here.astype(F32) * o_ref[rows, :].astype(F32)).T
        outs = []
        for h in range(2):
            lanes = head_lanes(h)
            delta = jnp.sum(meet[h * HD : (h + 1) * HD], axis=0, keepdims=True)
            s = rows_by_rows(jnp.where(lanes, k_here, 0), q_here) + bias_ref[keys, rows]
            p = jnp.exp(s - lse_ref[0, h : h + 1, rows])
            dp = rows_by_rows(jnp.where(lanes, v_here, 0), do_here)
            ds = (p * (dp - delta)).astype(BF)
            dv_acc[keys, :] += plain_dot(p.astype(BF), jnp.where(lanes, do_here, 0))
            dk_acc[keys, :] += plain_dot(ds, jnp.where(lanes, q_here, 0))
            outs.append(plain_dot(k_t[h * HD : (h + 1) * HD], ds))
        dq_ref[rows, :] = (jnp.concatenate(outs, axis=0).T * scale).astype(BF)
    dk_ref[...] = dk_acc[...].astype(BF)
    dv_ref[...] = dv_acc[...].astype(BF)


def attend_backward(q_scaled, keys_in, values_in, attended, grads_out, log_norms, first_seen):
    n_query, width = q_scaled.shape
    n_keys = keys_in.shape[0]
    pairs = width // PAIR
    column = lambda i: (0, i)
    q_spec = pl.BlockSpec((n_query, PAIR), column)
    k_spec = pl.BlockSpec((n_keys, PAIR), column)
    q_out = jax.ShapeDtypeStruct((n_query, width), BF)
    k_out = jax.ShapeDtypeStruct((n_keys, width), BF)
    return pl.pallas_call(
        functools.partial(attend_back_kernel, scale=1.0 / math.sqrt(HD)),
        grid=(pairs,),
        in_specs=[
            pl.BlockSpec((1, n_query), lambda i: (0, 0)),
            q_spec, k_spec, k_spec, q_spec, q_spec,
            pl.BlockSpec((1, 2, n_query), lambda i: (i, 0, 0)),
        ],
        out_specs=[q_spec, k_spec, k_spec],
        out_shape=[q_out, k_out, k_out],
        scratch_shapes=[
            pltpu.VMEM((n_keys, n_query), F32),
            pltpu.VMEM((n_keys, PAIR), F32),
            pltpu.VMEM((n_keys, PAIR), F32),
        ],
        compiler_params=pltpu.CompilerParams(vmem_limit_bytes=48 << 20),
        name="attend_backward",
    )(first_seen, q_scaled, keys_in, values_in, attended, grads_out, log_norms)


def adam_step(param, grad, first, second, steps_done, decay):
    first_new = BETA_ONE * first + (1.0 - BETA_ONE) * grad
    second_new = BETA_TWO * second + (1.0 - BETA_TWO) * grad * grad
    fix_one = 1.0 - BETA_ONE**steps_done
    fix_two = 1.0 - BETA_TWO**steps_done
    direction = first_new / fix_one / (jnp.sqrt(second_new / fix_two) + EPS_ADAM)
    return (first_new, second_new, param - LEARN_RATE * (direction + decay * param))


def take_kernel(picks_ref, from_ref, to_ref):
    to_ref[...] = from_ref[...]


def take_blocks(blocks, picks):
    shape = (blocks.shape[0], 1, *blocks.shape[2:])
    return pl.pallas_call(
        take_kernel,
        grid_spec=pltpu.PrefetchScalarGridSpec(
            num_scalar_prefetch=1,
            grid=picks.shape,
            in_specs=[pl.BlockSpec(shape, lambda i, p: (0, p[i], 0, 0))],
            out_specs=pl.BlockSpec(shape, lambda i, p: (0, i, 0, 0)),
        ),
        out_shape=jax.ShapeDtypeStruct((shape[0], picks.shape[0], *shape[2:]), blocks.dtype),
        compiler_params=pltpu.CompilerParams(vmem_limit_bytes=32 << 20),
        name="take_blocks",
    )(picks, blocks)


def gather_units(master, slot_of_unit):
    slots = lax.all_gather(master.astype(BF), ("tensor", "dp"), axis=0, tiled=True)
    n_tensor = lax.axis_size("tensor")
    slots = slots.reshape(n_tensor, -1, *master.shape[1:])
    return take_blocks(slots, slot_of_unit)


def scatter_units(units, unit_of_slot):
    slots = take_blocks(units, unit_of_slot)
    slots = slots.reshape(-1, *units.shape[2:])
    return lax.psum_scatter(slots, ("tensor", "dp"), scatter_dimension=0, tiled=True)


def send(src, dst, send_sem, recv_sem, to):
    copy = pltpu.make_async_remote_copy(
        src_ref=src, dst_ref=dst, send_sem=send_sem, recv_sem=recv_sem,
        device_id=to, device_id_type=MESH,
    )
    copy.start()


def arrived(ref, sem):
    pltpu.make_async_copy(ref, ref, sem).wait()


def place():
    d, t = lax.axis_index("dp"), lax.axis_index("tensor")
    return d, t, d % 2, (d // 2) % 2, d // 4


def greet(d, t, n_tensor):
    barrier = pltpu.get_barrier_semaphore()
    for k in range(1, 8):
        pl.semaphore_signal(barrier, inc=1, device_id=((d + k) % 8, t), device_id_type=MESH)
    for k in range(1, n_tensor):
        pl.semaphore_signal(barrier, inc=1, device_id=(d, (t + k) % n_tensor), device_id_type=MESH)
    pl.semaphore_wait(barrier, 6 + n_tensor)


def loop_with(count, body, events):
    def step(i, carry):
        body(i)
        for n, mine in events.items():
            @pl.when(i == n)
            def _(mine=mine):
                for event in mine:
                    event()
        return carry

    lax.fori_loop(0, count, step, 0)


def by_step(order, by_code, kinds):
    early, during = [], {kind: {} for kind in range(1, kinds + 1)}
    now, count = None, 0
    for code in order:
        if code < 0:
            now, count = -code, 0 if -code != now else count + 1
        elif now is None:
            early.append(by_code[code])
        else:
            during[now].setdefault(count, []).append(by_code[code])
    return early, during


def attend_pair(i, q_ref, k_ref, v_ref, o_ref, lse_ref, peak_ref, bias_ref):
    n_keys, n_query = bias_ref.shape
    size, span = q_tiles(n_query, n_keys)
    lanes = pl.ds(pl.multiple_of(i * PAIR, PAIR), PAIR)
    for j in range(n_query // size):
        rows, keys = pl.ds(j * size, size), pl.ds(j * size, span)
        v_t = v_ref[keys, lanes].T
        outs = []
        for h in range(2):
            k_h = jnp.where(head_lanes(h), k_ref[keys, lanes], 0)
            s = rows_by_rows(k_h, q_ref[rows, lanes]) + bias_ref[keys, rows]
            top = jnp.max(s, axis=0, keepdims=True)
            p = jnp.exp(s - top)
            total = jnp.sum(p, axis=0, keepdims=True)
            o_t = plain_dot(v_t[h * HD : (h + 1) * HD], p.astype(BF))
            outs.append(o_t / total)
            lse_ref[i, h : h + 1, rows] = top + jnp.log(total)
            peak_ref[i, h : h + 1, rows] = top
        o_ref[rows, lanes] = jnp.concatenate(outs, axis=0).T.astype(BF)


def paired(n_units):
    half = (n_units - 4) // 2
    return [0, 1, 2, 3] + [4 + i + half * b for i in range(half) for b in range(2)]


def gelu_parts(pre):
    square = pre * pre
    inner = jnp.tanh(GELU_A * (pre + GELU_B * (square * pre)))
    half = 0.5 * pre
    slope = 0.5 + 0.5 * inner + half * (1.0 - inner * inner) * (GELU_A + (3.0 * GELU_A * GELU_B) * square)
    return half + half * inner, slope


ORDER = (
    220, 100, 200, 600, 0, 601, 602, 500, 501, 801, 120, 502, 701, 1900, 110, 300, 802, 702, 800, 700, 901,
    1001, 610, 1000, 400, 902, 210, 1952, 1002, 900, 10, 1950, 310, 1951, 1953, -1, -1, -1, 20, 1901, 620, -1,
    611, -2, -2, -2, -2, 510, -3, -3, -3, 520, -3, -4, 511, 621, -4, -4, 521, 622, -4, 811, 512, 710, -4, 612,
    711, 810, -4, 410, -4, 522, -4, 820, 712, 720, 910, 911, 1011, 812, 320, -5, 1010, -6, 912, 721, 822, -6,
    1012, 1020, -6, 821, 420, 1022, 920, -6, 722, -6, -6, -6, -6, 921, 1021, -6, 922, -6, -6, -6, -6, -6,
)


def forward_kernel(
    n_tensor, back, scale,
    slot_ref, master_ref, a_ref, x_ref, dy_ref, bias_in_ref, first_ref, shared_ref,
    att_ref, ff_ref, wide_ref, q_ref, k_ref, v_ref, o_ref, lse_ref, peak_ref,
    out_ref, grad_ref, do_ref, ff_grad_ref, go_ref, fc_bias_ref, sums_ref,
    pieces, own, seen_ref, bias_rows, biases_ref, fc_rows, hidden_ref, second_ref, acc_ref, tiles_in, stage,
    swap_send, swap_recv, local_sem, a_send, a_recv, bias_send, bias_recv,
    z_send, z_recv, xy_send, xy_recv, core_send, core_recv, tile_sem, stage_sem,
):
    d, t, core, x, y = place()
    column = y * 2 + x
    by_x, by_y = d + 2 - 4 * x, d + 4 - 8 * y
    sibling = d + 1 - 2 * core
    first, last = t > 0, t < n_tensor - 1
    rows_here, width = a_ref.shape
    n_half = ff_ref.shape[0] // 2
    weights = (att_ref, ff_ref.at[pl.ds(0, n_half)], ff_ref.at[pl.ds(n_half, n_half)])
    starts = (0, 4, 4 + n_half, 4 + 2 * n_half)
    n_groups, steps = len(weights), n_tensor - 1
    slots = 2 * n_tensor - 1
    greet(d, t, n_tensor)

    def tokens_up(r):
        @pl.when(last & (t >= r))
        def _():
            source = a_ref if r == 0 else wide_ref.at[back - r]
            send(source, wide_ref.at[back - r - 1], a_send.at[r], a_recv.at[r], (d, t + 1))

    def tokens_in(r):
        @pl.when(t > r)
        def _():
            arrived(wide_ref.at[back - r - 1], a_recv.at[r])
        if r + 1 < back:
            tokens_up(r + 1)

    for k in range(1, 8):
        to = (d + k) % 8
        send(master_ref.at[:, to], pieces.at[d], swap_send.at[k - 1], swap_recv.at[k - 1], (to, t))
    tokens_up(0)
    mine = pltpu.make_async_copy(master_ref.at[:, d], pieces.at[d], local_sem.at[0])
    mine.start()
    for k in range(1, n_tensor):
        send(bias_in_ref, biases_ref.at[t], bias_send.at[k - 1], bias_recv.at[k - 1], (d, (t + k) % n_tensor))
    biases_ref[t] = bias_in_ref[...]
    wide_ref[back] = a_ref[...]
    for r in range(back):
        @pl.when(t < back - r)
        def _(r=r):
            wide_ref[r] = jnp.zeros((rows_here, width), BF)
    fill_bias(seen_ref, first_ref)
    mine.wait()
    for k in range(1, 8):
        arrived(pieces.at[(d + 8 - k) % 8], swap_recv.at[k - 1])
    cap = master_ref.shape[0]
    for n, u in enumerate(paired(own.shape[0])):
        slot = slot_ref[u]
        own[n] = pieces[slot // cap, slot % cap]

    def block(g, at, col, c):
        return weights[g].at[:, at, col, c]

    def route(at):
        side = at * 2 // n_tensor
        one, two = by_x + (by_y - by_x) * side, by_y + (by_x - by_y) * side
        col_x, col_y, col_xy = y * 2 + 1 - x, (1 - y) * 2 + x, (1 - y) * 2 + 1 - x
        return one, two, col_x + (col_y - col_x) * side, col_y + (col_x - col_y) * side, col_xy

    def onward(g, k, at, source):
        one, two, _, _, _ = route(at)
        here = block(g, at, column, core)
        send(source, here, xy_send.at[g], xy_recv.at[g, k, 0], (one, t))
        send(source, here, xy_send.at[g], xy_recv.at[g, k, 1], (two, t))

    def forward(g, k, at):
        one, two, from_one, _, _ = route(at)
        got = block(g, at, from_one, core)
        arrived(got, xy_recv.at[g, k, 0])
        send(got, got, xy_send.at[g], xy_recv.at[g, k, 2], (two, t))

    def settle(g, k, at):
        _, _, _, from_two, beyond = route(at)
        arrived(block(g, at, from_two, core), xy_recv.at[g, k, 1])
        arrived(block(g, at, beyond, core), xy_recv.at[g, k, 2])
        got = weights[g].at[:, at, :, core]
        send(got, got, core_send.at[g, k], core_recv.at[g, k], (sibling, t))

    def done(g, k, at):
        arrived(weights[g].at[:, at, :, 1 - core], core_recv.at[g, k])

    def given(g, k, at):
        arrived(weights[g].at[:, at, :, core], core_send.at[g, k])

    def z_go(g, s, up, source):
        i = 0 if up else 1

        @pl.when(last if up else first)
        def _():
            here = block(g, t if s == 0 else (t - s if up else t + s), column, core)
            send(source, here, z_send.at[g, i, s], z_recv.at[g, i, s], (d, t + 1 if up else t - 1))

    def z_step(s, up):
        at = t - 1 - s if up else t + 1 + s
        return 1 + 2 * s + (0 if up else 1), at, (at >= 0) if up else (at < n_tensor)

    def z_event(g, s, up):
        k, at, have = z_step(s, up)

        @pl.when(have)
        def _():
            got = block(g, at, column, core)
            arrived(got, z_recv.at[g, 0 if up else 1, s])
            if s + 1 < steps:
                z_go(g, s + 1, up, got)
            onward(g, k, at, got)

    def step(fn, g, s, up):
        k, at, have = z_step(s, up)
        pl.when(have)(functools.partial(fn, g, k, at))

    def each(fn, g, s):
        if s < 0:
            fn(g, 0, t)
        else:
            for up in (True, False):
                step(fn, g, s, up)

    local = []
    mine_of = [own.at[starts[g] : starts[g + 1]] for g in range(n_groups)]
    for g in range(n_groups):
        copy = pltpu.make_async_copy(mine_of[g], block(g, t, column, core), local_sem.at[1 + g])
        copy.start()
        local.append(copy)

    def own_settled(g):
        local[g].wait()
        settle(g, 0, t)

    by_code = {1900 + r: functools.partial(tokens_in, r) for r in range(back)}
    by_code |= {1951 + s: functools.partial(each, done, 0, s) for s in range(-1, steps)}
    for g in range(n_groups):
        by_code[200 + 10 * g] = functools.partial(onward, g, 0, t, mine_of[g])
        by_code[300 + 10 * g] = functools.partial(forward, g, 0, t)
        by_code[400 + 10 * g] = functools.partial(own_settled, g)
        for way, up in ((0, True), (100, False)):
            by_code[way + 10 * g] = functools.partial(z_go, g, 0, up, mine_of[g])
            for s in range(steps):
                by_code[500 + way + 10 * g + s] = functools.partial(z_event, g, s, up)
                by_code[700 + way + 10 * g + s] = functools.partial(step, forward, g, s, up)
                by_code[900 + way + 10 * g + s] = functools.partial(step, settle, g, s, up)
    tile = 256
    tiles = width // tile
    early, during = by_step(ORDER, by_code, 6)
    for event in early:
        event()
    for k in range(1, n_tensor):
        arrived(biases_ref.at[(t + n_tensor - k) % n_tensor], bias_recv.at[k - 1])
        arrived(bias_in_ref, bias_send.at[k - 1])
    per = width // n_tensor // 128
    for n in range(3):
        for at in range(n_tensor):
            for i in range(per):
                lanes = pl.ds((at * per + i) * 128, 128)
                bias_rows[n : n + 1, lanes] = biases_ref[at, n * per + i : n * per + i + 1]
    strip = fc_rows.shape[-1]
    for h in range(2):
        for at in range(n_tensor):
            for i in range(strip // 128):
                row = 3 * per + h * (strip // 128) + i
                fc_rows[h, at, 0:1, i * 128 : (i + 1) * 128] = biases_ref[at, row : row + 1]

    def project(n, own_only, into_ref, factor):
        def body(i):
            cols = pl.ds(pl.multiple_of(i * tile, tile), tile)
            w = att_ref[n, pl.ds(i * tile // (width // n_tensor), 1)].reshape(tile, width)
            for r in range(into_ref.shape[0] // rows_here):
                a = a_ref[...] if own_only else wide_ref[r]
                full = (rows_by_rows(a, w) + bias_rows[n : n + 1, cols]).astype(BF)
                into_ref[r * rows_here : (r + 1) * rows_here, cols] = full * jnp.asarray(factor, BF) if factor else full
        return body

    loop_with(tiles, project(0, True, q_ref, scale), during[1])
    loop_with(tiles, project(1, False, k_ref, None), during[2])
    loop_with(tiles, project(2, False, v_ref, None), during[3])
    loop_with(
        width // PAIR,
        lambda i: attend_pair(i, q_ref, k_ref, v_ref, o_ref, lse_ref, peak_ref, seen_ref),
        during[4],
    )
    w_out = att_ref[3].reshape(width, width)
    half = rows_here // 2
    for r in range(2):
        rows = pl.ds(r * half, half)
        hidden = x_ref[rows, :].astype(F32) + (plain_dot(o_ref[rows, :], w_out) + shared_ref[2:3, :])
        hidden_ref[rows, :] = hidden
        normed, _, _ = norm_rows(hidden, shared_ref[3:4, :], shared_ref[4:5, :])
        second_ref[rows, :] = normed.astype(BF)
        out_ref[rows, :] = hidden + shared_ref[5:6, :]
    acc_ref[...] = jnp.zeros_like(acc_ref)

    def tile_copies(h, at, b):
        for i in range(n_half // 2):
            yield pltpu.make_async_copy(
                ff_ref.at[h * n_half + 2 * i + b, at], tiles_in.at[b, i], tile_sem.at[b, i]
            )

    def grad_copies(h, at):
        for b in range(2):
            for i in range(n_half // 2):
                part = stage.at[b, i]
                yield pltpu.make_async_copy(part, ff_grad_ref.at[h * n_half + 2 * i + b, at], stage_sem.at[b, i])

    def feed(n):
        h, k = n // slots, n % slots
        at = t + (k + 1) // 2 * (1 - 2 * (k % 2))

        @pl.when((at >= 0) & (at < n_tensor))
        def _():
            arrived(ff_ref.at[pl.ds(h * n_half, n_half), at, :, 1 - core], core_recv.at[1 + h, k])
            for b in range(2):
                for copy in tile_copies(h, at, b):
                    copy.start()
            for copy in tile_copies(h, at, 0):
                copy.wait()
            w_fc = tiles_in[0].reshape(strip, width)
            second, dy = second_ref[...], dy_ref[...]
            activ, slope = gelu_parts(rows_by_rows(second, w_fc) + fc_rows[h, at])
            activ = activ.astype(BF)
            for copy in tile_copies(h, at, 1):
                copy.wait()
            w_proj = tiles_in[1].reshape(strip, width)
            grad_pre = (rows_by_rows(dy, w_proj) * slope).astype(BF)
            out_ref[...] += plain_dot(activ, w_proj)
            acc_ref[...] += plain_dot(grad_pre, w_fc)
            fc_bias_ref[h, at] = jnp.sum(grad_pre.astype(F32), axis=0, keepdims=True)

            @pl.when(n > 0)
            def _():
                for copy in grad_copies(h, at):
                    copy.wait()

            stage[0] = cols_by_cols(grad_pre, second).astype(BF).reshape(stage.shape[1:])
            stage[1] = cols_by_cols(activ, dy).astype(BF).reshape(stage.shape[1:])
            for copy in grad_copies(h, at):
                copy.start()

    for event in during[5].get(0, []):
        event()
    loop_with(2 * slots, feed, during[6])
    for copy in grad_copies(0, 0):
        copy.wait()

    part = min(128, rows_here)
    sums_ref[...] = jnp.zeros_like(sums_ref)

    def norm_back_rows(i, carry):
        rows = pl.ds(pl.multiple_of(i * part, part), part)
        _, hat, inverse = norm_rows(hidden_ref[rows, :], 1.0, 0.0)
        grad_second, grad_y = acc_ref[rows, :], dy_ref[rows, :].astype(F32)
        grad = grad_y + norm_back(grad_second, hat, inverse, shared_ref[3:4, :])
        low = grad.astype(BF)
        grad_ref[rows, :] = grad
        second_ref[rows, :] = low
        for n, term in enumerate((low.astype(F32), grad_second * hat, grad_second, grad_y)):
            sums_ref[n : n + 1, :] += jnp.sum(term, axis=0, keepdims=True)
        return carry

    lax.fori_loop(0, rows_here // part, norm_back_rows, 0)

    def out_back(i):
        cols = pl.ds(pl.multiple_of(i * tile, tile), tile)
        w = att_ref[3, pl.ds(i * tile // (width // n_tensor), 1)].reshape(tile, width)
        do_ref[:, cols] = rows_by_rows(second_ref[...], w).astype(BF)
        go_ref[pl.ds(pl.multiple_of(i * tile, tile), tile), :] = cols_by_cols(o_ref[:, cols], second_ref[...]).astype(BF)

    loop_with(tiles, out_back, {})

    for g in range(n_groups):
        for s in range(-1, steps):
            each(given, g, s)
        arrived(weights[g].at[:, :, pl.ds(0, 3), 0], xy_send.at[g])
        for up in (True, False):
            for s in range(steps):
                have = last if up else first
                if s > 0:
                    have = have & z_step(s - 1, up)[2]

                @pl.when(have)
                def _(g=g, s=s, up=up):
                    arrived(block(g, t, column, core), z_send.at[g, 0 if up else 1, s])
    for r in range(back):
        @pl.when(last & (t >= r))
        def _(r=r):
            arrived(a_ref, a_send.at[r])
    for k in range(1, 8):
        arrived(pieces.at[0], swap_send.at[k - 1])


def forward_spread(master_low, normed_low, tokens, out_grad, bias_row, first_seen, shared, slot_of_unit, n_tensor, back):
    cap, unit_rows, width = master_low.shape
    n_units = slot_of_unit.shape[0]
    n_ff = n_units - 4
    piece = unit_rows // 8
    rows = normed_low.shape[0]
    n_keys = (back + 1) * rows
    strip = n_ff // 4 * unit_rows
    bias_row = bias_row.reshape(-1, 128)
    any_spec = pl.BlockSpec(memory_space=pl.ANY)
    vmem = pl.BlockSpec(memory_space=pltpu.VMEM)
    dma = pltpu.SemaphoreType.DMA
    shape = jax.ShapeDtypeStruct
    units = lambda n: shape((n, n_tensor, 4, 2, piece, width), BF)
    stats = shape((width // PAIR, 2, rows), F32)
    low, high = shape((rows, width), BF), shape((rows, width), F32)
    keys = shape((n_keys, width), BF)
    outs = pl.pallas_call(
        functools.partial(forward_kernel, n_tensor, back, 1.0 / math.sqrt(HD)),
        out_shape=[
            units(4), units(n_ff), shape((back + 1, rows, width), BF), low, keys, keys, low, stats, stats,
            high, high, low, shape((n_ff, n_tensor, 4, 2, piece, width), BF), shape((width, width), BF),
            shape((2, n_tensor, 1, strip), F32), shape((4, width), F32),
        ],
        in_specs=[pl.BlockSpec(memory_space=pltpu.SMEM), any_spec] + [vmem] * 6,
        out_specs=[vmem, any_spec] + [vmem] * 10 + [any_spec] + [vmem] * 3,
        scratch_shapes=[
            pltpu.VMEM((8, cap, piece, width), BF),
            pltpu.VMEM((n_units, piece, width), BF),
            pltpu.VMEM((n_keys, rows), F32),
            pltpu.VMEM((3, width), F32),
            pltpu.VMEM((n_tensor, *bias_row.shape), F32),
            pltpu.VMEM((2, n_tensor, 1, strip), F32),
            pltpu.VMEM((rows, width), F32),
            pltpu.VMEM((rows, width), BF),
            pltpu.VMEM((rows, width), F32),
            pltpu.VMEM((2, n_ff // 4, 4, 2, piece, width), BF),
            pltpu.VMEM((2, n_ff // 4, 4, 2, piece, width), BF),
            dma((7,)), dma((7,)), dma((4,)), dma((back,)), dma((back,)),
            dma((n_tensor - 1,)), dma((n_tensor - 1,)),
            dma((3, 2, n_tensor - 1)), dma((3, 2, n_tensor - 1)),
            dma((3,)), dma((3, 2 * n_tensor - 1, 3)),
            dma((3, 2 * n_tensor - 1)), dma((3, 2 * n_tensor - 1)),
            dma((2, n_ff // 4)), dma((2, n_ff // 4)),
        ],
        compiler_params=pltpu.CompilerParams(collective_id=0, has_side_effects=True, vmem_limit_bytes=60 << 20),
        name="forward_spread",
    )(
        slot_of_unit, master_low.reshape(cap, 8, piece, width), normed_low, tokens, out_grad, bias_row, first_seen, shared
    )
    att, _, wide, *rest = outs
    return att.reshape(-1, width), wide.reshape(-1, width), *rest


def split_units(ref, count):
    many = ref.shape[0] // count
    return [ref.at[pl.ds(i * many, many)] for i in range(count)]


def add_blocks(into, part, count):
    def body(i, carry):
        a = into(i)
        a[...] = a[...] + part(i)[...]
        return carry

    lax.fori_loop(0, count, body, 0)


BACK_ORDER = (
    0, -1, -1, 103, 10, 100, -1, 102, 101, -1, 113, -1, 110, -1, 201, 203, 20, 202, -1, 112, 301, 213, -1, 302,
    303, 200, -2, 111, -2, -2, -2, 313, 900, 123, 120, -2, 300, 212, -2, 122, 121, -2, 600, 210, 502, -2, -2,
    30, -2, -2, 211, -2, 223, 133, 130, 503, 310, -3, 312, 602, 700, -3, 702, -3, 512, 311, -3, 403, 220, -4,
    -4, 221, -4, -4, 222, -5, 230, 610, -5, 401, 411, 323, 513, 402, 132, 501, 131, 601, 320, -5, 330, 321, -5,
    523, 231, 620, 233, 901, 322, 423, 331, 611, 232, 612, 701, 621, 522, 511, 333, 421, 412, 720, 521, 711,
    332, 722, 533, 710, 721, 532, 630, 631, 413, 712, 422, 730, 433, 531, 432, 732, 632, 731, 431, 622,
)


LAST_ORDER = (
    0, 103, 100, 900, 10, 102, 101, 203, 113, 110, 202, 200, 303, 201, 213, 300, 112, 301, 111, 313, 210, 302,
    901, 903, 910, 702, 503, 600, 212, 310, 911, 513, 211, 610, 312, 912, 501, 502, 700, 311, 403, 712, 601,
    612, 913, 512, 413, 710, 602, 701, 511, 611, 914, 402, 411, 711, 401, 412,
)


class Reducer:
    def __init__(self, groups, n_tensor, other, near, one, two, up_in, down_in, final, sems):
        self.groups, self.n_tensor = groups, n_tensor
        self.other, self.near, self.one, self.two = other, near, one, two
        self.up_in, self.down_in, self.final = up_in, down_in, final
        (
            self.near_sem, self.core_send, self.core_recv, self.one_send, self.one_recv,
            self.two_send, self.two_recv, self.z_send, self.z_recv,
        ) = sems
        self.d, self.t, self.core, self.x, self.y = place()
        self.by_x, self.by_y = self.d + 2 - 4 * self.x, self.d + 4 - 8 * self.y
        self.sibling = self.d + 1 - 2 * self.core
        self.order = sorted(range(n_tensor), key=lambda a: (-abs(2 * a - n_tensor + 1), -a))
        self.merges = [(g, at) for g in range(len(groups)) for at in self.order]
        self.starts, total = [], 0
        for refs in groups:
            self.starts.append(total)
            total += sum(r.shape[0] for r in refs)
        self.ends = [*self.starts[1:], total]

    @staticmethod
    def scratch(n_units, n_group, n_groups, n_refs, n_tensor, block):
        dma = pltpu.SemaphoreType.DMA
        return [
            pltpu.VMEM((n_units, n_tensor, 2, 2, *block), BF),
            pltpu.VMEM((2, n_group, 2, 2, *block), BF),
            pltpu.VMEM((n_units, n_tensor, 2, *block), BF),
            pltpu.VMEM((n_units, n_tensor, *block), BF),
            pltpu.VMEM((n_units, n_tensor, *block), BF),
            pltpu.VMEM((n_units, n_tensor, *block), BF),
            dma((2, n_refs)), dma((n_groups, n_refs)), dma((n_groups, n_refs)),
            dma((n_groups, n_tensor)), dma((n_groups, n_tensor)),
            dma((n_groups, n_tensor)), dma((n_groups, n_tensor)),
            dma((n_groups, n_tensor)), dma((n_groups, n_tensor, 2)),
        ]

    def parts(self, g):
        u = self.starts[g]
        for n, ref in enumerate(self.groups[g]):
            yield n, ref, u, ref.shape[0]
            u += ref.shape[0]

    def units(self, g):
        return pl.ds(self.starts[g], self.ends[g] - self.starts[g])

    def count(self, g):
        return self.ends[g] - self.starts[g]

    def near_copies(self, m):
        g, at = self.merges[m]
        for n, ref, u, many in self.parts(g):
            yield pltpu.make_async_copy(
                ref.at[:, at, :, :, self.core],
                self.near.at[m % 2, pl.ds(u - self.starts[g], many)],
                self.near_sem.at[m % 2, n],
            )

    def core_go(self, g):
        for n, ref, u, many in self.parts(g):
            send(
                ref.at[:, :, :, :, 1 - self.core], self.other.at[pl.ds(u, many)],
                self.core_send.at[g, n], self.core_recv.at[g, n], (self.sibling, self.t),
            )

    def start(self):
        for m in range(2):
            for copy in self.near_copies(m):
                copy.start()

    def by_rows(self, at):
        return at * 2 < self.n_tensor

    def first_hop(self, m):
        g, at = self.merges[m]
        if m % self.n_tensor == 0:
            for n, ref, u, many in self.parts(g):
                arrived(self.other.at[pl.ds(u, many)], self.core_recv.at[g, n])
        for copy in self.near_copies(m):
            copy.wait()
        u0 = self.starts[g]
        add_blocks(
            lambda i: self.other.at[u0 + i // 4, at, (i // 2) % 2, i % 2],
            lambda i: self.near.at[m % 2, i // 4, (i // 2) % 2, i % 2],
            4 * self.count(g),
        )
        if m + 2 < len(self.merges):
            for copy in self.near_copies(m + 2):
                copy.start()
        us = self.units(g)
        rows = self.by_rows(at)
        source = self.other.at[us, at, 1 - self.y] if rows else self.other.at[us, at, :, 1 - self.x]
        to = self.by_y if rows else self.by_x
        send(source, self.one.at[us, at], self.one_send.at[g, at], self.one_recv.at[g, at], (to, self.t))

    def second_hop(self, m):
        g, at = self.merges[m]
        us, u0 = self.units(g), self.starts[g]
        arrived(self.one.at[us, at], self.one_recv.at[g, at])
        if self.by_rows(at):
            into = lambda i: self.other.at[u0 + i // 2, at, self.y, i % 2]
            source, to = self.other.at[us, at, self.y, 1 - self.x], self.by_x
        else:
            into = lambda i: self.other.at[u0 + i // 2, at, i % 2, self.x]
            source, to = self.other.at[us, at, 1 - self.y, self.x], self.by_y
        add_blocks(into, lambda i: self.one.at[u0 + i // 2, at, i % 2], 2 * self.count(g))
        send(source, self.two.at[us, at], self.two_send.at[g, at], self.two_recv.at[g, at], (to, self.t))

    def plane_sum(self, m):
        g, at = self.merges[m]
        us, u0, n = self.units(g), self.starts[g], self.count(g)
        arrived(self.two.at[us, at], self.two_recv.at[g, at])
        add_blocks(lambda i: self.other.at[u0 + i, at, self.y, self.x], lambda i: self.two.at[u0 + i, at], n)
        if at > 0:
            pl.when(self.t == 0)(functools.partial(self.line_go, g, at, True))
        if at < self.n_tensor - 1:
            pl.when(self.t == self.n_tensor - 1)(functools.partial(self.line_go, g, at, False))

    def line_go(self, g, at, up):
        us = self.units(g)
        into, way, to = (self.up_in, 0, self.t + 1) if up else (self.down_in, 1, self.t - 1)
        send(self.other.at[us, at, self.y, self.x], into.at[us, at], self.z_send.at[g, at], self.z_recv.at[g, at, way], (self.d, to))

    def line_in(self, g, at, up):
        us, u0, n, t = self.units(g), self.starts[g], self.count(g), self.t
        buffer, way = (self.up_in, 0) if up else (self.down_in, 1)
        arrived(buffer.at[us, at], self.z_recv.at[g, at, way])
        add_blocks(lambda i: self.other.at[u0 + i, at, self.y, self.x], lambda i: buffer.at[u0 + i, at], n)
        pl.when(t < at if up else t > at)(functools.partial(self.line_go, g, at, up))

    def line(self, g, at, up, near):
        t, top = self.t, self.n_tensor - 1
        have = ((t <= at) & (t > 0)) if up else ((t >= at) & (t < top))
        half = t * 2 > top
        pl.when(have & (half if near else ~half))(functools.partial(self.line_in, g, at, up))

    def keep(self):
        for g in range(len(self.groups)):
            us = self.units(g)
            self.final[us] = self.other[us, self.t, self.y, self.x]

    def codes(self):
        out = {}
        for g in range(len(self.groups)):
            out[10 * g] = functools.partial(self.core_go, g)
            for i, at in enumerate(self.order):
                m, here = g * self.n_tensor + i, 10 * g + at
                out[100 + here] = functools.partial(self.first_hop, m)
                out[200 + here] = functools.partial(self.second_hop, m)
                out[300 + here] = functools.partial(self.plane_sum, m)
                for kind in range(4):
                    out[400 + 100 * kind + here] = functools.partial(self.line, g, at, kind < 2, kind % 2 == 0)
        return out

    def finish(self):
        for g in range(len(self.groups)):
            us = self.units(g)
            for n, ref, u, many in self.parts(g):
                arrived(self.other.at[pl.ds(u, many)], self.core_send.at[g, n])
            for at in range(self.n_tensor):
                arrived(self.one.at[us, at], self.one_send.at[g, at])
                arrived(self.two.at[us, at], self.two_send.at[g, at])

                @pl.when(self.t != at)
                def _(us=us, g=g, at=at):
                    arrived(self.up_in.at[us, at], self.z_send.at[g, at])


REDUCER = 15


def backward_kernel(
    n_tensor, back, scale,
    ff_grad_ref, q_ref, k_ref, v_ref, o_ref, do_ref, lse_ref, first_ref, wide_ref, att_ref,
    shard_ref, grad_ref, away, gq_ref, gk_ref, gv_ref, sums_ref, *scratch,
):
    reducer_scratch, (
        seen_ref, q_in, k_in, v_in, o_in, do_in, dq_ref, dk_ref, dv_ref, big, stage, dk_acc, dv_acc, away_in,
        pair_sem, load_sem, stage_sem, away_send, away_recv,
    ) = scratch[:REDUCER], scratch[REDUCER:]
    d, t, core, x, y = place()
    greet(d, t, n_tensor)
    other, near, one, two, up_in, down_in, *sems = reducer_scratch
    groups = [[part] for part in split_units(ff_grad_ref, BACK_GROUPS)]
    reducer = Reducer(groups, n_tensor, other, near, one, two, up_in, down_in, shard_ref, sems)
    reducer.start()
    by_code = reducer.codes()

    def give():
        @pl.when(t >= 2)
        def _():
            send(away.at[1], away_in, away_send, away_recv, (d, t - 1))

    def add_given():
        @pl.when((t >= 1) & (t + 1 < n_tensor))
        def _():
            arrived(away_in, away_recv)
            away[0] = (away[0].astype(F32) + away_in[...].astype(F32)).astype(BF)

    by_code |= {900: give, 901: add_given}
    early, during = by_step(BACK_ORDER, by_code, 5)
    for event in early:
        event()
    rows_here, width = do_ref.shape
    n_keys = k_ref.shape[0]
    size, span = q_tiles(rows_here, n_keys)
    sources = ((q_ref, q_in), (k_ref, k_in), (v_ref, v_in), (o_ref, o_in), (do_ref, do_in))

    def pair_copies(i):
        lanes = pl.ds(pl.multiple_of(i * PAIR, PAIR), PAIR)
        return [
            pltpu.make_async_copy(ref.at[:, lanes], buffer.at[i % 2], pair_sem.at[i % 2, n])
            for n, (ref, buffer) in enumerate(sources)
        ]

    for copy in pair_copies(0):
        copy.start()
    weights = pltpu.make_async_copy(att_ref.at[pl.ds(0, 3 * width)], big, load_sem.at[0])
    weights.start()
    fill_bias(seen_ref, first_ref)
    pairs = width // PAIR

    def attend_back(i):
        for copy in pair_copies(i):
            copy.wait()

        @pl.when(i + 1 < pairs)
        def _():
            for copy in pair_copies(i + 1):
                copy.start()

        slot = i % 2
        lanes_here = pl.ds(pl.multiple_of(i * PAIR, PAIR), PAIR)
        dk_acc[...] = jnp.zeros_like(dk_acc)
        dv_acc[...] = jnp.zeros_like(dv_acc)
        dq_sum = jnp.zeros((1, PAIR), F32)
        for j in range(rows_here // size):
            rows, keys = pl.ds(j * size, size), pl.ds(j * size, span)
            q_here, do_here = q_in[slot, rows, :], do_in[slot, rows, :]
            k_here, v_here = k_in[slot, keys, :], v_in[slot, keys, :]
            k_t = k_here.T
            meet = (do_here.astype(F32) * o_in[slot, rows, :].astype(F32)).T
            outs = []
            for h in range(2):
                lanes = head_lanes(h)
                delta = jnp.sum(meet[h * HD : (h + 1) * HD], axis=0, keepdims=True)
                s = rows_by_rows(jnp.where(lanes, k_here, 0), q_here) + seen_ref[keys, rows]
                p = jnp.exp(s - lse_ref[i, h : h + 1, rows])
                dp = rows_by_rows(jnp.where(lanes, v_here, 0), do_here)
                ds = (p * (dp - delta)).astype(BF)
                dv_acc[keys, :] += plain_dot(p.astype(BF), jnp.where(lanes, do_here, 0))
                dk_acc[keys, :] += plain_dot(ds, jnp.where(lanes, q_here, 0))
                outs.append(plain_dot(k_t[h * HD : (h + 1) * HD], ds))
            dq = (jnp.concatenate(outs, axis=0).T * scale).astype(BF)
            dq_ref[rows, lanes_here] = dq
            dq_sum += jnp.sum(dq.astype(F32), axis=0, keepdims=True)
        dk, dv = dk_acc[...].astype(BF), dv_acc[...].astype(BF)
        dk_ref[:, lanes_here] = dk
        dv_ref[:, lanes_here] = dv
        sums_ref[0:1, lanes_here] = dq_sum
        sums_ref[1:2, lanes_here] = jnp.sum(dk.astype(F32), axis=0, keepdims=True)
        sums_ref[2:3, lanes_here] = jnp.sum(dv.astype(F32), axis=0, keepdims=True)

    tile = 256
    tiles = width // tile

    def input_grad(r):
        rows = pl.ds((back - r) * rows_here, rows_here)

        def body(i):
            cols = pl.ds(pl.multiple_of(i * tile, tile), tile)
            total = plain_dot(dk_ref[rows, :], big[width : 2 * width, cols]) + plain_dot(dv_ref[rows, :], big[2 * width :, cols])
            if r == 0:
                grad_ref[:, cols] = total + plain_dot(dq_ref[...], big[:width, cols])
            else:
                away[r - 1, :, cols] = total.astype(BF)

        return body

    def weight_grad(n, from_ref, into_ref, first_row, many):
        def body(i):
            cols = pl.ds(pl.multiple_of(i * tile, tile), tile)
            slot = i % 2
            out = pltpu.make_async_copy(stage.at[slot], into_ref.at[pl.ds(i * tile, tile)], stage_sem.at[slot])

            @pl.when((i >= 2) | (n > 0))
            def _():
                out.wait()

            total = lax.dot_general(
                from_ref[:, cols], tokens_of(first_row, many), (((0,), (0,)), ((), ())), preferred_element_type=F32
            )
            stage[slot] = total.astype(BF)
            out.start()

        return body

    def tokens_of(first_row, many):
        return big[pl.ds(first_row, many), :]

    loop_with(pairs, attend_back, during[1])
    weights.wait()
    for n, r in enumerate(range(back, -1, -1)):
        loop_with(tiles, input_grad(r), {i - n * tiles: e for i, e in during[2].items() if i // tiles == n})
    load = pltpu.make_async_copy(wide_ref, big.at[pl.ds(0, n_keys)], load_sem.at[1])
    load.start()
    load.wait()
    own = n_keys - rows_here
    loop_with(tiles, weight_grad(0, dq_ref, gq_ref, own, rows_here), during[3])
    loop_with(tiles, weight_grad(1, dk_ref, gk_ref, 0, n_keys), during[4])
    loop_with(tiles, weight_grad(2, dv_ref, gv_ref, 0, n_keys), during[5])
    reducer.keep()
    for slot in range(2):
        arrived(stage.at[slot], stage_sem.at[slot])

    @pl.when(t >= 2)
    def _():
        arrived(away.at[1], away_send)
    reducer.finish()


def backward_reduce(grad_ff, q, k, v, o, do, lse, first_seen, wide, w_att, n_tensor, back):
    rows, width = q.shape
    n_keys = k.shape[0]
    n_ff = grad_ff.shape[0]
    block = grad_ff.shape[-2:]
    any_spec = pl.BlockSpec(memory_space=pl.ANY)
    vmem = pl.BlockSpec(memory_space=pltpu.VMEM)
    dma = pltpu.SemaphoreType.DMA
    shape = jax.ShapeDtypeStruct
    square = shape((width, width), BF)
    pair = lambda n: pltpu.VMEM((2, n, PAIR), BF)
    return pl.pallas_call(
        functools.partial(backward_kernel, n_tensor, back, 1.0 / math.sqrt(HD)),
        out_shape=[shape((n_ff, *block), BF), shape((rows, width), F32), shape((back, rows, width), BF), square, square, square, shape((3, width), F32)],
        in_specs=[any_spec] * 6 + [vmem, vmem] + [any_spec] * 2,
        out_specs=[vmem, vmem, vmem, any_spec, any_spec, any_spec, vmem],
        scratch_shapes=[
            *Reducer.scratch(n_ff, n_ff // BACK_GROUPS, BACK_GROUPS, 1, n_tensor, block),
            pltpu.VMEM((n_keys, rows), F32),
            pair(rows), pair(n_keys), pair(n_keys), pair(rows), pair(rows),
            pltpu.VMEM((rows, width), BF), pltpu.VMEM((n_keys, width), BF), pltpu.VMEM((n_keys, width), BF),
            pltpu.VMEM((3 * width, width), BF),
            pltpu.VMEM((2, 256, width), BF),
            pltpu.VMEM((n_keys, PAIR), F32), pltpu.VMEM((n_keys, PAIR), F32),
            pltpu.VMEM((rows, width), BF),
            dma((2, 5)), dma((2,)), dma((2,)), dma, dma,
        ],
        compiler_params=pltpu.CompilerParams(collective_id=1, has_side_effects=True, vmem_limit_bytes=60 << 20),
        name="backward_reduce",
    )(grad_ff, q, k, v, o, do, lse, first_seen, wide, w_att)


def join(row, a, b):
    return jnp.where(row == MAX_ROW, jnp.maximum(a, b), a + b)


def finish_kernel(
    n_tensor,
    unit_ref, gq_ref, gk_ref, gv_ref, go_ref, shard_ref, grad_ref, away_ref, hidden_ref, x_ref, shared_ref, v_ref,
    out_ref, vsum_ref, input_ref, *scratch,
):
    reducer_scratch, (
        final, outgo, v_in, v_z, away_in, swap_send, swap_recv, v_send, v_recv, local_sem, away_send, away_recv,
    ) = (
        scratch[:REDUCER], scratch[REDUCER:]
    )
    d, t, core, x, y = place()
    greet(d, t, n_tensor)
    other, near, one, two, up_in, down_in, *sems = reducer_scratch
    parts = [gq_ref, gk_ref, gv_ref, go_ref]
    groups = [parts[i : i + 4 // LAST_GROUPS] for i in range(0, 4, 4 // LAST_GROUPS)]
    reducer = Reducer(groups, n_tensor, other, near, one, two, up_in, down_in, final, sems)
    reducer.start()
    rows_here = x_ref.shape[0]
    n_att = other.shape[0]
    final[n_att:] = shard_ref[...]

    from_above, to_below = t + 1 < n_tensor, t >= 1

    @pl.when(~from_above)
    def _():
        away_in[...] = jnp.zeros_like(away_in)

    def give():
        @pl.when(to_below)
        def _():
            send(away_ref.at[0], away_in, away_send, away_recv, (d, t - 1))

    def got():
        @pl.when(from_above)
        def _():
            arrived(away_in, away_recv)

    vsum_ref[...] = v_ref[...]
    part = 128
    gain = shared_ref[0:1, :]

    def norm_back_rows(i, carry):
        rows = pl.ds(pl.multiple_of(i * part, part), part)
        _, hat, inverse = norm_rows(x_ref[rows, :].astype(F32), 1.0, 0.0)
        grad = grad_ref[rows, :] + away_in[rows, :].astype(F32)
        input_ref[rows, :] = hidden_ref[rows, :] + norm_back(grad, hat, inverse, gain)
        vsum_ref[0:1, :] += jnp.sum(grad * hat, axis=0, keepdims=True)
        vsum_ref[1:2, :] += jnp.sum(grad, axis=0, keepdims=True)
        return carry

    row = lax.broadcasted_iota(jnp.int32, vsum_ref.shape, 0)
    hops = (reducer.sibling, reducer.by_x, reducer.by_y)

    def vector_step(i):
        if i > 0:
            arrived(v_in.at[i - 1], v_recv.at[i - 1])
            arrived(v_in.at[i - 1], v_send.at[i - 1])
            vsum_ref[...] = join(row, vsum_ref[...], v_in[i - 1])
        if i < len(hops):
            send(vsum_ref, v_in.at[i], v_send.at[i], v_recv.at[i], (hops[i], t))
        else:
            for k in range(1, n_tensor):
                send(vsum_ref, v_z.at[k - 1], v_send.at[2 + k], v_recv.at[2 + k], (d, (t + k) % n_tensor))

    def vector_end():
        for k in range(1, n_tensor):
            arrived(v_z.at[k - 1], v_recv.at[2 + k])
            arrived(v_z.at[k - 1], v_send.at[2 + k])
        for k in range(1, n_tensor):
            vsum_ref[...] = join(row, vsum_ref[...], v_z[k - 1])

    by_code = reducer.codes()
    by_code |= {910 + i: functools.partial(vector_step, i) for i in range(len(hops) + 1)}
    by_code |= {900: give, 901: got, 914: vector_end}
    by_code[903] = lambda: lax.fori_loop(0, rows_here // part, norm_back_rows, 0)
    for code in LAST_ORDER:
        by_code[code]()
    reducer.keep()

    cap = out_ref.shape[0]
    for k in range(1, 9):
        to = (d + k) % 8
        for j in range(cap):
            outgo[to, j] = final[unit_ref[to * cap + j]]
        if k < 8:
            send(outgo.at[to], out_ref.at[:, d], swap_send.at[k - 1], swap_recv.at[k - 1], (to, t))
    keep = pltpu.make_async_copy(outgo.at[d], out_ref.at[:, d], local_sem.at[0])
    keep.start()
    for k in range(1, 8):
        arrived(out_ref.at[:, (d + 8 - k) % 8], swap_recv.at[k - 1])
    reducer.finish()
    for k in range(1, 8):
        arrived(outgo.at[0], swap_send.at[k - 1])

    @pl.when(to_below)
    def _():
        arrived(away_in, away_send)
    keep.wait()


def finish_reduce(grads, shard, grad_first, away, grad_hidden, tokens, shared, vectors, unit_of_slot, n_tensor, cap):
    block = shard.shape[1:]
    n_units = len(grads) + shard.shape[0]
    rows, width = tokens.shape
    any_spec = pl.BlockSpec(memory_space=pl.ANY)
    vmem = pl.BlockSpec(memory_space=pltpu.VMEM)
    dma = pltpu.SemaphoreType.DMA
    shape = jax.ShapeDtypeStruct
    out, vsum, input_grad = pl.pallas_call(
        functools.partial(finish_kernel, n_tensor),
        out_shape=[shape((cap, 8, *block), BF), shape(vectors.shape, F32), shape((rows, width), F32)],
        in_specs=[pl.BlockSpec(memory_space=pltpu.SMEM)] + [any_spec] * 4 + [vmem, vmem, any_spec] + [vmem] * 4,
        out_specs=[vmem, vmem, vmem],
        scratch_shapes=[
            *Reducer.scratch(len(grads), 4 // LAST_GROUPS, LAST_GROUPS, 4 // LAST_GROUPS, n_tensor, block),
            pltpu.VMEM((n_units, *block), BF),
            pltpu.VMEM((8, cap, *block), BF),
            pltpu.VMEM((3, *vectors.shape), F32),
            pltpu.VMEM((n_tensor - 1, *vectors.shape), F32),
            pltpu.VMEM(away.shape[1:], BF),
            dma((7,)), dma((7,)), dma((2 + n_tensor,)), dma((2 + n_tensor,)), dma((1,)),
            dma, dma,
        ],
        compiler_params=pltpu.CompilerParams(collective_id=2, has_side_effects=True, vmem_limit_bytes=48 << 20),
        name="finish_reduce",
    )(unit_of_slot, *grads, shard, grad_first, away, grad_hidden, tokens, shared, vectors)
    return out.reshape(cap, -1, width), vsum, input_grad


def feed_forward_kernel(
    hidden_ref, dy_ref, shared_ref, bias_ref, fc_ref, proj_ref,
    out_ref, grad_ref, low_ref, fc_grad_ref, proj_grad_ref, fc_bias_ref, sums_ref,
    second_ref, acc_ref,
):
    step = pl.program_id(0)

    @pl.when(step == 0)
    def _():
        normed, _, _ = norm_rows(hidden_ref[...], shared_ref[3:4, :], shared_ref[4:5, :])
        second_ref[...] = normed.astype(BF)
        out_ref[...] = hidden_ref[...] + shared_ref[5:6, :]
        acc_ref[...] = jnp.zeros_like(acc_ref)

    dy, second = dy_ref[...], second_ref[...]
    pre = rows_by_rows(second, fc_ref[...]) + bias_ref[0]
    cube = pre * pre
    inner = jnp.tanh(GELU_A * (pre + GELU_B * (cube * pre)))
    half = 0.5 * pre
    activ = (half + half * inner).astype(BF)
    slope = 0.5 + 0.5 * inner + half * (1.0 - inner * inner) * (GELU_A + (3.0 * GELU_A * GELU_B) * cube)
    out_ref[...] += plain_dot(activ, proj_ref[...])
    proj_grad_ref[...] = cols_by_cols(activ, dy).astype(BF)
    grad_pre = (rows_by_rows(dy, proj_ref[...]) * slope).astype(BF)
    fc_bias_ref[0] = jnp.sum(grad_pre.astype(F32), axis=0, keepdims=True)
    fc_grad_ref[...] = cols_by_cols(grad_pre, second).astype(BF)
    acc_ref[...] += plain_dot(grad_pre, fc_ref[...])

    @pl.when(step == pl.num_programs(0) - 1)
    def _():
        _, hat, inverse = norm_rows(hidden_ref[...], 1.0, 0.0)
        grad_second, grad_y = acc_ref[...], dy.astype(F32)
        grad = grad_y + norm_back(grad_second, hat, inverse, shared_ref[3:4, :])
        low = grad.astype(BF)
        grad_ref[...] = grad
        low_ref[...] = low
        for n, rows in enumerate((low.astype(F32), grad_second * hat, grad_second, grad_y)):
            sums_ref[n : n + 1, :] = jnp.sum(rows, axis=0, keepdims=True)


def feed_forward(hidden, out_grad, shared, b_fc, w_fc, w_proj):
    rows, width = hidden.shape
    tile = 512
    steps = w_fc.shape[0] // tile
    whole = lambda *dims: pl.BlockSpec(dims, lambda i: (0,) * len(dims))
    strip = pl.BlockSpec((tile, width), lambda i: (i, 0))
    bias = pl.BlockSpec((1, 1, tile), lambda i: (i, 0, 0))
    shape = jax.ShapeDtypeStruct
    out = pl.pallas_call(
        feed_forward_kernel,
        grid=(steps,),
        in_specs=[whole(rows, width), whole(rows, width), whole(*shared.shape), bias, strip, strip],
        out_specs=[whole(rows, width)] * 3 + [strip, strip, bias, whole(4, width)],
        out_shape=[
            shape((rows, width), F32), shape((rows, width), F32), shape((rows, width), BF),
            shape(w_fc.shape, BF), shape(w_proj.shape, BF), shape((steps, 1, tile), F32), shape((4, width), F32),
        ],
        scratch_shapes=[pltpu.VMEM((rows, width), BF), pltpu.VMEM((rows, width), F32)],
        compiler_params=pltpu.CompilerParams(vmem_limit_bytes=48 << 20),
        name="feed_forward",
    )(hidden, out_grad, shared, b_fc.reshape(steps, 1, tile), w_fc, w_proj)
    return (*out[:5], out[5].reshape(-1), out[6])


def per_device(
    tokens_in,
    out_grad,
    lengths,
    owners,
    matrix_master,
    matrix_m1,
    matrix_m2,
    shared_params,
    bias_params,
):
    n_tensor = lax.axis_size("tensor")
    n_data = lax.axis_size("dp")
    tensor_index = lax.axis_index("tensor")
    data_index = lax.axis_index("dp")
    rows_here, width = tokens_in.shape
    slot_cap = matrix_master.shape[1]
    unit_rows = matrix_master.shape[2]
    n_units = owners.shape[0]
    n_slots = n_data * slot_cap
    head_rows = width // n_tensor
    heads_here = head_rows // HD
    ff_rows = (n_units * unit_rows - 4 * head_rows) // 2
    slot_of_unit, unit_of_slot, occupied = slot_tables(owners, n_slots, slot_cap)


    back = -(-(DOC_MOST - 1) // rows_here)
    reach = back * rows_here
    own_kernels = n_data == 8 and n_tensor == 4 and back == 2 and head_rows == unit_rows and unit_rows % 128 == 0
    sizes = lengths[0]
    upto = jnp.arange(sizes.shape[0])[:, None] >= jnp.arange(sizes.shape[0])[None, :]
    bounds = jnp.sum(jnp.where(upto, sizes[None, :], 0), axis=1)
    places = tensor_index * rows_here + jnp.arange(rows_here, dtype=jnp.int32)
    starts = jnp.max(jnp.where(places[:, None] >= bounds[None, :], bounds[None, :], 0), axis=1)
    first_seen = (starts - tensor_index * rows_here + reach)[None, :]

    shared = shared_params[0]
    inputs_f32 = tokens_in.astype(F32)
    normed_one, hat_one, inverse_one = norm_rows(inputs_f32, shared[0], shared[1])
    normed_low = normed_one.astype(BF)
    if own_kernels:
        (
            w_att, normed_all, q_scaled, keys_in, values_in, attended, log_norms, peaks,
            layer_out, grad_hidden, grad_attended, grad_ff_w, grad_out_w, grad_fc_b, shared_rows,
        ) = forward_spread(
            matrix_master[0].astype(BF), normed_low, tokens_in, out_grad, bias_params[0, 0], first_seen, shared,
            slot_of_unit, n_tensor, back,
        )
    else:
        units = gather_units(matrix_master[0], slot_of_unit)
        stacks = units.reshape(n_tensor, n_units * unit_rows, width)
        part = lambda first, count: stacks[:, first : first + count].reshape(-1, width)
        w_q, w_k, w_v, w_out = (part(i * head_rows, head_rows) for i in range(4))
        w_fc = part(4 * head_rows, ff_rows)
        w_proj = part(4 * head_rows + ff_rows, ff_rows)
        all_bias = lax.all_gather(bias_params[0], "tensor", axis=0, tiled=True).reshape(n_tensor, -1)
        before = [
            lax.ppermute(normed_low, "tensor", [(i, i + r) for i in range(n_tensor - r)])
            for r in range(min(back, n_tensor - 1), 0, -1)
        ]
        blank = [jnp.zeros_like(normed_low)] * (back - len(before))
        normed_all = jnp.concatenate([*blank, *before, normed_low], axis=0)
        bias = lambda first, count: all_bias[:, first : first + count].reshape(-1)
        b_q, b_k, b_v = (bias(i * head_rows, head_rows) for i in range(3))
        b_fc = bias(3 * head_rows, ff_rows)
        q_scaled = (rows_by_rows(normed_low, w_q) + b_q).astype(BF) * jnp.asarray(1.0 / math.sqrt(HD), BF)
        keys_in = (rows_by_rows(normed_all, w_k) + b_k).astype(BF)
        values_in = (rows_by_rows(normed_all, w_v) + b_v).astype(BF)
        attended, log_norms, peaks = attend_forward(q_scaled, keys_in, values_in, first_seen)
        hidden = inputs_f32 + (plain_dot(attended, w_out) + shared[2])
        layer_out, grad_hidden, grad_hidden_low, grad_fc_w, grad_proj_w, grad_fc_b, shared_rows = feed_forward(
            hidden, out_grad, shared, b_fc, w_fc, w_proj
        )
        grad_out_w = cols_by_cols(attended, grad_hidden_low).astype(BF)
        grad_attended = rows_by_rows(grad_hidden_low, w_out).astype(BF)
    head_here = jnp.max(peaks, axis=2).reshape(-1)
    if own_kernels:
        in_blocks = lambda g: g.reshape(-1, n_tensor, 2, 2, 2, unit_rows // 8, width)
        shard, grad_first, away, grad_q_w, grad_k_w, grad_v_w, sums = backward_reduce(
            in_blocks(grad_ff_w), q_scaled, keys_in, values_in, attended, grad_attended,
            log_norms, first_seen, normed_all, w_att, n_tensor, back,
        )
        grad_fc_b = grad_fc_b.reshape(2, n_tensor, -1, unit_rows).swapaxes(1, 2)
        vectors = jnp.concatenate(
            [
                jnp.zeros((2, width), F32), shared_rows, sums, grad_fc_b.reshape(-1, width),
                jnp.pad(head_here, (0, width - head_here.shape[0]))[None], jnp.zeros((2, width), F32),
            ],
            axis=0,
        )
        grads = [in_blocks(g) for g in (grad_q_w, grad_k_w, grad_v_w, grad_out_w)]
        half = (n_units - 4) // 2
        later = unit_of_slot - 4
        spot_of_slot = jnp.where(later < 0, unit_of_slot, 4 + jnp.where(later < half, 2 * later, 2 * (later - half) + 1))
        my_grads, totals, input_grad = finish_reduce(
            grads, shard, grad_first, away, grad_hidden, tokens_in, shared, vectors, spot_of_slot, n_tensor, slot_cap
        )
        my_grads = my_grads.astype(F32)
        shared_grad = totals[:6]
        head_all = totals[MAX_ROW, : head_here.shape[0]]
        bias_total = totals[6:MAX_ROW].reshape(-1, n_tensor, unit_rows)
        bias_grad = lax.dynamic_index_in_dim(bias_total, tensor_index, 1, keepdims=False).reshape(-1)
    else:
        grad_q, grad_k, grad_v = attend_backward(
            q_scaled, keys_in, values_in, attended, grad_attended, log_norms, first_seen
        )
        grad_q_w = cols_by_cols(grad_q, normed_low)
        grad_k_w = cols_by_cols(grad_k, normed_all)
        grad_v_w = cols_by_cols(grad_v, normed_all)
        grad_wide = plain_dot(grad_k, w_k) + plain_dot(grad_v, w_v)
        grad_first = grad_wide[reach:] + plain_dot(grad_q, w_q)
        for r in range(1, min(back, n_tensor - 1) + 1):
            away = grad_wide[reach - r * rows_here : reach - (r - 1) * rows_here].astype(BF)
            grad_first += lax.ppermute(away, "tensor", [(i, i - r) for i in range(r, n_tensor)]).astype(F32)
        input_grad = grad_hidden + norm_back(grad_first, hat_one, inverse_one, shared[0])
        grad_qkv_b = [jnp.sum(g, axis=0, dtype=F32) for g in (grad_q, grad_k, grad_v)]
        first_rows = jnp.stack([jnp.sum(grad_first * hat_one, axis=0), jnp.sum(grad_first, axis=0)])
        shared_part = jnp.concatenate([first_rows, shared_rows], axis=0)
        by_tensor = lambda v: v.reshape(n_tensor, -1)
        bias_part = jnp.concatenate([by_tensor(v) for v in (*grad_qkv_b, grad_fc_b)], axis=1)
        head_all = lax.pmax(head_here, ("dp", "tensor"))
        shared_grad, bias_total = lax.psum((shared_part, bias_part), ("dp", "tensor"))
        bias_grad = lax.dynamic_index_in_dim(bias_total, tensor_index, 0, keepdims=False)
        by_stack = lambda g: g.astype(BF).reshape(n_tensor, -1, width)
        grad_units = jnp.concatenate(
            [by_stack(g) for g in (grad_q_w, grad_k_w, grad_v_w, grad_out_w, grad_fc_w, grad_proj_w)], axis=1
        ).reshape(units.shape)
        my_grads = scatter_units(grad_units, unit_of_slot).astype(F32)
    head_peak = lax.dynamic_slice_in_dim(head_all, tensor_index * heads_here, heads_here)

    my_units = lax.dynamic_slice_in_dim(unit_of_slot, data_index * slot_cap, slot_cap, 0)
    my_occupied = lax.dynamic_slice_in_dim(occupied, data_index * slot_cap, slot_cap, 0)[:, None, None]
    steps_done = float(STEP)
    first_new, second_new, master_new = adam_step(
        matrix_master[0], my_grads, matrix_m1[0], matrix_m2[0], steps_done, WEIGHT_DECAY
    )
    root_gamma = jnp.sqrt(CLIP_TAU / jnp.maximum(head_peak, CLIP_TAU))
    row_index = my_units[:, None] * unit_rows + jnp.arange(unit_rows, dtype=jnp.int32)[None, :]
    local_head = jnp.where(row_index < head_rows, row_index // HD, (row_index - head_rows) // HD)
    head_match = local_head[..., None] == jnp.arange(heads_here, dtype=jnp.int32)[None, None, :]
    picked_root = jnp.sum(jnp.where(head_match, root_gamma, 0.0), axis=-1)
    factor = jnp.where(row_index < 2 * head_rows, picked_root, 1.0)
    my_grads = jnp.where(my_occupied, my_grads, 0.0)
    master_new = jnp.where(my_occupied, master_new * factor[..., None], 0.0)
    first_new = jnp.where(my_occupied, first_new, 0.0)
    second_new = jnp.where(my_occupied, second_new, 0.0)
    shared_first, shared_second, shared_new = adam_step(
        shared, shared_grad, shared_params[1], shared_params[2], steps_done, 0.0
    )
    bias_first, bias_second, bias_new = adam_step(
        bias_params[0, 0], bias_grad, bias_params[1, 0], bias_params[2, 0], steps_done, 0.0
    )
    shared_out = jnp.stack([shared_grad, shared_first])
    bias_out = jnp.stack([bias_grad, bias_first])[:, None, :]
    return (
        layer_out,
        input_grad,
        head_peak,
        my_grads[None],
        first_new[None],
        second_new[None],
        master_new[None],
        shared_out,
        shared_second,
        shared_new,
        bias_out,
        bias_second[None],
        bias_new[None],
    )


def solution(mesh):
    in_specs = (
        P(("dp", "tensor"), None),
        P(("dp", "tensor"), None),
        P("dp", None),
        P(),
        P("tensor", "dp", None, None),
        P("tensor", "dp", None, None),
        P("tensor", "dp", None, None),
        P(),
        P(None, "tensor", None),
    )
    out_specs = (
        P(("dp", "tensor"), None),
        P(("dp", "tensor"), None),
        P("tensor"),
        P("tensor", "dp", None, None),
        P("tensor", "dp", None, None),
        P("tensor", "dp", None, None),
        P("tensor", "dp", None, None),
        P(),
        P(),
        P(),
        P(None, "tensor", None),
        P("tensor", None),
        P("tensor", None),
    )
    return jax.shard_map(
        per_device, mesh=mesh, in_specs=in_specs, out_specs=out_specs, check_vma=False
    )
```

```python
import functools
import math

import jax
import jax.numpy as jnp
from jax import lax
from jax.experimental import pallas as pl
from jax.experimental.pallas import tpu as pltpu
from jax.sharding import PartitionSpec as P

HD = 64
DOC_MOST = 1024
STEP = 10
PAIR = 2 * HD

EPS_NORM = 1e-05
BETA_ONE = 0.9
BETA_TWO = 0.95
LEARN_RATE = 0.08
WEIGHT_DECAY = 0.1
EPS_ADAM = 1e-08
CLIP_TAU = 10.0
MASKED = -1e30
GELU_A = 0.7978845608
GELU_B = 0.044715
BF = jnp.bfloat16
F32 = jnp.float32
MESH = pl.DeviceIdType.MESH
MAX_ROW = 13
BACK_GROUPS = 4
LAST_GROUPS = 2


def plain_dot(left, right):
    return jnp.dot(left, right, preferred_element_type=F32)


def rows_by_rows(left, right):
    return lax.dot_general(left, right, (((1,), (1,)), ((), ())), preferred_element_type=F32)


def cols_by_cols(left, right):
    return lax.dot_general(left, right, (((0,), (0,)), ((), ())), preferred_element_type=F32)


def gelu_tanh(values_in):
    return jax.nn.gelu(values_in, approximate=True)


def norm_rows(values_in, gain, shift):
    centre = jnp.mean(values_in, axis=-1, keepdims=True)
    shifted = values_in - centre
    inverse = lax.rsqrt(jnp.mean(shifted * shifted, axis=-1, keepdims=True) + EPS_NORM)
    normed = shifted * inverse
    return (normed * gain + shift, normed, inverse)


def norm_back(grad_in, normed, inverse, gain):
    scaled = grad_in * gain
    return inverse * (
        scaled
        - jnp.mean(scaled, axis=-1, keepdims=True)
        - normed * jnp.mean(scaled * normed, axis=-1, keepdims=True)
    )


def slot_tables(owners, n_slots, slot_cap):
    n_units = owners.shape[0]
    unit_order = jnp.arange(n_units, dtype=jnp.int32)
    same_owner = owners[:, None] == owners[None, :]
    earlier = unit_order[None, :] < unit_order[:, None]
    rank_counts = jnp.sum((same_owner & earlier).astype(jnp.int32), axis=1)
    slot_of_unit = owners * slot_cap + rank_counts
    matches = jnp.arange(n_slots, dtype=jnp.int32)[:, None] == slot_of_unit[None, :]
    occupied = jnp.any(matches, axis=1)
    unit_of_slot = jnp.sum(matches.astype(jnp.int32) * unit_order[None, :], axis=1)
    return (slot_of_unit, unit_of_slot, occupied)


def head_lanes(head):
    lane = lax.broadcasted_iota(jnp.int32, (1, PAIR), 1)
    return (lane < HD) if head == 0 else (lane >= HD)


def q_tiles(n_query, n_keys):
    size = min(256, n_query)
    reach = n_keys - n_query
    return size, reach + size


def fill_bias(bias_ref, first_ref):
    n_keys, n_query = bias_ref.shape
    reach = n_keys - n_query
    key = lax.broadcasted_iota(jnp.int32, (n_keys, n_query), 0)
    query = lax.broadcasted_iota(jnp.int32, (n_keys, n_query), 1) + reach
    seen = (key <= query) & (key >= first_ref[...])
    bias_ref[...] = jnp.where(seen, 0.0, MASKED)


def attend_kernel(first_ref, q_ref, k_ref, v_ref, o_ref, lse_ref, peak_ref, bias_ref):
    @pl.when(pl.program_id(0) == 0)
    def _():
        fill_bias(bias_ref, first_ref)

    n_keys, n_query = bias_ref.shape
    size, span = q_tiles(n_query, n_keys)
    for j in range(n_query // size):
        rows, keys = pl.ds(j * size, size), pl.ds(j * size, span)
        v_t = v_ref[keys, :].T
        outs = []
        for h in range(2):
            k_h = jnp.where(head_lanes(h), k_ref[keys, :], 0)
            s = rows_by_rows(k_h, q_ref[rows, :]) + bias_ref[keys, rows]
            top = jnp.max(s, axis=0, keepdims=True)
            p = jnp.exp(s - top)
            total = jnp.sum(p, axis=0, keepdims=True)
            o_t = plain_dot(v_t[h * HD : (h + 1) * HD], p.astype(BF))
            outs.append(o_t / total)
            lse_ref[0, h : h + 1, rows] = top + jnp.log(total)
            peak_ref[0, h : h + 1, rows] = top
        o_ref[rows, :] = jnp.concatenate(outs, axis=0).T.astype(BF)


def attend_forward(q_scaled, keys_in, values_in, first_seen):
    n_query, width = q_scaled.shape
    n_keys = keys_in.shape[0]
    pairs = width // PAIR
    column = lambda i: (0, i)
    stats = jax.ShapeDtypeStruct((pairs, 2, n_query), F32)
    stat_spec = pl.BlockSpec((1, 2, n_query), lambda i: (i, 0, 0))
    return pl.pallas_call(
        attend_kernel,
        grid=(pairs,),
        in_specs=[
            pl.BlockSpec((1, n_query), lambda i: (0, 0)),
            pl.BlockSpec((n_query, PAIR), column),
            pl.BlockSpec((n_keys, PAIR), column),
            pl.BlockSpec((n_keys, PAIR), column),
        ],
        out_specs=[pl.BlockSpec((n_query, PAIR), column), stat_spec, stat_spec],
        out_shape=[jax.ShapeDtypeStruct((n_query, width), BF), stats, stats],
        scratch_shapes=[pltpu.VMEM((n_keys, n_query), F32)],
        compiler_params=pltpu.CompilerParams(vmem_limit_bytes=48 << 20),
        name="attend_forward",
    )(first_seen, q_scaled, keys_in, values_in)


def attend_back_kernel(
    first_ref, q_ref, k_ref, v_ref, o_ref, do_ref, lse_ref, dq_ref, dk_ref, dv_ref,
    bias_ref, dk_acc, dv_acc, *, scale
):
    @pl.when(pl.program_id(0) == 0)
    def _():
        fill_bias(bias_ref, first_ref)

    n_keys, n_query = bias_ref.shape
    size, span = q_tiles(n_query, n_keys)
    dk_acc[...] = jnp.zeros_like(dk_acc)
    dv_acc[...] = jnp.zeros_like(dv_acc)
    for j in range(n_query // size):
        rows, keys = pl.ds(j * size, size), pl.ds(j * size, span)
        q_here, do_here = q_ref[rows, :], do_ref[rows, :]
        k_here, v_here = k_ref[keys, :], v_ref[keys, :]
        k_t = k_here.T
        meet = (do_here.astype(F32) * o_ref[rows, :].astype(F32)).T
        outs = []
        for h in range(2):
            lanes = head_lanes(h)
            delta = jnp.sum(meet[h * HD : (h + 1) * HD], axis=0, keepdims=True)
            s = rows_by_rows(jnp.where(lanes, k_here, 0), q_here) + bias_ref[keys, rows]
            p = jnp.exp(s - lse_ref[0, h : h + 1, rows])
            dp = rows_by_rows(jnp.where(lanes, v_here, 0), do_here)
            ds = (p * (dp - delta)).astype(BF)
            dv_acc[keys, :] += plain_dot(p.astype(BF), jnp.where(lanes, do_here, 0))
            dk_acc[keys, :] += plain_dot(ds, jnp.where(lanes, q_here, 0))
            outs.append(plain_dot(k_t[h * HD : (h + 1) * HD], ds))
        dq_ref[rows, :] = (jnp.concatenate(outs, axis=0).T * scale).astype(BF)
    dk_ref[...] = dk_acc[...].astype(BF)
    dv_ref[...] = dv_acc[...].astype(BF)


def attend_backward(q_scaled, keys_in, values_in, attended, grads_out, log_norms, first_seen):
    n_query, width = q_scaled.shape
    n_keys = keys_in.shape[0]
    pairs = width // PAIR
    column = lambda i: (0, i)
    q_spec = pl.BlockSpec((n_query, PAIR), column)
    k_spec = pl.BlockSpec((n_keys, PAIR), column)
    q_out = jax.ShapeDtypeStruct((n_query, width), BF)
    k_out = jax.ShapeDtypeStruct((n_keys, width), BF)
    return pl.pallas_call(
        functools.partial(attend_back_kernel, scale=1.0 / math.sqrt(HD)),
        grid=(pairs,),
        in_specs=[
            pl.BlockSpec((1, n_query), lambda i: (0, 0)),
            q_spec, k_spec, k_spec, q_spec, q_spec,
            pl.BlockSpec((1, 2, n_query), lambda i: (i, 0, 0)),
        ],
        out_specs=[q_spec, k_spec, k_spec],
        out_shape=[q_out, k_out, k_out],
        scratch_shapes=[
            pltpu.VMEM((n_keys, n_query), F32),
            pltpu.VMEM((n_keys, PAIR), F32),
            pltpu.VMEM((n_keys, PAIR), F32),
        ],
        compiler_params=pltpu.CompilerParams(vmem_limit_bytes=48 << 20),
        name="attend_backward",
    )(first_seen, q_scaled, keys_in, values_in, attended, grads_out, log_norms)


def adam_step(param, grad, first, second, steps_done, decay):
    first_new = BETA_ONE * first + (1.0 - BETA_ONE) * grad
    second_new = BETA_TWO * second + (1.0 - BETA_TWO) * grad * grad
    fix_one = 1.0 - BETA_ONE**steps_done
    fix_two = 1.0 - BETA_TWO**steps_done
    direction = first_new / fix_one / (jnp.sqrt(second_new / fix_two) + EPS_ADAM)
    return (first_new, second_new, param - LEARN_RATE * (direction + decay * param))


def take_kernel(picks_ref, from_ref, to_ref):
    to_ref[...] = from_ref[...]


def take_blocks(blocks, picks):
    shape = (blocks.shape[0], 1, *blocks.shape[2:])
    return pl.pallas_call(
        take_kernel,
        grid_spec=pltpu.PrefetchScalarGridSpec(
            num_scalar_prefetch=1,
            grid=picks.shape,
            in_specs=[pl.BlockSpec(shape, lambda i, p: (0, p[i], 0, 0))],
            out_specs=pl.BlockSpec(shape, lambda i, p: (0, i, 0, 0)),
        ),
        out_shape=jax.ShapeDtypeStruct((shape[0], picks.shape[0], *shape[2:]), blocks.dtype),
        compiler_params=pltpu.CompilerParams(vmem_limit_bytes=32 << 20),
        name="take_blocks",
    )(picks, blocks)


def gather_units(master, slot_of_unit):
    slots = lax.all_gather(master.astype(BF), ("tensor", "dp"), axis=0, tiled=True)
    n_tensor = lax.axis_size("tensor")
    slots = slots.reshape(n_tensor, -1, *master.shape[1:])
    return take_blocks(slots, slot_of_unit)


def scatter_units(units, unit_of_slot):
    slots = take_blocks(units, unit_of_slot)
    slots = slots.reshape(-1, *units.shape[2:])
    return lax.psum_scatter(slots, ("tensor", "dp"), scatter_dimension=0, tiled=True)


def send(src, dst, send_sem, recv_sem, to):
    copy = pltpu.make_async_remote_copy(
        src_ref=src, dst_ref=dst, send_sem=send_sem, recv_sem=recv_sem,
        device_id=to, device_id_type=MESH,
    )
    copy.start()


def arrived(ref, sem):
    pltpu.make_async_copy(ref, ref, sem).wait()


def place():
    d, t = lax.axis_index("dp"), lax.axis_index("tensor")
    return d, t, d % 2, (d // 2) % 2, d // 4


def greet(d, t, n_tensor):
    barrier = pltpu.get_barrier_semaphore()
    for k in range(1, 8):
        pl.semaphore_signal(barrier, inc=1, device_id=((d + k) % 8, t), device_id_type=MESH)
    for k in range(1, n_tensor):
        pl.semaphore_signal(barrier, inc=1, device_id=(d, (t + k) % n_tensor), device_id_type=MESH)
    pl.semaphore_wait(barrier, 6 + n_tensor)


def loop_with(count, body, events):
    def step(i, carry):
        body(i)
        for n, mine in events.items():
            @pl.when(i == n)
            def _(mine=mine):
                for event in mine:
                    event()
        return carry

    lax.fori_loop(0, count, step, 0)


def by_step(order, by_code, kinds):
    early, during = [], {kind: {} for kind in range(1, kinds + 1)}
    now, count = None, 0
    for code in order:
        if code < 0:
            now, count = -code, 0 if -code != now else count + 1
        elif now is None:
            early.append(by_code[code])
        else:
            during[now].setdefault(count, []).append(by_code[code])
    return early, during


def attend_pair(i, q_ref, k_ref, v_ref, o_ref, lse_ref, peak_ref, bias_ref):
    n_keys, n_query = bias_ref.shape
    size, span = q_tiles(n_query, n_keys)
    lanes = pl.ds(pl.multiple_of(i * PAIR, PAIR), PAIR)
    tiles = [(pl.ds(j * size, size), pl.ds(j * size, span)) for j in range(n_query // size)]
    scores = [
        [
            rows_by_rows(jnp.where(head_lanes(h), k_ref[keys, lanes], 0), q_ref[rows, lanes]) + bias_ref[keys, rows]
            for h in range(2)
        ]
        for rows, keys in tiles
    ]
    for j, (rows, keys) in enumerate(tiles):
        v_t = v_ref[keys, lanes].T
        outs = []
        for h in range(2):
            s = scores[j][h]
            top = jnp.max(s, axis=0, keepdims=True)
            p = jnp.exp(s - top)
            total = jnp.sum(p, axis=0, keepdims=True)
            o_t = plain_dot(v_t[h * HD : (h + 1) * HD], p.astype(BF))
            outs.append(o_t / total)
            lse_ref[i, h : h + 1, rows] = top + jnp.log(total)
            peak_ref[i, h : h + 1, rows] = top
        o_ref[rows, lanes] = jnp.concatenate(outs, axis=0).T.astype(BF)


def paired(n_units):
    half = (n_units - 4) // 2
    return [0, 1, 2, 3] + [4 + i + half * b for i in range(half) for b in range(2)]


def gelu_parts(pre):
    square = pre * pre
    inner = jnp.tanh(GELU_A * (pre + GELU_B * (square * pre)))
    half = 0.5 * pre
    slope = 0.5 + 0.5 * inner + half * (1.0 - inner * inner) * (GELU_A + (3.0 * GELU_A * GELU_B) * square)
    return half + half * inner, slope


ORDER = (
    220, 100, 200, 600, 0, 601, 602, 500, 501, 801, 120, 502, 701, 1900, 110, 300, 802, 702, 800, 700, 901,
    1001, 610, 1000, 400, 902, 210, 1952, 1002, 900, 10, 1950, 310, 1951, 1953, -1, -1, -1, 20, 1901, 620, -1,
    611, -2, -2, -2, -2, 510, -3, -3, -3, 520, -3, -4, 511, 621, -4, -4, 521, 622, -4, 811, 512, 710, -4, 612,
    711, 810, -4, 410, -4, 522, -4, 820, 712, 720, 910, 911, 1011, 812, 320, -5, 1010, -6, 912, 721, 822, -6,
    1012, 1020, -6, 821, 420, 1022, 920, -6, 722, -6, -6, -6, -6, 921, 1021, -6, 922, -6, -6, -6, -6, -6,
)


def forward_kernel(
    n_tensor, back, scale,
    slot_ref, master_ref, x_ref, dy_ref, bias_in_ref, first_ref, shared_ref,
    att_ref, ff_ref, wide_ref, q_ref, k_ref, v_ref, o_ref, lse_ref, peak_ref,
    out_ref, grad_ref, do_ref, ff_grad_ref, go_ref, fc_bias_ref, sums_ref,
    pieces, own, seen_ref, bias_rows, biases_ref, fc_rows, hidden_ref, second_ref, acc_ref, tiles_in, stage,
    swap_send, swap_recv, local_sem, a_send, a_recv, bias_send, bias_recv,
    z_send, z_recv, xy_send, xy_recv, core_send, core_recv, tile_sem, stage_sem,
):
    d, t, core, x, y = place()
    column = y * 2 + x
    by_x, by_y = d + 2 - 4 * x, d + 4 - 8 * y
    sibling = d + 1 - 2 * core
    first, last = t > 0, t < n_tensor - 1
    rows_here, width = x_ref.shape
    n_half = ff_ref.shape[0] // 2
    weights = (att_ref, ff_ref.at[pl.ds(0, n_half)], ff_ref.at[pl.ds(n_half, n_half)])
    starts = (0, 4, 4 + n_half, 4 + 2 * n_half)
    n_groups, steps = len(weights), n_tensor - 1
    slots = 2 * n_tensor - 1
    greet(d, t, n_tensor)

    def tokens_up(r):
        @pl.when(last & (t >= r))
        def _():
            send(wide_ref.at[back - r], wide_ref.at[back - r - 1], a_send.at[r], a_recv.at[r], (d, t + 1))

    def tokens_in(r):
        @pl.when(t > r)
        def _():
            arrived(wide_ref.at[back - r - 1], a_recv.at[r])
        if r + 1 < back:
            tokens_up(r + 1)

    for k in range(1, 8):
        to = (d + k) % 8
        send(master_ref.at[:, to], pieces.at[d], swap_send.at[k - 1], swap_recv.at[k - 1], (to, t))
    part = min(128, rows_here)
    for i in range(0, rows_here, part):
        rows = pl.ds(i, part)
        normed, _, _ = norm_rows(x_ref[rows, :].astype(F32), shared_ref[0:1, :], shared_ref[1:2, :])
        wide_ref[back, rows, :] = normed.astype(BF)
    tokens_up(0)
    mine = pltpu.make_async_copy(master_ref.at[:, d], pieces.at[d], local_sem.at[0])
    mine.start()
    for k in range(1, n_tensor):
        send(bias_in_ref, biases_ref.at[t], bias_send.at[k - 1], bias_recv.at[k - 1], (d, (t + k) % n_tensor))
    biases_ref[t] = bias_in_ref[...]
    for r in range(back):
        @pl.when(t < back - r)
        def _(r=r):
            wide_ref[r] = jnp.zeros((rows_here, width), BF)
    fill_bias(seen_ref, first_ref)
    mine.wait()
    for k in range(1, 8):
        arrived(pieces.at[(d + 8 - k) % 8], swap_recv.at[k - 1])
    cap = master_ref.shape[0]
    for n, u in enumerate(paired(own.shape[0])):
        slot = slot_ref[u]
        own[n] = pieces[slot // cap, slot % cap]

    def block(g, at, col, c):
        return weights[g].at[:, at, col, c]

    def route(at):
        side = at * 2 // n_tensor
        one, two = by_x + (by_y - by_x) * side, by_y + (by_x - by_y) * side
        col_x, col_y, col_xy = y * 2 + 1 - x, (1 - y) * 2 + x, (1 - y) * 2 + 1 - x
        return one, two, col_x + (col_y - col_x) * side, col_y + (col_x - col_y) * side, col_xy

    def onward(g, k, at, source):
        one, two, _, _, _ = route(at)
        here = block(g, at, column, core)
        send(source, here, xy_send.at[g], xy_recv.at[g, k, 0], (one, t))
        send(source, here, xy_send.at[g], xy_recv.at[g, k, 1], (two, t))

    def forward(g, k, at):
        one, two, from_one, _, _ = route(at)
        got = block(g, at, from_one, core)
        arrived(got, xy_recv.at[g, k, 0])
        send(got, got, xy_send.at[g], xy_recv.at[g, k, 2], (two, t))

    def settle(g, k, at):
        _, _, _, from_two, beyond = route(at)
        arrived(block(g, at, from_two, core), xy_recv.at[g, k, 1])
        arrived(block(g, at, beyond, core), xy_recv.at[g, k, 2])
        got = weights[g].at[:, at, :, core]
        send(got, got, core_send.at[g, k], core_recv.at[g, k], (sibling, t))

    def done(g, k, at):
        arrived(weights[g].at[:, at, :, 1 - core], core_recv.at[g, k])

    def given(g, k, at):
        arrived(weights[g].at[:, at, :, core], core_send.at[g, k])

    def z_go(g, s, up, source):
        i = 0 if up else 1

        @pl.when(last if up else first)
        def _():
            here = block(g, t if s == 0 else (t - s if up else t + s), column, core)
            send(source, here, z_send.at[g, i, s], z_recv.at[g, i, s], (d, t + 1 if up else t - 1))

    def z_step(s, up):
        at = t - 1 - s if up else t + 1 + s
        return 1 + 2 * s + (0 if up else 1), at, (at >= 0) if up else (at < n_tensor)

    def z_event(g, s, up):
        k, at, have = z_step(s, up)

        @pl.when(have)
        def _():
            got = block(g, at, column, core)
            arrived(got, z_recv.at[g, 0 if up else 1, s])
            if s + 1 < steps:
                z_go(g, s + 1, up, got)
            onward(g, k, at, got)

    def step(fn, g, s, up):
        k, at, have = z_step(s, up)
        pl.when(have)(functools.partial(fn, g, k, at))

    def each(fn, g, s):
        if s < 0:
            fn(g, 0, t)
        else:
            for up in (True, False):
                step(fn, g, s, up)

    local = []
    mine_of = [own.at[starts[g] : starts[g + 1]] for g in range(n_groups)]
    for g in range(n_groups):
        copy = pltpu.make_async_copy(mine_of[g], block(g, t, column, core), local_sem.at[1 + g])
        copy.start()
        local.append(copy)

    def own_settled(g):
        local[g].wait()
        settle(g, 0, t)

    by_code = {1900 + r: functools.partial(tokens_in, r) for r in range(back)}
    by_code |= {1951 + s: functools.partial(each, done, 0, s) for s in range(-1, steps)}
    for g in range(n_groups):
        by_code[200 + 10 * g] = functools.partial(onward, g, 0, t, mine_of[g])
        by_code[300 + 10 * g] = functools.partial(forward, g, 0, t)
        by_code[400 + 10 * g] = functools.partial(own_settled, g)
        for way, up in ((0, True), (100, False)):
            by_code[way + 10 * g] = functools.partial(z_go, g, 0, up, mine_of[g])
            for s in range(steps):
                by_code[500 + way + 10 * g + s] = functools.partial(z_event, g, s, up)
                by_code[700 + way + 10 * g + s] = functools.partial(step, forward, g, s, up)
                by_code[900 + way + 10 * g + s] = functools.partial(step, settle, g, s, up)
    tile = 256
    tiles = width // tile
    early, during = by_step(ORDER, by_code, 6)
    for event in early:
        event()
    for k in range(1, n_tensor):
        arrived(biases_ref.at[(t + n_tensor - k) % n_tensor], bias_recv.at[k - 1])
        arrived(bias_in_ref, bias_send.at[k - 1])
    per = width // n_tensor // 128
    for n in range(3):
        for at in range(n_tensor):
            for i in range(per):
                lanes = pl.ds((at * per + i) * 128, 128)
                bias_rows[n : n + 1, lanes] = biases_ref[at, n * per + i : n * per + i + 1]
    strip = fc_rows.shape[-1]
    for h in range(2):
        for at in range(n_tensor):
            for i in range(strip // 128):
                row = 3 * per + h * (strip // 128) + i
                fc_rows[h, at, 0:1, i * 128 : (i + 1) * 128] = biases_ref[at, row : row + 1]

    def project(n, own_only, into_ref, factor):
        def body(i):
            cols = pl.ds(pl.multiple_of(i * tile, tile), tile)
            w = att_ref[n, pl.ds(i * tile // (width // n_tensor), 1)].reshape(tile, width)
            for r in range(into_ref.shape[0] // rows_here):
                a = wide_ref[back if own_only else r]
                full = (rows_by_rows(a, w) + bias_rows[n : n + 1, cols]).astype(BF)
                into_ref[r * rows_here : (r + 1) * rows_here, cols] = full * jnp.asarray(factor, BF) if factor else full
        return body

    loop_with(tiles, project(0, True, q_ref, scale), during[1])
    loop_with(tiles, project(1, False, k_ref, None), during[2])
    loop_with(tiles, project(2, False, v_ref, None), during[3])
    loop_with(
        width // PAIR,
        lambda i: attend_pair(i, q_ref, k_ref, v_ref, o_ref, lse_ref, peak_ref, seen_ref),
        during[4],
    )
    w_out = att_ref[3].reshape(width, width)
    half = rows_here // 2
    for r in range(2):
        rows = pl.ds(r * half, half)
        hidden = x_ref[rows, :].astype(F32) + (plain_dot(o_ref[rows, :], w_out) + shared_ref[2:3, :])
        hidden_ref[rows, :] = hidden
        normed, _, _ = norm_rows(hidden, shared_ref[3:4, :], shared_ref[4:5, :])
        second_ref[rows, :] = normed.astype(BF)
        out_ref[rows, :] = hidden + shared_ref[5:6, :]
    acc_ref[...] = jnp.zeros_like(acc_ref)

    def tile_copies(h, at, b):
        for i in range(n_half // 2):
            yield pltpu.make_async_copy(
                ff_ref.at[h * n_half + 2 * i + b, at], tiles_in.at[b, i], tile_sem.at[b, i]
            )

    def grad_copies(h, at):
        for b in range(2):
            for i in range(n_half // 2):
                part = stage.at[b, i]
                yield pltpu.make_async_copy(part, ff_grad_ref.at[h * n_half + 2 * i + b, at], stage_sem.at[b, i])

    def feed(n):
        h, k = n // slots, n % slots
        at = t + (k + 1) // 2 * (1 - 2 * (k % 2))

        @pl.when((at >= 0) & (at < n_tensor))
        def _():
            arrived(ff_ref.at[pl.ds(h * n_half, n_half), at, :, 1 - core], core_recv.at[1 + h, k])
            for b in range(2):
                for copy in tile_copies(h, at, b):
                    copy.start()
            for copy in tile_copies(h, at, 0):
                copy.wait()
            w_fc = tiles_in[0].reshape(strip, width)
            second, dy = second_ref[...], dy_ref[...]
            pre = rows_by_rows(second, w_fc) + fc_rows[h, at]
            for copy in tile_copies(h, at, 1):
                copy.wait()
            w_proj = tiles_in[1].reshape(strip, width)
            grad_activ = rows_by_rows(dy, w_proj)
            activ, slope = gelu_parts(pre)
            activ = activ.astype(BF)
            grad_pre = (grad_activ * slope).astype(BF)
            out_ref[...] += plain_dot(activ, w_proj)
            acc_ref[...] += plain_dot(grad_pre, w_fc)
            fc_bias_ref[h, at] = jnp.sum(grad_pre.astype(F32), axis=0, keepdims=True)

            @pl.when(n > 0)
            def _():
                for copy in grad_copies(h, at):
                    copy.wait()

            stage[0] = cols_by_cols(grad_pre, second).astype(BF).reshape(stage.shape[1:])
            stage[1] = cols_by_cols(activ, dy).astype(BF).reshape(stage.shape[1:])
            for copy in grad_copies(h, at):
                copy.start()

    for event in during[5].get(0, []):
        event()
    loop_with(2 * slots, feed, during[6])
    for copy in grad_copies(0, 0):
        copy.wait()

    sums_ref[...] = jnp.zeros_like(sums_ref)

    def norm_back_rows(i, carry):
        rows = pl.ds(pl.multiple_of(i * part, part), part)
        _, hat, inverse = norm_rows(hidden_ref[rows, :], 1.0, 0.0)
        grad_second, grad_y = acc_ref[rows, :], dy_ref[rows, :].astype(F32)
        grad = grad_y + norm_back(grad_second, hat, inverse, shared_ref[3:4, :])
        low = grad.astype(BF)
        grad_ref[rows, :] = grad
        second_ref[rows, :] = low
        for n, term in enumerate((low.astype(F32), grad_second * hat, grad_second, grad_y)):
            sums_ref[n : n + 1, :] += jnp.sum(term, axis=0, keepdims=True)
        return carry

    lax.fori_loop(0, rows_here // part, norm_back_rows, 0)

    def out_back(i):
        cols = pl.ds(pl.multiple_of(i * tile, tile), tile)
        w = att_ref[3, pl.ds(i * tile // (width // n_tensor), 1)].reshape(tile, width)
        do_ref[:, cols] = rows_by_rows(second_ref[...], w).astype(BF)
        go_ref[pl.ds(pl.multiple_of(i * tile, tile), tile), :] = cols_by_cols(o_ref[:, cols], second_ref[...]).astype(BF)

    loop_with(tiles, out_back, {})

    for g in range(n_groups):
        for s in range(-1, steps):
            each(given, g, s)
        arrived(weights[g].at[:, :, pl.ds(0, 3), 0], xy_send.at[g])
        for up in (True, False):
            for s in range(steps):
                have = last if up else first
                if s > 0:
                    have = have & z_step(s - 1, up)[2]

                @pl.when(have)
                def _(g=g, s=s, up=up):
                    arrived(block(g, t, column, core), z_send.at[g, 0 if up else 1, s])
    for r in range(back):
        @pl.when(last & (t >= r))
        def _(r=r):
            arrived(wide_ref.at[back], a_send.at[r])
    for k in range(1, 8):
        arrived(pieces.at[0], swap_send.at[k - 1])


def forward_spread(master_low, tokens, out_grad, bias_row, first_seen, shared, slot_of_unit, n_tensor, back):
    cap, unit_rows, width = master_low.shape
    n_units = slot_of_unit.shape[0]
    n_ff = n_units - 4
    piece = unit_rows // 8
    rows = tokens.shape[0]
    n_keys = (back + 1) * rows
    strip = n_ff // 4 * unit_rows
    bias_row = bias_row.reshape(-1, 128)
    any_spec = pl.BlockSpec(memory_space=pl.ANY)
    vmem = pl.BlockSpec(memory_space=pltpu.VMEM)
    dma = pltpu.SemaphoreType.DMA
    shape = jax.ShapeDtypeStruct
    units = lambda n: shape((n, n_tensor, 4, 2, piece, width), BF)
    stats = shape((width // PAIR, 2, rows), F32)
    low, high = shape((rows, width), BF), shape((rows, width), F32)
    keys = shape((n_keys, width), BF)
    outs = pl.pallas_call(
        functools.partial(forward_kernel, n_tensor, back, 1.0 / math.sqrt(HD)),
        out_shape=[
            units(4), units(n_ff), shape((back + 1, rows, width), BF), low, keys, keys, low, stats, stats,
            high, high, low, shape((n_ff, n_tensor, 4, 2, piece, width), BF), shape((width, width), BF),
            shape((2, n_tensor, 1, strip), F32), shape((4, width), F32),
        ],
        in_specs=[pl.BlockSpec(memory_space=pltpu.SMEM), any_spec] + [vmem] * 5,
        out_specs=[vmem, any_spec] + [vmem] * 10 + [any_spec] + [vmem] * 3,
        scratch_shapes=[
            pltpu.VMEM((8, cap, piece, width), BF),
            pltpu.VMEM((n_units, piece, width), BF),
            pltpu.VMEM((n_keys, rows), F32),
            pltpu.VMEM((3, width), F32),
            pltpu.VMEM((n_tensor, *bias_row.shape), F32),
            pltpu.VMEM((2, n_tensor, 1, strip), F32),
            pltpu.VMEM((rows, width), F32),
            pltpu.VMEM((rows, width), BF),
            pltpu.VMEM((rows, width), F32),
            pltpu.VMEM((2, n_ff // 4, 4, 2, piece, width), BF),
            pltpu.VMEM((2, n_ff // 4, 4, 2, piece, width), BF),
            dma((7,)), dma((7,)), dma((4,)), dma((back,)), dma((back,)),
            dma((n_tensor - 1,)), dma((n_tensor - 1,)),
            dma((3, 2, n_tensor - 1)), dma((3, 2, n_tensor - 1)),
            dma((3,)), dma((3, 2 * n_tensor - 1, 3)),
            dma((3, 2 * n_tensor - 1)), dma((3, 2 * n_tensor - 1)),
            dma((2, n_ff // 4)), dma((2, n_ff // 4)),
        ],
        compiler_params=pltpu.CompilerParams(collective_id=0, has_side_effects=True, vmem_limit_bytes=60 << 20),
        name="forward_spread",
    )(
        slot_of_unit, master_low.reshape(cap, 8, piece, width), tokens, out_grad, bias_row, first_seen, shared
    )
    att, _, wide, *rest = outs
    return att.reshape(-1, width), wide.reshape(-1, width), *rest


def split_units(ref, count):
    many = ref.shape[0] // count
    return [ref.at[pl.ds(i * many, many)] for i in range(count)]


def add_blocks(into, part, count):
    def body(i, carry):
        a = into(i)
        a[...] = a[...] + part(i)[...]
        return carry

    lax.fori_loop(0, count, body, 0)


BACK_ORDER = (
    0, -1, -1, 103, 10, 100, -1, 102, 101, -1, 113, -1, 110, -1, 201, 203, 20, 202, -1, 112, 301, 213, -1, 302,
    303, 200, -2, 111, -2, -2, -2, 313, 900, 123, 120, -2, 300, 212, -2, 122, 121, -2, 600, 210, 502, -2, -2,
    30, -2, -2, 211, -2, 223, 133, 130, 503, 310, -3, 312, 602, 700, -3, 702, -3, 512, 311, -3, 403, 220, -4,
    -4, 221, -4, -4, 222, -5, 230, 610, -5, 401, 411, 323, 513, 402, 132, 501, 131, 601, 320, -5, 330, 321, -5,
    523, 231, 620, 233, 901, 322, 423, 331, 611, 232, 612, 701, 621, 522, 511, 333, 421, 412, 720, 521, 711,
    332, 722, 533, 710, 721, 532, 630, 631, 413, 712, 422, 730, 433, 531, 432, 732, 632, 731, 431, 622,
)


LAST_ORDER = (
    0, 103, 100, 900, 10, 102, 101, 203, 113, 110, 202, 200, 303, 201, 213, 300, 112, 301, 111, 313, 210, 302,
    901, 903, 910, 702, 503, 600, 212, 310, 911, 513, 211, 610, 312, 912, 501, 502, 700, 311, 403, 712, 601,
    612, 913, 512, 413, 710, 602, 701, 511, 611, 914, 402, 411, 711, 401, 412,
)


class Reducer:
    def __init__(self, groups, n_tensor, other, near, one, two, up_in, down_in, final, sems):
        self.groups, self.n_tensor = groups, n_tensor
        self.other, self.near, self.one, self.two = other, near, one, two
        self.up_in, self.down_in, self.final = up_in, down_in, final
        (
            self.near_sem, self.core_send, self.core_recv, self.one_send, self.one_recv,
            self.two_send, self.two_recv, self.z_send, self.z_recv,
        ) = sems
        self.d, self.t, self.core, self.x, self.y = place()
        self.by_x, self.by_y = self.d + 2 - 4 * self.x, self.d + 4 - 8 * self.y
        self.sibling = self.d + 1 - 2 * self.core
        self.order = sorted(range(n_tensor), key=lambda a: (-abs(2 * a - n_tensor + 1), -a))
        self.merges = [(g, at) for g in range(len(groups)) for at in self.order]
        self.starts, total = [], 0
        for refs in groups:
            self.starts.append(total)
            total += sum(r.shape[0] for r in refs)
        self.ends = [*self.starts[1:], total]

    @staticmethod
    def scratch(n_units, n_group, n_groups, n_refs, n_tensor, block):
        dma = pltpu.SemaphoreType.DMA
        return [
            pltpu.VMEM((n_units, n_tensor, 2, 2, *block), BF),
            pltpu.VMEM((2, n_group, 2, 2, *block), BF),
            pltpu.VMEM((n_units, n_tensor, 2, *block), BF),
            pltpu.VMEM((n_units, n_tensor, *block), BF),
            pltpu.VMEM((n_units, n_tensor, *block), BF),
            pltpu.VMEM((n_units, n_tensor, *block), BF),
            dma((2, n_refs)), dma((n_groups, n_refs)), dma((n_groups, n_refs)),
            dma((n_groups, n_tensor)), dma((n_groups, n_tensor)),
            dma((n_groups, n_tensor)), dma((n_groups, n_tensor)),
            dma((n_groups, n_tensor)), dma((n_groups, n_tensor, 2)),
        ]

    def parts(self, g):
        u = self.starts[g]
        for n, ref in enumerate(self.groups[g]):
            yield n, ref, u, ref.shape[0]
            u += ref.shape[0]

    def units(self, g):
        return pl.ds(self.starts[g], self.ends[g] - self.starts[g])

    def count(self, g):
        return self.ends[g] - self.starts[g]

    def near_copies(self, m):
        g, at = self.merges[m]
        for n, ref, u, many in self.parts(g):
            yield pltpu.make_async_copy(
                ref.at[:, at, :, :, self.core],
                self.near.at[m % 2, pl.ds(u - self.starts[g], many)],
                self.near_sem.at[m % 2, n],
            )

    def core_go(self, g):
        for n, ref, u, many in self.parts(g):
            send(
                ref.at[:, :, :, :, 1 - self.core], self.other.at[pl.ds(u, many)],
                self.core_send.at[g, n], self.core_recv.at[g, n], (self.sibling, self.t),
            )

    def start(self):
        for m in range(2):
            for copy in self.near_copies(m):
                copy.start()

    def by_rows(self, at):
        return at * 2 < self.n_tensor

    def first_hop(self, m):
        g, at = self.merges[m]
        if m % self.n_tensor == 0:
            for n, ref, u, many in self.parts(g):
                arrived(self.other.at[pl.ds(u, many)], self.core_recv.at[g, n])
        for copy in self.near_copies(m):
            copy.wait()
        u0 = self.starts[g]
        add_blocks(
            lambda i: self.other.at[u0 + i // 4, at, (i // 2) % 2, i % 2],
            lambda i: self.near.at[m % 2, i // 4, (i // 2) % 2, i % 2],
            4 * self.count(g),
        )
        if m + 2 < len(self.merges):
            for copy in self.near_copies(m + 2):
                copy.start()
        us = self.units(g)
        rows = self.by_rows(at)
        source = self.other.at[us, at, 1 - self.y] if rows else self.other.at[us, at, :, 1 - self.x]
        to = self.by_y if rows else self.by_x
        send(source, self.one.at[us, at], self.one_send.at[g, at], self.one_recv.at[g, at], (to, self.t))

    def second_hop(self, m):
        g, at = self.merges[m]
        us, u0 = self.units(g), self.starts[g]
        arrived(self.one.at[us, at], self.one_recv.at[g, at])
        if self.by_rows(at):
            into = lambda i: self.other.at[u0 + i // 2, at, self.y, i % 2]
            source, to = self.other.at[us, at, self.y, 1 - self.x], self.by_x
        else:
            into = lambda i: self.other.at[u0 + i // 2, at, i % 2, self.x]
            source, to = self.other.at[us, at, 1 - self.y, self.x], self.by_y
        add_blocks(into, lambda i: self.one.at[u0 + i // 2, at, i % 2], 2 * self.count(g))
        send(source, self.two.at[us, at], self.two_send.at[g, at], self.two_recv.at[g, at], (to, self.t))

    def plane_sum(self, m):
        g, at = self.merges[m]
        us, u0, n = self.units(g), self.starts[g], self.count(g)
        arrived(self.two.at[us, at], self.two_recv.at[g, at])
        add_blocks(lambda i: self.other.at[u0 + i, at, self.y, self.x], lambda i: self.two.at[u0 + i, at], n)
        if at > 0:
            pl.when(self.t == 0)(functools.partial(self.line_go, g, at, True))
        if at < self.n_tensor - 1:
            pl.when(self.t == self.n_tensor - 1)(functools.partial(self.line_go, g, at, False))

    def line_go(self, g, at, up):
        us = self.units(g)
        into, way, to = (self.up_in, 0, self.t + 1) if up else (self.down_in, 1, self.t - 1)
        send(self.other.at[us, at, self.y, self.x], into.at[us, at], self.z_send.at[g, at], self.z_recv.at[g, at, way], (self.d, to))

    def line_in(self, g, at, up):
        us, u0, n, t = self.units(g), self.starts[g], self.count(g), self.t
        buffer, way = (self.up_in, 0) if up else (self.down_in, 1)
        arrived(buffer.at[us, at], self.z_recv.at[g, at, way])
        add_blocks(lambda i: self.other.at[u0 + i, at, self.y, self.x], lambda i: buffer.at[u0 + i, at], n)
        pl.when(t < at if up else t > at)(functools.partial(self.line_go, g, at, up))

    def line(self, g, at, up, near):
        t, top = self.t, self.n_tensor - 1
        have = ((t <= at) & (t > 0)) if up else ((t >= at) & (t < top))
        half = t * 2 > top
        pl.when(have & (half if near else ~half))(functools.partial(self.line_in, g, at, up))

    def keep(self):
        for g in range(len(self.groups)):
            us = self.units(g)
            self.final[us] = self.other[us, self.t, self.y, self.x]

    def codes(self):
        out = {}
        for g in range(len(self.groups)):
            out[10 * g] = functools.partial(self.core_go, g)
            for i, at in enumerate(self.order):
                m, here = g * self.n_tensor + i, 10 * g + at
                out[100 + here] = functools.partial(self.first_hop, m)
                out[200 + here] = functools.partial(self.second_hop, m)
                out[300 + here] = functools.partial(self.plane_sum, m)
                for kind in range(4):
                    out[400 + 100 * kind + here] = functools.partial(self.line, g, at, kind < 2, kind % 2 == 0)
        return out

    def finish(self):
        for g in range(len(self.groups)):
            us = self.units(g)
            for n, ref, u, many in self.parts(g):
                arrived(self.other.at[pl.ds(u, many)], self.core_send.at[g, n])
            for at in range(self.n_tensor):
                arrived(self.one.at[us, at], self.one_send.at[g, at])
                arrived(self.two.at[us, at], self.two_send.at[g, at])

                @pl.when(self.t != at)
                def _(us=us, g=g, at=at):
                    arrived(self.up_in.at[us, at], self.z_send.at[g, at])


REDUCER = 15


def backward_kernel(
    n_tensor, back, scale,
    ff_grad_ref, q_ref, k_ref, v_ref, o_ref, do_ref, lse_ref, first_ref, wide_ref, att_ref,
    shard_ref, grad_ref, away, gq_ref, gk_ref, gv_ref, sums_ref, *scratch,
):
    reducer_scratch, (
        seen_ref, q_in, k_in, v_in, o_in, do_in, dq_ref, dk_ref, dv_ref, big, stage, dk_acc, dv_acc, away_in,
        pair_sem, load_sem, stage_sem, away_send, away_recv,
    ) = scratch[:REDUCER], scratch[REDUCER:]
    d, t, core, x, y = place()
    greet(d, t, n_tensor)
    other, near, one, two, up_in, down_in, *sems = reducer_scratch
    groups = [[part] for part in split_units(ff_grad_ref, BACK_GROUPS)]
    reducer = Reducer(groups, n_tensor, other, near, one, two, up_in, down_in, shard_ref, sems)
    reducer.start()
    by_code = reducer.codes()

    def give():
        @pl.when(t >= 2)
        def _():
            send(away.at[1], away_in, away_send, away_recv, (d, t - 1))

    def add_given():
        @pl.when((t >= 1) & (t + 1 < n_tensor))
        def _():
            arrived(away_in, away_recv)
            away[0] = (away[0].astype(F32) + away_in[...].astype(F32)).astype(BF)

    by_code |= {900: give, 901: add_given}
    early, during = by_step(BACK_ORDER, by_code, 5)
    for event in early:
        event()
    rows_here, width = do_ref.shape
    n_keys = k_ref.shape[0]
    size, span = q_tiles(rows_here, n_keys)
    sources = ((q_ref, q_in), (k_ref, k_in), (v_ref, v_in), (o_ref, o_in), (do_ref, do_in))

    def pair_copies(i):
        lanes = pl.ds(pl.multiple_of(i * PAIR, PAIR), PAIR)
        return [
            pltpu.make_async_copy(ref.at[:, lanes], buffer.at[i % 2], pair_sem.at[i % 2, n])
            for n, (ref, buffer) in enumerate(sources)
        ]

    for copy in pair_copies(0):
        copy.start()
    weights = pltpu.make_async_copy(att_ref.at[pl.ds(0, 3 * width)], big, load_sem.at[0])
    weights.start()
    fill_bias(seen_ref, first_ref)
    pairs = width // PAIR

    def attend_back(i):
        for copy in pair_copies(i):
            copy.wait()

        @pl.when(i + 1 < pairs)
        def _():
            for copy in pair_copies(i + 1):
                copy.start()

        slot = i % 2
        lanes_here = pl.ds(pl.multiple_of(i * PAIR, PAIR), PAIR)
        dk_acc[...] = jnp.zeros_like(dk_acc)
        dv_acc[...] = jnp.zeros_like(dv_acc)
        dq_sum = jnp.zeros((1, PAIR), F32)
        for j in range(rows_here // size):
            rows, keys = pl.ds(j * size, size), pl.ds(j * size, span)
            q_here, do_here = q_in[slot, rows, :], do_in[slot, rows, :]
            k_here, v_here = k_in[slot, keys, :], v_in[slot, keys, :]
            k_t = k_here.T
            meet = (do_here.astype(F32) * o_in[slot, rows, :].astype(F32)).T
            outs = []
            for h in range(2):
                lanes = head_lanes(h)
                delta = jnp.sum(meet[h * HD : (h + 1) * HD], axis=0, keepdims=True)
                s = rows_by_rows(jnp.where(lanes, k_here, 0), q_here) + seen_ref[keys, rows]
                p = jnp.exp(s - lse_ref[i, h : h + 1, rows])
                dp = rows_by_rows(jnp.where(lanes, v_here, 0), do_here)
                ds = (p * (dp - delta)).astype(BF)
                dv_acc[keys, :] += plain_dot(p.astype(BF), jnp.where(lanes, do_here, 0))
                dk_acc[keys, :] += plain_dot(ds, jnp.where(lanes, q_here, 0))
                outs.append(plain_dot(k_t[h * HD : (h + 1) * HD], ds))
            dq = (jnp.concatenate(outs, axis=0).T * scale).astype(BF)
            dq_ref[rows, lanes_here] = dq
            dq_sum += jnp.sum(dq.astype(F32), axis=0, keepdims=True)
        dk, dv = dk_acc[...].astype(BF), dv_acc[...].astype(BF)
        dk_ref[:, lanes_here] = dk
        dv_ref[:, lanes_here] = dv
        sums_ref[0:1, lanes_here] = dq_sum
        sums_ref[1:2, lanes_here] = jnp.sum(dk.astype(F32), axis=0, keepdims=True)
        sums_ref[2:3, lanes_here] = jnp.sum(dv.astype(F32), axis=0, keepdims=True)

    tile = 256
    tiles = width // tile

    def input_grad(r):
        rows = pl.ds((back - r) * rows_here, rows_here)

        def body(i):
            cols = pl.ds(pl.multiple_of(i * tile, tile), tile)
            total = plain_dot(dk_ref[rows, :], big[width : 2 * width, cols]) + plain_dot(dv_ref[rows, :], big[2 * width :, cols])
            if r == 0:
                grad_ref[:, cols] = total + plain_dot(dq_ref[...], big[:width, cols])
            else:
                away[r - 1, :, cols] = total.astype(BF)

        return body

    def weight_grad(n, from_ref, into_ref, first_row, many):
        def body(i):
            cols = pl.ds(pl.multiple_of(i * tile, tile), tile)
            slot = i % 2
            out = pltpu.make_async_copy(stage.at[slot], into_ref.at[pl.ds(i * tile, tile)], stage_sem.at[slot])

            @pl.when((i >= 2) | (n > 0))
            def _():
                out.wait()

            total = lax.dot_general(
                from_ref[:, cols], tokens_of(first_row, many), (((0,), (0,)), ((), ())), preferred_element_type=F32
            )
            stage[slot] = total.astype(BF)
            out.start()

        return body

    def tokens_of(first_row, many):
        return big[pl.ds(first_row, many), :]

    loop_with(pairs, attend_back, during[1])
    weights.wait()
    for n, r in enumerate(range(back, -1, -1)):
        loop_with(tiles, input_grad(r), {i - n * tiles: e for i, e in during[2].items() if i // tiles == n})
    load = pltpu.make_async_copy(wide_ref, big.at[pl.ds(0, n_keys)], load_sem.at[1])
    load.start()
    load.wait()
    own = n_keys - rows_here
    loop_with(tiles, weight_grad(0, dq_ref, gq_ref, own, rows_here), during[3])
    loop_with(tiles, weight_grad(1, dk_ref, gk_ref, 0, n_keys), during[4])
    loop_with(tiles, weight_grad(2, dv_ref, gv_ref, 0, n_keys), during[5])
    reducer.keep()
    for slot in range(2):
        arrived(stage.at[slot], stage_sem.at[slot])

    @pl.when(t >= 2)
    def _():
        arrived(away.at[1], away_send)
    reducer.finish()


def backward_reduce(grad_ff, q, k, v, o, do, lse, first_seen, wide, w_att, n_tensor, back):
    rows, width = q.shape
    n_keys = k.shape[0]
    n_ff = grad_ff.shape[0]
    block = grad_ff.shape[-2:]
    any_spec = pl.BlockSpec(memory_space=pl.ANY)
    vmem = pl.BlockSpec(memory_space=pltpu.VMEM)
    dma = pltpu.SemaphoreType.DMA
    shape = jax.ShapeDtypeStruct
    square = shape((width, width), BF)
    pair = lambda n: pltpu.VMEM((2, n, PAIR), BF)
    return pl.pallas_call(
        functools.partial(backward_kernel, n_tensor, back, 1.0 / math.sqrt(HD)),
        out_shape=[shape((n_ff, *block), BF), shape((rows, width), F32), shape((back, rows, width), BF), square, square, square, shape((3, width), F32)],
        in_specs=[any_spec] * 6 + [vmem, vmem] + [any_spec] * 2,
        out_specs=[vmem, vmem, vmem, any_spec, any_spec, any_spec, vmem],
        scratch_shapes=[
            *Reducer.scratch(n_ff, n_ff // BACK_GROUPS, BACK_GROUPS, 1, n_tensor, block),
            pltpu.VMEM((n_keys, rows), F32),
            pair(rows), pair(n_keys), pair(n_keys), pair(rows), pair(rows),
            pltpu.VMEM((rows, width), BF), pltpu.VMEM((n_keys, width), BF), pltpu.VMEM((n_keys, width), BF),
            pltpu.VMEM((3 * width, width), BF),
            pltpu.VMEM((2, 256, width), BF),
            pltpu.VMEM((n_keys, PAIR), F32), pltpu.VMEM((n_keys, PAIR), F32),
            pltpu.VMEM((rows, width), BF),
            dma((2, 5)), dma((2,)), dma((2,)), dma, dma,
        ],
        compiler_params=pltpu.CompilerParams(collective_id=1, has_side_effects=True, vmem_limit_bytes=60 << 20),
        name="backward_reduce",
    )(grad_ff, q, k, v, o, do, lse, first_seen, wide, w_att)


def join(row, a, b):
    return jnp.where(row == MAX_ROW, jnp.maximum(a, b), a + b)


def finish_kernel(
    n_tensor,
    unit_ref, gq_ref, gk_ref, gv_ref, go_ref, shard_ref, grad_ref, away_ref, hidden_ref, x_ref, shared_ref, v_ref,
    out_ref, vsum_ref, input_ref, *scratch,
):
    reducer_scratch, (
        final, outgo, v_in, v_z, away_in, swap_send, swap_recv, v_send, v_recv, local_sem, away_send, away_recv,
    ) = (
        scratch[:REDUCER], scratch[REDUCER:]
    )
    d, t, core, x, y = place()
    greet(d, t, n_tensor)
    other, near, one, two, up_in, down_in, *sems = reducer_scratch
    parts = [gq_ref, gk_ref, gv_ref, go_ref]
    groups = [parts[i : i + 4 // LAST_GROUPS] for i in range(0, 4, 4 // LAST_GROUPS)]
    reducer = Reducer(groups, n_tensor, other, near, one, two, up_in, down_in, final, sems)
    reducer.start()
    rows_here = x_ref.shape[0]
    n_att = other.shape[0]
    final[n_att:] = shard_ref[...]

    from_above, to_below = t + 1 < n_tensor, t >= 1

    @pl.when(~from_above)
    def _():
        away_in[...] = jnp.zeros_like(away_in)

    def give():
        @pl.when(to_below)
        def _():
            send(away_ref.at[0], away_in, away_send, away_recv, (d, t - 1))

    def got():
        @pl.when(from_above)
        def _():
            arrived(away_in, away_recv)

    vsum_ref[...] = v_ref[...]
    part = 128
    gain = shared_ref[0:1, :]

    def norm_back_rows(i, carry):
        rows = pl.ds(pl.multiple_of(i * part, part), part)
        _, hat, inverse = norm_rows(x_ref[rows, :].astype(F32), 1.0, 0.0)
        grad = grad_ref[rows, :] + away_in[rows, :].astype(F32)
        input_ref[rows, :] = hidden_ref[rows, :] + norm_back(grad, hat, inverse, gain)
        vsum_ref[0:1, :] += jnp.sum(grad * hat, axis=0, keepdims=True)
        vsum_ref[1:2, :] += jnp.sum(grad, axis=0, keepdims=True)
        return carry

    row = lax.broadcasted_iota(jnp.int32, vsum_ref.shape, 0)
    hops = (reducer.sibling, reducer.by_x, reducer.by_y)

    def vector_step(i):
        if i > 0:
            arrived(v_in.at[i - 1], v_recv.at[i - 1])
            arrived(v_in.at[i - 1], v_send.at[i - 1])
            vsum_ref[...] = join(row, vsum_ref[...], v_in[i - 1])
        if i < len(hops):
            send(vsum_ref, v_in.at[i], v_send.at[i], v_recv.at[i], (hops[i], t))
        else:
            for k in range(1, n_tensor):
                send(vsum_ref, v_z.at[k - 1], v_send.at[2 + k], v_recv.at[2 + k], (d, (t + k) % n_tensor))

    def vector_end():
        for k in range(1, n_tensor):
            arrived(v_z.at[k - 1], v_recv.at[2 + k])
            arrived(v_z.at[k - 1], v_send.at[2 + k])
        for k in range(1, n_tensor):
            vsum_ref[...] = join(row, vsum_ref[...], v_z[k - 1])

    by_code = reducer.codes()
    by_code |= {910 + i: functools.partial(vector_step, i) for i in range(len(hops) + 1)}
    by_code |= {900: give, 901: got, 914: vector_end}
    by_code[903] = lambda: lax.fori_loop(0, rows_here // part, norm_back_rows, 0)
    for code in LAST_ORDER:
        by_code[code]()
    reducer.keep()

    cap = out_ref.shape[0]
    for k in range(1, 9):
        to = (d + k) % 8
        for j in range(cap):
            outgo[to, j] = final[unit_ref[to * cap + j]]
        if k < 8:
            send(outgo.at[to], out_ref.at[:, d], swap_send.at[k - 1], swap_recv.at[k - 1], (to, t))
    keep = pltpu.make_async_copy(outgo.at[d], out_ref.at[:, d], local_sem.at[0])
    keep.start()
    for k in range(1, 8):
        arrived(out_ref.at[:, (d + 8 - k) % 8], swap_recv.at[k - 1])
    reducer.finish()
    for k in range(1, 8):
        arrived(outgo.at[0], swap_send.at[k - 1])

    @pl.when(to_below)
    def _():
        arrived(away_in, away_send)
    keep.wait()


def finish_reduce(grads, shard, grad_first, away, grad_hidden, tokens, shared, vectors, unit_of_slot, n_tensor, cap):
    block = shard.shape[1:]
    n_units = len(grads) + shard.shape[0]
    rows, width = tokens.shape
    any_spec = pl.BlockSpec(memory_space=pl.ANY)
    vmem = pl.BlockSpec(memory_space=pltpu.VMEM)
    dma = pltpu.SemaphoreType.DMA
    shape = jax.ShapeDtypeStruct
    out, vsum, input_grad = pl.pallas_call(
        functools.partial(finish_kernel, n_tensor),
        out_shape=[shape((cap, 8, *block), BF), shape(vectors.shape, F32), shape((rows, width), F32)],
        in_specs=[pl.BlockSpec(memory_space=pltpu.SMEM)] + [any_spec] * 4 + [vmem, vmem, any_spec] + [vmem] * 4,
        out_specs=[vmem, vmem, vmem],
        scratch_shapes=[
            *Reducer.scratch(len(grads), 4 // LAST_GROUPS, LAST_GROUPS, 4 // LAST_GROUPS, n_tensor, block),
            pltpu.VMEM((n_units, *block), BF),
            pltpu.VMEM((8, cap, *block), BF),
            pltpu.VMEM((3, *vectors.shape), F32),
            pltpu.VMEM((n_tensor - 1, *vectors.shape), F32),
            pltpu.VMEM(away.shape[1:], BF),
            dma((7,)), dma((7,)), dma((2 + n_tensor,)), dma((2 + n_tensor,)), dma((1,)),
            dma, dma,
        ],
        compiler_params=pltpu.CompilerParams(collective_id=2, has_side_effects=True, vmem_limit_bytes=48 << 20),
        name="finish_reduce",
    )(unit_of_slot, *grads, shard, grad_first, away, grad_hidden, tokens, shared, vectors)
    return out.reshape(cap, -1, width), vsum, input_grad


def feed_forward_kernel(
    hidden_ref, dy_ref, shared_ref, bias_ref, fc_ref, proj_ref,
    out_ref, grad_ref, low_ref, fc_grad_ref, proj_grad_ref, fc_bias_ref, sums_ref,
    second_ref, acc_ref,
):
    step = pl.program_id(0)

    @pl.when(step == 0)
    def _():
        normed, _, _ = norm_rows(hidden_ref[...], shared_ref[3:4, :], shared_ref[4:5, :])
        second_ref[...] = normed.astype(BF)
        out_ref[...] = hidden_ref[...] + shared_ref[5:6, :]
        acc_ref[...] = jnp.zeros_like(acc_ref)

    dy, second = dy_ref[...], second_ref[...]
    pre = rows_by_rows(second, fc_ref[...]) + bias_ref[0]
    cube = pre * pre
    inner = jnp.tanh(GELU_A * (pre + GELU_B * (cube * pre)))
    half = 0.5 * pre
    activ = (half + half * inner).astype(BF)
    slope = 0.5 + 0.5 * inner + half * (1.0 - inner * inner) * (GELU_A + (3.0 * GELU_A * GELU_B) * cube)
    out_ref[...] += plain_dot(activ, proj_ref[...])
    proj_grad_ref[...] = cols_by_cols(activ, dy).astype(BF)
    grad_pre = (rows_by_rows(dy, proj_ref[...]) * slope).astype(BF)
    fc_bias_ref[0] = jnp.sum(grad_pre.astype(F32), axis=0, keepdims=True)
    fc_grad_ref[...] = cols_by_cols(grad_pre, second).astype(BF)
    acc_ref[...] += plain_dot(grad_pre, fc_ref[...])

    @pl.when(step == pl.num_programs(0) - 1)
    def _():
        _, hat, inverse = norm_rows(hidden_ref[...], 1.0, 0.0)
        grad_second, grad_y = acc_ref[...], dy.astype(F32)
        grad = grad_y + norm_back(grad_second, hat, inverse, shared_ref[3:4, :])
        low = grad.astype(BF)
        grad_ref[...] = grad
        low_ref[...] = low
        for n, rows in enumerate((low.astype(F32), grad_second * hat, grad_second, grad_y)):
            sums_ref[n : n + 1, :] = jnp.sum(rows, axis=0, keepdims=True)


def feed_forward(hidden, out_grad, shared, b_fc, w_fc, w_proj):
    rows, width = hidden.shape
    tile = 512
    steps = w_fc.shape[0] // tile
    whole = lambda *dims: pl.BlockSpec(dims, lambda i: (0,) * len(dims))
    strip = pl.BlockSpec((tile, width), lambda i: (i, 0))
    bias = pl.BlockSpec((1, 1, tile), lambda i: (i, 0, 0))
    shape = jax.ShapeDtypeStruct
    out = pl.pallas_call(
        feed_forward_kernel,
        grid=(steps,),
        in_specs=[whole(rows, width), whole(rows, width), whole(*shared.shape), bias, strip, strip],
        out_specs=[whole(rows, width)] * 3 + [strip, strip, bias, whole(4, width)],
        out_shape=[
            shape((rows, width), F32), shape((rows, width), F32), shape((rows, width), BF),
            shape(w_fc.shape, BF), shape(w_proj.shape, BF), shape((steps, 1, tile), F32), shape((4, width), F32),
        ],
        scratch_shapes=[pltpu.VMEM((rows, width), BF), pltpu.VMEM((rows, width), F32)],
        compiler_params=pltpu.CompilerParams(vmem_limit_bytes=48 << 20),
        name="feed_forward",
    )(hidden, out_grad, shared, b_fc.reshape(steps, 1, tile), w_fc, w_proj)
    return (*out[:5], out[5].reshape(-1), out[6])


def per_device(
    tokens_in,
    out_grad,
    lengths,
    owners,
    matrix_master,
    matrix_m1,
    matrix_m2,
    shared_params,
    bias_params,
):
    n_tensor = lax.axis_size("tensor")
    n_data = lax.axis_size("dp")
    tensor_index = lax.axis_index("tensor")
    data_index = lax.axis_index("dp")
    rows_here, width = tokens_in.shape
    slot_cap = matrix_master.shape[1]
    unit_rows = matrix_master.shape[2]
    n_units = owners.shape[0]
    n_slots = n_data * slot_cap
    head_rows = width // n_tensor
    heads_here = head_rows // HD
    ff_rows = (n_units * unit_rows - 4 * head_rows) // 2
    slot_of_unit, unit_of_slot, occupied = slot_tables(owners, n_slots, slot_cap)


    back = -(-(DOC_MOST - 1) // rows_here)
    reach = back * rows_here
    own_kernels = n_data == 8 and n_tensor == 4 and back == 2 and head_rows == unit_rows and unit_rows % 128 == 0
    sizes = lengths[0]
    upto = jnp.arange(sizes.shape[0])[:, None] >= jnp.arange(sizes.shape[0])[None, :]
    bounds = jnp.sum(jnp.where(upto, sizes[None, :], 0), axis=1)
    places = tensor_index * rows_here + jnp.arange(rows_here, dtype=jnp.int32)
    starts = jnp.max(jnp.where(places[:, None] >= bounds[None, :], bounds[None, :], 0), axis=1)
    first_seen = (starts - tensor_index * rows_here + reach)[None, :]

    shared = shared_params[0]
    inputs_f32 = tokens_in.astype(F32)
    normed_one, hat_one, inverse_one = norm_rows(inputs_f32, shared[0], shared[1])
    normed_low = normed_one.astype(BF)
    if own_kernels:
        (
            w_att, normed_all, q_scaled, keys_in, values_in, attended, log_norms, peaks,
            layer_out, grad_hidden, grad_attended, grad_ff_w, grad_out_w, grad_fc_b, shared_rows,
        ) = forward_spread(
            matrix_master[0].astype(BF), tokens_in, out_grad, bias_params[0, 0], first_seen, shared,
            slot_of_unit, n_tensor, back,
        )
    else:
        units = gather_units(matrix_master[0], slot_of_unit)
        stacks = units.reshape(n_tensor, n_units * unit_rows, width)
        part = lambda first, count: stacks[:, first : first + count].reshape(-1, width)
        w_q, w_k, w_v, w_out = (part(i * head_rows, head_rows) for i in range(4))
        w_fc = part(4 * head_rows, ff_rows)
        w_proj = part(4 * head_rows + ff_rows, ff_rows)
        all_bias = lax.all_gather(bias_params[0], "tensor", axis=0, tiled=True).reshape(n_tensor, -1)
        before = [
            lax.ppermute(normed_low, "tensor", [(i, i + r) for i in range(n_tensor - r)])
            for r in range(min(back, n_tensor - 1), 0, -1)
        ]
        blank = [jnp.zeros_like(normed_low)] * (back - len(before))
        normed_all = jnp.concatenate([*blank, *before, normed_low], axis=0)
        bias = lambda first, count: all_bias[:, first : first + count].reshape(-1)
        b_q, b_k, b_v = (bias(i * head_rows, head_rows) for i in range(3))
        b_fc = bias(3 * head_rows, ff_rows)
        q_scaled = (rows_by_rows(normed_low, w_q) + b_q).astype(BF) * jnp.asarray(1.0 / math.sqrt(HD), BF)
        keys_in = (rows_by_rows(normed_all, w_k) + b_k).astype(BF)
        values_in = (rows_by_rows(normed_all, w_v) + b_v).astype(BF)
        attended, log_norms, peaks = attend_forward(q_scaled, keys_in, values_in, first_seen)
        hidden = inputs_f32 + (plain_dot(attended, w_out) + shared[2])
        layer_out, grad_hidden, grad_hidden_low, grad_fc_w, grad_proj_w, grad_fc_b, shared_rows = feed_forward(
            hidden, out_grad, shared, b_fc, w_fc, w_proj
        )
        grad_out_w = cols_by_cols(attended, grad_hidden_low).astype(BF)
        grad_attended = rows_by_rows(grad_hidden_low, w_out).astype(BF)
    head_here = jnp.max(peaks, axis=2).reshape(-1)
    if own_kernels:
        in_blocks = lambda g: g.reshape(-1, n_tensor, 2, 2, 2, unit_rows // 8, width)
        shard, grad_first, away, grad_q_w, grad_k_w, grad_v_w, sums = backward_reduce(
            in_blocks(grad_ff_w), q_scaled, keys_in, values_in, attended, grad_attended,
            log_norms, first_seen, normed_all, w_att, n_tensor, back,
        )
        grad_fc_b = grad_fc_b.reshape(2, n_tensor, -1, unit_rows).swapaxes(1, 2)
        vectors = jnp.concatenate(
            [
                jnp.zeros((2, width), F32), shared_rows, sums, grad_fc_b.reshape(-1, width),
                jnp.pad(head_here, (0, width - head_here.shape[0]))[None], jnp.zeros((2, width), F32),
            ],
            axis=0,
        )
        grads = [in_blocks(g) for g in (grad_q_w, grad_k_w, grad_v_w, grad_out_w)]
        half = (n_units - 4) // 2
        later = unit_of_slot - 4
        spot_of_slot = jnp.where(later < 0, unit_of_slot, 4 + jnp.where(later < half, 2 * later, 2 * (later - half) + 1))
        my_grads, totals, input_grad = finish_reduce(
            grads, shard, grad_first, away, grad_hidden, tokens_in, shared, vectors, spot_of_slot, n_tensor, slot_cap
        )
        my_grads = my_grads.astype(F32)
        shared_grad = totals[:6]
        head_all = totals[MAX_ROW, : head_here.shape[0]]
        bias_total = totals[6:MAX_ROW].reshape(-1, n_tensor, unit_rows)
        bias_grad = lax.dynamic_index_in_dim(bias_total, tensor_index, 1, keepdims=False).reshape(-1)
    else:
        grad_q, grad_k, grad_v = attend_backward(
            q_scaled, keys_in, values_in, attended, grad_attended, log_norms, first_seen
        )
        grad_q_w = cols_by_cols(grad_q, normed_low)
        grad_k_w = cols_by_cols(grad_k, normed_all)
        grad_v_w = cols_by_cols(grad_v, normed_all)
        grad_wide = plain_dot(grad_k, w_k) + plain_dot(grad_v, w_v)
        grad_first = grad_wide[reach:] + plain_dot(grad_q, w_q)
        for r in range(1, min(back, n_tensor - 1) + 1):
            away = grad_wide[reach - r * rows_here : reach - (r - 1) * rows_here].astype(BF)
            grad_first += lax.ppermute(away, "tensor", [(i, i - r) for i in range(r, n_tensor)]).astype(F32)
        input_grad = grad_hidden + norm_back(grad_first, hat_one, inverse_one, shared[0])
        grad_qkv_b = [jnp.sum(g, axis=0, dtype=F32) for g in (grad_q, grad_k, grad_v)]
        first_rows = jnp.stack([jnp.sum(grad_first * hat_one, axis=0), jnp.sum(grad_first, axis=0)])
        shared_part = jnp.concatenate([first_rows, shared_rows], axis=0)
        by_tensor = lambda v: v.reshape(n_tensor, -1)
        bias_part = jnp.concatenate([by_tensor(v) for v in (*grad_qkv_b, grad_fc_b)], axis=1)
        head_all = lax.pmax(head_here, ("dp", "tensor"))
        shared_grad, bias_total = lax.psum((shared_part, bias_part), ("dp", "tensor"))
        bias_grad = lax.dynamic_index_in_dim(bias_total, tensor_index, 0, keepdims=False)
        by_stack = lambda g: g.astype(BF).reshape(n_tensor, -1, width)
        grad_units = jnp.concatenate(
            [by_stack(g) for g in (grad_q_w, grad_k_w, grad_v_w, grad_out_w, grad_fc_w, grad_proj_w)], axis=1
        ).reshape(units.shape)
        my_grads = scatter_units(grad_units, unit_of_slot).astype(F32)
    head_peak = lax.dynamic_slice_in_dim(head_all, tensor_index * heads_here, heads_here)

    my_units = lax.dynamic_slice_in_dim(unit_of_slot, data_index * slot_cap, slot_cap, 0)
    my_occupied = lax.dynamic_slice_in_dim(occupied, data_index * slot_cap, slot_cap, 0)[:, None, None]
    steps_done = float(STEP)
    first_new, second_new, master_new = adam_step(
        matrix_master[0], my_grads, matrix_m1[0], matrix_m2[0], steps_done, WEIGHT_DECAY
    )
    root_gamma = jnp.sqrt(CLIP_TAU / jnp.maximum(head_peak, CLIP_TAU))
    row_index = my_units[:, None] * unit_rows + jnp.arange(unit_rows, dtype=jnp.int32)[None, :]
    local_head = jnp.where(row_index < head_rows, row_index // HD, (row_index - head_rows) // HD)
    head_match = local_head[..., None] == jnp.arange(heads_here, dtype=jnp.int32)[None, None, :]
    picked_root = jnp.sum(jnp.where(head_match, root_gamma, 0.0), axis=-1)
    factor = jnp.where(row_index < 2 * head_rows, picked_root, 1.0)
    my_grads = jnp.where(my_occupied, my_grads, 0.0)
    master_new = jnp.where(my_occupied, master_new * factor[..., None], 0.0)
    first_new = jnp.where(my_occupied, first_new, 0.0)
    second_new = jnp.where(my_occupied, second_new, 0.0)
    shared_first, shared_second, shared_new = adam_step(
        shared, shared_grad, shared_params[1], shared_params[2], steps_done, 0.0
    )
    bias_first, bias_second, bias_new = adam_step(
        bias_params[0, 0], bias_grad, bias_params[1, 0], bias_params[2, 0], steps_done, 0.0
    )
    shared_out = jnp.stack([shared_grad, shared_first])
    bias_out = jnp.stack([bias_grad, bias_first])[:, None, :]
    return (
        layer_out,
        input_grad,
        head_peak,
        my_grads[None],
        first_new[None],
        second_new[None],
        master_new[None],
        shared_out,
        shared_second,
        shared_new,
        bias_out,
        bias_second[None],
        bias_new[None],
    )


def solution(mesh):
    in_specs = (
        P(("dp", "tensor"), None),
        P(("dp", "tensor"), None),
        P("dp", None),
        P(),
        P("tensor", "dp", None, None),
        P("tensor", "dp", None, None),
        P("tensor", "dp", None, None),
        P(),
        P(None, "tensor", None),
    )
    out_specs = (
        P(("dp", "tensor"), None),
        P(("dp", "tensor"), None),
        P("tensor"),
        P("tensor", "dp", None, None),
        P("tensor", "dp", None, None),
        P("tensor", "dp", None, None),
        P("tensor", "dp", None, None),
        P(),
        P(),
        P(),
        P(None, "tensor", None),
        P("tensor", None),
        P("tensor", None),
    )
    return jax.shard_map(
        per_device, mesh=mesh, in_specs=in_specs, out_specs=out_specs, check_vma=False
    )
```

```python
import functools
import math

import jax
import jax.numpy as jnp
from jax import lax
from jax.experimental import pallas as pl
from jax.experimental.pallas import tpu as pltpu
from jax.sharding import PartitionSpec as P

HD = 64
DOC_MOST = 1024
STEP = 10
PAIR = 2 * HD

EPS_NORM = 1e-05
BETA_ONE = 0.9
BETA_TWO = 0.95
LEARN_RATE = 0.08
WEIGHT_DECAY = 0.1
EPS_ADAM = 1e-08
CLIP_TAU = 10.0
MASKED = -1e30
GELU_A = 0.7978845608
GELU_B = 0.044715
BF = jnp.bfloat16
F32 = jnp.float32
MESH = pl.DeviceIdType.MESH
MAX_ROW = 13
BACK_GROUPS = 4
LAST_GROUPS = 2


def plain_dot(left, right):
    return jnp.dot(left, right, preferred_element_type=F32)


def rows_by_rows(left, right):
    return lax.dot_general(left, right, (((1,), (1,)), ((), ())), preferred_element_type=F32)


def cols_by_cols(left, right):
    return lax.dot_general(left, right, (((0,), (0,)), ((), ())), preferred_element_type=F32)


def gelu_tanh(values_in):
    return jax.nn.gelu(values_in, approximate=True)


def norm_rows(values_in, gain, shift):
    centre = jnp.mean(values_in, axis=-1, keepdims=True)
    shifted = values_in - centre
    inverse = lax.rsqrt(jnp.mean(shifted * shifted, axis=-1, keepdims=True) + EPS_NORM)
    normed = shifted * inverse
    return (normed * gain + shift, normed, inverse)


def norm_back(grad_in, normed, inverse, gain):
    scaled = grad_in * gain
    return inverse * (
        scaled
        - jnp.mean(scaled, axis=-1, keepdims=True)
        - normed * jnp.mean(scaled * normed, axis=-1, keepdims=True)
    )


def slot_tables(owners, n_slots, slot_cap):
    n_units = owners.shape[0]
    unit_order = jnp.arange(n_units, dtype=jnp.int32)
    same_owner = owners[:, None] == owners[None, :]
    earlier = unit_order[None, :] < unit_order[:, None]
    rank_counts = jnp.sum((same_owner & earlier).astype(jnp.int32), axis=1)
    slot_of_unit = owners * slot_cap + rank_counts
    matches = jnp.arange(n_slots, dtype=jnp.int32)[:, None] == slot_of_unit[None, :]
    occupied = jnp.any(matches, axis=1)
    unit_of_slot = jnp.sum(matches.astype(jnp.int32) * unit_order[None, :], axis=1)
    return (slot_of_unit, unit_of_slot, occupied)


def head_lanes(head):
    lane = lax.broadcasted_iota(jnp.int32, (1, PAIR), 1)
    return (lane < HD) if head == 0 else (lane >= HD)


def q_tiles(n_query, n_keys):
    size = min(256, n_query)
    reach = n_keys - n_query
    return size, reach + size


def fill_bias(bias_ref, first_ref):
    n_keys, n_query = bias_ref.shape
    reach = n_keys - n_query
    key = lax.broadcasted_iota(jnp.int32, (n_keys, n_query), 0)
    query = lax.broadcasted_iota(jnp.int32, (n_keys, n_query), 1) + reach
    seen = (key <= query) & (key >= first_ref[...])
    bias_ref[...] = jnp.where(seen, 0.0, MASKED)


def attend_kernel(first_ref, q_ref, k_ref, v_ref, o_ref, lse_ref, peak_ref, bias_ref):
    @pl.when(pl.program_id(0) == 0)
    def _():
        fill_bias(bias_ref, first_ref)

    n_keys, n_query = bias_ref.shape
    size, span = q_tiles(n_query, n_keys)
    for j in range(n_query // size):
        rows, keys = pl.ds(j * size, size), pl.ds(j * size, span)
        v_t = v_ref[keys, :].T
        outs = []
        for h in range(2):
            k_h = jnp.where(head_lanes(h), k_ref[keys, :], 0)
            s = rows_by_rows(k_h, q_ref[rows, :]) + bias_ref[keys, rows]
            top = jnp.max(s, axis=0, keepdims=True)
            p = jnp.exp(s - top)
            total = jnp.sum(p, axis=0, keepdims=True)
            o_t = plain_dot(v_t[h * HD : (h + 1) * HD], p.astype(BF))
            outs.append(o_t / total)
            lse_ref[0, h : h + 1, rows] = top + jnp.log(total)
            peak_ref[0, h : h + 1, rows] = top
        o_ref[rows, :] = jnp.concatenate(outs, axis=0).T.astype(BF)


def attend_forward(q_scaled, keys_in, values_in, first_seen):
    n_query, width = q_scaled.shape
    n_keys = keys_in.shape[0]
    pairs = width // PAIR
    column = lambda i: (0, i)
    stats = jax.ShapeDtypeStruct((pairs, 2, n_query), F32)
    stat_spec = pl.BlockSpec((1, 2, n_query), lambda i: (i, 0, 0))
    return pl.pallas_call(
        attend_kernel,
        grid=(pairs,),
        in_specs=[
            pl.BlockSpec((1, n_query), lambda i: (0, 0)),
            pl.BlockSpec((n_query, PAIR), column),
            pl.BlockSpec((n_keys, PAIR), column),
            pl.BlockSpec((n_keys, PAIR), column),
        ],
        out_specs=[pl.BlockSpec((n_query, PAIR), column), stat_spec, stat_spec],
        out_shape=[jax.ShapeDtypeStruct((n_query, width), BF), stats, stats],
        scratch_shapes=[pltpu.VMEM((n_keys, n_query), F32)],
        compiler_params=pltpu.CompilerParams(vmem_limit_bytes=48 << 20),
        name="attend_forward",
    )(first_seen, q_scaled, keys_in, values_in)


def attend_back_kernel(
    first_ref, q_ref, k_ref, v_ref, o_ref, do_ref, lse_ref, dq_ref, dk_ref, dv_ref,
    bias_ref, dk_acc, dv_acc, *, scale
):
    @pl.when(pl.program_id(0) == 0)
    def _():
        fill_bias(bias_ref, first_ref)

    n_keys, n_query = bias_ref.shape
    size, span = q_tiles(n_query, n_keys)
    dk_acc[...] = jnp.zeros_like(dk_acc)
    dv_acc[...] = jnp.zeros_like(dv_acc)
    for j in range(n_query // size):
        rows, keys = pl.ds(j * size, size), pl.ds(j * size, span)
        q_here, do_here = q_ref[rows, :], do_ref[rows, :]
        k_here, v_here = k_ref[keys, :], v_ref[keys, :]
        k_t = k_here.T
        meet = (do_here.astype(F32) * o_ref[rows, :].astype(F32)).T
        outs = []
        for h in range(2):
            lanes = head_lanes(h)
            delta = jnp.sum(meet[h * HD : (h + 1) * HD], axis=0, keepdims=True)
            s = rows_by_rows(jnp.where(lanes, k_here, 0), q_here) + bias_ref[keys, rows]
            p = jnp.exp(s - lse_ref[0, h : h + 1, rows])
            dp = rows_by_rows(jnp.where(lanes, v_here, 0), do_here)
            ds = (p * (dp - delta)).astype(BF)
            dv_acc[keys, :] += plain_dot(p.astype(BF), jnp.where(lanes, do_here, 0))
            dk_acc[keys, :] += plain_dot(ds, jnp.where(lanes, q_here, 0))
            outs.append(plain_dot(k_t[h * HD : (h + 1) * HD], ds))
        dq_ref[rows, :] = (jnp.concatenate(outs, axis=0).T * scale).astype(BF)
    dk_ref[...] = dk_acc[...].astype(BF)
    dv_ref[...] = dv_acc[...].astype(BF)


def attend_backward(q_scaled, keys_in, values_in, attended, grads_out, log_norms, first_seen):
    n_query, width = q_scaled.shape
    n_keys = keys_in.shape[0]
    pairs = width // PAIR
    column = lambda i: (0, i)
    q_spec = pl.BlockSpec((n_query, PAIR), column)
    k_spec = pl.BlockSpec((n_keys, PAIR), column)
    q_out = jax.ShapeDtypeStruct((n_query, width), BF)
    k_out = jax.ShapeDtypeStruct((n_keys, width), BF)
    return pl.pallas_call(
        functools.partial(attend_back_kernel, scale=1.0 / math.sqrt(HD)),
        grid=(pairs,),
        in_specs=[
            pl.BlockSpec((1, n_query), lambda i: (0, 0)),
            q_spec, k_spec, k_spec, q_spec, q_spec,
            pl.BlockSpec((1, 2, n_query), lambda i: (i, 0, 0)),
        ],
        out_specs=[q_spec, k_spec, k_spec],
        out_shape=[q_out, k_out, k_out],
        scratch_shapes=[
            pltpu.VMEM((n_keys, n_query), F32),
            pltpu.VMEM((n_keys, PAIR), F32),
            pltpu.VMEM((n_keys, PAIR), F32),
        ],
        compiler_params=pltpu.CompilerParams(vmem_limit_bytes=48 << 20),
        name="attend_backward",
    )(first_seen, q_scaled, keys_in, values_in, attended, grads_out, log_norms)


def adam_step(param, grad, first, second, steps_done, decay):
    first_new = BETA_ONE * first + (1.0 - BETA_ONE) * grad
    second_new = BETA_TWO * second + (1.0 - BETA_TWO) * grad * grad
    fix_one = 1.0 - BETA_ONE**steps_done
    fix_two = 1.0 - BETA_TWO**steps_done
    direction = first_new / fix_one / (jnp.sqrt(second_new / fix_two) + EPS_ADAM)
    return (first_new, second_new, param - LEARN_RATE * (direction + decay * param))


def owner_kernel(grad_in, master_ref, first_ref, second_ref, factor_ref, keep_ref, grad_ref, m1_ref, m2_ref, new_ref):
    grad = grad_in[...].astype(F32)
    first, second, new = adam_step(master_ref[...], grad, first_ref[...], second_ref[...], float(STEP), WEIGHT_DECAY)
    keep = keep_ref[...] > 0.5
    for ref, value in ((grad_ref, grad), (m1_ref, first), (m2_ref, second), (new_ref, new * factor_ref[...])):
        ref[...] = jnp.where(keep, value, 0.0)


def owner_step(grads, master, first, second, factor, keep):
    shape = master.shape
    rows, width = shape[0] * shape[1], shape[2]
    part = min(64, rows)
    wide = pl.BlockSpec((part, width), lambda i: (i, 0))
    thin = pl.BlockSpec((part, 1), lambda i: (i, 0))
    flat = lambda v: v.reshape(rows, -1)
    outs = pl.pallas_call(
        owner_kernel,
        grid=(rows // part,),
        in_specs=[wide] * 4 + [thin] * 2,
        out_specs=[wide] * 4,
        out_shape=[jax.ShapeDtypeStruct((rows, width), F32)] * 4,
        compiler_params=pltpu.CompilerParams(vmem_limit_bytes=60 << 20),
        name="owner_step",
    )(*(flat(v) for v in (grads, master, first, second, factor, keep)))
    return [v.reshape(shape) for v in outs]


def take_kernel(picks_ref, from_ref, to_ref):
    to_ref[...] = from_ref[...]


def take_blocks(blocks, picks):
    shape = (blocks.shape[0], 1, *blocks.shape[2:])
    return pl.pallas_call(
        take_kernel,
        grid_spec=pltpu.PrefetchScalarGridSpec(
            num_scalar_prefetch=1,
            grid=picks.shape,
            in_specs=[pl.BlockSpec(shape, lambda i, p: (0, p[i], 0, 0))],
            out_specs=pl.BlockSpec(shape, lambda i, p: (0, i, 0, 0)),
        ),
        out_shape=jax.ShapeDtypeStruct((shape[0], picks.shape[0], *shape[2:]), blocks.dtype),
        compiler_params=pltpu.CompilerParams(vmem_limit_bytes=32 << 20),
        name="take_blocks",
    )(picks, blocks)


def gather_units(master, slot_of_unit):
    slots = lax.all_gather(master.astype(BF), ("tensor", "dp"), axis=0, tiled=True)
    n_tensor = lax.axis_size("tensor")
    slots = slots.reshape(n_tensor, -1, *master.shape[1:])
    return take_blocks(slots, slot_of_unit)


def scatter_units(units, unit_of_slot):
    slots = take_blocks(units, unit_of_slot)
    slots = slots.reshape(-1, *units.shape[2:])
    return lax.psum_scatter(slots, ("tensor", "dp"), scatter_dimension=0, tiled=True)


def send(src, dst, send_sem, recv_sem, to):
    copy = pltpu.make_async_remote_copy(
        src_ref=src, dst_ref=dst, send_sem=send_sem, recv_sem=recv_sem,
        device_id=to, device_id_type=MESH,
    )
    copy.start()


def arrived(ref, sem):
    pltpu.make_async_copy(ref, ref, sem).wait()


def place():
    d, t = lax.axis_index("dp"), lax.axis_index("tensor")
    return d, t, d % 2, (d // 2) % 2, d // 4


def greet(d, t, n_tensor):
    barrier = pltpu.get_barrier_semaphore()
    for k in range(1, 8):
        pl.semaphore_signal(barrier, inc=1, device_id=((d + k) % 8, t), device_id_type=MESH)
    for k in range(1, n_tensor):
        pl.semaphore_signal(barrier, inc=1, device_id=(d, (t + k) % n_tensor), device_id_type=MESH)
    pl.semaphore_wait(barrier, 6 + n_tensor)


def loop_with(count, body, events):
    def step(i, carry):
        body(i)
        for n, mine in events.items():
            @pl.when(i == n)
            def _(mine=mine):
                for event in mine:
                    event()
        return carry

    lax.fori_loop(0, count, step, 0)


def by_step(order, by_code, kinds):
    early, during = [], {kind: {} for kind in range(1, kinds + 1)}
    now, count = None, 0
    for code in order:
        if code < 0:
            now, count = -code, 0 if -code != now else count + 1
        elif now is None:
            early.append(by_code[code])
        else:
            during[now].setdefault(count, []).append(by_code[code])
    return early, during


def attend_pair(i, q_ref, k_ref, v_ref, o_ref, lse_ref, peak_ref, bias_ref):
    n_keys, n_query = bias_ref.shape
    size, span = q_tiles(n_query, n_keys)
    lanes = pl.ds(pl.multiple_of(i * PAIR, PAIR), PAIR)
    tiles = [(pl.ds(j * size, size), pl.ds(j * size, span)) for j in range(n_query // size)]
    scores = [
        [
            rows_by_rows(jnp.where(head_lanes(h), k_ref[keys, lanes], 0), q_ref[rows, lanes]) + bias_ref[keys, rows]
            for h in range(2)
        ]
        for rows, keys in tiles
    ]
    for j, (rows, keys) in enumerate(tiles):
        v_t = v_ref[keys, lanes].T
        outs = []
        for h in range(2):
            s = scores[j][h]
            top = jnp.max(s, axis=0, keepdims=True)
            p = jnp.exp(s - top)
            total = jnp.sum(p, axis=0, keepdims=True)
            o_t = plain_dot(v_t[h * HD : (h + 1) * HD], p.astype(BF))
            outs.append(o_t / total)
            lse_ref[i, h : h + 1, rows] = top + jnp.log(total)
            peak_ref[i, h : h + 1, rows] = top
        o_ref[rows, lanes] = jnp.concatenate(outs, axis=0).T.astype(BF)


def paired(n_units):
    half = (n_units - 4) // 2
    return [0, 1, 2, 3] + [4 + i + half * b for i in range(half) for b in range(2)]


def gelu_parts(pre):
    square = pre * pre
    inner = jnp.tanh(GELU_A * (pre + GELU_B * (square * pre)))
    half = 0.5 * pre
    slope = 0.5 + 0.5 * inner + half * (1.0 - inner * inner) * (GELU_A + (3.0 * GELU_A * GELU_B) * square)
    return half + half * inner, slope


ORDER = (
    220, 100, 200, 600, 0, 601, 602, 500, 501, 801, 120, 502, 701, 1900, 110, 300, 802, 702, 800, 700, 901,
    1001, 610, 1000, 400, 902, 210, 1952, 1002, 900, 10, 1950, 310, 1951, 1953, -1, -1, -1, 20, 1901, 620, -1,
    611, -2, -2, -2, -2, 510, -3, -3, -3, 520, -3, -4, 511, 621, -4, -4, 521, 622, -4, 811, 512, 710, -4, 612,
    711, 810, -4, 410, -4, 522, -4, 820, 712, 720, 910, 911, 1011, 812, 320, -5, 1010, -6, 912, 721, 822, -6,
    1012, 1020, -6, 821, 420, 1022, 920, -6, 722, -6, -6, -6, -6, 921, 1021, -6, 922, -6, -6, -6, -6, -6,
)


def forward_kernel(
    n_tensor, back, scale,
    slot_ref, master_ref, x_ref, dy_ref, bias_in_ref, first_ref, shared_ref,
    att_ref, ff_ref, wide_ref, q_ref, k_ref, v_ref, o_ref, lse_ref, peak_ref,
    out_ref, grad_ref, do_ref, ff_grad_ref, go_ref, fc_bias_ref, sums_ref,
    pieces, own, seen_ref, bias_rows, biases_ref, fc_rows, hidden_ref, second_ref, acc_ref, tiles_in, stage,
    swap_send, swap_recv, local_sem, a_send, a_recv, bias_send, bias_recv,
    z_send, z_recv, xy_send, xy_recv, core_send, core_recv, tile_sem, stage_sem,
):
    d, t, core, x, y = place()
    column = y * 2 + x
    by_x, by_y = d + 2 - 4 * x, d + 4 - 8 * y
    sibling = d + 1 - 2 * core
    first, last = t > 0, t < n_tensor - 1
    rows_here, width = x_ref.shape
    n_half = ff_ref.shape[0] // 2
    weights = (att_ref, ff_ref.at[pl.ds(0, n_half)], ff_ref.at[pl.ds(n_half, n_half)])
    starts = (0, 4, 4 + n_half, 4 + 2 * n_half)
    n_groups, steps = len(weights), n_tensor - 1
    slots = 2 * n_tensor - 1
    greet(d, t, n_tensor)

    def tokens_up(r):
        @pl.when(last & (t >= r))
        def _():
            send(wide_ref.at[back - r], wide_ref.at[back - r - 1], a_send.at[r], a_recv.at[r], (d, t + 1))

    def tokens_in(r):
        @pl.when(t > r)
        def _():
            arrived(wide_ref.at[back - r - 1], a_recv.at[r])
        if r + 1 < back:
            tokens_up(r + 1)

    for k in range(1, 8):
        to = (d + k) % 8
        send(master_ref.at[:, to], pieces.at[d], swap_send.at[k - 1], swap_recv.at[k - 1], (to, t))
    part = min(128, rows_here)
    for i in range(0, rows_here, part):
        rows = pl.ds(i, part)
        normed, _, _ = norm_rows(x_ref[rows, :].astype(F32), shared_ref[0:1, :], shared_ref[1:2, :])
        wide_ref[back, rows, :] = normed.astype(BF)
    tokens_up(0)
    mine = pltpu.make_async_copy(master_ref.at[:, d], pieces.at[d], local_sem.at[0])
    mine.start()
    for k in range(1, n_tensor):
        send(bias_in_ref, biases_ref.at[t], bias_send.at[k - 1], bias_recv.at[k - 1], (d, (t + k) % n_tensor))
    biases_ref[t] = bias_in_ref[...]
    for r in range(back):
        @pl.when(t < back - r)
        def _(r=r):
            wide_ref[r] = jnp.zeros((rows_here, width), BF)
    fill_bias(seen_ref, first_ref)
    mine.wait()
    for k in range(1, 8):
        arrived(pieces.at[(d + 8 - k) % 8], swap_recv.at[k - 1])
    cap = master_ref.shape[0]
    for n, u in enumerate(paired(own.shape[0])):
        slot = slot_ref[u]
        own[n] = pieces[slot // cap, slot % cap]

    def block(g, at, col, c):
        return weights[g].at[:, at, col, c]

    def route(at):
        side = at * 2 // n_tensor
        one, two = by_x + (by_y - by_x) * side, by_y + (by_x - by_y) * side
        col_x, col_y, col_xy = y * 2 + 1 - x, (1 - y) * 2 + x, (1 - y) * 2 + 1 - x
        return one, two, col_x + (col_y - col_x) * side, col_y + (col_x - col_y) * side, col_xy

    def onward(g, k, at, source):
        one, two, _, _, _ = route(at)
        here = block(g, at, column, core)
        send(source, here, xy_send.at[g], xy_recv.at[g, k, 0], (one, t))
        send(source, here, xy_send.at[g], xy_recv.at[g, k, 1], (two, t))

    def forward(g, k, at):
        one, two, from_one, _, _ = route(at)
        got = block(g, at, from_one, core)
        arrived(got, xy_recv.at[g, k, 0])
        send(got, got, xy_send.at[g], xy_recv.at[g, k, 2], (two, t))

    def settle(g, k, at):
        _, _, _, from_two, beyond = route(at)
        arrived(block(g, at, from_two, core), xy_recv.at[g, k, 1])
        arrived(block(g, at, beyond, core), xy_recv.at[g, k, 2])
        got = weights[g].at[:, at, :, core]
        send(got, got, core_send.at[g, k], core_recv.at[g, k], (sibling, t))

    def done(g, k, at):
        arrived(weights[g].at[:, at, :, 1 - core], core_recv.at[g, k])

    def given(g, k, at):
        arrived(weights[g].at[:, at, :, core], core_send.at[g, k])

    def z_go(g, s, up, source):
        i = 0 if up else 1

        @pl.when(last if up else first)
        def _():
            here = block(g, t if s == 0 else (t - s if up else t + s), column, core)
            send(source, here, z_send.at[g, i, s], z_recv.at[g, i, s], (d, t + 1 if up else t - 1))

    def z_step(s, up):
        at = t - 1 - s if up else t + 1 + s
        return 1 + 2 * s + (0 if up else 1), at, (at >= 0) if up else (at < n_tensor)

    def z_event(g, s, up):
        k, at, have = z_step(s, up)

        @pl.when(have)
        def _():
            got = block(g, at, column, core)
            arrived(got, z_recv.at[g, 0 if up else 1, s])
            if s + 1 < steps:
                z_go(g, s + 1, up, got)
            onward(g, k, at, got)

    def step(fn, g, s, up):
        k, at, have = z_step(s, up)
        pl.when(have)(functools.partial(fn, g, k, at))

    def each(fn, g, s):
        if s < 0:
            fn(g, 0, t)
        else:
            for up in (True, False):
                step(fn, g, s, up)

    local = []
    mine_of = [own.at[starts[g] : starts[g + 1]] for g in range(n_groups)]
    for g in range(n_groups):
        copy = pltpu.make_async_copy(mine_of[g], block(g, t, column, core), local_sem.at[1 + g])
        copy.start()
        local.append(copy)

    def own_settled(g):
        local[g].wait()
        settle(g, 0, t)

    by_code = {1900 + r: functools.partial(tokens_in, r) for r in range(back)}
    by_code |= {1951 + s: functools.partial(each, done, 0, s) for s in range(-1, steps)}
    for g in range(n_groups):
        by_code[200 + 10 * g] = functools.partial(onward, g, 0, t, mine_of[g])
        by_code[300 + 10 * g] = functools.partial(forward, g, 0, t)
        by_code[400 + 10 * g] = functools.partial(own_settled, g)
        for way, up in ((0, True), (100, False)):
            by_code[way + 10 * g] = functools.partial(z_go, g, 0, up, mine_of[g])
            for s in range(steps):
                by_code[500 + way + 10 * g + s] = functools.partial(z_event, g, s, up)
                by_code[700 + way + 10 * g + s] = functools.partial(step, forward, g, s, up)
                by_code[900 + way + 10 * g + s] = functools.partial(step, settle, g, s, up)
    tile = 256
    tiles = width // tile
    early, during = by_step(ORDER, by_code, 6)
    for event in early:
        event()
    for k in range(1, n_tensor):
        arrived(biases_ref.at[(t + n_tensor - k) % n_tensor], bias_recv.at[k - 1])
        arrived(bias_in_ref, bias_send.at[k - 1])
    per = width // n_tensor // 128
    for n in range(3):
        for at in range(n_tensor):
            for i in range(per):
                lanes = pl.ds((at * per + i) * 128, 128)
                bias_rows[n : n + 1, lanes] = biases_ref[at, n * per + i : n * per + i + 1]
    strip = fc_rows.shape[-1]
    for h in range(2):
        for at in range(n_tensor):
            for i in range(strip // 128):
                row = 3 * per + h * (strip // 128) + i
                fc_rows[h, at, 0:1, i * 128 : (i + 1) * 128] = biases_ref[at, row : row + 1]

    def project(n, own_only, into_ref, factor):
        def body(i):
            cols = pl.ds(pl.multiple_of(i * tile, tile), tile)
            w = att_ref[n, pl.ds(i * tile // (width // n_tensor), 1)].reshape(tile, width)
            for r in range(into_ref.shape[0] // rows_here):
                a = wide_ref[back if own_only else r]
                full = (rows_by_rows(a, w) + bias_rows[n : n + 1, cols]).astype(BF)
                into_ref[r * rows_here : (r + 1) * rows_here, cols] = full * jnp.asarray(factor, BF) if factor else full
        return body

    loop_with(tiles, project(0, True, q_ref, scale), during[1])
    loop_with(tiles, project(1, False, k_ref, None), during[2])
    loop_with(tiles, project(2, False, v_ref, None), during[3])
    loop_with(
        width // PAIR,
        lambda i: attend_pair(i, q_ref, k_ref, v_ref, o_ref, lse_ref, peak_ref, seen_ref),
        during[4],
    )
    w_out = att_ref[3].reshape(width, width)
    half = rows_here // 2
    for r in range(2):
        rows = pl.ds(r * half, half)
        hidden = x_ref[rows, :].astype(F32) + (plain_dot(o_ref[rows, :], w_out) + shared_ref[2:3, :])
        hidden_ref[rows, :] = hidden
        normed, _, _ = norm_rows(hidden, shared_ref[3:4, :], shared_ref[4:5, :])
        second_ref[rows, :] = normed.astype(BF)
        out_ref[rows, :] = hidden + shared_ref[5:6, :]
    acc_ref[...] = jnp.zeros_like(acc_ref)

    def tile_copies(h, at, b):
        for i in range(n_half // 2):
            yield pltpu.make_async_copy(
                ff_ref.at[h * n_half + 2 * i + b, at], tiles_in.at[b, i], tile_sem.at[b, i]
            )

    def grad_copies(h, at):
        for b in range(2):
            for i in range(n_half // 2):
                part = stage.at[b, i]
                yield pltpu.make_async_copy(part, ff_grad_ref.at[h * n_half + 2 * i + b, at], stage_sem.at[b, i])

    def feed(n):
        h, k = n // slots, n % slots
        at = t + (k + 1) // 2 * (1 - 2 * (k % 2))

        @pl.when((at >= 0) & (at < n_tensor))
        def _():
            arrived(ff_ref.at[pl.ds(h * n_half, n_half), at, :, 1 - core], core_recv.at[1 + h, k])
            for b in range(2):
                for copy in tile_copies(h, at, b):
                    copy.start()
            for copy in tile_copies(h, at, 0):
                copy.wait()
            w_fc = tiles_in[0].reshape(strip, width)
            second, dy = second_ref[...], dy_ref[...]
            pre = rows_by_rows(second, w_fc) + fc_rows[h, at]
            for copy in tile_copies(h, at, 1):
                copy.wait()
            w_proj = tiles_in[1].reshape(strip, width)
            grad_activ = rows_by_rows(dy, w_proj)
            activ, slope = gelu_parts(pre)
            activ = activ.astype(BF)
            grad_pre = (grad_activ * slope).astype(BF)
            out_ref[...] += plain_dot(activ, w_proj)
            acc_ref[...] += plain_dot(grad_pre, w_fc)
            fc_bias_ref[h, at] = jnp.sum(grad_pre.astype(F32), axis=0, keepdims=True)

            @pl.when(n > 0)
            def _():
                for copy in grad_copies(h, at):
                    copy.wait()

            stage[0] = cols_by_cols(grad_pre, second).astype(BF).reshape(stage.shape[1:])
            stage[1] = cols_by_cols(activ, dy).astype(BF).reshape(stage.shape[1:])
            for copy in grad_copies(h, at):
                copy.start()

    for event in during[5].get(0, []):
        event()
    loop_with(2 * slots, feed, during[6])
    for copy in grad_copies(0, 0):
        copy.wait()

    sums_ref[...] = jnp.zeros_like(sums_ref)

    def norm_back_rows(i, carry):
        rows = pl.ds(pl.multiple_of(i * part, part), part)
        _, hat, inverse = norm_rows(hidden_ref[rows, :], 1.0, 0.0)
        grad_second, grad_y = acc_ref[rows, :], dy_ref[rows, :].astype(F32)
        grad = grad_y + norm_back(grad_second, hat, inverse, shared_ref[3:4, :])
        low = grad.astype(BF)
        grad_ref[rows, :] = grad
        second_ref[rows, :] = low
        for n, term in enumerate((low.astype(F32), grad_second * hat, grad_second, grad_y)):
            sums_ref[n : n + 1, :] += jnp.sum(term, axis=0, keepdims=True)
        return carry

    lax.fori_loop(0, rows_here // part, norm_back_rows, 0)

    def out_back(i):
        cols = pl.ds(pl.multiple_of(i * tile, tile), tile)
        w = att_ref[3, pl.ds(i * tile // (width // n_tensor), 1)].reshape(tile, width)
        do_ref[:, cols] = rows_by_rows(second_ref[...], w).astype(BF)
        go_ref[pl.ds(pl.multiple_of(i * tile, tile), tile), :] = cols_by_cols(o_ref[:, cols], second_ref[...]).astype(BF)

    loop_with(tiles, out_back, {})

    for g in range(n_groups):
        for s in range(-1, steps):
            each(given, g, s)
        arrived(weights[g].at[:, :, pl.ds(0, 3), 0], xy_send.at[g])
        for up in (True, False):
            for s in range(steps):
                have = last if up else first
                if s > 0:
                    have = have & z_step(s - 1, up)[2]

                @pl.when(have)
                def _(g=g, s=s, up=up):
                    arrived(block(g, t, column, core), z_send.at[g, 0 if up else 1, s])
    for r in range(back):
        @pl.when(last & (t >= r))
        def _(r=r):
            arrived(wide_ref.at[back], a_send.at[r])
    for k in range(1, 8):
        arrived(pieces.at[0], swap_send.at[k - 1])


def forward_spread(master_low, tokens, out_grad, bias_row, first_seen, shared, slot_of_unit, n_tensor, back):
    cap, unit_rows, width = master_low.shape
    n_units = slot_of_unit.shape[0]
    n_ff = n_units - 4
    piece = unit_rows // 8
    rows = tokens.shape[0]
    n_keys = (back + 1) * rows
    strip = n_ff // 4 * unit_rows
    bias_row = bias_row.reshape(-1, 128)
    any_spec = pl.BlockSpec(memory_space=pl.ANY)
    vmem = pl.BlockSpec(memory_space=pltpu.VMEM)
    dma = pltpu.SemaphoreType.DMA
    shape = jax.ShapeDtypeStruct
    units = lambda n: shape((n, n_tensor, 4, 2, piece, width), BF)
    stats = shape((width // PAIR, 2, rows), F32)
    low, high = shape((rows, width), BF), shape((rows, width), F32)
    keys = shape((n_keys, width), BF)
    outs = pl.pallas_call(
        functools.partial(forward_kernel, n_tensor, back, 1.0 / math.sqrt(HD)),
        out_shape=[
            units(4), units(n_ff), shape((back + 1, rows, width), BF), low, keys, keys, low, stats, stats,
            high, high, low, shape((n_ff, n_tensor, 4, 2, piece, width), BF), shape((width, width), BF),
            shape((2, n_tensor, 1, strip), F32), shape((4, width), F32),
        ],
        in_specs=[pl.BlockSpec(memory_space=pltpu.SMEM), any_spec] + [vmem] * 5,
        out_specs=[vmem, any_spec] + [vmem] * 10 + [any_spec] + [vmem] * 3,
        scratch_shapes=[
            pltpu.VMEM((8, cap, piece, width), BF),
            pltpu.VMEM((n_units, piece, width), BF),
            pltpu.VMEM((n_keys, rows), F32),
            pltpu.VMEM((3, width), F32),
            pltpu.VMEM((n_tensor, *bias_row.shape), F32),
            pltpu.VMEM((2, n_tensor, 1, strip), F32),
            pltpu.VMEM((rows, width), F32),
            pltpu.VMEM((rows, width), BF),
            pltpu.VMEM((rows, width), F32),
            pltpu.VMEM((2, n_ff // 4, 4, 2, piece, width), BF),
            pltpu.VMEM((2, n_ff // 4, 4, 2, piece, width), BF),
            dma((7,)), dma((7,)), dma((4,)), dma((back,)), dma((back,)),
            dma((n_tensor - 1,)), dma((n_tensor - 1,)),
            dma((3, 2, n_tensor - 1)), dma((3, 2, n_tensor - 1)),
            dma((3,)), dma((3, 2 * n_tensor - 1, 3)),
            dma((3, 2 * n_tensor - 1)), dma((3, 2 * n_tensor - 1)),
            dma((2, n_ff // 4)), dma((2, n_ff // 4)),
        ],
        compiler_params=pltpu.CompilerParams(collective_id=0, has_side_effects=True, vmem_limit_bytes=60 << 20),
        name="forward_spread",
    )(
        slot_of_unit, master_low.reshape(cap, 8, piece, width), tokens, out_grad, bias_row, first_seen, shared
    )
    att, _, wide, *rest = outs
    return att.reshape(-1, width), wide.reshape(-1, width), *rest


def split_units(ref, count):
    many = ref.shape[0] // count
    return [ref.at[pl.ds(i * many, many)] for i in range(count)]


def add_blocks(into, part, count):
    def body(i, carry):
        a = into(i)
        a[...] = a[...] + part(i)[...]
        return carry

    lax.fori_loop(0, count, body, 0)


BACK_ORDER = (
    0, -1, -1, 103, 10, 100, -1, 102, 101, -1, 113, -1, 110, -1, 201, 203, 20, 202, -1, 112, 301, 213, -1, 302,
    303, 200, -2, 111, -2, -2, -2, 313, 900, 123, 120, -2, 300, 212, -2, 122, 121, -2, 600, 210, 502, -2, -2,
    30, -2, -2, 211, -2, 223, 133, 130, 503, 310, -3, 312, 602, 700, -3, 702, -3, 512, 311, -3, 403, 220, -4,
    -4, 221, -4, -4, 222, -5, 230, 610, -5, 401, 411, 323, 513, 402, 132, 501, 131, 601, 320, -5, 330, 321, -5,
    523, 231, 620, 233, 901, 322, 423, 331, 611, 232, 612, 701, 621, 522, 511, 333, 421, 412, 720, 521, 711,
    332, 722, 533, 710, 721, 532, 630, 631, 413, 712, 422, 730, 433, 531, 432, 732, 632, 731, 431, 622,
)


LAST_ORDER = (
    0, 103, 100, 900, 10, 102, 101, 203, 113, 110, 202, 200, 303, 201, 213, 300, 112, 301, 111, 313, 210, 302,
    901, 903, 910, 702, 503, 600, 212, 310, 911, 513, 211, 610, 312, 912, 501, 502, 700, 311, 403, 712, 601,
    612, 913, 512, 413, 710, 602, 701, 511, 611, 914, 402, 411, 711, 401, 412,
)


class Reducer:
    def __init__(self, groups, n_tensor, other, near, one, two, up_in, down_in, final, sems):
        self.groups, self.n_tensor = groups, n_tensor
        self.other, self.near, self.one, self.two = other, near, one, two
        self.up_in, self.down_in, self.final = up_in, down_in, final
        (
            self.near_sem, self.core_send, self.core_recv, self.one_send, self.one_recv,
            self.two_send, self.two_recv, self.z_send, self.z_recv,
        ) = sems
        self.d, self.t, self.core, self.x, self.y = place()
        self.by_x, self.by_y = self.d + 2 - 4 * self.x, self.d + 4 - 8 * self.y
        self.sibling = self.d + 1 - 2 * self.core
        self.order = sorted(range(n_tensor), key=lambda a: (-abs(2 * a - n_tensor + 1), -a))
        self.merges = [(g, at) for g in range(len(groups)) for at in self.order]
        self.starts, total = [], 0
        for refs in groups:
            self.starts.append(total)
            total += sum(r.shape[0] for r in refs)
        self.ends = [*self.starts[1:], total]

    @staticmethod
    def scratch(n_units, n_group, n_groups, n_refs, n_tensor, block):
        dma = pltpu.SemaphoreType.DMA
        return [
            pltpu.VMEM((n_units, n_tensor, 2, 2, *block), BF),
            pltpu.VMEM((2, n_group, 2, 2, *block), BF),
            pltpu.VMEM((n_units, n_tensor, 2, *block), BF),
            pltpu.VMEM((n_units, n_tensor, *block), BF),
            pltpu.VMEM((n_units, n_tensor, *block), BF),
            pltpu.VMEM((n_units, n_tensor, *block), BF),
            dma((2, n_refs)), dma((n_groups, n_refs)), dma((n_groups, n_refs)),
            dma((n_groups, n_tensor)), dma((n_groups, n_tensor)),
            dma((n_groups, n_tensor)), dma((n_groups, n_tensor)),
            dma((n_groups, n_tensor)), dma((n_groups, n_tensor, 2)),
        ]

    def parts(self, g):
        u = self.starts[g]
        for n, ref in enumerate(self.groups[g]):
            yield n, ref, u, ref.shape[0]
            u += ref.shape[0]

    def units(self, g):
        return pl.ds(self.starts[g], self.ends[g] - self.starts[g])

    def count(self, g):
        return self.ends[g] - self.starts[g]

    def near_copies(self, m):
        g, at = self.merges[m]
        for n, ref, u, many in self.parts(g):
            yield pltpu.make_async_copy(
                ref.at[:, at, :, :, self.core],
                self.near.at[m % 2, pl.ds(u - self.starts[g], many)],
                self.near_sem.at[m % 2, n],
            )

    def core_go(self, g):
        for n, ref, u, many in self.parts(g):
            send(
                ref.at[:, :, :, :, 1 - self.core], self.other.at[pl.ds(u, many)],
                self.core_send.at[g, n], self.core_recv.at[g, n], (self.sibling, self.t),
            )

    def start(self):
        for m in range(2):
            for copy in self.near_copies(m):
                copy.start()

    def by_rows(self, at):
        return at * 2 < self.n_tensor

    def first_hop(self, m):
        g, at = self.merges[m]
        if m % self.n_tensor == 0:
            for n, ref, u, many in self.parts(g):
                arrived(self.other.at[pl.ds(u, many)], self.core_recv.at[g, n])
        for copy in self.near_copies(m):
            copy.wait()
        u0 = self.starts[g]
        add_blocks(
            lambda i: self.other.at[u0 + i // 4, at, (i // 2) % 2, i % 2],
            lambda i: self.near.at[m % 2, i // 4, (i // 2) % 2, i % 2],
            4 * self.count(g),
        )
        if m + 2 < len(self.merges):
            for copy in self.near_copies(m + 2):
                copy.start()
        us = self.units(g)
        rows = self.by_rows(at)
        source = self.other.at[us, at, 1 - self.y] if rows else self.other.at[us, at, :, 1 - self.x]
        to = self.by_y if rows else self.by_x
        send(source, self.one.at[us, at], self.one_send.at[g, at], self.one_recv.at[g, at], (to, self.t))

    def second_hop(self, m):
        g, at = self.merges[m]
        us, u0 = self.units(g), self.starts[g]
        arrived(self.one.at[us, at], self.one_recv.at[g, at])
        if self.by_rows(at):
            into = lambda i: self.other.at[u0 + i // 2, at, self.y, i % 2]
            source, to = self.other.at[us, at, self.y, 1 - self.x], self.by_x
        else:
            into = lambda i: self.other.at[u0 + i // 2, at, i % 2, self.x]
            source, to = self.other.at[us, at, 1 - self.y, self.x], self.by_y
        add_blocks(into, lambda i: self.one.at[u0 + i // 2, at, i % 2], 2 * self.count(g))
        send(source, self.two.at[us, at], self.two_send.at[g, at], self.two_recv.at[g, at], (to, self.t))

    def plane_sum(self, m):
        g, at = self.merges[m]
        us, u0, n = self.units(g), self.starts[g], self.count(g)
        arrived(self.two.at[us, at], self.two_recv.at[g, at])
        add_blocks(lambda i: self.other.at[u0 + i, at, self.y, self.x], lambda i: self.two.at[u0 + i, at], n)
        if at > 0:
            pl.when(self.t == 0)(functools.partial(self.line_go, g, at, True))
        if at < self.n_tensor - 1:
            pl.when(self.t == self.n_tensor - 1)(functools.partial(self.line_go, g, at, False))

    def line_go(self, g, at, up):
        us = self.units(g)
        into, way, to = (self.up_in, 0, self.t + 1) if up else (self.down_in, 1, self.t - 1)
        send(self.other.at[us, at, self.y, self.x], into.at[us, at], self.z_send.at[g, at], self.z_recv.at[g, at, way], (self.d, to))

    def line_in(self, g, at, up):
        us, u0, n, t = self.units(g), self.starts[g], self.count(g), self.t
        buffer, way = (self.up_in, 0) if up else (self.down_in, 1)
        arrived(buffer.at[us, at], self.z_recv.at[g, at, way])
        add_blocks(lambda i: self.other.at[u0 + i, at, self.y, self.x], lambda i: buffer.at[u0 + i, at], n)
        pl.when(t < at if up else t > at)(functools.partial(self.line_go, g, at, up))

    def line(self, g, at, up, near):
        t, top = self.t, self.n_tensor - 1
        have = ((t <= at) & (t > 0)) if up else ((t >= at) & (t < top))
        half = t * 2 > top
        pl.when(have & (half if near else ~half))(functools.partial(self.line_in, g, at, up))

    def keep(self):
        for g in range(len(self.groups)):
            us = self.units(g)
            self.final[us] = self.other[us, self.t, self.y, self.x]

    def codes(self):
        out = {}
        for g in range(len(self.groups)):
            out[10 * g] = functools.partial(self.core_go, g)
            for i, at in enumerate(self.order):
                m, here = g * self.n_tensor + i, 10 * g + at
                out[100 + here] = functools.partial(self.first_hop, m)
                out[200 + here] = functools.partial(self.second_hop, m)
                out[300 + here] = functools.partial(self.plane_sum, m)
                for kind in range(4):
                    out[400 + 100 * kind + here] = functools.partial(self.line, g, at, kind < 2, kind % 2 == 0)
        return out

    def finish(self):
        for g in range(len(self.groups)):
            us = self.units(g)
            for n, ref, u, many in self.parts(g):
                arrived(self.other.at[pl.ds(u, many)], self.core_send.at[g, n])
            for at in range(self.n_tensor):
                arrived(self.one.at[us, at], self.one_send.at[g, at])
                arrived(self.two.at[us, at], self.two_send.at[g, at])

                @pl.when(self.t != at)
                def _(us=us, g=g, at=at):
                    arrived(self.up_in.at[us, at], self.z_send.at[g, at])


REDUCER = 15


def backward_kernel(
    n_tensor, back, scale,
    ff_grad_ref, q_ref, k_ref, v_ref, o_ref, do_ref, lse_ref, first_ref, wide_ref, att_ref,
    shard_ref, grad_ref, away, gq_ref, gk_ref, gv_ref, sums_ref, *scratch,
):
    reducer_scratch, (
        seen_ref, q_in, k_in, v_in, o_in, do_in, dq_ref, dk_ref, dv_ref, big, stage, dk_acc, dv_acc, away_in,
        pair_sem, load_sem, stage_sem, away_send, away_recv,
    ) = scratch[:REDUCER], scratch[REDUCER:]
    d, t, core, x, y = place()
    greet(d, t, n_tensor)
    other, near, one, two, up_in, down_in, *sems = reducer_scratch
    groups = [[part] for part in split_units(ff_grad_ref, BACK_GROUPS)]
    reducer = Reducer(groups, n_tensor, other, near, one, two, up_in, down_in, shard_ref, sems)
    reducer.start()
    by_code = reducer.codes()

    def give():
        @pl.when(t >= 2)
        def _():
            send(away.at[1], away_in, away_send, away_recv, (d, t - 1))

    def add_given():
        @pl.when((t >= 1) & (t + 1 < n_tensor))
        def _():
            arrived(away_in, away_recv)
            away[0] = (away[0].astype(F32) + away_in[...].astype(F32)).astype(BF)

    by_code |= {900: give, 901: add_given}
    early, during = by_step(BACK_ORDER, by_code, 5)
    for event in early:
        event()
    rows_here, width = do_ref.shape
    n_keys = k_ref.shape[0]
    size, span = q_tiles(rows_here, n_keys)
    sources = ((q_ref, q_in), (k_ref, k_in), (v_ref, v_in), (o_ref, o_in), (do_ref, do_in))

    def pair_copies(i):
        lanes = pl.ds(pl.multiple_of(i * PAIR, PAIR), PAIR)
        return [
            pltpu.make_async_copy(ref.at[:, lanes], buffer.at[i % 2], pair_sem.at[i % 2, n])
            for n, (ref, buffer) in enumerate(sources)
        ]

    for copy in pair_copies(0):
        copy.start()
    weights = pltpu.make_async_copy(att_ref.at[pl.ds(0, 3 * width)], big, load_sem.at[0])
    weights.start()
    fill_bias(seen_ref, first_ref)
    pairs = width // PAIR

    def attend_back(i):
        for copy in pair_copies(i):
            copy.wait()

        @pl.when(i + 1 < pairs)
        def _():
            for copy in pair_copies(i + 1):
                copy.start()

        slot = i % 2
        lanes_here = pl.ds(pl.multiple_of(i * PAIR, PAIR), PAIR)
        dk_acc[...] = jnp.zeros_like(dk_acc)
        dv_acc[...] = jnp.zeros_like(dv_acc)
        dq_sum = jnp.zeros((1, PAIR), F32)
        for j in range(rows_here // size):
            rows, keys = pl.ds(j * size, size), pl.ds(j * size, span)
            q_here, do_here = q_in[slot, rows, :], do_in[slot, rows, :]
            k_here, v_here = k_in[slot, keys, :], v_in[slot, keys, :]
            k_t = k_here.T
            meet = (do_here.astype(F32) * o_in[slot, rows, :].astype(F32)).T
            outs = []
            for h in range(2):
                lanes = head_lanes(h)
                delta = jnp.sum(meet[h * HD : (h + 1) * HD], axis=0, keepdims=True)
                s = rows_by_rows(jnp.where(lanes, k_here, 0), q_here) + seen_ref[keys, rows]
                p = jnp.exp(s - lse_ref[i, h : h + 1, rows])
                dp = rows_by_rows(jnp.where(lanes, v_here, 0), do_here)
                ds = (p * (dp - delta)).astype(BF)
                dv_acc[keys, :] += plain_dot(p.astype(BF), jnp.where(lanes, do_here, 0))
                dk_acc[keys, :] += plain_dot(ds, jnp.where(lanes, q_here, 0))
                outs.append(plain_dot(k_t[h * HD : (h + 1) * HD], ds))
            dq = (jnp.concatenate(outs, axis=0).T * scale).astype(BF)
            dq_ref[rows, lanes_here] = dq
            dq_sum += jnp.sum(dq.astype(F32), axis=0, keepdims=True)
        dk, dv = dk_acc[...].astype(BF), dv_acc[...].astype(BF)
        dk_ref[:, lanes_here] = dk
        dv_ref[:, lanes_here] = dv
        sums_ref[0:1, lanes_here] = dq_sum
        sums_ref[1:2, lanes_here] = jnp.sum(dk.astype(F32), axis=0, keepdims=True)
        sums_ref[2:3, lanes_here] = jnp.sum(dv.astype(F32), axis=0, keepdims=True)

    tile = 256
    tiles = width // tile

    def input_grad(r):
        rows = pl.ds((back - r) * rows_here, rows_here)

        def body(i):
            cols = pl.ds(pl.multiple_of(i * tile, tile), tile)
            total = plain_dot(dk_ref[rows, :], big[width : 2 * width, cols]) + plain_dot(dv_ref[rows, :], big[2 * width :, cols])
            if r == 0:
                grad_ref[:, cols] = total + plain_dot(dq_ref[...], big[:width, cols])
            else:
                away[r - 1, :, cols] = total.astype(BF)

        return body

    def weight_grad(n, from_ref, into_ref, first_row, many):
        def body(i):
            cols = pl.ds(pl.multiple_of(i * tile, tile), tile)
            slot = i % 2
            out = pltpu.make_async_copy(stage.at[slot], into_ref.at[pl.ds(i * tile, tile)], stage_sem.at[slot])

            @pl.when((i >= 2) | (n > 0))
            def _():
                out.wait()

            total = lax.dot_general(
                from_ref[:, cols], tokens_of(first_row, many), (((0,), (0,)), ((), ())), preferred_element_type=F32
            )
            stage[slot] = total.astype(BF)
            out.start()

        return body

    def tokens_of(first_row, many):
        return big[pl.ds(first_row, many), :]

    loop_with(pairs, attend_back, during[1])
    weights.wait()
    for n, r in enumerate(range(back, -1, -1)):
        loop_with(tiles, input_grad(r), {i - n * tiles: e for i, e in during[2].items() if i // tiles == n})
    load = pltpu.make_async_copy(wide_ref, big.at[pl.ds(0, n_keys)], load_sem.at[1])
    load.start()
    load.wait()
    own = n_keys - rows_here
    loop_with(tiles, weight_grad(0, dq_ref, gq_ref, own, rows_here), during[3])
    loop_with(tiles, weight_grad(1, dk_ref, gk_ref, 0, n_keys), during[4])
    loop_with(tiles, weight_grad(2, dv_ref, gv_ref, 0, n_keys), during[5])
    reducer.keep()
    for slot in range(2):
        arrived(stage.at[slot], stage_sem.at[slot])

    @pl.when(t >= 2)
    def _():
        arrived(away.at[1], away_send)
    reducer.finish()


def backward_reduce(grad_ff, q, k, v, o, do, lse, first_seen, wide, w_att, n_tensor, back):
    rows, width = q.shape
    n_keys = k.shape[0]
    n_ff = grad_ff.shape[0]
    block = grad_ff.shape[-2:]
    any_spec = pl.BlockSpec(memory_space=pl.ANY)
    vmem = pl.BlockSpec(memory_space=pltpu.VMEM)
    dma = pltpu.SemaphoreType.DMA
    shape = jax.ShapeDtypeStruct
    square = shape((width, width), BF)
    pair = lambda n: pltpu.VMEM((2, n, PAIR), BF)
    return pl.pallas_call(
        functools.partial(backward_kernel, n_tensor, back, 1.0 / math.sqrt(HD)),
        out_shape=[shape((n_ff, *block), BF), shape((rows, width), F32), shape((back, rows, width), BF), square, square, square, shape((3, width), F32)],
        in_specs=[any_spec] * 6 + [vmem, vmem] + [any_spec] * 2,
        out_specs=[vmem, vmem, vmem, any_spec, any_spec, any_spec, vmem],
        scratch_shapes=[
            *Reducer.scratch(n_ff, n_ff // BACK_GROUPS, BACK_GROUPS, 1, n_tensor, block),
            pltpu.VMEM((n_keys, rows), F32),
            pair(rows), pair(n_keys), pair(n_keys), pair(rows), pair(rows),
            pltpu.VMEM((rows, width), BF), pltpu.VMEM((n_keys, width), BF), pltpu.VMEM((n_keys, width), BF),
            pltpu.VMEM((3 * width, width), BF),
            pltpu.VMEM((2, 256, width), BF),
            pltpu.VMEM((n_keys, PAIR), F32), pltpu.VMEM((n_keys, PAIR), F32),
            pltpu.VMEM((rows, width), BF),
            dma((2, 5)), dma((2,)), dma((2,)), dma, dma,
        ],
        compiler_params=pltpu.CompilerParams(collective_id=1, has_side_effects=True, vmem_limit_bytes=60 << 20),
        name="backward_reduce",
    )(grad_ff, q, k, v, o, do, lse, first_seen, wide, w_att)


def join(row, a, b):
    return jnp.where(row == MAX_ROW, jnp.maximum(a, b), a + b)


def finish_kernel(
    n_tensor,
    unit_ref, gq_ref, gk_ref, gv_ref, go_ref, shard_ref, grad_ref, away_ref, hidden_ref, x_ref, shared_ref, v_ref,
    out_ref, vsum_ref, input_ref, *scratch,
):
    reducer_scratch, (
        final, outgo, v_in, v_z, away_in, swap_send, swap_recv, v_send, v_recv, local_sem, away_send, away_recv,
    ) = (
        scratch[:REDUCER], scratch[REDUCER:]
    )
    d, t, core, x, y = place()
    greet(d, t, n_tensor)
    other, near, one, two, up_in, down_in, *sems = reducer_scratch
    parts = [gq_ref, gk_ref, gv_ref, go_ref]
    groups = [parts[i : i + 4 // LAST_GROUPS] for i in range(0, 4, 4 // LAST_GROUPS)]
    reducer = Reducer(groups, n_tensor, other, near, one, two, up_in, down_in, final, sems)
    reducer.start()
    rows_here = x_ref.shape[0]
    n_att = other.shape[0]
    final[n_att:] = shard_ref[...]

    from_above, to_below = t + 1 < n_tensor, t >= 1

    @pl.when(~from_above)
    def _():
        away_in[...] = jnp.zeros_like(away_in)

    def give():
        @pl.when(to_below)
        def _():
            send(away_ref.at[0], away_in, away_send, away_recv, (d, t - 1))

    def got():
        @pl.when(from_above)
        def _():
            arrived(away_in, away_recv)

    vsum_ref[...] = v_ref[...]
    part = 128
    gain = shared_ref[0:1, :]

    def norm_back_rows(i, carry):
        rows = pl.ds(pl.multiple_of(i * part, part), part)
        _, hat, inverse = norm_rows(x_ref[rows, :].astype(F32), 1.0, 0.0)
        grad = grad_ref[rows, :] + away_in[rows, :].astype(F32)
        input_ref[rows, :] = hidden_ref[rows, :] + norm_back(grad, hat, inverse, gain)
        vsum_ref[0:1, :] += jnp.sum(grad * hat, axis=0, keepdims=True)
        vsum_ref[1:2, :] += jnp.sum(grad, axis=0, keepdims=True)
        return carry

    row = lax.broadcasted_iota(jnp.int32, vsum_ref.shape, 0)
    hops = (reducer.sibling, reducer.by_x, reducer.by_y)

    def vector_step(i):
        if i > 0:
            arrived(v_in.at[i - 1], v_recv.at[i - 1])
            arrived(v_in.at[i - 1], v_send.at[i - 1])
            vsum_ref[...] = join(row, vsum_ref[...], v_in[i - 1])
        if i < len(hops):
            send(vsum_ref, v_in.at[i], v_send.at[i], v_recv.at[i], (hops[i], t))
        else:
            for k in range(1, n_tensor):
                send(vsum_ref, v_z.at[k - 1], v_send.at[2 + k], v_recv.at[2 + k], (d, (t + k) % n_tensor))

    def vector_end():
        for k in range(1, n_tensor):
            arrived(v_z.at[k - 1], v_recv.at[2 + k])
            arrived(v_z.at[k - 1], v_send.at[2 + k])
        for k in range(1, n_tensor):
            vsum_ref[...] = join(row, vsum_ref[...], v_z[k - 1])

    by_code = reducer.codes()
    by_code |= {910 + i: functools.partial(vector_step, i) for i in range(len(hops) + 1)}
    by_code |= {900: give, 901: got, 914: vector_end}
    by_code[903] = lambda: lax.fori_loop(0, rows_here // part, norm_back_rows, 0)
    for code in LAST_ORDER:
        by_code[code]()
    reducer.keep()

    cap = out_ref.shape[0]
    for k in range(1, 9):
        to = (d + k) % 8
        for j in range(cap):
            outgo[to, j] = final[unit_ref[to * cap + j]]
        if k < 8:
            send(outgo.at[to], out_ref.at[:, d], swap_send.at[k - 1], swap_recv.at[k - 1], (to, t))
    keep = pltpu.make_async_copy(outgo.at[d], out_ref.at[:, d], local_sem.at[0])
    keep.start()
    for k in range(1, 8):
        arrived(out_ref.at[:, (d + 8 - k) % 8], swap_recv.at[k - 1])
    reducer.finish()
    for k in range(1, 8):
        arrived(outgo.at[0], swap_send.at[k - 1])

    @pl.when(to_below)
    def _():
        arrived(away_in, away_send)
    keep.wait()


def finish_reduce(grads, shard, grad_first, away, grad_hidden, tokens, shared, vectors, unit_of_slot, n_tensor, cap):
    block = shard.shape[1:]
    n_units = len(grads) + shard.shape[0]
    rows, width = tokens.shape
    any_spec = pl.BlockSpec(memory_space=pl.ANY)
    vmem = pl.BlockSpec(memory_space=pltpu.VMEM)
    dma = pltpu.SemaphoreType.DMA
    shape = jax.ShapeDtypeStruct
    out, vsum, input_grad = pl.pallas_call(
        functools.partial(finish_kernel, n_tensor),
        out_shape=[shape((cap, 8, *block), BF), shape(vectors.shape, F32), shape((rows, width), F32)],
        in_specs=[pl.BlockSpec(memory_space=pltpu.SMEM)] + [any_spec] * 4 + [vmem, vmem, any_spec] + [vmem] * 4,
        out_specs=[vmem, vmem, vmem],
        scratch_shapes=[
            *Reducer.scratch(len(grads), 4 // LAST_GROUPS, LAST_GROUPS, 4 // LAST_GROUPS, n_tensor, block),
            pltpu.VMEM((n_units, *block), BF),
            pltpu.VMEM((8, cap, *block), BF),
            pltpu.VMEM((3, *vectors.shape), F32),
            pltpu.VMEM((n_tensor - 1, *vectors.shape), F32),
            pltpu.VMEM(away.shape[1:], BF),
            dma((7,)), dma((7,)), dma((2 + n_tensor,)), dma((2 + n_tensor,)), dma((1,)),
            dma, dma,
        ],
        compiler_params=pltpu.CompilerParams(collective_id=2, has_side_effects=True, vmem_limit_bytes=48 << 20),
        name="finish_reduce",
    )(unit_of_slot, *grads, shard, grad_first, away, grad_hidden, tokens, shared, vectors)
    return out.reshape(cap, -1, width), vsum, input_grad


def feed_forward_kernel(
    hidden_ref, dy_ref, shared_ref, bias_ref, fc_ref, proj_ref,
    out_ref, grad_ref, low_ref, fc_grad_ref, proj_grad_ref, fc_bias_ref, sums_ref,
    second_ref, acc_ref,
):
    step = pl.program_id(0)

    @pl.when(step == 0)
    def _():
        normed, _, _ = norm_rows(hidden_ref[...], shared_ref[3:4, :], shared_ref[4:5, :])
        second_ref[...] = normed.astype(BF)
        out_ref[...] = hidden_ref[...] + shared_ref[5:6, :]
        acc_ref[...] = jnp.zeros_like(acc_ref)

    dy, second = dy_ref[...], second_ref[...]
    pre = rows_by_rows(second, fc_ref[...]) + bias_ref[0]
    cube = pre * pre
    inner = jnp.tanh(GELU_A * (pre + GELU_B * (cube * pre)))
    half = 0.5 * pre
    activ = (half + half * inner).astype(BF)
    slope = 0.5 + 0.5 * inner + half * (1.0 - inner * inner) * (GELU_A + (3.0 * GELU_A * GELU_B) * cube)
    out_ref[...] += plain_dot(activ, proj_ref[...])
    proj_grad_ref[...] = cols_by_cols(activ, dy).astype(BF)
    grad_pre = (rows_by_rows(dy, proj_ref[...]) * slope).astype(BF)
    fc_bias_ref[0] = jnp.sum(grad_pre.astype(F32), axis=0, keepdims=True)
    fc_grad_ref[...] = cols_by_cols(grad_pre, second).astype(BF)
    acc_ref[...] += plain_dot(grad_pre, fc_ref[...])

    @pl.when(step == pl.num_programs(0) - 1)
    def _():
        _, hat, inverse = norm_rows(hidden_ref[...], 1.0, 0.0)
        grad_second, grad_y = acc_ref[...], dy.astype(F32)
        grad = grad_y + norm_back(grad_second, hat, inverse, shared_ref[3:4, :])
        low = grad.astype(BF)
        grad_ref[...] = grad
        low_ref[...] = low
        for n, rows in enumerate((low.astype(F32), grad_second * hat, grad_second, grad_y)):
            sums_ref[n : n + 1, :] = jnp.sum(rows, axis=0, keepdims=True)


def feed_forward(hidden, out_grad, shared, b_fc, w_fc, w_proj):
    rows, width = hidden.shape
    tile = 512
    steps = w_fc.shape[0] // tile
    whole = lambda *dims: pl.BlockSpec(dims, lambda i: (0,) * len(dims))
    strip = pl.BlockSpec((tile, width), lambda i: (i, 0))
    bias = pl.BlockSpec((1, 1, tile), lambda i: (i, 0, 0))
    shape = jax.ShapeDtypeStruct
    out = pl.pallas_call(
        feed_forward_kernel,
        grid=(steps,),
        in_specs=[whole(rows, width), whole(rows, width), whole(*shared.shape), bias, strip, strip],
        out_specs=[whole(rows, width)] * 3 + [strip, strip, bias, whole(4, width)],
        out_shape=[
            shape((rows, width), F32), shape((rows, width), F32), shape((rows, width), BF),
            shape(w_fc.shape, BF), shape(w_proj.shape, BF), shape((steps, 1, tile), F32), shape((4, width), F32),
        ],
        scratch_shapes=[pltpu.VMEM((rows, width), BF), pltpu.VMEM((rows, width), F32)],
        compiler_params=pltpu.CompilerParams(vmem_limit_bytes=48 << 20),
        name="feed_forward",
    )(hidden, out_grad, shared, b_fc.reshape(steps, 1, tile), w_fc, w_proj)
    return (*out[:5], out[5].reshape(-1), out[6])


def per_device(
    tokens_in,
    out_grad,
    lengths,
    owners,
    matrix_master,
    matrix_m1,
    matrix_m2,
    shared_params,
    bias_params,
):
    n_tensor = lax.axis_size("tensor")
    n_data = lax.axis_size("dp")
    tensor_index = lax.axis_index("tensor")
    data_index = lax.axis_index("dp")
    rows_here, width = tokens_in.shape
    slot_cap = matrix_master.shape[1]
    unit_rows = matrix_master.shape[2]
    n_units = owners.shape[0]
    n_slots = n_data * slot_cap
    head_rows = width // n_tensor
    heads_here = head_rows // HD
    ff_rows = (n_units * unit_rows - 4 * head_rows) // 2
    slot_of_unit, unit_of_slot, occupied = slot_tables(owners, n_slots, slot_cap)


    back = -(-(DOC_MOST - 1) // rows_here)
    reach = back * rows_here
    own_kernels = n_data == 8 and n_tensor == 4 and back == 2 and head_rows == unit_rows and unit_rows % 128 == 0
    sizes = lengths[0]
    upto = jnp.arange(sizes.shape[0])[:, None] >= jnp.arange(sizes.shape[0])[None, :]
    bounds = jnp.sum(jnp.where(upto, sizes[None, :], 0), axis=1)
    places = tensor_index * rows_here + jnp.arange(rows_here, dtype=jnp.int32)
    starts = jnp.max(jnp.where(places[:, None] >= bounds[None, :], bounds[None, :], 0), axis=1)
    first_seen = (starts - tensor_index * rows_here + reach)[None, :]

    shared = shared_params[0]
    inputs_f32 = tokens_in.astype(F32)
    normed_one, hat_one, inverse_one = norm_rows(inputs_f32, shared[0], shared[1])
    normed_low = normed_one.astype(BF)
    if own_kernels:
        (
            w_att, normed_all, q_scaled, keys_in, values_in, attended, log_norms, peaks,
            layer_out, grad_hidden, grad_attended, grad_ff_w, grad_out_w, grad_fc_b, shared_rows,
        ) = forward_spread(
            matrix_master[0].astype(BF), tokens_in, out_grad, bias_params[0, 0], first_seen, shared,
            slot_of_unit, n_tensor, back,
        )
    else:
        units = gather_units(matrix_master[0], slot_of_unit)
        stacks = units.reshape(n_tensor, n_units * unit_rows, width)
        part = lambda first, count: stacks[:, first : first + count].reshape(-1, width)
        w_q, w_k, w_v, w_out = (part(i * head_rows, head_rows) for i in range(4))
        w_fc = part(4 * head_rows, ff_rows)
        w_proj = part(4 * head_rows + ff_rows, ff_rows)
        all_bias = lax.all_gather(bias_params[0], "tensor", axis=0, tiled=True).reshape(n_tensor, -1)
        before = [
            lax.ppermute(normed_low, "tensor", [(i, i + r) for i in range(n_tensor - r)])
            for r in range(min(back, n_tensor - 1), 0, -1)
        ]
        blank = [jnp.zeros_like(normed_low)] * (back - len(before))
        normed_all = jnp.concatenate([*blank, *before, normed_low], axis=0)
        bias = lambda first, count: all_bias[:, first : first + count].reshape(-1)
        b_q, b_k, b_v = (bias(i * head_rows, head_rows) for i in range(3))
        b_fc = bias(3 * head_rows, ff_rows)
        q_scaled = (rows_by_rows(normed_low, w_q) + b_q).astype(BF) * jnp.asarray(1.0 / math.sqrt(HD), BF)
        keys_in = (rows_by_rows(normed_all, w_k) + b_k).astype(BF)
        values_in = (rows_by_rows(normed_all, w_v) + b_v).astype(BF)
        attended, log_norms, peaks = attend_forward(q_scaled, keys_in, values_in, first_seen)
        hidden = inputs_f32 + (plain_dot(attended, w_out) + shared[2])
        layer_out, grad_hidden, grad_hidden_low, grad_fc_w, grad_proj_w, grad_fc_b, shared_rows = feed_forward(
            hidden, out_grad, shared, b_fc, w_fc, w_proj
        )
        grad_out_w = cols_by_cols(attended, grad_hidden_low).astype(BF)
        grad_attended = rows_by_rows(grad_hidden_low, w_out).astype(BF)
    head_here = jnp.max(peaks, axis=2).reshape(-1)
    if own_kernels:
        in_blocks = lambda g: g.reshape(-1, n_tensor, 2, 2, 2, unit_rows // 8, width)
        shard, grad_first, away, grad_q_w, grad_k_w, grad_v_w, sums = backward_reduce(
            in_blocks(grad_ff_w), q_scaled, keys_in, values_in, attended, grad_attended,
            log_norms, first_seen, normed_all, w_att, n_tensor, back,
        )
        grad_fc_b = grad_fc_b.reshape(2, n_tensor, -1, unit_rows).swapaxes(1, 2)
        vectors = jnp.concatenate(
            [
                jnp.zeros((2, width), F32), shared_rows, sums, grad_fc_b.reshape(-1, width),
                jnp.pad(head_here, (0, width - head_here.shape[0]))[None], jnp.zeros((2, width), F32),
            ],
            axis=0,
        )
        grads = [in_blocks(g) for g in (grad_q_w, grad_k_w, grad_v_w, grad_out_w)]
        half = (n_units - 4) // 2
        later = unit_of_slot - 4
        spot_of_slot = jnp.where(later < 0, unit_of_slot, 4 + jnp.where(later < half, 2 * later, 2 * (later - half) + 1))
        my_grads, totals, input_grad = finish_reduce(
            grads, shard, grad_first, away, grad_hidden, tokens_in, shared, vectors, spot_of_slot, n_tensor, slot_cap
        )
        shared_grad = totals[:6]
        head_all = totals[MAX_ROW, : head_here.shape[0]]
        bias_total = totals[6:MAX_ROW].reshape(-1, n_tensor, unit_rows)
        bias_grad = lax.dynamic_index_in_dim(bias_total, tensor_index, 1, keepdims=False).reshape(-1)
    else:
        grad_q, grad_k, grad_v = attend_backward(
            q_scaled, keys_in, values_in, attended, grad_attended, log_norms, first_seen
        )
        grad_q_w = cols_by_cols(grad_q, normed_low)
        grad_k_w = cols_by_cols(grad_k, normed_all)
        grad_v_w = cols_by_cols(grad_v, normed_all)
        grad_wide = plain_dot(grad_k, w_k) + plain_dot(grad_v, w_v)
        grad_first = grad_wide[reach:] + plain_dot(grad_q, w_q)
        for r in range(1, min(back, n_tensor - 1) + 1):
            away = grad_wide[reach - r * rows_here : reach - (r - 1) * rows_here].astype(BF)
            grad_first += lax.ppermute(away, "tensor", [(i, i - r) for i in range(r, n_tensor)]).astype(F32)
        input_grad = grad_hidden + norm_back(grad_first, hat_one, inverse_one, shared[0])
        grad_qkv_b = [jnp.sum(g, axis=0, dtype=F32) for g in (grad_q, grad_k, grad_v)]
        first_rows = jnp.stack([jnp.sum(grad_first * hat_one, axis=0), jnp.sum(grad_first, axis=0)])
        shared_part = jnp.concatenate([first_rows, shared_rows], axis=0)
        by_tensor = lambda v: v.reshape(n_tensor, -1)
        bias_part = jnp.concatenate([by_tensor(v) for v in (*grad_qkv_b, grad_fc_b)], axis=1)
        head_all = lax.pmax(head_here, ("dp", "tensor"))
        shared_grad, bias_total = lax.psum((shared_part, bias_part), ("dp", "tensor"))
        bias_grad = lax.dynamic_index_in_dim(bias_total, tensor_index, 0, keepdims=False)
        by_stack = lambda g: g.astype(BF).reshape(n_tensor, -1, width)
        grad_units = jnp.concatenate(
            [by_stack(g) for g in (grad_q_w, grad_k_w, grad_v_w, grad_out_w, grad_fc_w, grad_proj_w)], axis=1
        ).reshape(units.shape)
        my_grads = scatter_units(grad_units, unit_of_slot)
    head_peak = lax.dynamic_slice_in_dim(head_all, tensor_index * heads_here, heads_here)

    my_units = lax.dynamic_slice_in_dim(unit_of_slot, data_index * slot_cap, slot_cap, 0)
    my_occupied = lax.dynamic_slice_in_dim(occupied, data_index * slot_cap, slot_cap, 0)[:, None, None]
    steps_done = float(STEP)
    root_gamma = jnp.sqrt(CLIP_TAU / jnp.maximum(head_peak, CLIP_TAU))
    row_index = my_units[:, None] * unit_rows + jnp.arange(unit_rows, dtype=jnp.int32)[None, :]
    local_head = jnp.where(row_index < head_rows, row_index // HD, (row_index - head_rows) // HD)
    head_match = local_head[..., None] == jnp.arange(heads_here, dtype=jnp.int32)[None, None, :]
    picked_root = jnp.sum(jnp.where(head_match, root_gamma, 0.0), axis=-1)
    factor = jnp.where(row_index < 2 * head_rows, picked_root, 1.0)
    kept = jnp.broadcast_to(my_occupied.astype(F32), (slot_cap, unit_rows, 1))
    my_grads, first_new, second_new, master_new = owner_step(
        my_grads, matrix_master[0], matrix_m1[0], matrix_m2[0], factor[..., None], kept
    )
    shared_first, shared_second, shared_new = adam_step(
        shared, shared_grad, shared_params[1], shared_params[2], steps_done, 0.0
    )
    bias_first, bias_second, bias_new = adam_step(
        bias_params[0, 0], bias_grad, bias_params[1, 0], bias_params[2, 0], steps_done, 0.0
    )
    shared_out = jnp.stack([shared_grad, shared_first])
    bias_out = jnp.stack([bias_grad, bias_first])[:, None, :]
    return (
        layer_out,
        input_grad,
        head_peak,
        my_grads[None],
        first_new[None],
        second_new[None],
        master_new[None],
        shared_out,
        shared_second,
        shared_new,
        bias_out,
        bias_second[None],
        bias_new[None],
    )


def solution(mesh):
    in_specs = (
        P(("dp", "tensor"), None),
        P(("dp", "tensor"), None),
        P("dp", None),
        P(),
        P("tensor", "dp", None, None),
        P("tensor", "dp", None, None),
        P("tensor", "dp", None, None),
        P(),
        P(None, "tensor", None),
    )
    out_specs = (
        P(("dp", "tensor"), None),
        P(("dp", "tensor"), None),
        P("tensor"),
        P("tensor", "dp", None, None),
        P("tensor", "dp", None, None),
        P("tensor", "dp", None, None),
        P("tensor", "dp", None, None),
        P(),
        P(),
        P(),
        P(None, "tensor", None),
        P("tensor", None),
        P("tensor", None),
    )
    return jax.shard_map(
        per_device, mesh=mesh, in_specs=in_specs, out_specs=out_specs, check_vma=False
    )
```
